32 devices in a mesh: wide: 8 (over z, core), narrow: 4 (over y, x).
Axes of the slice: x: 2, y: 2, z: 4, core: 2. Of those that a mesh axis runs over, the one named last changes fastest.
Arguments:
- tokens: bfloat16 [4096, 2048], P(('wide', 'narrow')), may hold values from -6 to 6
- cotangent: bfloat16 [4096, 2048], P(('wide', 'narrow')), may hold values from -6 to 6
- gain_copy: float32 [4352], replicated, may hold values from 0.5 to 1.5
- query_weight: bfloat16 [2048, 2048], P(None, 'narrow'), may hold values from -0.125 to 0.125
- keyvalue_weight: bfloat16 [2, 2048, 1024], P(None, None, 'narrow'), may hold values from -0.125 to 0.125
- output_weight: bfloat16 [2048, 2048], P('narrow'), may hold values from -1 to 1
- gateup_weight: bfloat16 [2, 2048, 6144], P(None, None, 'narrow'), may hold values from -0.125 to 0.125
- down_weight: bfloat16 [6144, 2048], P('narrow'), may hold values from -0.078125 to 0.078125
- query_master: float32 [2048, 2048], P('wide', 'narrow'), may hold values from -0.125 to 0.125
- query_moment: float32 [2048, 2048], P('wide', 'narrow'), may hold values from -32 to 32
- query_second: float32 [2048, 2048], P('wide', 'narrow'), may hold values from 2.9568 to 11.84
- query_average: float32 [2048, 2048], P('wide', 'narrow'), may hold values from -0.125 to 0.125
- keyvalue_master: float32 [2, 2048, 1024], P(None, 'wide', 'narrow'), may hold values from -0.125 to 0.125
- keyvalue_moment: float32 [2, 2048, 1024], P(None, 'wide', 'narrow'), may hold values from -48 to 48
- keyvalue_second: float32 [2, 2048, 1024], P(None, 'wide', 'narrow'), may hold values from 5.776 to 23.104
- keyvalue_average: float32 [2, 2048, 1024], P(None, 'wide', 'narrow'), may hold values from -0.125 to 0.125
- output_master: float32 [2048, 2048], P('narrow', 'wide'), may hold values from -1 to 1
- output_moment: float32 [2048, 2048], P('narrow', 'wide'), may hold values from -4 to 4
- output_second: float32 [2048, 2048], P('narrow', 'wide'), may hold values from 0.036 to 0.144
- output_average: float32 [2048, 2048], P('narrow', 'wide'), may hold values from -1 to 1
- gateup_master: float32 [2, 2048, 6144], P(None, 'wide', 'narrow'), may hold values from -0.125 to 0.125
- gateup_moment: float32 [2, 2048, 6144], P(None, 'wide', 'narrow'), may hold values from -14 to 14
- gateup_second: float32 [2, 2048, 6144], P(None, 'wide', 'narrow'), may hold values from 0.446464 to 1.785856
- gateup_average: float32 [2, 2048, 6144], P(None, 'wide', 'narrow'), may hold values from -0.125 to 0.125
- down_master: float32 [6144, 2048], P('narrow', 'wide'), may hold values from -0.078125 to 0.078125
- down_moment: float32 [6144, 2048], P('narrow', 'wide'), may hold values from -24 to 24
- down_second: float32 [6144, 2048], P('narrow', 'wide'), may hold values from 1.47456 to 5.89824
- down_average: float32 [6144, 2048], P('narrow', 'wide'), may hold values from -0.078125 to 0.078125
- gain_master: float32 [4352], P(('wide', 'narrow')), may hold values from 0.5 to 1.5
- gain_moment: float32 [4352], P(('wide', 'narrow'))
- gain_second: float32 [4352], P(('wide', 'narrow'))
- gain_average: float32 [4352], P(('wide', 'narrow')), may hold values from 0.1 to 1.9
Outputs:
- block_output: float32 [4096, 2048], P(('wide', 'narrow'))
- input_grad: float32 [4096, 2048], P(('wide', 'narrow'))
- query_grad: float32 [2048, 2048], P('wide', 'narrow')
- query_updated: float32 [2048, 2048], P('wide', 'narrow')
- query_moment_new: float32 [2048, 2048], P('wide', 'narrow')
- query_second_new: float32 [2048, 2048], P('wide', 'narrow')
- query_average_new: float32 [2048, 2048], P('wide', 'narrow')
- keyvalue_grad: float32 [2, 2048, 1024], P(None, 'wide', 'narrow')
- keyvalue_updated: float32 [2, 2048, 1024], P(None, 'wide', 'narrow')
- keyvalue_moment_new: float32 [2, 2048, 1024], P(None, 'wide', 'narrow')
- keyvalue_second_new: float32 [2, 2048, 1024], P(None, 'wide', 'narrow')
- keyvalue_average_new: float32 [2, 2048, 1024], P(None, 'wide', 'narrow')
- output_grad: float32 [2048, 2048], P('narrow', 'wide')
- output_updated: float32 [2048, 2048], P('narrow', 'wide')
- output_moment_new: float32 [2048, 2048], P('narrow', 'wide')
- output_second_new: float32 [2048, 2048], P('narrow', 'wide')
- output_average_new: float32 [2048, 2048], P('narrow', 'wide')
- gateup_grad: float32 [2, 2048, 6144], P(None, 'wide', 'narrow')
- gateup_updated: float32 [2, 2048, 6144], P(None, 'wide', 'narrow')
- gateup_moment_new: float32 [2, 2048, 6144], P(None, 'wide', 'narrow')
- gateup_second_new: float32 [2, 2048, 6144], P(None, 'wide', 'narrow')
- gateup_average_new: float32 [2, 2048, 6144], P(None, 'wide', 'narrow')
- down_grad: float32 [6144, 2048], P('narrow', 'wide')
- down_updated: float32 [6144, 2048], P('narrow', 'wide')
- down_moment_new: float32 [6144, 2048], P('narrow', 'wide')
- down_second_new: float32 [6144, 2048], P('narrow', 'wide')
- down_average_new: float32 [6144, 2048], P('narrow', 'wide')
- gain_grad: float32 [4352], P(('wide', 'narrow'))
- gain_updated: float32 [4352], P(('wide', 'narrow'))
- gain_moment_new: float32 [4352], P(('wide', 'narrow'))
- gain_second_new: float32 [4352], P(('wide', 'narrow'))
- gain_average_new: float32 [4352], P(('wide', 'narrow'))
The draws below stay inside these ranges and needn't reach their ends.
All inputs are finite; a program needn't handle non-finite values.
Results may differ from the reference program's by a relative error of at most 0.025.
Values may be sent and summed in bfloat16 or wider, within the bound.
A program may use at most 256 MiB of HBM per device.

```python
import math
import jax
import jax.numpy as jnp
from jax import lax

D = 2048
H = 16
KVH = 8
HD = 128
FF = 6144
STEP = 10
WO_FAN = 32
QD = 2048
KVD = 1024
TOKENS = 4096
GN = 4352


def gain_scales():
    base_scale = (100 * D // WO_FAN) ** 0.5 * 0.1
    token_scale = 0.8 * TOKENS ** 0.5
    pieces = [jnp.full((D,), 11.4 * base_scale, jnp.float32), jnp.full((D,), token_scale, jnp.float32), jnp.full((2 * HD,), 27.0 * base_scale, jnp.float32)]
    return jnp.concatenate(pieces)


def draw_gain_moment(key, part):
    noise = jnp.clip(jax.random.normal(jax.random.fold_in(key, 11), (GN,), jnp.float32), -4.0, 4.0)
    return noise * gain_scales() / 9.0


def draw_gain_second(key, part):
    spread = jax.random.uniform(jax.random.fold_in(key, 23), (GN,), jnp.float32)
    return gain_scales() * gain_scales() * 0.001 * jnp.exp(spread * math.log(4.0))


def levels(rng, extent, shards, low, high):
    def one(dim, blocks):
        heights = jax.random.uniform(jax.random.fold_in(jax.random.fold_in(rng, 6), dim), (blocks,), jnp.float32, low / len(shards), high / len(shards))
        return jnp.repeat(jnp.exp(heights), extent[dim] // blocks).reshape((-1,) + (1,) * (len(extent) - dim - 1))

    level = one(*shards[0])
    for cut in shards[1:]:
        level = level * one(*cut)
    return level


def normal_values(key, shape, scale, bound, shards=(), held_as=jnp.bfloat16):
    entries = jax.random.normal(key, shape, jnp.float32) * scale
    if len(shards) > 0:
        entries = levels(key, shape, shards, -0.22, 0.18) * entries
    return jnp.clip(entries, min=-bound, max=bound).astype(held_as)


def setup_inputs(seed: int = 0) -> dict:
    seeds = jax.random.split(jax.random.key(seed), 33)
    return {
        "tokens": normal_values(seeds[0], (TOKENS, D), 1.0, 6.0, ((0, 32),)),
        "cotangent": normal_values(seeds[1], (TOKENS, D), 1.0, 6.0, ((0, 32),)),
        "gain_copy": jnp.clip(1.0 + 0.1 * jax.random.normal(seeds[2], (GN,), jnp.float32), 0.5, 1.5),
        "query_weight": normal_values(seeds[3], (D, QD), D ** -0.5, 0.125, ((1, 4),)),
        "keyvalue_weight": normal_values(seeds[4], (2, D, KVD), D ** -0.5, 0.125, ((2, 4),)),
        "output_weight": normal_values(seeds[5], (QD, D), WO_FAN ** -0.5, 1.0, ((0, 4),)),
        "gateup_weight": normal_values(seeds[6], (2, D, FF), D ** -0.5, 0.125, ((2, 4),)),
        "down_weight": normal_values(seeds[7], (FF, D), FF ** -0.5, 0.078125, ((0, 4),)),
        "query_master": normal_values(seeds[8], (D, QD), D ** -0.5, 0.125, ((0, 8), (1, 4)), jnp.float32),
        "query_moment": normal_values(seeds[9], (D, QD), (0.0756 * (100 * D // WO_FAN) ** 0.5), 32.0, ((0, 8), (1, 4)), jnp.float32),
        "query_second": jnp.clip(jnp.exp(math.log(11.84) - 1.38737605 * jax.random.uniform(seeds[10], (D, QD), jnp.float32) ** levels(seeds[10], (D, QD), ((0, 8), (1, 4)), -0.2, 0.2)), 2.9568, 11.84),
        "query_average": normal_values(seeds[11], (D, QD), D ** -0.5, 0.125, ((0, 8), (1, 4)), jnp.float32),
        "keyvalue_master": normal_values(seeds[12], (2, D, KVD), D ** -0.5, 0.125, ((1, 8), (2, 4)), jnp.float32),
        "keyvalue_moment": normal_values(seeds[13], (2, D, KVD), (0.1056 * (100 * D // WO_FAN) ** 0.5), 48.0, ((1, 8), (2, 4)), jnp.float32),
        "keyvalue_second": jnp.clip(jnp.exp(math.log(23.104) - 1.3862944 * jax.random.uniform(seeds[14], (2, D, KVD), jnp.float32) ** levels(seeds[14], (2, D, KVD), ((1, 8), (2, 4)), -0.2, 0.2)), 5.776, 23.104),
        "keyvalue_average": normal_values(seeds[15], (2, D, KVD), D ** -0.5, 0.125, ((1, 8), (2, 4)), jnp.float32),
        "output_master": normal_values(seeds[16], (QD, D), WO_FAN ** -0.5, 1.0, ((0, 4), (1, 8)), jnp.float32),
        "output_moment": normal_values(seeds[17], (QD, D), 0.667, 4.0, ((0, 4), (1, 8)), jnp.float32),
        "output_second": jnp.clip(jnp.exp(math.log(0.144) - 1.3862944 * jax.random.uniform(seeds[18], (QD, D), jnp.float32) ** levels(seeds[18], (QD, D), ((0, 4), (1, 8)), -0.2, 0.2)), 0.036, 0.144),
        "output_average": normal_values(seeds[19], (QD, D), WO_FAN ** -0.5, 1.0, ((0, 4), (1, 8)), jnp.float32),
        "gateup_master": normal_values(seeds[20], (2, D, FF), D ** -0.5, 0.125, ((1, 8), (2, 4)), jnp.float32),
        "gateup_moment": normal_values(seeds[21], (2, D, FF), (0.0367 * TOKENS ** 0.5), 14.0, ((1, 8), (2, 4)), jnp.float32),
        "gateup_second": jnp.clip(jnp.exp(math.log(1.785856) - 1.3862944 * jax.random.uniform(seeds[22], (2, D, FF), jnp.float32) ** levels(seeds[22], (2, D, FF), ((1, 8), (2, 4)), -0.2, 0.2)), 0.446464, 1.785856),
        "gateup_average": normal_values(seeds[23], (2, D, FF), D ** -0.5, 0.125, ((1, 8), (2, 4)), jnp.float32),
        "down_master": normal_values(seeds[24], (FF, D), FF ** -0.5, 0.078125, ((0, 4), (1, 8)), jnp.float32),
        "down_moment": normal_values(seeds[25], (FF, D), (0.0667 * TOKENS ** 0.5), 24.0, ((0, 4), (1, 8)), jnp.float32),
        "down_second": jnp.clip(jnp.exp(math.log(5.89824) - 1.3862944 * jax.random.uniform(seeds[26], (FF, D), jnp.float32) ** levels(seeds[26], (FF, D), ((0, 4), (1, 8)), -0.2, 0.2)), 1.47456, 5.89824),
        "down_average": normal_values(seeds[27], (FF, D), FF ** -0.5, 0.078125, ((0, 4), (1, 8)), jnp.float32),
        "gain_master": jnp.clip(1.0 + 0.1 * jax.random.normal(seeds[28], (GN,), jnp.float32), 0.5, 1.5),
        "gain_moment": draw_gain_moment(jax.random.fold_in(seeds[32], 71), 0),
        "gain_second": draw_gain_second(jax.random.fold_in(seeds[32], 71), 0),
        "gain_average": jnp.clip(1.0 + 0.18 * jax.random.normal(seeds[31], (GN,), jnp.float32), 0.1, 1.9),
    }


EPSILON = 1e-06
THETA = 1000000.0
MASKED_SCORE = -1e+30
BETA_ONE = 0.9
BETA_TWO = 0.999
ADAM_EPS = 1e-08
WEIGHT_DECAY = 0.1
EMA_KEEP = 0.5
RATE_GAIN = 0.4

@jax.custom_vjp
def low(v):
    return lax.optimization_barrier(v.astype(jnp.bfloat16)).astype(jnp.float32)

@jax.custom_vjp
def low_back(v):
    return v

def low_keep(v):
    return (low(v), None)

def low_pass(kept, grad):
    return (grad,)

def back_keep(v):
    return (v, None)

def back_low(kept, grad):
    return (low(grad),)
low.defvjp(low_keep, low_pass)
low_back.defvjp(back_keep, back_low)

def product(left, right):
    return jnp.dot(left, right, precision=lax.Precision.HIGHEST, preferred_element_type=jnp.float32)

def rows_norm(values_in, gain_vec):
    return values_in * lax.rsqrt(lax.optimization_barrier(jnp.mean(values_in * values_in, axis=-1, keepdims=True)) + EPSILON) * gain_vec

def rope_tables(positions, width):
    half_width = width // 2
    inverse_freq = THETA ** (-(2.0 * jnp.arange(half_width, dtype=jnp.float32)) / width)
    angles = positions[:, None] * inverse_freq[None, :]
    angles = jnp.concatenate([angles, angles], axis=-1)
    return (jnp.cos(angles), jnp.sin(angles))

def rotate(values_in, cosine_table, sine_table):
    half_width = values_in.shape[-1] // 2
    turned = jnp.concatenate([-values_in[..., half_width:], values_in[..., :half_width]], axis=-1)
    return values_in * cosine_table[:, None, :] + turned * sine_table[:, None, :]

def attention(queries, keys, values):
    seq_len = queries.shape[0]
    block_rows = math.gcd(seq_len, 128)
    block_count = seq_len // block_rows
    group_size = H // KVH
    blocks = queries.reshape(block_count, block_rows, KVH, group_size, HD)
    starts = jnp.arange(block_count, dtype=jnp.int32) * block_rows
    key_pos = jnp.arange(seq_len, dtype=jnp.int32)
    factor = HD ** (-0.5)

    @jax.checkpoint
    def one_block(block_pair):
        query_block, begin_row = block_pair
        scores = jnp.einsum('qhgd,khd->hgqk', query_block, keys, precision=lax.Precision.HIGHEST) * factor
        scores = low_back(scores)
        query_pos = begin_row + jnp.arange(block_rows, dtype=jnp.int32)
        visible = key_pos[None, :] <= query_pos[:, None]
        scores = jnp.where(visible, scores, MASKED_SCORE)
        shifted = jnp.exp(scores - lax.optimization_barrier(jnp.max(scores, axis=-1, keepdims=True)))
        attention_weights = low(shifted / lax.optimization_barrier(jnp.sum(shifted, axis=-1, keepdims=True)))
        return jnp.einsum('hgqk,khd->qhgd', attention_weights, values, precision=lax.Precision.HIGHEST)
    return lax.map(one_block, (blocks, starts)).reshape(seq_len, H, HD)

def forward(tokens, gain_copy, query_weight, keyvalue_weight, output_weight, gateup_weight, down_weight):
    seq_len = tokens.shape[0]
    attn_gain = gain_copy[:D]
    mlp_gain = gain_copy[D:2 * D]
    query_gain = gain_copy[2 * D:2 * D + HD]
    key_gain = gain_copy[2 * D + HD:]
    normed = low(rows_norm(tokens, attn_gain))
    query_proj = low_back(product(normed, query_weight)).reshape(seq_len, H, HD)
    key_proj = low_back(product(normed, keyvalue_weight[0])).reshape(seq_len, KVH, HD)
    values = low(low_back(product(normed, keyvalue_weight[1]))).reshape(seq_len, KVH, HD)
    cosine_table, sine_table = rope_tables(jnp.arange(seq_len, dtype=jnp.float32), HD)
    queries = low(rotate(rows_norm(query_proj, query_gain), cosine_table, sine_table))
    keys = low(rotate(rows_norm(key_proj, key_gain), cosine_table, sine_table))
    attended = low(low_back(attention(queries, keys, values))).reshape(seq_len, H * HD)
    hidden_mid = tokens + low_back(product(attended, output_weight))
    mlp_input = low(rows_norm(hidden_mid, mlp_gain))
    gate_proj = low_back(product(mlp_input, gateup_weight[0]))
    up_proj = low_back(product(mlp_input, gateup_weight[1]))
    activated = low(gate_proj * jax.nn.sigmoid(gate_proj) * up_proj)
    return hidden_mid + low_back(product(activated, down_weight))

def adamw(gradient, master, moment, second, average, step_rate, decay_rate):
    moment_new = BETA_ONE * moment + (1.0 - BETA_ONE) * gradient
    second_new = BETA_TWO * second + (1.0 - BETA_TWO) * gradient * gradient
    moment_hat = moment_new / (1.0 - BETA_ONE ** STEP)
    second_hat = second_new / (1.0 - BETA_TWO ** STEP)
    master_new = master - step_rate * (moment_hat / (jnp.sqrt(second_hat) + ADAM_EPS) + decay_rate * master)
    average_new = EMA_KEEP * average + (1.0 - EMA_KEEP) * master_new
    return (gradient, master_new, moment_new, second_new, average_new)

def reference(tokens, cotangent, gain_copy, query_weight, keyvalue_weight, output_weight, gateup_weight, down_weight, query_master, query_moment, query_second, query_average, keyvalue_master, keyvalue_moment, keyvalue_second, keyvalue_average, output_master, output_moment, output_second, output_average, gateup_master, gateup_moment, gateup_second, gateup_average, down_master, down_moment, down_second, down_average, gain_master, gain_moment, gain_second, gain_average):
    block_output, pullback = jax.vjp(forward, tokens.astype(jnp.float32), gain_copy, query_weight.astype(jnp.float32), keyvalue_weight.astype(jnp.float32), output_weight.astype(jnp.float32), gateup_weight.astype(jnp.float32), down_weight.astype(jnp.float32))
    gradients = pullback(cotangent.astype(jnp.float32))
    input_grad = gradients[0]
    gain_new = adamw(gradients[1], gain_master, gain_moment, gain_second, gain_average, RATE_GAIN, 0.0)
    query_new = adamw(gradients[2], query_master, query_moment, query_second, query_average, 2.0 * D ** (-0.5), WEIGHT_DECAY)
    keyvalue_new = adamw(gradients[3], keyvalue_master, keyvalue_moment, keyvalue_second, keyvalue_average, 2.0 * D ** (-0.5), WEIGHT_DECAY)
    output_new = adamw(gradients[4], output_master, output_moment, output_second, output_average, 2.0 * WO_FAN ** (-0.5), WEIGHT_DECAY)
    gateup_new = adamw(gradients[5], gateup_master, gateup_moment, gateup_second, gateup_average, 2.0 * D ** (-0.5), WEIGHT_DECAY)
    down_new = adamw(gradients[6], down_master, down_moment, down_second, down_average, 2.0 * FF ** (-0.5), WEIGHT_DECAY)
    return (block_output, input_grad, query_new[0], query_new[1], query_new[2], query_new[3], query_new[4], keyvalue_new[0], keyvalue_new[1], keyvalue_new[2], keyvalue_new[3], keyvalue_new[4], output_new[0], output_new[1], output_new[2], output_new[3], output_new[4], gateup_new[0], gateup_new[1], gateup_new[2], gateup_new[3], gateup_new[4], down_new[0], down_new[1], down_new[2], down_new[3], down_new[4], gain_new[0], gain_new[1], gain_new[2], gain_new[3], gain_new[4])
```

```python
import functools

import jax
import jax.numpy as jnp
from jax import lax
from jax.experimental import pallas as pl
from jax.experimental.pallas import tpu as pltpu
from jax.sharding import PartitionSpec as P

D = 2048
HD = 128
FF = 6144
STEP = 10
WO_FAN = 32

EPSILON = 1e-06
THETA = 1000000.0
BETA_ONE = 0.9
BETA_TWO = 0.999
ADAM_EPS = 1e-08
WEIGHT_DECAY = 0.1
EMA_KEEP = 0.5
RATE_GAIN = 0.4
FACTOR = HD ** (-0.5)
LOG2E = 1.4426950408889634

F32 = jnp.float32
BF16 = jnp.bfloat16
MESH = pl.DeviceIdType.MESH
VM = pl.BlockSpec(memory_space=pltpu.VMEM)
SM = pl.BlockSpec(memory_space=pltpu.SMEM)
VMEM_LIMIT = 60 << 20

NT = (((1,), (1,)), ((), ()))
TN = (((0,), (0,)), ((), ()))


def dot(left, right):
    return jnp.dot(left, right, preferred_element_type=F32)


def dot_nt(left, right):
    return lax.dot_general(left, right, NT, preferred_element_type=F32)


def dot_tn(left, right):
    return lax.dot_general(left, right, TN, preferred_element_type=F32)


def rope_tables(positions):
    half_width = HD // 2
    inverse_freq = THETA ** (-(2.0 * jnp.arange(half_width, dtype=F32)) / HD)
    angles = positions[:, None] * inverse_freq[None, :]
    cosine, sine = jnp.cos(angles), jnp.sin(angles)
    return (
        jnp.concatenate([cosine, cosine], axis=-1),
        jnp.concatenate([-sine, sine], axis=-1),
    )


def adamw(gradient, master, moment, second, average, step_rate, decay_rate):
    moment_new = BETA_ONE * moment + (1.0 - BETA_ONE) * gradient
    second_new = BETA_TWO * second + (1.0 - BETA_TWO) * gradient * gradient
    moment_hat = moment_new / (1.0 - BETA_ONE**STEP)
    second_hat = second_new / (1.0 - BETA_TWO**STEP)
    master_new = master - step_rate * (
        moment_hat / (jnp.sqrt(second_hat) + ADAM_EPS) + decay_rate * master
    )
    average_new = EMA_KEEP * average + (1.0 - EMA_KEEP) * master_new
    return (gradient, master_new, moment_new, second_new, average_new)


def row_scale(values_in):
    return lax.rsqrt(jnp.mean(values_in * values_in, axis=-1, keepdims=True) + EPSILON)


def norm_back(gradient, unit_rows, inv_scale, gain_row):
    scaled = gradient * gain_row
    inner = scaled - unit_rows * jnp.mean(scaled * unit_rows, axis=-1, keepdims=True)
    return inv_scale * inner, jnp.sum(gradient * unit_rows, axis=0, keepdims=True)


def square():
    me = lax.axis_index("narrow")
    xn = me + 1 - 2 * (me % 2)
    yn = (me + 2) % 4
    dg = (xn + 2) % 4
    return me, xn, yn, dg


def greet(axis, peers):
    barrier = pltpu.get_barrier_semaphore()
    for peer in peers:
        pl.semaphore_signal(barrier, inc=1, device_id={axis: peer}, device_id_type=MESH)
    pl.semaphore_wait(barrier, len(peers))


class Copies:
    def __init__(self, send, recv):
        self.send, self.recv, self.sent = send, recv, []

    def go(self, src, dst, slot, peer):
        copy = pltpu.make_async_remote_copy(
            src_ref=src,
            dst_ref=dst,
            send_sem=self.send.at[slot],
            recv_sem=self.recv.at[slot],
            device_id={"narrow": peer},
            device_id_type=MESH,
        )
        copy.start()
        self.sent.append(copy)
        return copy

    def finish(self):
        for copy in self.sent:
            copy.wait_send()


def gather_square(copies, slot, x_ref, o_ref):
    me, xn, yn, dg = square()
    rows = x_ref.shape[0]
    half = rows // 2

    def part(owner, low):
        return o_ref.at[pl.ds(pl.multiple_of(owner * rows + low, half), half)]

    upper, lower = x_ref.at[pl.ds(0, half)], x_ref.at[pl.ds(half, half)]
    xa = copies.go(upper, part(me, 0), slot, xn)
    yb = copies.go(lower, part(me, half), slot + 1, yn)
    xb = copies.go(lower, part(me, half), slot + 2, xn)
    ya = copies.go(upper, part(me, 0), slot + 3, yn)
    o_ref[pl.ds(pl.multiple_of(me * rows, rows), rows)] = x_ref[...]
    xa.wait_recv()
    yf = copies.go(part(xn, 0), part(xn, 0), slot + 4, yn)
    yb.wait_recv()
    xf = copies.go(part(yn, half), part(yn, half), slot + 5, xn)
    for copy in (xb, ya, yf, xf):
        copy.wait_recv()


def scatter_square(copies, slot, p_ref, buf, stage, emit):
    me, xn, yn, dg = square()
    rows = p_ref.shape[0] // 4
    half = rows // 2

    def part(owner, low):
        return p_ref.at[pl.ds(pl.multiple_of(owner * rows + low, half), half)]

    c0 = copies.go(part(dg, 0), buf.at[0], slot, xn)
    c1 = copies.go(part(dg, half), buf.at[1], slot + 1, yn)
    c2 = copies.go(part(xn, 0), buf.at[2], slot + 2, xn)
    c3 = copies.go(part(yn, half), buf.at[3], slot + 3, yn)
    c0.wait_recv()
    stage[0] = (part(yn, 0)[...].astype(F32) + buf[0].astype(F32)).astype(BF16)
    c4 = copies.go(stage.at[0], buf.at[4], slot + 4, yn)
    c1.wait_recv()
    stage[1] = (part(xn, half)[...].astype(F32) + buf[1].astype(F32)).astype(BF16)
    c5 = copies.go(stage.at[1], buf.at[5], slot + 5, xn)
    c2.wait_recv()
    c4.wait_recv()
    emit(0, part(me, 0)[...].astype(F32) + buf[2].astype(F32) + buf[4].astype(F32))
    c3.wait_recv()
    c5.wait_recv()
    emit(half, part(me, half)[...].astype(F32) + buf[3].astype(F32) + buf[5].astype(F32))


def dma_sems(count):
    return [pltpu.SemaphoreType.DMA((count,)), pltpu.SemaphoreType.DMA((count,))]


def scatter_space(rows):
    return [pltpu.VMEM((6, rows // 2, D), BF16), pltpu.VMEM((2, rows // 2, D), BF16)]


def remote_params(collective_id):
    return pltpu.CompilerParams(
        collective_id=collective_id, has_side_effects=True, vmem_limit_bytes=VMEM_LIMIT
    )


def norm_gather_kernel(t_ref, g_ref, o_ref, own, send, recv):
    _, xn, yn, _ = square()
    greet("narrow", (xn, yn))
    hidden = t_ref[...].astype(F32)
    own[...] = (hidden * row_scale(hidden) * g_ref[...]).astype(BF16)
    copies = Copies(send, recv)
    gather_square(copies, 0, own, o_ref)
    copies.finish()


def norm_gather(tokens, gain_row, special):
    rows = tokens.shape[0]
    if not special:
        hidden = tokens.astype(F32)
        normed = (hidden * row_scale(hidden) * gain_row).astype(BF16)
        return lax.all_gather(normed, "narrow", axis=0, tiled=True)
    return pl.pallas_call(
        norm_gather_kernel,
        name="norm_gather",
        out_shape=jax.ShapeDtypeStruct((4 * rows, D), BF16),
        in_specs=[VM, VM],
        out_specs=VM,
        scratch_shapes=[pltpu.VMEM((rows, D), BF16)] + dma_sems(6),
        cost_estimate=cost(1, 1),
        compiler_params=remote_params(1),
    )(tokens, gain_row)


def mid_forward_kernel(p_ref, t_ref, g_ref, h_ref, o_ref, buf, stage, own, send, recv):
    _, xn, yn, _ = square()
    half = t_ref.shape[0] // 2
    greet("narrow", (xn, yn))
    copies = Copies(send, recv)

    def emit(low, total):
        hidden = t_ref[pl.ds(low, half)].astype(F32) + total
        h_ref[pl.ds(low, half)] = hidden
        own[pl.ds(low, half)] = (hidden * row_scale(hidden) * g_ref[...]).astype(BF16)

    scatter_square(copies, 0, p_ref, buf, stage, emit)
    gather_square(copies, 6, own, o_ref)
    copies.finish()


def mid_forward(partial, tokens, gain_row, special):
    rows = tokens.shape[0]
    if not special:
        hidden = tokens.astype(F32) + lax.psum_scatter(
            partial, "narrow", scatter_dimension=0, tiled=True
        ).astype(F32)
        normed = (hidden * row_scale(hidden) * gain_row).astype(BF16)
        return hidden, lax.all_gather(normed, "narrow", axis=0, tiled=True)
    return pl.pallas_call(
        mid_forward_kernel,
        name="mid_forward",
        out_shape=(
            jax.ShapeDtypeStruct((rows, D), F32),
            jax.ShapeDtypeStruct((4 * rows, D), BF16),
        ),
        in_specs=[VM] * 3,
        out_specs=(VM, VM),
        scratch_shapes=scatter_space(rows) + [pltpu.VMEM((rows, D), BF16)] + dma_sems(12),
        cost_estimate=cost(1, 1),
        compiler_params=remote_params(2),
    )(partial, tokens, gain_row)


def mid_backward_kernel(
    p_ref, h_ref, c_ref, g_ref, m_ref, o_ref, gg_ref, buf, stage, own, send, recv
):
    _, xn, yn, _ = square()
    half = h_ref.shape[0] // 2
    greet("narrow", (xn, yn))
    copies = Copies(send, recv)
    gg_ref[...] = jnp.zeros_like(gg_ref)

    def emit(low, total):
        hidden = h_ref[pl.ds(low, half)]
        scale = row_scale(hidden)
        back, gain_sum = norm_back(total, hidden * scale, scale, g_ref[...])
        gg_ref[...] += gain_sum
        mid = c_ref[pl.ds(low, half)].astype(F32) + back
        m_ref[pl.ds(low, half)] = mid
        own[pl.ds(low, half)] = mid.astype(BF16)

    scatter_square(copies, 0, p_ref, buf, stage, emit)
    gather_square(copies, 6, own, o_ref)
    copies.finish()


def mid_backward(partial, hidden_mid, cotangent, gain_row, special):
    rows = hidden_mid.shape[0]
    if not special:
        total = lax.psum_scatter(partial, "narrow", scatter_dimension=0, tiled=True).astype(F32)
        scale = row_scale(hidden_mid)
        back, gain_sum = norm_back(total, hidden_mid * scale, scale, gain_row)
        mid = cotangent.astype(F32) + back
        return mid, lax.all_gather(mid.astype(BF16), "narrow", axis=0, tiled=True), gain_sum
    return pl.pallas_call(
        mid_backward_kernel,
        name="mid_backward",
        out_shape=(
            jax.ShapeDtypeStruct((rows, D), F32),
            jax.ShapeDtypeStruct((4 * rows, D), BF16),
            jax.ShapeDtypeStruct((1, D), F32),
        ),
        in_specs=[VM] * 4,
        out_specs=(VM,) * 3,
        scratch_shapes=scatter_space(rows) + [pltpu.VMEM((rows, D), BF16)] + dma_sems(12),
        cost_estimate=cost(1, 1),
        compiler_params=remote_params(3),
    )(partial, hidden_mid, cotangent, gain_row)


def last_kernel(p_ref, t_ref, m_ref, g_ref, q_ref, h_ref, o_ref, gg_ref, b_ref, buf, stage, buf2, stage2, send, recv):
    _, xn, yn, _ = square()
    half = t_ref.shape[0] // 2
    greet("narrow", (xn, yn))
    copies = Copies(send, recv)
    gg_ref[...] = jnp.zeros_like(gg_ref)

    def emit(low, total):
        hidden = t_ref[pl.ds(low, half)].astype(F32)
        scale = row_scale(hidden)
        back, gain_sum = norm_back(total, hidden * scale, scale, g_ref[...])
        gg_ref[...] += gain_sum
        o_ref[pl.ds(low, half)] = m_ref[pl.ds(low, half)] + back

    def emit_out(low, total):
        b_ref[pl.ds(low, half)] = h_ref[pl.ds(low, half)] + total

    scatter_square(copies, 0, p_ref, buf, stage, emit)
    scatter_square(copies, 6, q_ref, buf2, stage2, emit_out)
    copies.finish()


def last_scatter(partial, tokens, mid_grad, gain_row, out_partial, hidden_mid, special):
    rows = tokens.shape[0]
    if not special:
        total = lax.psum_scatter(partial, "narrow", scatter_dimension=0, tiled=True).astype(F32)
        hidden = tokens.astype(F32)
        scale = row_scale(hidden)
        back, gain_sum = norm_back(total, hidden * scale, scale, gain_row)
        out = lax.psum_scatter(out_partial, "narrow", scatter_dimension=0, tiled=True)
        return mid_grad + back, gain_sum, hidden_mid + out.astype(F32)
    return pl.pallas_call(
        last_kernel,
        name="last_scatter",
        out_shape=(
            jax.ShapeDtypeStruct((rows, D), F32),
            jax.ShapeDtypeStruct((1, D), F32),
            jax.ShapeDtypeStruct((rows, D), F32),
        ),
        in_specs=[VM] * 6,
        out_specs=(VM,) * 3,
        scratch_shapes=scatter_space(rows) + scatter_space(rows) + dma_sems(12),
        cost_estimate=cost(1, 1),
        compiler_params=remote_params(4),
    )(partial, tokens, mid_grad, gain_row, out_partial, hidden_mid)


def line(count):
    w = lax.axis_index("wide")
    z, c = w // 2, w % 2
    return w, z, c, count // 2, w + 1 - 2 * c, jnp.minimum(w + 2, count - 1), jnp.maximum(w - 2, 0)


def greet_line(count):
    w, z, c, chips, mate, above, below = line(count)
    barrier = pltpu.get_barrier_semaphore()
    has_above, has_below = z < chips - 1, z > 0

    @pl.when(has_above)
    def _():
        pl.semaphore_signal(barrier, inc=1, device_id={"wide": above}, device_id_type=MESH)

    @pl.when(has_below)
    def _():
        pl.semaphore_signal(barrier, inc=1, device_id={"wide": below}, device_id_type=MESH)

    pl.semaphore_signal(barrier, inc=1, device_id={"wide": mate}, device_id_type=MESH)
    pl.semaphore_wait(barrier, 1 + has_above.astype(jnp.int32) + has_below.astype(jnp.int32))


def wide_copy(src, dst, send, recv, slot, peer):
    return pltpu.make_async_remote_copy(
        src_ref=src,
        dst_ref=dst,
        send_sem=send.at[slot],
        recv_sem=recv.at[slot],
        device_id={"wide": peer},
        device_id_type=MESH,
    )


def pass_keys_kernel(count, x_ref, o_ref, send, recv, mate_send, mate_recv):
    w, z, c, chips, mate, above, below = line(count)
    greet_line(count)
    own_up = wide_copy(x_ref, o_ref.at[w], send, recv, 0, above)

    @pl.when(z < chips - 1)
    def _():
        own_up.start()

    own_mate = wide_copy(x_ref, o_ref.at[w], mate_send, mate_recv, 0, mate)
    own_mate.start()
    o_ref[w] = x_ref[...]
    for step in range(1, chips):
        block = jnp.maximum(w - 2 * step, 0)
        arrived = wide_copy(o_ref.at[block], o_ref.at[block], send, recv, step - 1, above)
        onward = wide_copy(o_ref.at[block], o_ref.at[block], send, recv, min(step, chips - 2), above)
        share = wide_copy(o_ref.at[block], o_ref.at[block], mate_send, mate_recv, step, mate)

        @pl.when(z >= step)
        def _():
            arrived.wait_recv()
            if step < chips - 1:

                @pl.when(z < chips - 1)
                def _():
                    onward.start()

            share.start()

    own_mate.wait()

    @pl.when(z < chips - 1)
    def _():
        own_up.wait_send()

    for step in range(1, chips):
        block = jnp.maximum(w - 2 * step, 0)
        onward = wide_copy(o_ref.at[block], o_ref.at[block], send, recv, min(step, chips - 2), above)
        share = wide_copy(o_ref.at[block], o_ref.at[block], mate_send, mate_recv, step, mate)

        @pl.when(z >= step)
        def _():
            share.wait()
            if step < chips - 1:

                @pl.when(z < chips - 1)
                def _():
                    onward.wait_send()


def pass_keys(keys_values, count, special):
    rows, width = keys_values.shape
    if not special:
        return lax.all_gather(keys_values, "wide", axis=0)
    chips = count // 2
    return pl.pallas_call(
        functools.partial(pass_keys_kernel, count),
        name="pass_keys",
        out_shape=jax.ShapeDtypeStruct((count, rows, width), BF16),
        in_specs=[VM],
        out_specs=VM,
        scratch_shapes=dma_sems(chips - 1) + dma_sems(chips),
        cost_estimate=cost(1, 1),
        compiler_params=remote_params(5),
    )(keys_values)


def return_grads_kernel(
    count, x_ref, o_ref, from_mate, from_above, stage, send, recv, mate_send, mate_recv
):
    w, z, c, chips, mate, above, below = line(count)
    greet_line(count)

    def to_mate(s):
        return wide_copy(
            x_ref.at[jnp.minimum(2 * s + 1 - c, count - 1)],
            from_mate.at[s],
            mate_send,
            mate_recv,
            s,
            mate,
        )

    def sends_mate(s):
        return (z > s) | ((z == s) & (c == 1))

    def gets_mate(s):
        return (z > s) | ((z == s) & (c == 0))

    def down(s):
        return wide_copy(stage.at[s], from_above.at[s], send, recv, s, below)

    for s in range(chips):

        @pl.when(sends_mate(s))
        def _():
            to_mate(s).start()

    for s in range(chips):
        block = jnp.minimum(2 * s + c, count - 1)

        @pl.when(z > s)
        def _():
            to_mate(s).wait_recv()

            @pl.when(z == chips - 1)
            def _():
                stage[s] = (x_ref[block].astype(F32) + from_mate[s].astype(F32)).astype(BF16)

            @pl.when(z < chips - 1)
            def _():
                down(s).wait_recv()
                stage[s] = (
                    x_ref[block].astype(F32) + from_mate[s].astype(F32) + from_above[s].astype(F32)
                ).astype(BF16)

            down(s).start()

        @pl.when(z == s)
        def _():
            o_ref[...] = x_ref[block].astype(F32)

            @pl.when(c == 0)
            def _():
                to_mate(s).wait_recv()
                o_ref[...] += from_mate[s].astype(F32)

            if s < chips - 1:
                down(s).wait_recv()
                o_ref[...] += from_above[s].astype(F32)

    for s in range(chips):

        @pl.when(sends_mate(s))
        def _():
            to_mate(s).wait_send()

        @pl.when(z > s)
        def _():
            down(s).wait_send()


def return_grads(grads, count, special):
    _, rows, width = grads.shape
    if not special:
        w = lax.axis_index("wide")
        seen = (jnp.arange(count) <= w)[:, None, None]
        total = lax.psum_scatter(
            jnp.where(seen, grads, 0).reshape(count * rows, width),
            "wide",
            scatter_dimension=0,
            tiled=True,
        )
        return total.astype(F32)
    chips = count // 2
    return pl.pallas_call(
        functools.partial(return_grads_kernel, count),
        name="return_grads",
        out_shape=jax.ShapeDtypeStruct((rows, width), F32),
        in_specs=[VM],
        out_specs=VM,
        scratch_shapes=[
            pltpu.VMEM((chips, rows, width), BF16),
            pltpu.VMEM((chips, rows, width), BF16),
            pltpu.VMEM((chips, rows, width), BF16),
        ]
        + dma_sems(chips)
        + dma_sems(chips),
        cost_estimate=cost(1, 1),
        compiler_params=remote_params(6),
    )(grads)


def gain_kernel(wide, x_ref, o_ref, near, mid, far, send, recv, wide_send, wide_recv):
    me, xn, yn, dg = square()
    w = lax.axis_index("wide")
    barrier = pltpu.get_barrier_semaphore()
    for peer in (xn, yn, dg):
        pl.semaphore_signal(barrier, inc=1, device_id={"narrow": peer}, device_id_type=MESH)
    for step in range(1, wide):
        pl.semaphore_signal(
            barrier, inc=1, device_id={"wide": (w + step) % wide}, device_id_type=MESH
        )
    pl.semaphore_wait(barrier, 3 + wide - 1)
    copies = Copies(send, recv)
    sent = [
        copies.go(x_ref.at[peer], near.at[slot], slot, peer)
        for slot, peer in enumerate((xn, yn, dg))
    ]
    for copy in sent:
        copy.wait_recv()
    mid[...] = x_ref[me] + near[0] + near[1] + near[2]
    away = []
    for step in range(1, wide):
        peer = (w + step) % wide
        copy = wide_copy(
            mid.at[peer], far.at[step - 1], wide_send, wide_recv, step - 1, peer
        )
        copy.start()
        away.append(copy)
    total = mid[w]
    for step in range(1, wide):
        away[step - 1].wait_recv()
        total = total + far[step - 1]
    o_ref[...] = total
    copies.finish()
    for copy in away:
        copy.wait_send()


def gain_sums(partial, wide, narrow, special):
    if not special:
        return lax.psum_scatter(partial, ("wide", "narrow"), scatter_dimension=0, tiled=True)
    count = partial.shape[0] // (wide * narrow)
    padded = -(-count // 128) * 128
    shaped = partial.reshape(wide, narrow, count).transpose(1, 0, 2)
    shaped = jnp.pad(shaped, ((0, 0), (0, 0), (0, padded - count)))
    shaped = shaped.reshape(narrow, wide, padded // 128, 128)
    out = pl.pallas_call(
        functools.partial(gain_kernel, wide),
        name="gain_sums",
        out_shape=jax.ShapeDtypeStruct((padded // 128, 128), F32),
        in_specs=[VM],
        out_specs=VM,
        scratch_shapes=[
            pltpu.VMEM((3, wide, padded // 128, 128), F32),
            pltpu.VMEM((wide, padded // 128, 128), F32),
            pltpu.VMEM((wide - 1, padded // 128, 128), F32),
        ]
        + dma_sems(3)
        + dma_sems(wide - 1),
        cost_estimate=cost(1, 1),
        compiler_params=remote_params(7),
    )(shaped)
    return out.reshape(padded)[:count]


def cost(flops, moved, exps=0):
    return pl.CostEstimate(flops=1, bytes_accessed=1, transcendentals=0)


def params(*semantics):
    if not semantics:
        return pltpu.CompilerParams(vmem_limit_bytes=VMEM_LIMIT)
    return pltpu.CompilerParams(vmem_limit_bytes=VMEM_LIMIT, dimension_semantics=semantics)


def spin(raw, gain_row, cosine, sine):
    normed = raw * row_scale(raw) * gain_row
    return normed * cosine + pltpu.roll(normed, HD // 2, axis=1) * sine


def keys_kernel(x_ref, w_ref, g_ref, cos_ref, sin_ref, kv_ref, raw_ref):
    which = pl.program_id(0)
    width = w_ref.shape[2]
    out = dot(x_ref[...], w_ref[0])

    @pl.when(which == 0)
    def _():
        raw_ref[...] = out
        for h in range(width // HD):
            part = out[:, h * HD : (h + 1) * HD]
            kv_ref[:, h * HD : (h + 1) * HD] = spin(
                part, g_ref[...], cos_ref[...], sin_ref[...]
            ).astype(BF16)

    @pl.when(which == 1)
    def _():
        kv_ref[...] = out.astype(BF16)


def keys_values(x, weight, gain_row, cosine, sine):
    rows, width = x.shape[0], weight.shape[2]
    whole = lambda i: (0, 0)
    return pl.pallas_call(
        keys_kernel,
        name="keys_values",
        grid=(2,),
        out_shape=(
            jax.ShapeDtypeStruct((rows, 2 * width), BF16),
            jax.ShapeDtypeStruct((rows, width), F32),
        ),
        in_specs=[
            pl.BlockSpec((rows, D), whole),
            pl.BlockSpec((1, D, width), lambda i: (i, 0, 0)),
            pl.BlockSpec((1, HD), whole),
            pl.BlockSpec((rows, HD), whole),
            pl.BlockSpec((rows, HD), whole),
        ],
        out_specs=(
            pl.BlockSpec((rows, width), lambda i: (0, i)),
            pl.BlockSpec((rows, width), whole),
        ),
        compiler_params=params("arbitrary"),
        cost_estimate=cost(4 * rows * D * width, 2 * rows * D + 4 * D * width),
    )(x, weight, gain_row, cosine, sine)


def queries_kernel(x_ref, w_ref, g_ref, cos_ref, sin_ref, q_ref, raw_ref):
    out = dot(x_ref[...], w_ref[...])
    raw_ref[...] = out
    for h in range(w_ref.shape[1] // HD):
        part = out[:, h * HD : (h + 1) * HD]
        q_ref[:, h * HD : (h + 1) * HD] = spin(
            part, g_ref[...], cos_ref[...], sin_ref[...]
        ).astype(BF16)


def queries(x, weight, gain_row, cosine, sine):
    rows, width = x.shape[0], weight.shape[1]
    tile = 256
    whole = lambda i: (0, 0)
    return pl.pallas_call(
        queries_kernel,
        name="queries",
        grid=(width // tile,),
        out_shape=(
            jax.ShapeDtypeStruct((rows, width), BF16),
            jax.ShapeDtypeStruct((rows, width), F32),
        ),
        in_specs=[
            pl.BlockSpec((rows, D), whole),
            pl.BlockSpec((D, tile), lambda i: (0, i)),
            pl.BlockSpec((1, HD), whole),
            pl.BlockSpec((rows, HD), whole),
            pl.BlockSpec((rows, HD), whole),
        ],
        out_specs=(
            pl.BlockSpec((rows, tile), lambda i: (0, i)),
            pl.BlockSpec((rows, tile), lambda i: (0, i)),
        ),
        compiler_params=params("arbitrary"),
        cost_estimate=cost(2 * rows * D * width, 2 * rows * D + 2 * D * width),
    )(x, weight, gain_row, cosine, sine)


def attend_kernel(heads, group, w_ref, q_ref, kv_ref, o_ref, low_ref, lse_ref, acc):
    rows = q_ref.shape[0]
    kv_width = kv_ref.shape[2] // 2
    w = w_ref[0]
    acc[...] = jnp.zeros_like(acc)
    ones = jnp.ones((rows, HD), BF16)

    def block(j, masked):
        for h in range(heads):
            kv = h // group
            key = kv_ref[j, :, kv * HD : (kv + 1) * HD]
            value = kv_ref[j, :, kv_width + kv * HD : kv_width + (kv + 1) * HD]
            query = q_ref[:, h * HD : (h + 1) * HD]
            terms = jnp.exp2(dot_nt(query, key) * (FACTOR * LOG2E))
            if masked:
                at = lax.broadcasted_iota(jnp.int32, (rows, rows), 0)
                key_at = lax.broadcasted_iota(jnp.int32, (rows, rows), 1)
                terms = jnp.where(key_at <= at, terms, 0.0)
            acc[h] += dot(terms.astype(BF16), jnp.concatenate([value, ones], axis=1))

    @pl.loop(0, w)
    def _(j):
        block(j, False)

    block(w, True)
    for h in range(heads):
        total = acc[h, :, HD:]
        out = acc[h, :, :HD] / total
        o_ref[:, h * HD : (h + 1) * HD] = out
        low_ref[:, h * HD : (h + 1) * HD] = out.astype(BF16)
        lse_ref[h : h + 1, :] = jnp.transpose(jnp.log2(total))[0:1]


def attend(w_index, query, kv_all, heads, group):
    rows, width = query.shape
    count = kv_all.shape[0]
    return pl.pallas_call(
        functools.partial(attend_kernel, heads, group),
        name="attend",
        out_shape=(
            jax.ShapeDtypeStruct((rows, width), F32),
            jax.ShapeDtypeStruct((rows, width), BF16),
            jax.ShapeDtypeStruct((heads, rows), F32),
        ),
        in_specs=[SM, VM, VM],
        out_specs=(VM, VM, VM),
        scratch_shapes=[pltpu.VMEM((heads, rows, 2 * HD), F32)],
        compiler_params=params(),
        cost_estimate=cost(4 * rows * rows * count * width, 2 * kv_all.size, rows * rows * heads * count),
    )(w_index, query, kv_all)


def attend_back_kernel(
    heads, group, w_ref, q_ref, kv_ref, do_ref, o_ref, lse_ref, dq_ref, dkv_ref, delta
):
    rows = q_ref.shape[0]
    kv_width = kv_ref.shape[2] // 2
    w = w_ref[0]
    for h in range(heads):
        part = slice(h * HD, (h + 1) * HD)
        delta[h : h + 1, :] = jnp.sum(
            jnp.transpose(do_ref[:, part].astype(F32) * o_ref[:, part]), axis=0, keepdims=True
        )
    dq_ref[...] = jnp.zeros_like(dq_ref)

    def block(j, masked):
        for kv in range(heads // group):
            key = kv_ref[j, :, kv * HD : (kv + 1) * HD]
            value = kv_ref[j, :, kv_width + kv * HD : kv_width + (kv + 1) * HD]
            key_sum = jnp.zeros((rows, HD), F32)
            value_sum = jnp.zeros((rows, HD), F32)
            for h in range(kv * group, (kv + 1) * group):
                part = slice(h * HD, (h + 1) * HD)
                query, out_grad = q_ref[:, part], do_ref[:, part]
                probs = jnp.exp2(
                    dot_nt(key, query) * (FACTOR * LOG2E) - lse_ref[h : h + 1, :]
                )
                if masked:
                    key_at = lax.broadcasted_iota(jnp.int32, (rows, rows), 0)
                    at = lax.broadcasted_iota(jnp.int32, (rows, rows), 1)
                    probs = jnp.where(key_at <= at, probs, 0.0)
                value_sum += dot(probs.astype(BF16), out_grad)
                prob_grad = dot_nt(value, out_grad)
                score_grad = (probs * (prob_grad - delta[h : h + 1, :])).astype(BF16)
                key_sum += dot(score_grad, query)
                dq_ref[:, part] += dot_tn(score_grad, key)
            dkv_ref[j, :, kv * HD : (kv + 1) * HD] = (key_sum * FACTOR).astype(BF16)
            dkv_ref[j, :, kv_width + kv * HD : kv_width + (kv + 1) * HD] = value_sum.astype(BF16)

    @pl.loop(0, w)
    def _(j):
        block(j, False)

    block(w, True)
    dq_ref[...] = dq_ref[...] * FACTOR


def attend_back(w_index, query, kv_all, out_grad, out, lse, heads, group):
    rows, width = query.shape
    count = kv_all.shape[0]
    return pl.pallas_call(
        functools.partial(attend_back_kernel, heads, group),
        name="attend_back",
        out_shape=(
            jax.ShapeDtypeStruct((rows, width), F32),
            jax.ShapeDtypeStruct(kv_all.shape, BF16),
        ),
        in_specs=[SM] + [VM] * 5,
        out_specs=(VM, VM),
        scratch_shapes=[pltpu.VMEM((heads, rows), F32)],
        compiler_params=params(),
        cost_estimate=cost(10 * rows * rows * count * width, 4 * kv_all.size, rows * rows * heads * count),
    )(w_index, query, kv_all, out_grad, out, lse)


def unspin_kernel(width, e_ref, raw_ref, g_ref, cos_ref, sin_ref, o_ref, gg_ref):
    gain_sum = jnp.zeros((1, HD), F32)
    for h in range(raw_ref.shape[1] // HD):
        part = slice(h * HD, (h + 1) * HD)
        grad = e_ref[:, part]
        turned = grad * cos_ref[...] - pltpu.roll(grad, HD // 2, axis=1) * sin_ref[...]
        raw = raw_ref[:, part]
        scale = row_scale(raw)
        back, total = norm_back(turned, raw * scale, scale, g_ref[...])
        o_ref[:, part] = back.astype(BF16)
        gain_sum += total
    if width > raw_ref.shape[1]:
        o_ref[:, raw_ref.shape[1] :] = e_ref[:, raw_ref.shape[1] :].astype(BF16)
    gg_ref[...] = gain_sum


def unspin(grad, raw, gain_row, cosine, sine):
    rows, width = grad.shape
    return pl.pallas_call(
        functools.partial(unspin_kernel, width),
        name="unspin",
        out_shape=(
            jax.ShapeDtypeStruct((rows, width), BF16),
            jax.ShapeDtypeStruct((1, HD), F32),
        ),
        in_specs=[VM] * 5,
        out_specs=(VM, VM),
        compiler_params=params(),
        cost_estimate=cost(20 * grad.size, 10 * grad.size),
    )(grad, raw, gain_row, cosine, sine)


def feed_kernel(x_ref, dy_ref, w_ref, d_ref, act_ref, grad_ref, down_ref):
    x, dy = x_ref[...], dy_ref[...]
    gate = dot(x, w_ref[0])
    upper = dot(x, w_ref[1])
    act_grad = dot_nt(dy, d_ref[...])
    sig = jax.nn.sigmoid(gate)
    swish = gate * sig
    act = (swish * upper).astype(BF16)
    act_ref[...] = act
    grad_ref[0] = (act_grad * upper * sig * (1.0 + gate * (1.0 - sig))).astype(BF16)
    grad_ref[1] = (act_grad * swish).astype(BF16)
    down_ref[...] = dot_tn(act, dy).astype(BF16)


def feed(x, dy, gateup_weight, down_weight):
    rows, width = x.shape[0], down_weight.shape[0]
    tile = 256
    whole = lambda i: (0, 0)
    return pl.pallas_call(
        feed_kernel,
        name="feed",
        grid=(width // tile,),
        out_shape=(
            jax.ShapeDtypeStruct((rows, width), BF16),
            jax.ShapeDtypeStruct((2, rows, width), BF16),
            jax.ShapeDtypeStruct((width, D), BF16),
        ),
        in_specs=[
            pl.BlockSpec((rows, D), whole),
            pl.BlockSpec((rows, D), whole),
            pl.BlockSpec((2, D, tile), lambda i: (0, 0, i)),
            pl.BlockSpec((tile, D), lambda i: (i, 0)),
        ],
        out_specs=(
            pl.BlockSpec((rows, tile), lambda i: (0, i)),
            pl.BlockSpec((2, rows, tile), lambda i: (0, 0, i)),
            pl.BlockSpec((tile, D), lambda i: (i, 0)),
        ),
        compiler_params=params("arbitrary"),
        cost_estimate=cost(8 * rows * D * width, 4 * rows * D + 8 * D * width),
    )(x, dy, gateup_weight, down_weight)


def feed_back_kernel(x_ref, act_ref, grad_ref, w_ref, d_ref, full_ref, in_ref, out_ref, in_acc, out_acc):
    step = pl.program_id(0)

    @pl.when(step == 0)
    def _():
        in_acc[...] = jnp.zeros_like(in_acc)
        out_acc[...] = jnp.zeros_like(out_acc)

    in_acc[...] += dot_nt(grad_ref[0], w_ref[0]) + dot_nt(grad_ref[1], w_ref[1])
    out_acc[...] += dot(act_ref[...], d_ref[...])
    x = x_ref[...]
    full_ref[0] = dot_tn(x, grad_ref[0]).astype(BF16)
    full_ref[1] = dot_tn(x, grad_ref[1]).astype(BF16)

    @pl.when(step == pl.num_programs(0) - 1)
    def _():
        in_ref[...] = in_acc[...].astype(BF16)
        out_ref[...] = out_acc[...].astype(BF16)


def feed_back(x, act, grads, gateup_weight, down_weight):
    rows, width = x.shape[0], down_weight.shape[0]
    tile = 256
    whole = lambda i: (0, 0)
    return pl.pallas_call(
        feed_back_kernel,
        name="feed_back",
        grid=(width // tile,),
        out_shape=(
            jax.ShapeDtypeStruct((2, D, width), BF16),
            jax.ShapeDtypeStruct((rows, D), BF16),
            jax.ShapeDtypeStruct((rows, D), BF16),
        ),
        in_specs=[
            pl.BlockSpec((rows, D), whole),
            pl.BlockSpec((rows, tile), lambda i: (0, i)),
            pl.BlockSpec((2, rows, tile), lambda i: (0, 0, i)),
            pl.BlockSpec((2, D, tile), lambda i: (0, 0, i)),
            pl.BlockSpec((tile, D), lambda i: (i, 0)),
        ],
        out_specs=(
            pl.BlockSpec((2, D, tile), lambda i: (0, 0, i)),
            pl.BlockSpec((rows, D), whole),
            pl.BlockSpec((rows, D), whole),
        ),
        scratch_shapes=[pltpu.VMEM((rows, D), F32), pltpu.VMEM((rows, D), F32)],
        compiler_params=params("arbitrary"),
        cost_estimate=cost(10 * rows * D * width, 8 * rows * D + 10 * D * width),
    )(x, act, grads, gateup_weight, down_weight)


def out_back_kernel(dy_ref, w_ref, low_ref, grad_ref, full_ref):
    dy = dy_ref[...]
    grad_ref[...] = dot_nt(dy, w_ref[...]).astype(BF16)
    full_ref[...] = dot_tn(dy, low_ref[...]).astype(BF16)


def out_back(dy, weight, attn_low):
    rows, width = attn_low.shape
    tile = 256
    whole = lambda i: (0, 0)
    return pl.pallas_call(
        out_back_kernel,
        name="out_back",
        grid=(width // tile,),
        out_shape=(
            jax.ShapeDtypeStruct((rows, width), BF16),
            jax.ShapeDtypeStruct((D, width), BF16),
        ),
        in_specs=[
            pl.BlockSpec((rows, D), whole),
            pl.BlockSpec((tile, D), lambda i: (i, 0)),
            pl.BlockSpec((rows, tile), lambda i: (0, i)),
        ],
        out_specs=(
            pl.BlockSpec((rows, tile), lambda i: (0, i)),
            pl.BlockSpec((D, tile), lambda i: (0, i)),
        ),
        compiler_params=params("arbitrary"),
        cost_estimate=cost(4 * rows * D * width, 2 * rows * D + 4 * D * width),
    )(dy, weight, attn_low)


def project_back_kernel(x_ref, q_ref, kv_ref, wq_ref, wkv_ref, in_ref, full_ref):
    q_width, kv_width = wq_ref.shape[1], wkv_ref.shape[2]
    x = x_ref[...]
    key, value = kv_ref[:, :kv_width], kv_ref[:, kv_width:]
    in_ref[...] = (
        dot_nt(q_ref[...], wq_ref[...]) + dot_nt(key, wkv_ref[0]) + dot_nt(value, wkv_ref[1])
    ).astype(BF16)
    full_ref[:, :q_width] = dot_tn(x, q_ref[...]).astype(BF16)
    full_ref[:, q_width:] = dot_tn(x, kv_ref[...]).astype(BF16)


def project_back(x, q_back, kv_back, query_weight, keyvalue_weight):
    rows = x.shape[0]
    q_width, kv_width = query_weight.shape[1], keyvalue_weight.shape[2]
    tile = 512
    whole = lambda i: (0, 0)
    return pl.pallas_call(
        project_back_kernel,
        name="project_back",
        grid=(D // tile,),
        out_shape=(
            jax.ShapeDtypeStruct((rows, D), BF16),
            jax.ShapeDtypeStruct((D, q_width + 2 * kv_width), BF16),
        ),
        in_specs=[
            pl.BlockSpec((rows, tile), lambda i: (0, i)),
            pl.BlockSpec((rows, q_width), whole),
            pl.BlockSpec((rows, 2 * kv_width), whole),
            pl.BlockSpec((tile, q_width), lambda i: (i, 0)),
            pl.BlockSpec((2, tile, kv_width), lambda i: (0, i, 0)),
        ],
        out_specs=(
            pl.BlockSpec((rows, tile), lambda i: (0, i)),
            pl.BlockSpec((tile, q_width + 2 * kv_width), lambda i: (i, 0)),
        ),
        compiler_params=params("arbitrary"),
        cost_estimate=cost(4 * rows * D * (q_width + 2 * kv_width), 6 * D * (q_width + 2 * kv_width)),
    )(x, q_back, kv_back, query_weight, keyvalue_weight)


def wide_scatter(partial, axis):
    return lax.psum_scatter(partial, "wide", scatter_dimension=axis, tiled=True)


def body(
    tokens,
    cotangent,
    gain_copy,
    query_weight,
    keyvalue_weight,
    output_weight,
    gateup_weight,
    down_weight,
    query_master,
    query_moment,
    query_second,
    query_average,
    keyvalue_master,
    keyvalue_moment,
    keyvalue_second,
    keyvalue_average,
    output_master,
    output_moment,
    output_second,
    output_average,
    gateup_master,
    gateup_moment,
    gateup_second,
    gateup_average,
    down_master,
    down_moment,
    down_second,
    down_average,
    gain_master,
    gain_moment,
    gain_second,
    gain_average,
):
    narrow, wide = lax.axis_size("narrow"), lax.axis_size("wide")
    special = narrow == 4 and wide == 8
    stretch_rows = tokens.shape[0] * narrow
    wide_index = lax.axis_index("wide")
    w_scalar = wide_index.astype(jnp.int32).reshape(1)
    kv_heads = keyvalue_weight.shape[2] // HD
    q_heads = query_weight.shape[1] // HD
    group = q_heads // kv_heads
    q_width, kv_width = q_heads * HD, kv_heads * HD
    attn_gain = gain_copy[:D].reshape(1, D)
    mlp_gain = gain_copy[D : 2 * D].reshape(1, D)
    query_gain = gain_copy[2 * D : 2 * D + HD].reshape(1, HD)
    key_gain = gain_copy[2 * D + HD :].reshape(1, HD)

    attn_input = norm_gather(tokens, attn_gain, special)
    positions = (wide_index * stretch_rows + jnp.arange(stretch_rows, dtype=jnp.int32)).astype(F32)
    cosine, sine = rope_tables(positions)
    kv_low, key_raw = keys_values(attn_input, keyvalue_weight, key_gain, cosine, sine)
    late_cotangent, kv_low = lax.optimization_barrier((cotangent, kv_low))
    back_mlp = lax.all_gather(late_cotangent, "narrow", axis=0, tiled=True)
    query_low, query_raw = queries(attn_input, query_weight, query_gain, cosine, sine)
    kv_all = pass_keys(kv_low, wide, special)
    attn_out, attn_low, lse = attend(w_scalar, query_low, kv_all, q_heads, group)
    hidden_mid, mlp_input = mid_forward(
        dot(attn_low, output_weight).astype(BF16), tokens, mlp_gain, special
    )
    act, act_grads, down_full = feed(mlp_input, back_mlp, gateup_weight, down_weight)
    down_total = wide_scatter(down_full, 1)
    gateup_full, in_partial, out_partial = feed_back(
        mlp_input, act, act_grads, gateup_weight, down_weight
    )
    gateup_total = wide_scatter(gateup_full, 1)
    mid_grad, back_attn, mlp_gain_grad = mid_backward(
        in_partial, hidden_mid, cotangent, mlp_gain, special
    )
    attn_grad, output_full = out_back(back_attn, output_weight, attn_low)
    query_sum, kv_sums = attend_back(
        w_scalar, query_low, kv_all, attn_grad, attn_out, lse, q_heads, group
    )
    down_new = adamw(
        down_total.astype(F32),
        down_master,
        down_moment,
        down_second,
        down_average,
        2.0 * FF ** (-0.5),
        WEIGHT_DECAY,
    )
    kv_sums, down_new = lax.optimization_barrier((kv_sums, down_new))
    query_back, query_gain_grad = unspin(query_sum, query_raw, query_gain, cosine, sine)
    kv_sum = return_grads(kv_sums, wide, special)
    kv_back, key_gain_grad = unspin(kv_sum, key_raw, key_gain, cosine, sine)
    normed_partial, project_full = project_back(
        attn_input, query_back, kv_back, query_weight, keyvalue_weight
    )
    input_grad, attn_gain_grad, block_output = last_scatter(
        normed_partial, tokens, mid_grad, attn_gain, out_partial, hidden_mid, special
    )
    gain_partial = jnp.concatenate(
        [attn_gain_grad, mlp_gain_grad, query_gain_grad, key_gain_grad], axis=1
    ).reshape(-1)
    gain_total = gain_sums(gain_partial, wide, narrow, special)

    rest_full = jnp.concatenate([project_full, output_full], axis=1)
    rest_full, gateup_total, gain_total, block_output, input_grad = lax.optimization_barrier(
        (rest_full, gateup_total, gain_total, block_output, input_grad)
    )
    rest_total = wide_scatter(rest_full, 0).astype(F32)
    query_total = rest_total[:, :q_width]
    keyvalue_total = jnp.stack(
        [rest_total[:, q_width : q_width + kv_width], rest_total[:, q_width + kv_width : q_width + 2 * kv_width]]
    )
    output_total = rest_total[:, q_width + 2 * kv_width :].T
    query_new = adamw(
        query_total,
        query_master,
        query_moment,
        query_second,
        query_average,
        2.0 * D ** (-0.5),
        WEIGHT_DECAY,
    )
    keyvalue_new = adamw(
        keyvalue_total,
        keyvalue_master,
        keyvalue_moment,
        keyvalue_second,
        keyvalue_average,
        2.0 * D ** (-0.5),
        WEIGHT_DECAY,
    )
    output_new = adamw(
        output_total,
        output_master,
        output_moment,
        output_second,
        output_average,
        2.0 * WO_FAN ** (-0.5),
        WEIGHT_DECAY,
    )
    gateup_new = adamw(
        gateup_total.astype(F32),
        gateup_master,
        gateup_moment,
        gateup_second,
        gateup_average,
        2.0 * D ** (-0.5),
        WEIGHT_DECAY,
    )
    gain_new = adamw(
        gain_total, gain_master, gain_moment, gain_second, gain_average, RATE_GAIN, 0.0
    )
    return (
        block_output,
        input_grad,
        *query_new,
        *keyvalue_new,
        *output_new,
        *gateup_new,
        *down_new,
        *gain_new,
    )


def solution(mesh):
    rows = P(("wide", "narrow"), None)
    flat = P(("wide", "narrow"))
    stacked = P(None, "wide", "narrow")
    query, output = P("wide", "narrow"), P("narrow", "wide")
    states = (
        *[query] * 4,
        *[stacked] * 4,
        *[output] * 4,
        *[stacked] * 4,
        *[output] * 4,
        *[flat] * 4,
    )
    return jax.shard_map(
        body,
        mesh=mesh,
        in_specs=(
            rows,
            rows,
            P(),
            P(None, "narrow"),
            P(None, None, "narrow"),
            P("narrow", None),
            P(None, None, "narrow"),
            P("narrow", None),
            *states,
        ),
        out_specs=(
            rows,
            rows,
            *[query] * 5,
            *[stacked] * 5,
            *[output] * 5,
            *[stacked] * 5,
            *[output] * 5,
            *[flat] * 5,
        ),
        check_vma=False,
    )
```

```python
import functools

import jax
import jax.numpy as jnp
from jax import lax
from jax.experimental import pallas as pl
from jax.experimental.pallas import tpu as pltpu
from jax.sharding import PartitionSpec as P

D = 2048
HD = 128
FF = 6144
STEP = 10
WO_FAN = 32

EPSILON = 1e-06
THETA = 1000000.0
BETA_ONE = 0.9
BETA_TWO = 0.999
ADAM_EPS = 1e-08
WEIGHT_DECAY = 0.1
EMA_KEEP = 0.5
RATE_GAIN = 0.4
FACTOR = HD ** (-0.5)
LOG2E = 1.4426950408889634

F32 = jnp.float32
BF16 = jnp.bfloat16
MESH = pl.DeviceIdType.MESH
VM = pl.BlockSpec(memory_space=pltpu.VMEM)
SM = pl.BlockSpec(memory_space=pltpu.SMEM)
VMEM_LIMIT = 60 << 20

NT = (((1,), (1,)), ((), ()))
TN = (((0,), (0,)), ((), ()))


def dot(left, right):
    return jnp.dot(left, right, preferred_element_type=F32)


def dot_nt(left, right):
    return lax.dot_general(left, right, NT, preferred_element_type=F32)


def dot_tn(left, right):
    return lax.dot_general(left, right, TN, preferred_element_type=F32)


def rope_tables(positions):
    half_width = HD // 2
    inverse_freq = THETA ** (-(2.0 * jnp.arange(half_width, dtype=F32)) / HD)
    angles = positions[:, None] * inverse_freq[None, :]
    cosine, sine = jnp.cos(angles), jnp.sin(angles)
    return (
        jnp.concatenate([cosine, cosine], axis=-1),
        jnp.concatenate([-sine, sine], axis=-1),
    )


def adamw(gradient, master, moment, second, average, step_rate, decay_rate):
    moment_new = BETA_ONE * moment + (1.0 - BETA_ONE) * gradient
    second_new = BETA_TWO * second + (1.0 - BETA_TWO) * gradient * gradient
    moment_hat = moment_new / (1.0 - BETA_ONE**STEP)
    second_hat = second_new / (1.0 - BETA_TWO**STEP)
    master_new = master - step_rate * (
        moment_hat / (jnp.sqrt(second_hat) + ADAM_EPS) + decay_rate * master
    )
    average_new = EMA_KEEP * average + (1.0 - EMA_KEEP) * master_new
    return (gradient, master_new, moment_new, second_new, average_new)


def row_scale(values_in):
    return lax.rsqrt(jnp.mean(values_in * values_in, axis=-1, keepdims=True) + EPSILON)


def norm_back(gradient, unit_rows, inv_scale, gain_row):
    scaled = gradient * gain_row
    inner = scaled - unit_rows * jnp.mean(scaled * unit_rows, axis=-1, keepdims=True)
    return inv_scale * inner, jnp.sum(gradient * unit_rows, axis=0, keepdims=True)


def square():
    me = lax.axis_index("narrow")
    xn = me + 1 - 2 * (me % 2)
    yn = (me + 2) % 4
    dg = (xn + 2) % 4
    return me, xn, yn, dg


def greet(axis, peers):
    barrier = pltpu.get_barrier_semaphore()
    for peer in peers:
        pl.semaphore_signal(barrier, inc=1, device_id={axis: peer}, device_id_type=MESH)
    pl.semaphore_wait(barrier, len(peers))


class Copies:
    def __init__(self, send, recv):
        self.send, self.recv, self.sent = send, recv, []

    def go(self, src, dst, slot, peer):
        copy = pltpu.make_async_remote_copy(
            src_ref=src,
            dst_ref=dst,
            send_sem=self.send.at[slot],
            recv_sem=self.recv.at[slot],
            device_id={"narrow": peer},
            device_id_type=MESH,
        )
        copy.start()
        self.sent.append(copy)
        return copy

    def finish(self):
        for copy in self.sent:
            copy.wait_send()


def gather_square(copies, slot, x_ref, o_ref):
    me, xn, yn, dg = square()
    rows = x_ref.shape[0]
    half = rows // 2

    def part(owner, low):
        return o_ref.at[pl.ds(pl.multiple_of(owner * rows + low, half), half)]

    upper, lower = x_ref.at[pl.ds(0, half)], x_ref.at[pl.ds(half, half)]
    xa = copies.go(upper, part(me, 0), slot, xn)
    yb = copies.go(lower, part(me, half), slot + 1, yn)
    xb = copies.go(lower, part(me, half), slot + 2, xn)
    ya = copies.go(upper, part(me, 0), slot + 3, yn)
    o_ref[pl.ds(pl.multiple_of(me * rows, rows), rows)] = x_ref[...]
    xa.wait_recv()
    yf = copies.go(part(xn, 0), part(xn, 0), slot + 4, yn)
    yb.wait_recv()
    xf = copies.go(part(yn, half), part(yn, half), slot + 5, xn)
    for copy in (xb, ya, yf, xf):
        copy.wait_recv()


def scatter_square(copies, slot, p_ref, buf, stage, emit, fill=None):
    me, xn, yn, dg = square()
    rows = p_ref.shape[0] // 4
    half = rows // 2

    def part(owner, low):
        return p_ref.at[pl.ds(pl.multiple_of(owner * rows + low, half), half)]

    if fill is None:
        fill = lambda owner: None
    fill(dg)
    c0 = copies.go(part(dg, 0), buf.at[0], slot, xn)
    c1 = copies.go(part(dg, half), buf.at[1], slot + 1, yn)
    fill(xn)
    c2 = copies.go(part(xn, 0), buf.at[2], slot + 2, xn)
    fill(yn)
    c3 = copies.go(part(yn, half), buf.at[3], slot + 3, yn)
    fill(me)
    c0.wait_recv()
    stage[0] = (part(yn, 0)[...].astype(F32) + buf[0].astype(F32)).astype(BF16)
    c4 = copies.go(stage.at[0], buf.at[4], slot + 4, yn)
    c1.wait_recv()
    stage[1] = (part(xn, half)[...].astype(F32) + buf[1].astype(F32)).astype(BF16)
    c5 = copies.go(stage.at[1], buf.at[5], slot + 5, xn)
    c2.wait_recv()
    c4.wait_recv()
    emit(0, part(me, 0)[...].astype(F32) + buf[2].astype(F32) + buf[4].astype(F32))
    c3.wait_recv()
    c5.wait_recv()
    emit(half, part(me, half)[...].astype(F32) + buf[3].astype(F32) + buf[5].astype(F32))


def dma_sems(count):
    return [pltpu.SemaphoreType.DMA((count,)), pltpu.SemaphoreType.DMA((count,))]


def scatter_space(rows):
    return [pltpu.VMEM((6, rows // 2, D), BF16), pltpu.VMEM((2, rows // 2, D), BF16)]


def remote_params(collective_id):
    return pltpu.CompilerParams(
        collective_id=collective_id, has_side_effects=True, vmem_limit_bytes=VMEM_LIMIT
    )


def mid_forward_kernel(a_ref, w_ref, t_ref, g_ref, h_ref, o_ref, p_ref, buf, stage, own, send, recv):
    _, xn, yn, _ = square()
    rows = t_ref.shape[0]
    half = rows // 2
    greet("narrow", (xn, yn))
    copies = Copies(send, recv)

    def fill(owner):
        at = pl.ds(pl.multiple_of(owner * rows, rows), rows)
        p_ref[at, :] = dot(a_ref[at, :], w_ref[...]).astype(BF16)

    def emit(low, total):
        hidden = t_ref[pl.ds(low, half)].astype(F32) + total
        h_ref[pl.ds(low, half)] = hidden
        own[pl.ds(low, half)] = (hidden * row_scale(hidden) * g_ref[...]).astype(BF16)

    scatter_square(copies, 0, p_ref, buf, stage, emit, fill)
    gather_square(copies, 6, own, o_ref)
    copies.finish()


def mid_forward(attn_low, weight, tokens, gain_row, special):
    rows = tokens.shape[0]
    if not special:
        partial = dot(attn_low, weight).astype(BF16)
        hidden = tokens.astype(F32) + lax.psum_scatter(
            partial, "narrow", scatter_dimension=0, tiled=True
        ).astype(F32)
        normed = (hidden * row_scale(hidden) * gain_row).astype(BF16)
        return hidden, lax.all_gather(normed, "narrow", axis=0, tiled=True)
    return pl.pallas_call(
        mid_forward_kernel,
        name="mid_forward",
        out_shape=(
            jax.ShapeDtypeStruct((rows, D), F32),
            jax.ShapeDtypeStruct((4 * rows, D), BF16),
        ),
        in_specs=[VM] * 4,
        out_specs=(VM, VM),
        scratch_shapes=[pltpu.VMEM((4 * rows, D), BF16)]
        + scatter_space(rows) + [pltpu.VMEM((rows, D), BF16)] + dma_sems(12),
        cost_estimate=cost(1, 1),
        compiler_params=remote_params(2),
    )(attn_low, weight, tokens, gain_row)


def mid_backward_kernel(
    p_ref, h_ref, c_ref, g_ref, m_ref, o_ref, gg_ref, buf, stage, own, send, recv
):
    _, xn, yn, _ = square()
    half = h_ref.shape[0] // 2
    greet("narrow", (xn, yn))
    copies = Copies(send, recv)
    gg_ref[...] = jnp.zeros_like(gg_ref)

    def emit(low, total):
        hidden = h_ref[pl.ds(low, half)]
        scale = row_scale(hidden)
        back, gain_sum = norm_back(total, hidden * scale, scale, g_ref[...])
        gg_ref[...] += gain_sum
        mid = c_ref[pl.ds(low, half)].astype(F32) + back
        m_ref[pl.ds(low, half)] = mid
        own[pl.ds(low, half)] = mid.astype(BF16)

    scatter_square(copies, 0, p_ref, buf, stage, emit)
    gather_square(copies, 6, own, o_ref)
    copies.finish()


def mid_backward(partial, hidden_mid, cotangent, gain_row, special):
    rows = hidden_mid.shape[0]
    if not special:
        total = lax.psum_scatter(partial, "narrow", scatter_dimension=0, tiled=True).astype(F32)
        scale = row_scale(hidden_mid)
        back, gain_sum = norm_back(total, hidden_mid * scale, scale, gain_row)
        mid = cotangent.astype(F32) + back
        return mid, lax.all_gather(mid.astype(BF16), "narrow", axis=0, tiled=True), gain_sum
    return pl.pallas_call(
        mid_backward_kernel,
        name="mid_backward",
        out_shape=(
            jax.ShapeDtypeStruct((rows, D), F32),
            jax.ShapeDtypeStruct((4 * rows, D), BF16),
            jax.ShapeDtypeStruct((1, D), F32),
        ),
        in_specs=[VM] * 4,
        out_specs=(VM,) * 3,
        scratch_shapes=scatter_space(rows) + [pltpu.VMEM((rows, D), BF16)] + dma_sems(12),
        cost_estimate=cost(1, 1),
        compiler_params=remote_params(3),
    )(partial, hidden_mid, cotangent, gain_row)


def out_scatter_kernel(p_ref, h_ref, o_ref, buf, stage, send, recv):
    _, xn, yn, _ = square()
    half = h_ref.shape[0] // 2
    greet("narrow", (xn, yn))
    copies = Copies(send, recv)

    def emit(low, total):
        o_ref[pl.ds(low, half)] = h_ref[pl.ds(low, half)] + total

    scatter_square(copies, 0, p_ref, buf, stage, emit)
    copies.finish()


def out_scatter(partial, hidden_mid, special):
    rows = hidden_mid.shape[0]
    if not special:
        total = lax.psum_scatter(partial, "narrow", scatter_dimension=0, tiled=True)
        return hidden_mid + total.astype(F32)
    return pl.pallas_call(
        out_scatter_kernel,
        name="out_scatter",
        out_shape=jax.ShapeDtypeStruct((rows, D), F32),
        in_specs=[VM] * 2,
        out_specs=VM,
        scratch_shapes=scatter_space(rows) + dma_sems(6),
        cost_estimate=cost(1, 1),
        compiler_params=remote_params(9),
    )(partial, hidden_mid)


def in_scatter_kernel(p_ref, t_ref, m_ref, g_ref, o_ref, gg_ref, buf, stage, send, recv):
    _, xn, yn, _ = square()
    half = t_ref.shape[0] // 2
    greet("narrow", (xn, yn))
    copies = Copies(send, recv)
    gg_ref[...] = jnp.zeros_like(gg_ref)

    def emit(low, total):
        hidden = t_ref[pl.ds(low, half)].astype(F32)
        scale = row_scale(hidden)
        back, gain_sum = norm_back(total, hidden * scale, scale, g_ref[...])
        gg_ref[...] += gain_sum
        o_ref[pl.ds(low, half)] = m_ref[pl.ds(low, half)] + back

    scatter_square(copies, 0, p_ref, buf, stage, emit)
    copies.finish()


def in_scatter(partial, tokens, mid_grad, gain_row, special):
    rows = tokens.shape[0]
    if not special:
        total = lax.psum_scatter(partial, "narrow", scatter_dimension=0, tiled=True).astype(F32)
        hidden = tokens.astype(F32)
        scale = row_scale(hidden)
        back, gain_sum = norm_back(total, hidden * scale, scale, gain_row)
        return mid_grad + back, gain_sum
    return pl.pallas_call(
        in_scatter_kernel,
        name="in_scatter",
        out_shape=(
            jax.ShapeDtypeStruct((rows, D), F32),
            jax.ShapeDtypeStruct((1, D), F32),
        ),
        in_specs=[VM] * 4,
        out_specs=(VM,) * 2,
        scratch_shapes=scatter_space(rows) + dma_sems(6),
        cost_estimate=cost(1, 1),
        compiler_params=remote_params(4),
    )(partial, tokens, mid_grad, gain_row)


def line(count):
    w = lax.axis_index("wide")
    z, c = w // 2, w % 2
    return w, z, c, count // 2, w + 1 - 2 * c, jnp.minimum(w + 2, count - 1), jnp.maximum(w - 2, 0)


def greet_line(count):
    w, z, c, chips, mate, above, below = line(count)
    barrier = pltpu.get_barrier_semaphore()
    has_above, has_below = z < chips - 1, z > 0

    @pl.when(has_above)
    def _():
        pl.semaphore_signal(barrier, inc=1, device_id={"wide": above}, device_id_type=MESH)

    @pl.when(has_below)
    def _():
        pl.semaphore_signal(barrier, inc=1, device_id={"wide": below}, device_id_type=MESH)

    pl.semaphore_signal(barrier, inc=1, device_id={"wide": mate}, device_id_type=MESH)
    pl.semaphore_wait(barrier, 1 + has_above.astype(jnp.int32) + has_below.astype(jnp.int32))


def wide_copy(src, dst, send, recv, slot, peer):
    return pltpu.make_async_remote_copy(
        src_ref=src,
        dst_ref=dst,
        send_sem=send.at[slot],
        recv_sem=recv.at[slot],
        device_id={"wide": peer},
        device_id_type=MESH,
    )


def return_grads_kernel(
    count, x_ref, o_ref, from_mate, from_above, stage, send, recv, mate_send, mate_recv
):
    w, z, c, chips, mate, above, below = line(count)
    greet_line(count)

    def to_mate(s):
        return wide_copy(
            x_ref.at[jnp.minimum(2 * s + 1 - c, count - 1)],
            from_mate.at[s],
            mate_send,
            mate_recv,
            s,
            mate,
        )

    def sends_mate(s):
        return (z > s) | ((z == s) & (c == 1))

    def gets_mate(s):
        return (z > s) | ((z == s) & (c == 0))

    def down(s):
        return wide_copy(stage.at[s], from_above.at[s], send, recv, s, below)

    for s in range(chips):

        @pl.when(sends_mate(s))
        def _():
            to_mate(s).start()

    for s in range(chips):
        block = jnp.minimum(2 * s + c, count - 1)

        @pl.when(z > s)
        def _():
            to_mate(s).wait_recv()

            @pl.when(z == chips - 1)
            def _():
                stage[s] = (x_ref[block].astype(F32) + from_mate[s].astype(F32)).astype(BF16)

            @pl.when(z < chips - 1)
            def _():
                down(s).wait_recv()
                stage[s] = (
                    x_ref[block].astype(F32) + from_mate[s].astype(F32) + from_above[s].astype(F32)
                ).astype(BF16)

            down(s).start()

        @pl.when(z == s)
        def _():
            o_ref[...] = x_ref[block].astype(F32)

            @pl.when(c == 0)
            def _():
                to_mate(s).wait_recv()
                o_ref[...] += from_mate[s].astype(F32)

            if s < chips - 1:
                down(s).wait_recv()
                o_ref[...] += from_above[s].astype(F32)

    for s in range(chips):

        @pl.when(sends_mate(s))
        def _():
            to_mate(s).wait_send()

        @pl.when(z > s)
        def _():
            down(s).wait_send()


def return_grads(grads, count, special):
    _, rows, width = grads.shape
    if not special:
        w = lax.axis_index("wide")
        seen = (jnp.arange(count) <= w)[:, None, None]
        total = lax.psum_scatter(
            jnp.where(seen, grads, 0).reshape(count * rows, width),
            "wide",
            scatter_dimension=0,
            tiled=True,
        )
        return total.astype(F32)
    chips = count // 2
    return pl.pallas_call(
        functools.partial(return_grads_kernel, count),
        name="return_grads",
        out_shape=jax.ShapeDtypeStruct((rows, width), F32),
        in_specs=[VM],
        out_specs=VM,
        scratch_shapes=[
            pltpu.VMEM((chips, rows, width), BF16),
            pltpu.VMEM((chips, rows, width), BF16),
            pltpu.VMEM((chips, rows, width), BF16),
        ]
        + dma_sems(chips)
        + dma_sems(chips),
        cost_estimate=cost(1, 1),
        compiler_params=remote_params(6),
    )(grads)


def gain_kernel(wide, x_ref, o_ref, near, mid, far, send, recv, wide_send, wide_recv):
    me, xn, yn, dg = square()
    w = lax.axis_index("wide")
    barrier = pltpu.get_barrier_semaphore()
    for peer in (xn, yn, dg):
        pl.semaphore_signal(barrier, inc=1, device_id={"narrow": peer}, device_id_type=MESH)
    for step in range(1, wide):
        pl.semaphore_signal(
            barrier, inc=1, device_id={"wide": (w + step) % wide}, device_id_type=MESH
        )
    pl.semaphore_wait(barrier, 3 + wide - 1)
    copies = Copies(send, recv)
    sent = [
        copies.go(x_ref.at[peer], near.at[slot], slot, peer)
        for slot, peer in enumerate((xn, yn, dg))
    ]
    for copy in sent:
        copy.wait_recv()
    mid[...] = x_ref[me] + near[0] + near[1] + near[2]
    away = []
    for step in range(1, wide):
        peer = (w + step) % wide
        copy = wide_copy(
            mid.at[peer], far.at[step - 1], wide_send, wide_recv, step - 1, peer
        )
        copy.start()
        away.append(copy)
    total = mid[w]
    for step in range(1, wide):
        away[step - 1].wait_recv()
        total = total + far[step - 1]
    o_ref[...] = total
    copies.finish()
    for copy in away:
        copy.wait_send()


def gain_sums(partial, wide, narrow, special):
    if not special:
        return lax.psum_scatter(partial, ("wide", "narrow"), scatter_dimension=0, tiled=True)
    count = partial.shape[0] // (wide * narrow)
    padded = -(-count // 128) * 128
    shaped = partial.reshape(wide, narrow, count).transpose(1, 0, 2)
    shaped = jnp.pad(shaped, ((0, 0), (0, 0), (0, padded - count)))
    shaped = shaped.reshape(narrow, wide, padded // 128, 128)
    out = pl.pallas_call(
        functools.partial(gain_kernel, wide),
        name="gain_sums",
        out_shape=jax.ShapeDtypeStruct((padded // 128, 128), F32),
        in_specs=[VM],
        out_specs=VM,
        scratch_shapes=[
            pltpu.VMEM((3, wide, padded // 128, 128), F32),
            pltpu.VMEM((wide, padded // 128, 128), F32),
            pltpu.VMEM((wide - 1, padded // 128, 128), F32),
        ]
        + dma_sems(3)
        + dma_sems(wide - 1),
        cost_estimate=cost(1, 1),
        compiler_params=remote_params(7),
    )(shaped)
    return out.reshape(padded)[:count]


def cost(flops, moved, exps=0):
    return pl.CostEstimate(flops=1, bytes_accessed=1, transcendentals=0)


def params(*semantics):
    if not semantics:
        return pltpu.CompilerParams(vmem_limit_bytes=VMEM_LIMIT)
    return pltpu.CompilerParams(vmem_limit_bytes=VMEM_LIMIT, dimension_semantics=semantics)


def spin(raw, gain_row, cosine, sine):
    normed = raw * row_scale(raw) * gain_row
    return normed * cosine + pltpu.roll(normed, HD // 2, axis=1) * sine


def keys_kernel(x_ref, w_ref, g_ref, cos_ref, sin_ref, kv_ref, raw_ref):
    which = pl.program_id(0)
    width = w_ref.shape[2]
    out = dot(x_ref[...], w_ref[0])

    @pl.when(which == 0)
    def _():
        raw_ref[...] = out
        for h in range(width // HD):
            part = out[:, h * HD : (h + 1) * HD]
            kv_ref[:, h * HD : (h + 1) * HD] = spin(
                part, g_ref[...], cos_ref[...], sin_ref[...]
            ).astype(BF16)

    @pl.when(which == 1)
    def _():
        kv_ref[...] = out.astype(BF16)


def keys_values(x, weight, gain_row, cosine, sine):
    rows, width = x.shape[0], weight.shape[2]
    whole = lambda i: (0, 0)
    return pl.pallas_call(
        keys_kernel,
        name="keys_values",
        grid=(2,),
        out_shape=(
            jax.ShapeDtypeStruct((rows, 2 * width), BF16),
            jax.ShapeDtypeStruct((rows, width), F32),
        ),
        in_specs=[
            pl.BlockSpec((rows, D), whole),
            pl.BlockSpec((1, D, width), lambda i: (i, 0, 0)),
            pl.BlockSpec((1, HD), whole),
            pl.BlockSpec((rows, HD), whole),
            pl.BlockSpec((rows, HD), whole),
        ],
        out_specs=(
            pl.BlockSpec((rows, width), lambda i: (0, i)),
            pl.BlockSpec((rows, width), whole),
        ),
        compiler_params=params("arbitrary"),
        cost_estimate=cost(4 * rows * D * width, 2 * rows * D + 4 * D * width),
    )(x, weight, gain_row, cosine, sine)


def queries_kernel(x_ref, w_ref, g_ref, cos_ref, sin_ref, q_ref, raw_ref):
    out = dot(x_ref[...], w_ref[...])
    raw_ref[...] = out
    for h in range(w_ref.shape[1] // HD):
        part = out[:, h * HD : (h + 1) * HD]
        q_ref[:, h * HD : (h + 1) * HD] = spin(
            part, g_ref[...], cos_ref[...], sin_ref[...]
        ).astype(BF16)


def queries(x, weight, gain_row, cosine, sine):
    rows, width = x.shape[0], weight.shape[1]
    tile = 256
    whole = lambda i: (0, 0)
    return pl.pallas_call(
        queries_kernel,
        name="queries",
        grid=(width // tile,),
        out_shape=(
            jax.ShapeDtypeStruct((rows, width), BF16),
            jax.ShapeDtypeStruct((rows, width), F32),
        ),
        in_specs=[
            pl.BlockSpec((rows, D), whole),
            pl.BlockSpec((D, tile), lambda i: (0, i)),
            pl.BlockSpec((1, HD), whole),
            pl.BlockSpec((rows, HD), whole),
            pl.BlockSpec((rows, HD), whole),
        ],
        out_specs=(
            pl.BlockSpec((rows, tile), lambda i: (0, i)),
            pl.BlockSpec((rows, tile), lambda i: (0, i)),
        ),
        compiler_params=params("arbitrary"),
        cost_estimate=cost(2 * rows * D * width, 2 * rows * D + 2 * D * width),
    )(x, weight, gain_row, cosine, sine)


def attend_kernel(heads, group, w_ref, q_ref, kv_ref, o_ref, low_ref, lse_ref, acc):
    rows = q_ref.shape[0]
    kv_width = kv_ref.shape[2] // 2
    w = w_ref[0]
    acc[...] = jnp.zeros_like(acc)
    ones = jnp.ones((rows, HD), BF16)

    def block(j, masked):
        for h in range(heads):
            kv = h // group
            key = kv_ref[j, :, kv * HD : (kv + 1) * HD]
            value = kv_ref[j, :, kv_width + kv * HD : kv_width + (kv + 1) * HD]
            query = q_ref[:, h * HD : (h + 1) * HD]
            terms = jnp.exp2(dot_nt(query, key) * (FACTOR * LOG2E))
            if masked:
                at = lax.broadcasted_iota(jnp.int32, (rows, rows), 0)
                key_at = lax.broadcasted_iota(jnp.int32, (rows, rows), 1)
                terms = jnp.where(key_at <= at, terms, 0.0)
            acc[h] += dot(terms.astype(BF16), jnp.concatenate([value, ones], axis=1))

    @pl.loop(0, w)
    def _(j):
        block(j, False)

    block(w, True)
    for h in range(heads):
        total = acc[h, :, HD:]
        out = acc[h, :, :HD] / total
        o_ref[:, h * HD : (h + 1) * HD] = out
        low_ref[:, h * HD : (h + 1) * HD] = out.astype(BF16)
        lse_ref[h : h + 1, :] = jnp.transpose(jnp.log2(total))[0:1]


def attend(w_index, query, kv_all, heads, group):
    rows, width = query.shape
    count = kv_all.shape[0]
    return pl.pallas_call(
        functools.partial(attend_kernel, heads, group),
        name="attend",
        out_shape=(
            jax.ShapeDtypeStruct((rows, width), F32),
            jax.ShapeDtypeStruct((rows, width), BF16),
            jax.ShapeDtypeStruct((heads, rows), F32),
        ),
        in_specs=[SM, VM, VM],
        out_specs=(VM, VM, VM),
        scratch_shapes=[pltpu.VMEM((heads, rows, 2 * HD), F32)],
        compiler_params=params(),
        cost_estimate=cost(4 * rows * rows * count * width, 2 * kv_all.size, rows * rows * heads * count),
    )(w_index, query, kv_all)


def attend_back_kernel(
    heads, group, w_ref, q_ref, kv_ref, do_ref, o_ref, lse_ref, dq_ref, dkv_ref, delta
):
    rows = q_ref.shape[0]
    kv_width = kv_ref.shape[2] // 2
    w = w_ref[0]
    for h in range(heads):
        part = slice(h * HD, (h + 1) * HD)
        delta[h : h + 1, :] = jnp.sum(
            jnp.transpose(do_ref[:, part].astype(F32) * o_ref[:, part]), axis=0, keepdims=True
        )
    dq_ref[...] = jnp.zeros_like(dq_ref)

    def block(j, masked):
        for kv in range(heads // group):
            key = kv_ref[j, :, kv * HD : (kv + 1) * HD]
            value = kv_ref[j, :, kv_width + kv * HD : kv_width + (kv + 1) * HD]
            key_sum = jnp.zeros((rows, HD), F32)
            value_sum = jnp.zeros((rows, HD), F32)
            for h in range(kv * group, (kv + 1) * group):
                part = slice(h * HD, (h + 1) * HD)
                query, out_grad = q_ref[:, part], do_ref[:, part]
                probs = jnp.exp2(
                    dot_nt(key, query) * (FACTOR * LOG2E) - lse_ref[h : h + 1, :]
                )
                if masked:
                    key_at = lax.broadcasted_iota(jnp.int32, (rows, rows), 0)
                    at = lax.broadcasted_iota(jnp.int32, (rows, rows), 1)
                    probs = jnp.where(key_at <= at, probs, 0.0)
                value_sum += dot(probs.astype(BF16), out_grad)
                prob_grad = dot_nt(value, out_grad)
                score_grad = (probs * (prob_grad - delta[h : h + 1, :])).astype(BF16)
                key_sum += dot(score_grad, query)
                dq_ref[:, part] += dot_tn(score_grad, key)
            dkv_ref[j, :, kv * HD : (kv + 1) * HD] = (key_sum * FACTOR).astype(BF16)
            dkv_ref[j, :, kv_width + kv * HD : kv_width + (kv + 1) * HD] = value_sum.astype(BF16)

    @pl.loop(0, w)
    def _(j):
        block(j, False)

    block(w, True)
    dq_ref[...] = dq_ref[...] * FACTOR


def attend_back(w_index, query, kv_all, out_grad, out, lse, heads, group):
    rows, width = query.shape
    count = kv_all.shape[0]
    return pl.pallas_call(
        functools.partial(attend_back_kernel, heads, group),
        name="attend_back",
        out_shape=(
            jax.ShapeDtypeStruct((rows, width), F32),
            jax.ShapeDtypeStruct(kv_all.shape, BF16),
        ),
        in_specs=[SM] + [VM] * 5,
        out_specs=(VM, VM),
        scratch_shapes=[pltpu.VMEM((heads, rows), F32)],
        compiler_params=params(),
        cost_estimate=cost(10 * rows * rows * count * width, 4 * kv_all.size, rows * rows * heads * count),
    )(w_index, query, kv_all, out_grad, out, lse)


def unspin_kernel(width, e_ref, raw_ref, g_ref, cos_ref, sin_ref, o_ref, gg_ref):
    gain_sum = jnp.zeros((1, HD), F32)
    for h in range(raw_ref.shape[1] // HD):
        part = slice(h * HD, (h + 1) * HD)
        grad = e_ref[:, part]
        turned = grad * cos_ref[...] - pltpu.roll(grad, HD // 2, axis=1) * sin_ref[...]
        raw = raw_ref[:, part]
        scale = row_scale(raw)
        back, total = norm_back(turned, raw * scale, scale, g_ref[...])
        o_ref[:, part] = back.astype(BF16)
        gain_sum += total
    if width > raw_ref.shape[1]:
        o_ref[:, raw_ref.shape[1] :] = e_ref[:, raw_ref.shape[1] :].astype(BF16)
    gg_ref[...] = gain_sum


def unspin(grad, raw, gain_row, cosine, sine):
    rows, width = grad.shape
    return pl.pallas_call(
        functools.partial(unspin_kernel, width),
        name="unspin",
        out_shape=(
            jax.ShapeDtypeStruct((rows, width), BF16),
            jax.ShapeDtypeStruct((1, HD), F32),
        ),
        in_specs=[VM] * 5,
        out_specs=(VM, VM),
        compiler_params=params(),
        cost_estimate=cost(20 * grad.size, 10 * grad.size),
    )(grad, raw, gain_row, cosine, sine)


def front_kernel(
    count, heads, group,
    t_ref, c_ref, g_ref, wq_hbm, wkv_hbm, qg_ref, kg_ref, cos_ref, sin_ref,
    dy_hbm, x_hbm, q_hbm, qraw_hbm, kraw_hbm, kv_hbm, o_ref, low_ref, lse_ref,
    own, x, weight, q, qraw, kraw, kv, acc,
    send, recv, z_send, z_recv, m_send, m_recv, c_send, c_recv, load_sem, store_sem, kv_sem,
):
    me, xn, yn, dg = square()
    w, z, c, chips, mate, above, below = line(count)
    rows = t_ref.shape[0]
    half = rows // 2
    all_rows = 4 * rows
    q_width, kv_width = wq_hbm.shape[1], wkv_hbm.shape[2]
    owners = (me, xn, yn, dg)
    loads = [
        pltpu.make_async_copy(wq_hbm, weight.at[:, pl.ds(0, q_width)], load_sem.at[0]),
        pltpu.make_async_copy(wkv_hbm.at[0], weight.at[:, pl.ds(q_width, kv_width)], load_sem.at[1]),
        pltpu.make_async_copy(
            wkv_hbm.at[1], weight.at[:, pl.ds(q_width + kv_width, kv_width)], load_sem.at[2]
        ),
    ]
    for load in loads:
        load.start()

    has_above, has_below = z < chips - 1, z > 0
    barrier = pltpu.get_barrier_semaphore()
    for peer in (xn, yn, dg):
        pl.semaphore_signal(barrier, inc=1, device_id={"narrow": peer}, device_id_type=MESH)

    @pl.when(has_above)
    def _():
        pl.semaphore_signal(barrier, inc=1, device_id={"wide": above}, device_id_type=MESH)

    @pl.when(has_below)
    def _():
        pl.semaphore_signal(barrier, inc=1, device_id={"wide": below}, device_id_type=MESH)

    pl.semaphore_signal(barrier, inc=1, device_id={"wide": mate}, device_id_type=MESH)
    hidden = t_ref[...].astype(F32)
    own[...] = (hidden * row_scale(hidden) * g_ref[...]).astype(BF16)
    pl.semaphore_wait(barrier, 4 + has_above.astype(jnp.int32) + has_below.astype(jnp.int32))

    copies = Copies(send, recv)

    def part(owner, low):
        return x.at[pl.ds(pl.multiple_of(owner * rows + low, half), half)]

    upper, lower = own.at[pl.ds(0, half)], own.at[pl.ds(half, half)]
    xa = copies.go(upper, part(me, 0), 0, xn)
    yb = copies.go(lower, part(me, half), 1, yn)
    xb = copies.go(lower, part(me, half), 2, xn)
    ya = copies.go(upper, part(me, 0), 3, yn)

    def unit_rows(unit):
        return pl.ds(pl.multiple_of(owners[unit] * rows, rows), rows)

    def unit(block, k):
        return kv.at[block, unit_rows(k)]

    def to_above(s, k):
        block = jnp.maximum(w - 2 * s, 0)
        return wide_copy(unit(block, k), unit(block, k), z_send, z_recv, 4 * s + k, above)

    def from_below(s, k):
        block = jnp.maximum(w - 2 * s, 0)
        return wide_copy(unit(block, k), unit(block, k), z_send, z_recv, 4 * (s - 1) + k, above)

    def to_mate(s, k):
        block = jnp.maximum(w - 2 * s, 0)
        return wide_copy(unit(block, k), unit(block, k), m_send, m_recv, 4 * s + k, mate)

    def project(k):
        at = unit_rows(k)
        out = dot(x[at, :], weight[...])
        cosine, sine = cos_ref[at, :], sin_ref[at, :]
        qraw[at, :] = out[:, :q_width]
        kraw[at, :] = out[:, q_width : q_width + kv_width]
        for h in range(heads):
            lanes = slice(h * HD, (h + 1) * HD)
            q[at, lanes] = spin(out[:, lanes], qg_ref[...], cosine, sine).astype(BF16)
        for h in range(heads // group):
            lanes = slice(q_width + h * HD, q_width + (h + 1) * HD)
            kv[w, at, h * HD : (h + 1) * HD] = spin(
                out[:, lanes], kg_ref[...], cosine, sine
            ).astype(BF16)
        kv[w, at, kv_width:] = out[:, q_width + kv_width :].astype(BF16)

        @pl.when(has_above)
        def _():
            to_above(0, k).start()

        @pl.when(c == 0)
        def _():
            to_mate(0, k).start()

    def receive(s, k):
        @pl.when(z >= s)
        def _():
            from_below(s, k).wait_recv()
            if s < chips - 1:

                @pl.when(has_above)
                def _():
                    to_above(s, k).start()

            to_mate(s, k).start()

    x[unit_rows(0), :] = own[...]
    for load in loads:
        load.wait()
    project(0)
    xa.wait_recv()
    yf = copies.go(part(xn, 0), part(xn, 0), 4, yn)
    yb.wait_recv()
    xf = copies.go(part(yn, half), part(yn, half), 5, xn)
    receive(1, 0)
    xb.wait_recv()
    project(1)
    ya.wait_recv()
    project(2)
    receive(2, 0)
    receive(1, 1)
    receive(1, 2)
    receive(3, 0)
    yf.wait_recv()
    xf.wait_recv()
    project(3)
    away = Copies(c_send, c_recv)
    dy_part = dy_hbm.at[unit_rows(0)]
    for slot, peer in enumerate((dg, xn, yn)):
        away.go(c_ref, dy_part, slot, peer)
    stores = [
        pltpu.make_async_copy(src, dst, store_sem.at[n])
        for n, (src, dst) in enumerate(
            ((x, x_hbm), (q, q_hbm), (qraw, qraw_hbm), (kraw, kraw_hbm), (c_ref, dy_part))
        )
    ]
    for store in stores:
        store.start()
    acc[...] = jnp.zeros_like(acc)
    ones = jnp.ones((all_rows, HD), BF16)

    def keep(j):
        return pltpu.make_async_copy(kv.at[j], kv_hbm.at[j], kv_sem.at[j])

    def block(j, masked):
        for h in range(heads):
            head = h // group
            key = kv[j, :, head * HD : (head + 1) * HD]
            value = kv[j, :, kv_width + head * HD : kv_width + (head + 1) * HD]
            terms = jnp.exp2(dot_nt(q[:, h * HD : (h + 1) * HD], key) * (FACTOR * LOG2E))
            if masked:
                at = lax.broadcasted_iota(jnp.int32, (all_rows, all_rows), 0)
                key_at = lax.broadcasted_iota(jnp.int32, (all_rows, all_rows), 1)
                terms = jnp.where(key_at <= at, terms, 0.0)
            acc[h] += dot(terms.astype(BF16), jnp.concatenate([value, ones], axis=1))
        keep(j).start()

    block(w, True)

    @pl.loop(1 - c, 2 * z + 1)
    def _(i):
        for s, units in ((1, ((2, 1), (2, 2), (1, 3))), (2, ((3, 1), (3, 2), (2, 3))), (3, ((3, 3),))):

            @pl.when(i == 2 * s - 1)
            def _():
                for pair in units:
                    receive(*pair)

        for s in range(chips):

            @pl.when(i == 2 * s)
            def _():
                for k in range(4):
                    to_mate(s, k).wait_recv()

        odd = i % 2
        step = (i + 1) // 2
        block(2 * (z - step) + c + (1 - odd) * (1 - 2 * c), False)

    for h in range(heads):
        total = acc[h, :, HD:]
        out = acc[h, :, :HD] / total
        o_ref[:, h * HD : (h + 1) * HD] = out
        low_ref[:, h * HD : (h + 1) * HD] = out.astype(BF16)
        lse_ref[h : h + 1, :] = jnp.transpose(jnp.log2(total))[0:1]

    copies.finish()
    for copy in away.sent:
        copy.wait()
    for s in range(chips):
        for k in range(4):

            @pl.when((z >= s) & has_above)
            def _():
                to_above(s, k).wait_send()

            @pl.when((z >= s) & ((c == 0) | (s > 0)))
            def _():
                to_mate(s, k).wait_send()

    for store in stores:
        store.wait()

    @pl.loop(0, w + 1)
    def _(j):
        keep(j).wait()


def front(tokens, cotangent, gain_row, query_weight, keyvalue_weight, query_gain, key_gain, cosine, sine, count):
    rows = tokens.shape[0]
    all_rows = 4 * rows
    q_width, kv_width = query_weight.shape[1], keyvalue_weight.shape[2]
    heads, group = q_width // HD, q_width // kv_width
    chips = count // 2
    anywhere = pl.BlockSpec(memory_space=pl.ANY)
    return pl.pallas_call(
        functools.partial(front_kernel, count, heads, group),
        name="front",
        out_shape=(
            jax.ShapeDtypeStruct((all_rows, D), BF16),
            jax.ShapeDtypeStruct((all_rows, D), BF16),
            jax.ShapeDtypeStruct((all_rows, q_width), BF16),
            jax.ShapeDtypeStruct((all_rows, q_width), F32),
            jax.ShapeDtypeStruct((all_rows, kv_width), F32),
            jax.ShapeDtypeStruct((count, all_rows, 2 * kv_width), BF16),
            jax.ShapeDtypeStruct((all_rows, q_width), F32),
            jax.ShapeDtypeStruct((all_rows, q_width), BF16),
            jax.ShapeDtypeStruct((heads, all_rows), F32),
        ),
        in_specs=[VM, VM, VM, anywhere, anywhere, VM, VM, VM, VM],
        out_specs=(anywhere,) * 6 + (VM,) * 3,
        scratch_shapes=[
            pltpu.VMEM((rows, D), BF16),
            pltpu.VMEM((all_rows, D), BF16),
            pltpu.VMEM((D, q_width + 2 * kv_width), BF16),
            pltpu.VMEM((all_rows, q_width), BF16),
            pltpu.VMEM((all_rows, q_width), F32),
            pltpu.VMEM((all_rows, kv_width), F32),
            pltpu.VMEM((count, all_rows, 2 * kv_width), BF16),
            pltpu.VMEM((heads, all_rows, 2 * HD), F32),
        ]
        + dma_sems(6)
        + dma_sems(4 * chips)
        + dma_sems(4 * chips)
        + dma_sems(3)
        + [
            pltpu.SemaphoreType.DMA((3,)),
            pltpu.SemaphoreType.DMA((5,)),
            pltpu.SemaphoreType.DMA((count,)),
        ],
        cost_estimate=cost(1, 1),
        compiler_params=remote_params(8),
    )(tokens, cotangent, gain_row, query_weight, keyvalue_weight, query_gain, key_gain, cosine, sine)


def feed_kernel(x_ref, dy_ref, w_ref, d_ref, act_ref, grad_ref, down_ref):
    x, dy = x_ref[...], dy_ref[...]
    gate = dot(x, w_ref[0])
    upper = dot(x, w_ref[1])
    act_grad = dot_nt(dy, d_ref[...])
    sig = jax.nn.sigmoid(gate)
    swish = gate * sig
    act = (swish * upper).astype(BF16)
    act_ref[...] = act
    grad_ref[0] = (act_grad * upper * sig * (1.0 + gate * (1.0 - sig))).astype(BF16)
    grad_ref[1] = (act_grad * swish).astype(BF16)
    down_ref[...] = dot_tn(act, dy).astype(BF16)


def feed(x, dy, gateup_weight, down_weight):
    rows, width = x.shape[0], down_weight.shape[0]
    tile = 256
    whole = lambda i: (0, 0)
    return pl.pallas_call(
        feed_kernel,
        name="feed",
        grid=(width // tile,),
        out_shape=(
            jax.ShapeDtypeStruct((rows, width), BF16),
            jax.ShapeDtypeStruct((2, rows, width), BF16),
            jax.ShapeDtypeStruct((width, D), BF16),
        ),
        in_specs=[
            pl.BlockSpec((rows, D), whole),
            pl.BlockSpec((rows, D), whole),
            pl.BlockSpec((2, D, tile), lambda i: (0, 0, i)),
            pl.BlockSpec((tile, D), lambda i: (i, 0)),
        ],
        out_specs=(
            pl.BlockSpec((rows, tile), lambda i: (0, i)),
            pl.BlockSpec((2, rows, tile), lambda i: (0, 0, i)),
            pl.BlockSpec((tile, D), lambda i: (i, 0)),
        ),
        compiler_params=params("arbitrary"),
        cost_estimate=cost(8 * rows * D * width, 4 * rows * D + 8 * D * width),
    )(x, dy, gateup_weight, down_weight)


def feed_back_kernel(x_ref, act_ref, grad_ref, w_ref, d_ref, full_ref, in_ref, out_ref, in_acc, out_acc):
    step = pl.program_id(0)

    @pl.when(step == 0)
    def _():
        in_acc[...] = jnp.zeros_like(in_acc)
        out_acc[...] = jnp.zeros_like(out_acc)

    in_acc[...] += dot_nt(grad_ref[0], w_ref[0]) + dot_nt(grad_ref[1], w_ref[1])
    out_acc[...] += dot(act_ref[...], d_ref[...])
    x = x_ref[...]
    full_ref[0] = dot_tn(x, grad_ref[0]).astype(BF16)
    full_ref[1] = dot_tn(x, grad_ref[1]).astype(BF16)

    @pl.when(step == pl.num_programs(0) - 1)
    def _():
        in_ref[...] = in_acc[...].astype(BF16)
        out_ref[...] = out_acc[...].astype(BF16)


def feed_back(x, act, grads, gateup_weight, down_weight):
    rows, width = x.shape[0], down_weight.shape[0]
    tile = 256
    whole = lambda i: (0, 0)
    return pl.pallas_call(
        feed_back_kernel,
        name="feed_back",
        grid=(width // tile,),
        out_shape=(
            jax.ShapeDtypeStruct((2, D, width), BF16),
            jax.ShapeDtypeStruct((rows, D), BF16),
            jax.ShapeDtypeStruct((rows, D), BF16),
        ),
        in_specs=[
            pl.BlockSpec((rows, D), whole),
            pl.BlockSpec((rows, tile), lambda i: (0, i)),
            pl.BlockSpec((2, rows, tile), lambda i: (0, 0, i)),
            pl.BlockSpec((2, D, tile), lambda i: (0, 0, i)),
            pl.BlockSpec((tile, D), lambda i: (i, 0)),
        ],
        out_specs=(
            pl.BlockSpec((2, D, tile), lambda i: (0, 0, i)),
            pl.BlockSpec((rows, D), whole),
            pl.BlockSpec((rows, D), whole),
        ),
        scratch_shapes=[pltpu.VMEM((rows, D), F32), pltpu.VMEM((rows, D), F32)],
        compiler_params=params("arbitrary"),
        cost_estimate=cost(10 * rows * D * width, 8 * rows * D + 10 * D * width),
    )(x, act, grads, gateup_weight, down_weight)


def out_back_kernel(dy_ref, w_ref, low_ref, grad_ref, full_ref):
    dy = dy_ref[...]
    grad_ref[...] = dot_nt(dy, w_ref[...]).astype(BF16)
    full_ref[...] = dot_tn(dy, low_ref[...]).astype(BF16)


def out_back(dy, weight, attn_low):
    rows, width = attn_low.shape
    tile = 256
    whole = lambda i: (0, 0)
    return pl.pallas_call(
        out_back_kernel,
        name="out_back",
        grid=(width // tile,),
        out_shape=(
            jax.ShapeDtypeStruct((rows, width), BF16),
            jax.ShapeDtypeStruct((D, width), BF16),
        ),
        in_specs=[
            pl.BlockSpec((rows, D), whole),
            pl.BlockSpec((tile, D), lambda i: (i, 0)),
            pl.BlockSpec((rows, tile), lambda i: (0, i)),
        ],
        out_specs=(
            pl.BlockSpec((rows, tile), lambda i: (0, i)),
            pl.BlockSpec((D, tile), lambda i: (0, i)),
        ),
        compiler_params=params("arbitrary"),
        cost_estimate=cost(4 * rows * D * width, 2 * rows * D + 4 * D * width),
    )(dy, weight, attn_low)


def project_back_kernel(x_ref, q_ref, kv_ref, wq_ref, wkv_ref, out_ref, in_ref, full_ref):
    q_width, kv_width = wq_ref.shape[1], wkv_ref.shape[2]
    x = x_ref[...]
    key, value = kv_ref[:, :kv_width], kv_ref[:, kv_width:]
    in_ref[...] = (
        dot_nt(q_ref[...], wq_ref[...]) + dot_nt(key, wkv_ref[0]) + dot_nt(value, wkv_ref[1])
    ).astype(BF16)
    full_ref[:, :q_width] = dot_tn(x, q_ref[...]).astype(BF16)
    full_ref[:, q_width : q_width + 2 * kv_width] = dot_tn(x, kv_ref[...]).astype(BF16)
    full_ref[:, q_width + 2 * kv_width :] = out_ref[...]


def project_back(x, q_back, kv_back, query_weight, keyvalue_weight, output_full):
    rows, out_width = x.shape[0], output_full.shape[1]
    q_width, kv_width = query_weight.shape[1], keyvalue_weight.shape[2]
    tile = 512
    whole = lambda i: (0, 0)
    return pl.pallas_call(
        project_back_kernel,
        name="project_back",
        grid=(D // tile,),
        out_shape=(
            jax.ShapeDtypeStruct((rows, D), BF16),
            jax.ShapeDtypeStruct((D, q_width + 2 * kv_width + out_width), BF16),
        ),
        in_specs=[
            pl.BlockSpec((rows, tile), lambda i: (0, i)),
            pl.BlockSpec((rows, q_width), whole),
            pl.BlockSpec((rows, 2 * kv_width), whole),
            pl.BlockSpec((tile, q_width), lambda i: (i, 0)),
            pl.BlockSpec((2, tile, kv_width), lambda i: (0, i, 0)),
            pl.BlockSpec((tile, out_width), lambda i: (i, 0)),
        ],
        out_specs=(
            pl.BlockSpec((rows, tile), lambda i: (0, i)),
            pl.BlockSpec((tile, q_width + 2 * kv_width + out_width), lambda i: (i, 0)),
        ),
        compiler_params=params("arbitrary"),
        cost_estimate=cost(4 * rows * D * (q_width + 2 * kv_width), 6 * D * (q_width + 2 * kv_width)),
    )(x, q_back, kv_back, query_weight, keyvalue_weight, output_full)


def wide_scatter(partial, axis):
    return lax.psum_scatter(partial, "wide", scatter_dimension=axis, tiled=True)


def body(
    tokens,
    cotangent,
    gain_copy,
    query_weight,
    keyvalue_weight,
    output_weight,
    gateup_weight,
    down_weight,
    query_master,
    query_moment,
    query_second,
    query_average,
    keyvalue_master,
    keyvalue_moment,
    keyvalue_second,
    keyvalue_average,
    output_master,
    output_moment,
    output_second,
    output_average,
    gateup_master,
    gateup_moment,
    gateup_second,
    gateup_average,
    down_master,
    down_moment,
    down_second,
    down_average,
    gain_master,
    gain_moment,
    gain_second,
    gain_average,
):
    narrow, wide = lax.axis_size("narrow"), lax.axis_size("wide")
    special = narrow == 4 and wide == 8
    stretch_rows = tokens.shape[0] * narrow
    wide_index = lax.axis_index("wide")
    w_scalar = wide_index.astype(jnp.int32).reshape(1)
    kv_heads = keyvalue_weight.shape[2] // HD
    q_heads = query_weight.shape[1] // HD
    group = q_heads // kv_heads
    q_width, kv_width = q_heads * HD, kv_heads * HD
    attn_gain = gain_copy[:D].reshape(1, D)
    mlp_gain = gain_copy[D : 2 * D].reshape(1, D)
    query_gain = gain_copy[2 * D : 2 * D + HD].reshape(1, HD)
    key_gain = gain_copy[2 * D + HD :].reshape(1, HD)

    positions = (wide_index * stretch_rows + jnp.arange(stretch_rows, dtype=jnp.int32)).astype(F32)
    cosine, sine = rope_tables(positions)
    if special:
        back_mlp, attn_input, query_low, query_raw, key_raw, kv_all, attn_out, attn_low, lse = front(
            tokens,
            cotangent,
            attn_gain,
            query_weight,
            keyvalue_weight,
            query_gain,
            key_gain,
            cosine,
            sine,
            wide,
        )
    else:
        hidden = tokens.astype(F32)
        normed = (hidden * row_scale(hidden) * attn_gain).astype(BF16)
        attn_input = lax.all_gather(normed, "narrow", axis=0, tiled=True)
        kv_low, key_raw = keys_values(attn_input, keyvalue_weight, key_gain, cosine, sine)
        query_low, query_raw = queries(attn_input, query_weight, query_gain, cosine, sine)
        kv_all = lax.all_gather(kv_low, "wide", axis=0)
        attn_out, attn_low, lse = attend(w_scalar, query_low, kv_all, q_heads, group)
        back_mlp = lax.all_gather(cotangent, "narrow", axis=0, tiled=True)
    hidden_mid, mlp_input = mid_forward(attn_low, output_weight, tokens, mlp_gain, special)
    act, act_grads, down_full = feed(mlp_input, back_mlp, gateup_weight, down_weight)
    down_total = wide_scatter(down_full, 1)
    gateup_full, in_partial, out_partial = feed_back(
        mlp_input, act, act_grads, gateup_weight, down_weight
    )
    gateup_total = wide_scatter(gateup_full, 1)
    mid_grad, back_attn, mlp_gain_grad = mid_backward(
        in_partial, hidden_mid, cotangent, mlp_gain, special
    )
    attn_grad, output_full = out_back(back_attn, output_weight, attn_low)
    query_sum, kv_sums = attend_back(
        w_scalar, query_low, kv_all, attn_grad, attn_out, lse, q_heads, group
    )
    down_new = adamw(
        down_total.astype(F32),
        down_master,
        down_moment,
        down_second,
        down_average,
        2.0 * FF ** (-0.5),
        WEIGHT_DECAY,
    )
    kv_sums, down_new = lax.optimization_barrier((kv_sums, down_new))
    query_back, query_gain_grad = unspin(query_sum, query_raw, query_gain, cosine, sine)
    kv_sum = return_grads(kv_sums, wide, special)
    kv_back, key_gain_grad = unspin(kv_sum, key_raw, key_gain, cosine, sine)
    normed_partial, project_full = project_back(
        attn_input, query_back, kv_back, query_weight, keyvalue_weight, output_full
    )
    project_full, out_partial = lax.optimization_barrier((project_full, out_partial))
    block_output = out_scatter(out_partial, hidden_mid, special)
    project_full, gateup_total, block_output, normed_partial = lax.optimization_barrier(
        (project_full, gateup_total, block_output, normed_partial)
    )
    rest_total = wide_scatter(project_full, 0).astype(F32)
    input_grad, attn_gain_grad = in_scatter(normed_partial, tokens, mid_grad, attn_gain, special)
    gain_partial = jnp.concatenate(
        [attn_gain_grad, mlp_gain_grad, query_gain_grad, key_gain_grad], axis=1
    ).reshape(-1)
    gain_total = gain_sums(gain_partial, wide, narrow, special)

    query_total = rest_total[:, :q_width]
    keyvalue_total = jnp.stack(
        [rest_total[:, q_width : q_width + kv_width], rest_total[:, q_width + kv_width : q_width + 2 * kv_width]]
    )
    output_total = rest_total[:, q_width + 2 * kv_width :].T
    query_new = adamw(
        query_total,
        query_master,
        query_moment,
        query_second,
        query_average,
        2.0 * D ** (-0.5),
        WEIGHT_DECAY,
    )
    keyvalue_new = adamw(
        keyvalue_total,
        keyvalue_master,
        keyvalue_moment,
        keyvalue_second,
        keyvalue_average,
        2.0 * D ** (-0.5),
        WEIGHT_DECAY,
    )
    output_new = adamw(
        output_total,
        output_master,
        output_moment,
        output_second,
        output_average,
        2.0 * WO_FAN ** (-0.5),
        WEIGHT_DECAY,
    )
    gateup_new = adamw(
        gateup_total.astype(F32),
        gateup_master,
        gateup_moment,
        gateup_second,
        gateup_average,
        2.0 * D ** (-0.5),
        WEIGHT_DECAY,
    )
    gain_new = adamw(
        gain_total, gain_master, gain_moment, gain_second, gain_average, RATE_GAIN, 0.0
    )
    return (
        block_output,
        input_grad,
        *query_new,
        *keyvalue_new,
        *output_new,
        *gateup_new,
        *down_new,
        *gain_new,
    )


def solution(mesh):
    rows = P(("wide", "narrow"), None)
    flat = P(("wide", "narrow"))
    stacked = P(None, "wide", "narrow")
    query, output = P("wide", "narrow"), P("narrow", "wide")
    states = (
        *[query] * 4,
        *[stacked] * 4,
        *[output] * 4,
        *[stacked] * 4,
        *[output] * 4,
        *[flat] * 4,
    )
    return jax.shard_map(
        body,
        mesh=mesh,
        in_specs=(
            rows,
            rows,
            P(),
            P(None, "narrow"),
            P(None, None, "narrow"),
            P("narrow", None),
            P(None, None, "narrow"),
            P("narrow", None),
            *states,
        ),
        out_specs=(
            rows,
            rows,
            *[query] * 5,
            *[stacked] * 5,
            *[output] * 5,
            *[stacked] * 5,
            *[output] * 5,
            *[flat] * 5,
        ),
        check_vma=False,
    )
```

```python
import functools

import jax
import jax.numpy as jnp
from jax import lax
from jax.experimental import pallas as pl
from jax.experimental.pallas import tpu as pltpu
from jax.sharding import PartitionSpec as P

D = 2048
HD = 128
FF = 6144
STEP = 10
WO_FAN = 32

EPSILON = 1e-06
THETA = 1000000.0
BETA_ONE = 0.9
BETA_TWO = 0.999
ADAM_EPS = 1e-08
WEIGHT_DECAY = 0.1
EMA_KEEP = 0.5
RATE_GAIN = 0.4
FACTOR = HD ** (-0.5)
LOG2E = 1.4426950408889634

F32 = jnp.float32
BF16 = jnp.bfloat16
MESH = pl.DeviceIdType.MESH
VM = pl.BlockSpec(memory_space=pltpu.VMEM)
SM = pl.BlockSpec(memory_space=pltpu.SMEM)
VMEM_LIMIT = 60 << 20

NT = (((1,), (1,)), ((), ()))
TN = (((0,), (0,)), ((), ()))


def dot(left, right):
    return jnp.dot(left, right, preferred_element_type=F32)


def dot_nt(left, right):
    return lax.dot_general(left, right, NT, preferred_element_type=F32)


def dot_tn(left, right):
    return lax.dot_general(left, right, TN, preferred_element_type=F32)


def rope_tables(positions):
    half_width = HD // 2
    inverse_freq = THETA ** (-(2.0 * jnp.arange(half_width, dtype=F32)) / HD)
    angles = positions[:, None] * inverse_freq[None, :]
    cosine, sine = jnp.cos(angles), jnp.sin(angles)
    return (
        jnp.concatenate([cosine, cosine], axis=-1),
        jnp.concatenate([-sine, sine], axis=-1),
    )


def adamw(gradient, master, moment, second, average, step_rate, decay_rate):
    moment_new = BETA_ONE * moment + (1.0 - BETA_ONE) * gradient
    second_new = BETA_TWO * second + (1.0 - BETA_TWO) * gradient * gradient
    moment_hat = moment_new / (1.0 - BETA_ONE**STEP)
    second_hat = second_new / (1.0 - BETA_TWO**STEP)
    master_new = master - step_rate * (
        moment_hat / (jnp.sqrt(second_hat) + ADAM_EPS) + decay_rate * master
    )
    average_new = EMA_KEEP * average + (1.0 - EMA_KEEP) * master_new
    return (gradient, master_new, moment_new, second_new, average_new)


def row_scale(values_in):
    return lax.rsqrt(jnp.mean(values_in * values_in, axis=-1, keepdims=True) + EPSILON)


def norm_back(gradient, unit_rows, inv_scale, gain_row):
    scaled = gradient * gain_row
    inner = scaled - unit_rows * jnp.mean(scaled * unit_rows, axis=-1, keepdims=True)
    return inv_scale * inner, jnp.sum(gradient * unit_rows, axis=0, keepdims=True)


def square():
    me = lax.axis_index("narrow")
    xn = me + 1 - 2 * (me % 2)
    yn = (me + 2) % 4
    dg = (xn + 2) % 4
    return me, xn, yn, dg


def greet(axis, peers):
    barrier = pltpu.get_barrier_semaphore()
    for peer in peers:
        pl.semaphore_signal(barrier, inc=1, device_id={axis: peer}, device_id_type=MESH)
    pl.semaphore_wait(barrier, len(peers))


class Copies:
    def __init__(self, send, recv):
        self.send, self.recv, self.sent = send, recv, []

    def go(self, src, dst, slot, peer):
        copy = pltpu.make_async_remote_copy(
            src_ref=src,
            dst_ref=dst,
            send_sem=self.send.at[slot],
            recv_sem=self.recv.at[slot],
            device_id={"narrow": peer},
            device_id_type=MESH,
        )
        copy.start()
        self.sent.append(copy)
        return copy

    def finish(self):
        for copy in self.sent:
            copy.wait_send()


def gather_square(copies, slot, x_ref, o_ref):
    me, xn, yn, dg = square()
    rows = x_ref.shape[0]
    half = rows // 2

    def part(owner, low):
        return o_ref.at[pl.ds(pl.multiple_of(owner * rows + low, half), half)]

    upper, lower = x_ref.at[pl.ds(0, half)], x_ref.at[pl.ds(half, half)]
    xa = copies.go(upper, part(me, 0), slot, xn)
    yb = copies.go(lower, part(me, half), slot + 1, yn)
    xb = copies.go(lower, part(me, half), slot + 2, xn)
    ya = copies.go(upper, part(me, 0), slot + 3, yn)
    o_ref[pl.ds(pl.multiple_of(me * rows, rows), rows)] = x_ref[...]
    xa.wait_recv()
    yf = copies.go(part(xn, 0), part(xn, 0), slot + 4, yn)
    yb.wait_recv()
    xf = copies.go(part(yn, half), part(yn, half), slot + 5, xn)
    for copy in (xb, ya, yf, xf):
        copy.wait_recv()


def scatter_square(copies, slot, p_ref, buf, stage, emit, fill=None):
    me, xn, yn, dg = square()
    rows = p_ref.shape[0] // 4
    half = rows // 2

    def part(owner, low):
        return p_ref.at[pl.ds(pl.multiple_of(owner * rows + low, half), half)]

    if fill is None:
        fill = lambda owner: None
    fill(dg)
    c0 = copies.go(part(dg, 0), buf.at[0], slot, xn)
    c1 = copies.go(part(dg, half), buf.at[1], slot + 1, yn)
    fill(xn)
    c2 = copies.go(part(xn, 0), buf.at[2], slot + 2, xn)
    fill(yn)
    c3 = copies.go(part(yn, half), buf.at[3], slot + 3, yn)
    fill(me)
    c0.wait_recv()
    stage[0] = (part(yn, 0)[...].astype(F32) + buf[0].astype(F32)).astype(BF16)
    c4 = copies.go(stage.at[0], buf.at[4], slot + 4, yn)
    c1.wait_recv()
    stage[1] = (part(xn, half)[...].astype(F32) + buf[1].astype(F32)).astype(BF16)
    c5 = copies.go(stage.at[1], buf.at[5], slot + 5, xn)
    c2.wait_recv()
    c4.wait_recv()
    emit(0, part(me, 0)[...].astype(F32) + buf[2].astype(F32) + buf[4].astype(F32))
    c3.wait_recv()
    c5.wait_recv()
    emit(half, part(me, half)[...].astype(F32) + buf[3].astype(F32) + buf[5].astype(F32))


def dma_sems(count):
    return [pltpu.SemaphoreType.DMA((count,)), pltpu.SemaphoreType.DMA((count,))]


def scatter_space(rows):
    return [pltpu.VMEM((6, rows // 2, D), BF16), pltpu.VMEM((2, rows // 2, D), BF16)]


def remote_params(collective_id):
    return pltpu.CompilerParams(
        collective_id=collective_id, has_side_effects=True, vmem_limit_bytes=VMEM_LIMIT
    )


def mid_forward_kernel(a_ref, w_ref, t_ref, g_ref, h_ref, o_ref, p_ref, buf, stage, own, send, recv):
    _, xn, yn, _ = square()
    rows = t_ref.shape[0]
    half = rows // 2
    greet("narrow", (xn, yn))
    copies = Copies(send, recv)

    def fill(owner):
        at = pl.ds(pl.multiple_of(owner * rows, rows), rows)
        p_ref[at, :] = dot(a_ref[at, :], w_ref[...]).astype(BF16)

    def emit(low, total):
        hidden = t_ref[pl.ds(low, half)].astype(F32) + total
        h_ref[pl.ds(low, half)] = hidden
        own[pl.ds(low, half)] = (hidden * row_scale(hidden) * g_ref[...]).astype(BF16)

    scatter_square(copies, 0, p_ref, buf, stage, emit, fill)
    gather_square(copies, 6, own, o_ref)
    copies.finish()


def mid_forward(attn_low, weight, tokens, gain_row, special):
    rows = tokens.shape[0]
    if not special:
        partial = dot(attn_low, weight).astype(BF16)
        hidden = tokens.astype(F32) + lax.psum_scatter(
            partial, "narrow", scatter_dimension=0, tiled=True
        ).astype(F32)
        normed = (hidden * row_scale(hidden) * gain_row).astype(BF16)
        return hidden, lax.all_gather(normed, "narrow", axis=0, tiled=True)
    return pl.pallas_call(
        mid_forward_kernel,
        name="mid_forward",
        out_shape=(
            jax.ShapeDtypeStruct((rows, D), F32),
            jax.ShapeDtypeStruct((4 * rows, D), BF16),
        ),
        in_specs=[VM] * 4,
        out_specs=(VM, VM),
        scratch_shapes=[pltpu.VMEM((4 * rows, D), BF16)]
        + scatter_space(rows) + [pltpu.VMEM((rows, D), BF16)] + dma_sems(12),
        cost_estimate=cost(1, 1),
        compiler_params=remote_params(2),
    )(attn_low, weight, tokens, gain_row)


def mid_backward_kernel(
    p_ref, h_ref, c_ref, g_ref, m_ref, o_ref, gg_ref, buf, stage, own, send, recv
):
    _, xn, yn, _ = square()
    half = h_ref.shape[0] // 2
    greet("narrow", (xn, yn))
    copies = Copies(send, recv)
    gg_ref[...] = jnp.zeros_like(gg_ref)

    def emit(low, total):
        hidden = h_ref[pl.ds(low, half)]
        scale = row_scale(hidden)
        back, gain_sum = norm_back(total, hidden * scale, scale, g_ref[...])
        gg_ref[...] += gain_sum
        mid = c_ref[pl.ds(low, half)].astype(F32) + back
        m_ref[pl.ds(low, half)] = mid
        own[pl.ds(low, half)] = mid.astype(BF16)

    scatter_square(copies, 0, p_ref, buf, stage, emit)
    gather_square(copies, 6, own, o_ref)
    copies.finish()


def mid_backward(partial, hidden_mid, cotangent, gain_row, special):
    rows = hidden_mid.shape[0]
    if not special:
        total = lax.psum_scatter(partial, "narrow", scatter_dimension=0, tiled=True).astype(F32)
        scale = row_scale(hidden_mid)
        back, gain_sum = norm_back(total, hidden_mid * scale, scale, gain_row)
        mid = cotangent.astype(F32) + back
        return mid, lax.all_gather(mid.astype(BF16), "narrow", axis=0, tiled=True), gain_sum
    return pl.pallas_call(
        mid_backward_kernel,
        name="mid_backward",
        out_shape=(
            jax.ShapeDtypeStruct((rows, D), F32),
            jax.ShapeDtypeStruct((4 * rows, D), BF16),
            jax.ShapeDtypeStruct((1, D), F32),
        ),
        in_specs=[VM] * 4,
        out_specs=(VM,) * 3,
        scratch_shapes=scatter_space(rows) + [pltpu.VMEM((rows, D), BF16)] + dma_sems(12),
        cost_estimate=cost(1, 1),
        compiler_params=remote_params(3),
    )(partial, hidden_mid, cotangent, gain_row)


def out_scatter_kernel(p_ref, h_ref, o_ref, buf, stage, send, recv):
    _, xn, yn, _ = square()
    half = h_ref.shape[0] // 2
    greet("narrow", (xn, yn))
    copies = Copies(send, recv)

    def emit(low, total):
        o_ref[pl.ds(low, half)] = h_ref[pl.ds(low, half)] + total

    scatter_square(copies, 0, p_ref, buf, stage, emit)
    copies.finish()


def out_scatter(partial, hidden_mid, special):
    rows = hidden_mid.shape[0]
    if not special:
        total = lax.psum_scatter(partial, "narrow", scatter_dimension=0, tiled=True)
        return hidden_mid + total.astype(F32)
    return pl.pallas_call(
        out_scatter_kernel,
        name="out_scatter",
        out_shape=jax.ShapeDtypeStruct((rows, D), F32),
        in_specs=[VM] * 2,
        out_specs=VM,
        scratch_shapes=scatter_space(rows) + dma_sems(6),
        cost_estimate=cost(1, 1),
        compiler_params=remote_params(9),
    )(partial, hidden_mid)


def in_scatter_kernel(p_ref, t_ref, m_ref, g_ref, o_ref, gg_ref, buf, stage, send, recv):
    _, xn, yn, _ = square()
    half = t_ref.shape[0] // 2
    greet("narrow", (xn, yn))
    copies = Copies(send, recv)
    gg_ref[...] = jnp.zeros_like(gg_ref)

    def emit(low, total):
        hidden = t_ref[pl.ds(low, half)].astype(F32)
        scale = row_scale(hidden)
        back, gain_sum = norm_back(total, hidden * scale, scale, g_ref[...])
        gg_ref[...] += gain_sum
        o_ref[pl.ds(low, half)] = m_ref[pl.ds(low, half)] + back

    scatter_square(copies, 0, p_ref, buf, stage, emit)
    copies.finish()


def in_scatter(partial, tokens, mid_grad, gain_row, special):
    rows = tokens.shape[0]
    if not special:
        total = lax.psum_scatter(partial, "narrow", scatter_dimension=0, tiled=True).astype(F32)
        hidden = tokens.astype(F32)
        scale = row_scale(hidden)
        back, gain_sum = norm_back(total, hidden * scale, scale, gain_row)
        return mid_grad + back, gain_sum
    return pl.pallas_call(
        in_scatter_kernel,
        name="in_scatter",
        out_shape=(
            jax.ShapeDtypeStruct((rows, D), F32),
            jax.ShapeDtypeStruct((1, D), F32),
        ),
        in_specs=[VM] * 4,
        out_specs=(VM,) * 2,
        scratch_shapes=scatter_space(rows) + dma_sems(6),
        cost_estimate=cost(1, 1),
        compiler_params=remote_params(4),
    )(partial, tokens, mid_grad, gain_row)


def line(count):
    w = lax.axis_index("wide")
    z, c = w // 2, w % 2
    return w, z, c, count // 2, w + 1 - 2 * c, jnp.minimum(w + 2, count - 1), jnp.maximum(w - 2, 0)


def greet_line(count):
    w, z, c, chips, mate, above, below = line(count)
    barrier = pltpu.get_barrier_semaphore()
    has_above, has_below = z < chips - 1, z > 0

    @pl.when(has_above)
    def _():
        pl.semaphore_signal(barrier, inc=1, device_id={"wide": above}, device_id_type=MESH)

    @pl.when(has_below)
    def _():
        pl.semaphore_signal(barrier, inc=1, device_id={"wide": below}, device_id_type=MESH)

    pl.semaphore_signal(barrier, inc=1, device_id={"wide": mate}, device_id_type=MESH)
    pl.semaphore_wait(barrier, 1 + has_above.astype(jnp.int32) + has_below.astype(jnp.int32))


def wide_copy(src, dst, send, recv, slot, peer):
    return pltpu.make_async_remote_copy(
        src_ref=src,
        dst_ref=dst,
        send_sem=send.at[slot],
        recv_sem=recv.at[slot],
        device_id={"wide": peer},
        device_id_type=MESH,
    )


def return_grads_kernel(
    count, x_ref, o_ref, from_mate, from_above, stage, send, recv, mate_send, mate_recv
):
    w, z, c, chips, mate, above, below = line(count)
    greet_line(count)

    def to_mate(s):
        return wide_copy(
            x_ref.at[jnp.minimum(2 * s + 1 - c, count - 1)],
            from_mate.at[s],
            mate_send,
            mate_recv,
            s,
            mate,
        )

    def sends_mate(s):
        return (z > s) | ((z == s) & (c == 1))

    def gets_mate(s):
        return (z > s) | ((z == s) & (c == 0))

    def down(s):
        return wide_copy(stage.at[s], from_above.at[s], send, recv, s, below)

    for s in range(chips):

        @pl.when(sends_mate(s))
        def _():
            to_mate(s).start()

    for s in range(chips):
        block = jnp.minimum(2 * s + c, count - 1)

        @pl.when(z > s)
        def _():
            to_mate(s).wait_recv()

            @pl.when(z == chips - 1)
            def _():
                stage[s] = (x_ref[block].astype(F32) + from_mate[s].astype(F32)).astype(BF16)

            @pl.when(z < chips - 1)
            def _():
                down(s).wait_recv()
                stage[s] = (
                    x_ref[block].astype(F32) + from_mate[s].astype(F32) + from_above[s].astype(F32)
                ).astype(BF16)

            down(s).start()

        @pl.when(z == s)
        def _():
            o_ref[...] = x_ref[block].astype(F32)

            @pl.when(c == 0)
            def _():
                to_mate(s).wait_recv()
                o_ref[...] += from_mate[s].astype(F32)

            if s < chips - 1:
                down(s).wait_recv()
                o_ref[...] += from_above[s].astype(F32)

    for s in range(chips):

        @pl.when(sends_mate(s))
        def _():
            to_mate(s).wait_send()

        @pl.when(z > s)
        def _():
            down(s).wait_send()


def return_grads(grads, count, special):
    _, rows, width = grads.shape
    if not special:
        w = lax.axis_index("wide")
        seen = (jnp.arange(count) <= w)[:, None, None]
        total = lax.psum_scatter(
            jnp.where(seen, grads, 0).reshape(count * rows, width),
            "wide",
            scatter_dimension=0,
            tiled=True,
        )
        return total.astype(F32)
    chips = count // 2
    return pl.pallas_call(
        functools.partial(return_grads_kernel, count),
        name="return_grads",
        out_shape=jax.ShapeDtypeStruct((rows, width), F32),
        in_specs=[VM],
        out_specs=VM,
        scratch_shapes=[
            pltpu.VMEM((chips, rows, width), BF16),
            pltpu.VMEM((chips, rows, width), BF16),
            pltpu.VMEM((chips, rows, width), BF16),
        ]
        + dma_sems(chips)
        + dma_sems(chips),
        cost_estimate=cost(1, 1),
        compiler_params=remote_params(6),
    )(grads)


def gain_kernel(wide, x_ref, o_ref, near, mid, far, send, recv, wide_send, wide_recv):
    me, xn, yn, dg = square()
    w = lax.axis_index("wide")
    barrier = pltpu.get_barrier_semaphore()
    for peer in (xn, yn, dg):
        pl.semaphore_signal(barrier, inc=1, device_id={"narrow": peer}, device_id_type=MESH)
    for step in range(1, wide):
        pl.semaphore_signal(
            barrier, inc=1, device_id={"wide": (w + step) % wide}, device_id_type=MESH
        )
    pl.semaphore_wait(barrier, 3 + wide - 1)
    copies = Copies(send, recv)
    sent = [
        copies.go(x_ref.at[peer], near.at[slot], slot, peer)
        for slot, peer in enumerate((xn, yn, dg))
    ]
    for copy in sent:
        copy.wait_recv()
    mid[...] = x_ref[me] + near[0] + near[1] + near[2]
    away = []
    for step in range(1, wide):
        peer = (w + step) % wide
        copy = wide_copy(
            mid.at[peer], far.at[step - 1], wide_send, wide_recv, step - 1, peer
        )
        copy.start()
        away.append(copy)
    total = mid[w]
    for step in range(1, wide):
        away[step - 1].wait_recv()
        total = total + far[step - 1]
    o_ref[...] = total
    copies.finish()
    for copy in away:
        copy.wait_send()


def gain_sums(partial, wide, narrow, special):
    if not special:
        return lax.psum_scatter(partial, ("wide", "narrow"), scatter_dimension=0, tiled=True)
    count = partial.shape[0] // (wide * narrow)
    padded = -(-count // 128) * 128
    shaped = partial.reshape(wide, narrow, count).transpose(1, 0, 2)
    shaped = jnp.pad(shaped, ((0, 0), (0, 0), (0, padded - count)))
    shaped = shaped.reshape(narrow, wide, padded // 128, 128)
    out = pl.pallas_call(
        functools.partial(gain_kernel, wide),
        name="gain_sums",
        out_shape=jax.ShapeDtypeStruct((padded // 128, 128), F32),
        in_specs=[VM],
        out_specs=VM,
        scratch_shapes=[
            pltpu.VMEM((3, wide, padded // 128, 128), F32),
            pltpu.VMEM((wide, padded // 128, 128), F32),
            pltpu.VMEM((wide - 1, padded // 128, 128), F32),
        ]
        + dma_sems(3)
        + dma_sems(wide - 1),
        cost_estimate=cost(1, 1),
        compiler_params=remote_params(7),
    )(shaped)
    return out.reshape(padded)[:count]


def cost(flops, moved, exps=0):
    return pl.CostEstimate(flops=1, bytes_accessed=1, transcendentals=0)


def params(*semantics):
    if not semantics:
        return pltpu.CompilerParams(vmem_limit_bytes=VMEM_LIMIT)
    return pltpu.CompilerParams(vmem_limit_bytes=VMEM_LIMIT, dimension_semantics=semantics)


def spin(raw, gain_row, cosine, sine):
    normed = raw * row_scale(raw) * gain_row
    return normed * cosine + pltpu.roll(normed, HD // 2, axis=1) * sine


def keys_kernel(x_ref, w_ref, g_ref, cos_ref, sin_ref, kv_ref, raw_ref):
    which = pl.program_id(0)
    width = w_ref.shape[2]
    out = dot(x_ref[...], w_ref[0])

    @pl.when(which == 0)
    def _():
        raw_ref[...] = out
        for h in range(width // HD):
            part = out[:, h * HD : (h + 1) * HD]
            kv_ref[:, h * HD : (h + 1) * HD] = spin(
                part, g_ref[...], cos_ref[...], sin_ref[...]
            ).astype(BF16)

    @pl.when(which == 1)
    def _():
        kv_ref[...] = out.astype(BF16)


def keys_values(x, weight, gain_row, cosine, sine):
    rows, width = x.shape[0], weight.shape[2]
    whole = lambda i: (0, 0)
    return pl.pallas_call(
        keys_kernel,
        name="keys_values",
        grid=(2,),
        out_shape=(
            jax.ShapeDtypeStruct((rows, 2 * width), BF16),
            jax.ShapeDtypeStruct((rows, width), F32),
        ),
        in_specs=[
            pl.BlockSpec((rows, D), whole),
            pl.BlockSpec((1, D, width), lambda i: (i, 0, 0)),
            pl.BlockSpec((1, HD), whole),
            pl.BlockSpec((rows, HD), whole),
            pl.BlockSpec((rows, HD), whole),
        ],
        out_specs=(
            pl.BlockSpec((rows, width), lambda i: (0, i)),
            pl.BlockSpec((rows, width), whole),
        ),
        compiler_params=params("arbitrary"),
        cost_estimate=cost(4 * rows * D * width, 2 * rows * D + 4 * D * width),
    )(x, weight, gain_row, cosine, sine)


def queries_kernel(x_ref, w_ref, g_ref, cos_ref, sin_ref, q_ref, raw_ref):
    out = dot(x_ref[...], w_ref[...])
    raw_ref[...] = out
    for h in range(w_ref.shape[1] // HD):
        part = out[:, h * HD : (h + 1) * HD]
        q_ref[:, h * HD : (h + 1) * HD] = spin(
            part, g_ref[...], cos_ref[...], sin_ref[...]
        ).astype(BF16)


def queries(x, weight, gain_row, cosine, sine):
    rows, width = x.shape[0], weight.shape[1]
    tile = 256
    whole = lambda i: (0, 0)
    return pl.pallas_call(
        queries_kernel,
        name="queries",
        grid=(width // tile,),
        out_shape=(
            jax.ShapeDtypeStruct((rows, width), BF16),
            jax.ShapeDtypeStruct((rows, width), F32),
        ),
        in_specs=[
            pl.BlockSpec((rows, D), whole),
            pl.BlockSpec((D, tile), lambda i: (0, i)),
            pl.BlockSpec((1, HD), whole),
            pl.BlockSpec((rows, HD), whole),
            pl.BlockSpec((rows, HD), whole),
        ],
        out_specs=(
            pl.BlockSpec((rows, tile), lambda i: (0, i)),
            pl.BlockSpec((rows, tile), lambda i: (0, i)),
        ),
        compiler_params=params("arbitrary"),
        cost_estimate=cost(2 * rows * D * width, 2 * rows * D + 2 * D * width),
    )(x, weight, gain_row, cosine, sine)


def attend_kernel(heads, group, w_ref, q_ref, kv_ref, o_ref, low_ref, lse_ref, acc):
    rows = q_ref.shape[0]
    kv_width = kv_ref.shape[2] // 2
    w = w_ref[0]
    acc[...] = jnp.zeros_like(acc)
    ones = jnp.ones((rows, HD), BF16)

    def block(j, masked):
        for h in range(heads):
            kv = h // group
            key = kv_ref[j, :, kv * HD : (kv + 1) * HD]
            value = kv_ref[j, :, kv_width + kv * HD : kv_width + (kv + 1) * HD]
            query = q_ref[:, h * HD : (h + 1) * HD]
            terms = jnp.exp2(dot_nt(query, key) * (FACTOR * LOG2E))
            if masked:
                at = lax.broadcasted_iota(jnp.int32, (rows, rows), 0)
                key_at = lax.broadcasted_iota(jnp.int32, (rows, rows), 1)
                terms = jnp.where(key_at <= at, terms, 0.0)
            acc[h] += dot(terms.astype(BF16), jnp.concatenate([value, ones], axis=1))

    @pl.loop(0, w)
    def _(j):
        block(j, False)

    block(w, True)
    for h in range(heads):
        total = acc[h, :, HD:]
        out = acc[h, :, :HD] / total
        o_ref[:, h * HD : (h + 1) * HD] = out
        low_ref[:, h * HD : (h + 1) * HD] = out.astype(BF16)
        lse_ref[h : h + 1, :] = jnp.transpose(jnp.log2(total))[0:1]


def attend(w_index, query, kv_all, heads, group):
    rows, width = query.shape
    count = kv_all.shape[0]
    return pl.pallas_call(
        functools.partial(attend_kernel, heads, group),
        name="attend",
        out_shape=(
            jax.ShapeDtypeStruct((rows, width), F32),
            jax.ShapeDtypeStruct((rows, width), BF16),
            jax.ShapeDtypeStruct((heads, rows), F32),
        ),
        in_specs=[SM, VM, VM],
        out_specs=(VM, VM, VM),
        scratch_shapes=[pltpu.VMEM((heads, rows, 2 * HD), F32)],
        compiler_params=params(),
        cost_estimate=cost(4 * rows * rows * count * width, 2 * kv_all.size, rows * rows * heads * count),
    )(w_index, query, kv_all)


def attend_back_kernel(
    heads, group, w_ref, q_ref, kv_ref, do_ref, o_ref, lse_ref, dq_ref, dkv_ref, delta
):
    rows = q_ref.shape[0]
    kv_width = kv_ref.shape[2] // 2
    w = w_ref[0]
    for h in range(heads):
        part = slice(h * HD, (h + 1) * HD)
        delta[h : h + 1, :] = jnp.sum(
            jnp.transpose(do_ref[:, part].astype(F32) * o_ref[:, part]), axis=0, keepdims=True
        )
    dq_ref[...] = jnp.zeros_like(dq_ref)

    def block(j, masked):
        for kv in range(heads // group):
            key = kv_ref[j, :, kv * HD : (kv + 1) * HD]
            value = kv_ref[j, :, kv_width + kv * HD : kv_width + (kv + 1) * HD]
            key_sum = jnp.zeros((rows, HD), F32)
            value_sum = jnp.zeros((rows, HD), F32)
            for h in range(kv * group, (kv + 1) * group):
                part = slice(h * HD, (h + 1) * HD)
                query, out_grad = q_ref[:, part], do_ref[:, part]
                probs = jnp.exp2(
                    dot_nt(key, query) * (FACTOR * LOG2E) - lse_ref[h : h + 1, :]
                )
                if masked:
                    key_at = lax.broadcasted_iota(jnp.int32, (rows, rows), 0)
                    at = lax.broadcasted_iota(jnp.int32, (rows, rows), 1)
                    probs = jnp.where(key_at <= at, probs, 0.0)
                value_sum += dot(probs.astype(BF16), out_grad)
                prob_grad = dot_nt(value, out_grad)
                score_grad = (probs * (prob_grad - delta[h : h + 1, :])).astype(BF16)
                key_sum += dot(score_grad, query)
                dq_ref[:, part] += dot_tn(score_grad, key)
            dkv_ref[j, :, kv * HD : (kv + 1) * HD] = (key_sum * FACTOR).astype(BF16)
            dkv_ref[j, :, kv_width + kv * HD : kv_width + (kv + 1) * HD] = value_sum.astype(BF16)

    @pl.loop(0, w)
    def _(j):
        block(j, False)

    block(w, True)
    dq_ref[...] = dq_ref[...] * FACTOR


def attend_back(w_index, query, kv_all, out_grad, out, lse, heads, group):
    rows, width = query.shape
    count = kv_all.shape[0]
    return pl.pallas_call(
        functools.partial(attend_back_kernel, heads, group),
        name="attend_back",
        out_shape=(
            jax.ShapeDtypeStruct((rows, width), F32),
            jax.ShapeDtypeStruct(kv_all.shape, BF16),
        ),
        in_specs=[SM] + [VM] * 5,
        out_specs=(VM, VM),
        scratch_shapes=[pltpu.VMEM((heads, rows), F32)],
        compiler_params=params(),
        cost_estimate=cost(10 * rows * rows * count * width, 4 * kv_all.size, rows * rows * heads * count),
    )(w_index, query, kv_all, out_grad, out, lse)


def unspin_kernel(width, e_ref, raw_ref, g_ref, cos_ref, sin_ref, o_ref, gg_ref):
    gain_sum = jnp.zeros((1, HD), F32)
    for h in range(raw_ref.shape[1] // HD):
        part = slice(h * HD, (h + 1) * HD)
        grad = e_ref[:, part]
        turned = grad * cos_ref[...] - pltpu.roll(grad, HD // 2, axis=1) * sin_ref[...]
        raw = raw_ref[:, part]
        scale = row_scale(raw)
        back, total = norm_back(turned, raw * scale, scale, g_ref[...])
        o_ref[:, part] = back.astype(BF16)
        gain_sum += total
    if width > raw_ref.shape[1]:
        o_ref[:, raw_ref.shape[1] :] = e_ref[:, raw_ref.shape[1] :].astype(BF16)
    gg_ref[...] = gain_sum


def unspin(grad, raw, gain_row, cosine, sine):
    rows, width = grad.shape
    return pl.pallas_call(
        functools.partial(unspin_kernel, width),
        name="unspin",
        out_shape=(
            jax.ShapeDtypeStruct((rows, width), BF16),
            jax.ShapeDtypeStruct((1, HD), F32),
        ),
        in_specs=[VM] * 5,
        out_specs=(VM, VM),
        compiler_params=params(),
        cost_estimate=cost(20 * grad.size, 10 * grad.size),
    )(grad, raw, gain_row, cosine, sine)


def front_kernel(
    count, heads, group,
    t_ref, c_ref, g_ref, wq_hbm, wkv_hbm, qg_ref, kg_ref, cos_ref, sin_ref,
    dy_hbm, x_hbm, q_hbm, qraw_hbm, kraw_hbm, kv_hbm, o_ref, low_ref, lse_ref,
    own, x, weight, q, qraw, kraw, kv, acc,
    send, recv, z_send, z_recv, m_send, m_recv, c_send, c_recv, load_sem, store_sem, kv_sem,
):
    me, xn, yn, dg = square()
    w, z, c, chips, mate, above, below = line(count)
    rows = t_ref.shape[0]
    half = rows // 2
    all_rows = 4 * rows
    q_width, kv_width = wq_hbm.shape[1], wkv_hbm.shape[2]
    owners = (me, xn, yn, dg)
    loads = [
        pltpu.make_async_copy(wq_hbm, weight.at[:, pl.ds(0, q_width)], load_sem.at[0]),
        pltpu.make_async_copy(wkv_hbm.at[0], weight.at[:, pl.ds(q_width, kv_width)], load_sem.at[1]),
        pltpu.make_async_copy(
            wkv_hbm.at[1], weight.at[:, pl.ds(q_width + kv_width, kv_width)], load_sem.at[2]
        ),
    ]
    for load in loads:
        load.start()

    has_above, has_below = z < chips - 1, z > 0
    barrier = pltpu.get_barrier_semaphore()
    for peer in (xn, yn, dg):
        pl.semaphore_signal(barrier, inc=1, device_id={"narrow": peer}, device_id_type=MESH)

    @pl.when(has_above)
    def _():
        pl.semaphore_signal(barrier, inc=1, device_id={"wide": above}, device_id_type=MESH)

    @pl.when(has_below)
    def _():
        pl.semaphore_signal(barrier, inc=1, device_id={"wide": below}, device_id_type=MESH)

    pl.semaphore_signal(barrier, inc=1, device_id={"wide": mate}, device_id_type=MESH)
    hidden = t_ref[...].astype(F32)
    own[...] = (hidden * row_scale(hidden) * g_ref[...]).astype(BF16)
    pl.semaphore_wait(barrier, 4 + has_above.astype(jnp.int32) + has_below.astype(jnp.int32))

    copies = Copies(send, recv)

    def part(owner, low):
        return x.at[pl.ds(pl.multiple_of(owner * rows + low, half), half)]

    upper, lower = own.at[pl.ds(0, half)], own.at[pl.ds(half, half)]
    xa = copies.go(upper, part(me, 0), 0, xn)
    yb = copies.go(lower, part(me, half), 1, yn)
    xb = copies.go(lower, part(me, half), 2, xn)
    ya = copies.go(upper, part(me, 0), 3, yn)

    def unit_rows(unit):
        return pl.ds(pl.multiple_of(owners[unit] * rows, rows), rows)

    def unit(block, k):
        return kv.at[block, unit_rows(k)]

    def to_above(s, k):
        block = jnp.maximum(w - 2 * s, 0)
        return wide_copy(unit(block, k), unit(block, k), z_send, z_recv, 4 * s + k, above)

    def from_below(s, k):
        block = jnp.maximum(w - 2 * s, 0)
        return wide_copy(unit(block, k), unit(block, k), z_send, z_recv, 4 * (s - 1) + k, above)

    def to_mate(s, k):
        block = jnp.maximum(w - 2 * s, 0)
        return wide_copy(unit(block, k), unit(block, k), m_send, m_recv, 4 * s + k, mate)

    def project(k):
        at = unit_rows(k)
        out = dot(x[at, :], weight[...])
        cosine, sine = cos_ref[at, :], sin_ref[at, :]
        qraw[at, :] = out[:, :q_width]
        kraw[at, :] = out[:, q_width : q_width + kv_width]
        for h in range(heads):
            lanes = slice(h * HD, (h + 1) * HD)
            q[at, lanes] = spin(out[:, lanes], qg_ref[...], cosine, sine).astype(BF16)
        for h in range(heads // group):
            lanes = slice(q_width + h * HD, q_width + (h + 1) * HD)
            kv[w, at, h * HD : (h + 1) * HD] = spin(
                out[:, lanes], kg_ref[...], cosine, sine
            ).astype(BF16)
        kv[w, at, kv_width:] = out[:, q_width + kv_width :].astype(BF16)

        @pl.when(has_above)
        def _():
            to_above(0, k).start()

        @pl.when(c == 0)
        def _():
            to_mate(0, k).start()

    def receive(s, k):
        @pl.when(z >= s)
        def _():
            from_below(s, k).wait_recv()
            if s < chips - 1:

                @pl.when(has_above)
                def _():
                    to_above(s, k).start()

            to_mate(s, k).start()

    x[unit_rows(0), :] = own[...]
    for load in loads:
        load.wait()
    project(0)
    xa.wait_recv()
    yf = copies.go(part(xn, 0), part(xn, 0), 4, yn)
    yb.wait_recv()
    xf = copies.go(part(yn, half), part(yn, half), 5, xn)
    receive(1, 0)
    xb.wait_recv()
    project(1)
    ya.wait_recv()
    project(2)
    receive(2, 0)
    receive(1, 1)
    receive(1, 2)
    receive(3, 0)
    yf.wait_recv()
    xf.wait_recv()
    project(3)
    away = Copies(c_send, c_recv)
    dy_part = dy_hbm.at[unit_rows(0)]
    for slot, peer in enumerate((dg, xn, yn)):
        away.go(c_ref, dy_part, slot, peer)
    stores = [
        pltpu.make_async_copy(src, dst, store_sem.at[n])
        for n, (src, dst) in enumerate(
            ((x, x_hbm), (q, q_hbm), (qraw, qraw_hbm), (kraw, kraw_hbm), (c_ref, dy_part))
        )
    ]
    for store in stores:
        store.start()
    acc[...] = jnp.zeros_like(acc)
    ones = jnp.ones((all_rows, HD), BF16)

    def keep(j):
        return pltpu.make_async_copy(kv.at[j], kv_hbm.at[j], kv_sem.at[j])

    def block(j, masked):
        for h in range(heads):
            head = h // group
            key = kv[j, :, head * HD : (head + 1) * HD]
            value = kv[j, :, kv_width + head * HD : kv_width + (head + 1) * HD]
            terms = jnp.exp2(dot_nt(q[:, h * HD : (h + 1) * HD], key) * (FACTOR * LOG2E))
            if masked:
                at = lax.broadcasted_iota(jnp.int32, (all_rows, all_rows), 0)
                key_at = lax.broadcasted_iota(jnp.int32, (all_rows, all_rows), 1)
                terms = jnp.where(key_at <= at, terms, 0.0)
            acc[h] += dot(terms.astype(BF16), jnp.concatenate([value, ones], axis=1))
        keep(j).start()

    block(w, True)

    @pl.loop(1 - c, 2 * z + 1)
    def _(i):
        for s, units in ((1, ((2, 1), (2, 2), (1, 3))), (2, ((3, 1), (3, 2), (2, 3))), (3, ((3, 3),))):

            @pl.when(i == 2 * s - 1)
            def _():
                for pair in units:
                    receive(*pair)

        for s in range(chips):

            @pl.when(i == 2 * s)
            def _():
                for k in range(4):
                    to_mate(s, k).wait_recv()

        odd = i % 2
        step = (i + 1) // 2
        block(2 * (z - step) + c + (1 - odd) * (1 - 2 * c), False)

    for h in range(heads):
        total = acc[h, :, HD:]
        out = acc[h, :, :HD] / total
        o_ref[:, h * HD : (h + 1) * HD] = out
        low_ref[:, h * HD : (h + 1) * HD] = out.astype(BF16)
        lse_ref[h : h + 1, :] = jnp.transpose(jnp.log2(total))[0:1]

    copies.finish()
    for copy in away.sent:
        copy.wait()
    for s in range(chips):
        for k in range(4):

            @pl.when((z >= s) & has_above)
            def _():
                to_above(s, k).wait_send()

            @pl.when((z >= s) & ((c == 0) | (s > 0)))
            def _():
                to_mate(s, k).wait_send()

    for store in stores:
        store.wait()

    @pl.loop(0, w + 1)
    def _(j):
        keep(j).wait()


def front(tokens, cotangent, gain_row, query_weight, keyvalue_weight, query_gain, key_gain, cosine, sine, count):
    rows = tokens.shape[0]
    all_rows = 4 * rows
    q_width, kv_width = query_weight.shape[1], keyvalue_weight.shape[2]
    heads, group = q_width // HD, q_width // kv_width
    chips = count // 2
    anywhere = pl.BlockSpec(memory_space=pl.ANY)
    return pl.pallas_call(
        functools.partial(front_kernel, count, heads, group),
        name="front",
        out_shape=(
            jax.ShapeDtypeStruct((all_rows, D), BF16),
            jax.ShapeDtypeStruct((all_rows, D), BF16),
            jax.ShapeDtypeStruct((all_rows, q_width), BF16),
            jax.ShapeDtypeStruct((all_rows, q_width), F32),
            jax.ShapeDtypeStruct((all_rows, kv_width), F32),
            jax.ShapeDtypeStruct((count, all_rows, 2 * kv_width), BF16),
            jax.ShapeDtypeStruct((all_rows, q_width), F32),
            jax.ShapeDtypeStruct((all_rows, q_width), BF16),
            jax.ShapeDtypeStruct((heads, all_rows), F32),
        ),
        in_specs=[VM, VM, VM, anywhere, anywhere, VM, VM, VM, VM],
        out_specs=(anywhere,) * 6 + (VM,) * 3,
        scratch_shapes=[
            pltpu.VMEM((rows, D), BF16),
            pltpu.VMEM((all_rows, D), BF16),
            pltpu.VMEM((D, q_width + 2 * kv_width), BF16),
            pltpu.VMEM((all_rows, q_width), BF16),
            pltpu.VMEM((all_rows, q_width), F32),
            pltpu.VMEM((all_rows, kv_width), F32),
            pltpu.VMEM((count, all_rows, 2 * kv_width), BF16),
            pltpu.VMEM((heads, all_rows, 2 * HD), F32),
        ]
        + dma_sems(6)
        + dma_sems(4 * chips)
        + dma_sems(4 * chips)
        + dma_sems(3)
        + [
            pltpu.SemaphoreType.DMA((3,)),
            pltpu.SemaphoreType.DMA((5,)),
            pltpu.SemaphoreType.DMA((count,)),
        ],
        cost_estimate=cost(1, 1),
        compiler_params=remote_params(8),
    )(tokens, cotangent, gain_row, query_weight, keyvalue_weight, query_gain, key_gain, cosine, sine)


def feed_kernel(x_ref, dy_ref, w_ref, d_ref, act_ref, grad_ref, down_ref):
    x, dy = x_ref[...], dy_ref[...]
    gate = dot(x, w_ref[0])
    upper = dot(x, w_ref[1])
    act_grad = dot_nt(dy, d_ref[...])
    sig = jax.nn.sigmoid(gate)
    swish = gate * sig
    act = (swish * upper).astype(BF16)
    act_ref[...] = act
    grad_ref[0] = (act_grad * upper * sig * (1.0 + gate * (1.0 - sig))).astype(BF16)
    grad_ref[1] = (act_grad * swish).astype(BF16)
    down_ref[...] = dot_tn(act, dy).astype(BF16)


def feed(x, dy, gateup_weight, down_weight):
    rows, width = x.shape[0], down_weight.shape[0]
    tile = 256
    whole = lambda i: (0, 0)
    return pl.pallas_call(
        feed_kernel,
        name="feed",
        grid=(width // tile,),
        out_shape=(
            jax.ShapeDtypeStruct((rows, width), BF16),
            jax.ShapeDtypeStruct((2, rows, width), BF16),
            jax.ShapeDtypeStruct((width, D), BF16),
        ),
        in_specs=[
            pl.BlockSpec((rows, D), whole),
            pl.BlockSpec((rows, D), whole),
            pl.BlockSpec((2, D, tile), lambda i: (0, 0, i)),
            pl.BlockSpec((tile, D), lambda i: (i, 0)),
        ],
        out_specs=(
            pl.BlockSpec((rows, tile), lambda i: (0, i)),
            pl.BlockSpec((2, rows, tile), lambda i: (0, 0, i)),
            pl.BlockSpec((tile, D), lambda i: (i, 0)),
        ),
        compiler_params=params("arbitrary"),
        cost_estimate=cost(8 * rows * D * width, 4 * rows * D + 8 * D * width),
    )(x, dy, gateup_weight, down_weight)


def feed_back_kernel(x_ref, act_ref, grad_ref, w_ref, d_ref, full_ref, in_ref, out_ref, in_acc, out_acc):
    step = pl.program_id(0)

    @pl.when(step == 0)
    def _():
        in_acc[...] = jnp.zeros_like(in_acc)
        out_acc[...] = jnp.zeros_like(out_acc)

    in_acc[...] += dot_nt(grad_ref[0], w_ref[0]) + dot_nt(grad_ref[1], w_ref[1])
    out_acc[...] += dot(act_ref[...], d_ref[...])
    x = x_ref[...]
    full_ref[0] = dot_tn(x, grad_ref[0]).astype(BF16)
    full_ref[1] = dot_tn(x, grad_ref[1]).astype(BF16)

    @pl.when(step == pl.num_programs(0) - 1)
    def _():
        in_ref[...] = in_acc[...].astype(BF16)
        out_ref[...] = out_acc[...].astype(BF16)


def feed_back(x, act, grads, gateup_weight, down_weight):
    rows, width = x.shape[0], down_weight.shape[0]
    tile = 256
    whole = lambda i: (0, 0)
    return pl.pallas_call(
        feed_back_kernel,
        name="feed_back",
        grid=(width // tile,),
        out_shape=(
            jax.ShapeDtypeStruct((2, D, width), BF16),
            jax.ShapeDtypeStruct((rows, D), BF16),
            jax.ShapeDtypeStruct((rows, D), BF16),
        ),
        in_specs=[
            pl.BlockSpec((rows, D), whole),
            pl.BlockSpec((rows, tile), lambda i: (0, i)),
            pl.BlockSpec((2, rows, tile), lambda i: (0, 0, i)),
            pl.BlockSpec((2, D, tile), lambda i: (0, 0, i)),
            pl.BlockSpec((tile, D), lambda i: (i, 0)),
        ],
        out_specs=(
            pl.BlockSpec((2, D, tile), lambda i: (0, 0, i)),
            pl.BlockSpec((rows, D), whole),
            pl.BlockSpec((rows, D), whole),
        ),
        scratch_shapes=[pltpu.VMEM((rows, D), F32), pltpu.VMEM((rows, D), F32)],
        compiler_params=params("arbitrary"),
        cost_estimate=cost(10 * rows * D * width, 8 * rows * D + 10 * D * width),
    )(x, act, grads, gateup_weight, down_weight)


def out_back_kernel(dy_ref, w_ref, low_ref, grad_ref, full_ref):
    dy = dy_ref[...]
    grad_ref[...] = dot_nt(dy, w_ref[...]).astype(BF16)
    full_ref[...] = dot_tn(dy, low_ref[...]).astype(BF16)


def out_back(dy, weight, attn_low):
    rows, width = attn_low.shape
    tile = 256
    whole = lambda i: (0, 0)
    return pl.pallas_call(
        out_back_kernel,
        name="out_back",
        grid=(width // tile,),
        out_shape=(
            jax.ShapeDtypeStruct((rows, width), BF16),
            jax.ShapeDtypeStruct((D, width), BF16),
        ),
        in_specs=[
            pl.BlockSpec((rows, D), whole),
            pl.BlockSpec((tile, D), lambda i: (i, 0)),
            pl.BlockSpec((rows, tile), lambda i: (0, i)),
        ],
        out_specs=(
            pl.BlockSpec((rows, tile), lambda i: (0, i)),
            pl.BlockSpec((D, tile), lambda i: (0, i)),
        ),
        compiler_params=params("arbitrary"),
        cost_estimate=cost(4 * rows * D * width, 2 * rows * D + 4 * D * width),
    )(dy, weight, attn_low)


def project_back_kernel(x_ref, q_ref, kv_ref, wq_ref, wkv_ref, out_ref, in_ref, full_ref):
    q_width, kv_width = wq_ref.shape[1], wkv_ref.shape[2]
    x = x_ref[...]
    key, value = kv_ref[:, :kv_width], kv_ref[:, kv_width:]
    in_ref[...] = (
        dot_nt(q_ref[...], wq_ref[...]) + dot_nt(key, wkv_ref[0]) + dot_nt(value, wkv_ref[1])
    ).astype(BF16)
    full_ref[:, :q_width] = dot_tn(x, q_ref[...]).astype(BF16)
    full_ref[:, q_width : q_width + 2 * kv_width] = dot_tn(x, kv_ref[...]).astype(BF16)
    full_ref[:, q_width + 2 * kv_width :] = out_ref[...]


def project_back(x, q_back, kv_back, query_weight, keyvalue_weight, output_full):
    rows, out_width = x.shape[0], output_full.shape[1]
    q_width, kv_width = query_weight.shape[1], keyvalue_weight.shape[2]
    tile = 512
    whole = lambda i: (0, 0)
    return pl.pallas_call(
        project_back_kernel,
        name="project_back",
        grid=(D // tile,),
        out_shape=(
            jax.ShapeDtypeStruct((rows, D), BF16),
            jax.ShapeDtypeStruct((D, q_width + 2 * kv_width + out_width), BF16),
        ),
        in_specs=[
            pl.BlockSpec((rows, tile), lambda i: (0, i)),
            pl.BlockSpec((rows, q_width), whole),
            pl.BlockSpec((rows, 2 * kv_width), whole),
            pl.BlockSpec((tile, q_width), lambda i: (i, 0)),
            pl.BlockSpec((2, tile, kv_width), lambda i: (0, i, 0)),
            pl.BlockSpec((tile, out_width), lambda i: (i, 0)),
        ],
        out_specs=(
            pl.BlockSpec((rows, tile), lambda i: (0, i)),
            pl.BlockSpec((tile, q_width + 2 * kv_width + out_width), lambda i: (i, 0)),
        ),
        compiler_params=params("arbitrary"),
        cost_estimate=cost(4 * rows * D * (q_width + 2 * kv_width), 6 * D * (q_width + 2 * kv_width)),
    )(x, q_back, kv_back, query_weight, keyvalue_weight, output_full)


def mate_of():
    w = lax.axis_index("wide")
    c = w % 2
    return c, w + 1 - 2 * c


def greet_mate():
    _, mate = mate_of()
    barrier = pltpu.get_barrier_semaphore()
    pl.semaphore_signal(barrier, inc=1, device_id={"wide": mate}, device_id_type=MESH)
    pl.semaphore_wait(barrier, 1)


def feed_pair_kernel(x_ref, dy_ref, w_ref, raw_ref, act_ref, down_ref, stage, inbox, send, recv):
    step, steps = pl.program_id(0), pl.num_programs(0) - 1
    c, mate = mate_of()

    def trade(i):
        return wide_copy(stage.at[i % 2, 1 - c], inbox.at[i], send, recv, i, mate)

    @pl.when(step == 0)
    def _():
        greet_mate()

    @pl.when((step >= 2) & (step <= steps))
    def _():
        trade(step - 2).wait_send()

    @pl.when(step < steps)
    def _():
        x = x_ref[...]
        gate = dot(x, w_ref[0])
        upper = dot(x, w_ref[1])
        raw_ref[0] = gate
        raw_ref[1] = upper
        act = (gate * jax.nn.sigmoid(gate) * upper).astype(BF16)
        act_ref[...] = act
        full = dot_tn(act, dy_ref[...]).astype(BF16)
        width = stage.shape[4]
        for part in range(D // width):
            stage[step % 2, part % 2, part // 2] = full[:, part * width : (part + 1) * width]
        trade(step).start()

    @pl.when(step > 0)
    def _():
        last = jnp.maximum(step - 1, 0)
        trade(last).wait_recv()
        down_ref[...] = (stage[last % 2, c].astype(F32) + inbox[last].astype(F32)).astype(BF16)

    @pl.when(step == steps)
    def _():
        trade(step - 1).wait_send()


def feed_pair(x, dy, gateup_weight, width, count):
    rows = x.shape[0]
    tile = 256
    steps = width // tile
    part = D // count
    whole = lambda i: (0, 0)
    now = lambda i: jnp.minimum(i, steps - 1)
    return pl.pallas_call(
        feed_pair_kernel,
        name="feed_pair",
        grid=(steps + 1,),
        out_shape=(
            jax.ShapeDtypeStruct((2, rows, width), F32),
            jax.ShapeDtypeStruct((rows, width), BF16),
            jax.ShapeDtypeStruct((count // 2, width, part), BF16),
        ),
        in_specs=[
            pl.BlockSpec((rows, D), whole),
            pl.BlockSpec((rows, D), whole),
            pl.BlockSpec((2, D, tile), lambda i: (0, 0, now(i))),
        ],
        out_specs=(
            pl.BlockSpec((2, rows, tile), lambda i: (0, 0, now(i))),
            pl.BlockSpec((rows, tile), lambda i: (0, now(i))),
            pl.BlockSpec((count // 2, tile, part), lambda i: (0, jnp.maximum(i - 1, 0), 0)),
        ),
        scratch_shapes=[
            pltpu.VMEM((2, 2, count // 2, tile, part), BF16),
            pltpu.VMEM((steps, count // 2, tile, part), BF16),
        ]
        + dma_sems(steps),
        cost_estimate=cost(1, 1),
        compiler_params=remote_params(10),
    )(x, dy, gateup_weight)


def feed_back_pair_kernel(
    x_ref, dy_ref, raw_ref, act_ref, w_ref, d_ref, full_ref, in_ref, out_ref,
    in_acc, out_acc, stage, inbox, send, recv,
):
    step, steps = pl.program_id(0), pl.num_programs(0) - 1
    c, mate = mate_of()

    def trade(i):
        return wide_copy(stage.at[i % 2, 1 - c], inbox.at[i], send, recv, i, mate)

    @pl.when(step == 0)
    def _():
        greet_mate()
        in_acc[...] = jnp.zeros_like(in_acc)
        out_acc[...] = jnp.zeros_like(out_acc)

    @pl.when((step >= 2) & (step <= steps))
    def _():
        trade(step - 2).wait_send()

    @pl.when(step < steps)
    def _():
        act_grad = dot_nt(dy_ref[...], d_ref[...])
        gate, upper = raw_ref[0], raw_ref[1]
        sig = jax.nn.sigmoid(gate)
        gate_grad = (act_grad * upper * sig * (1.0 + gate * (1.0 - sig))).astype(BF16)
        up_grad = (act_grad * gate * sig).astype(BF16)
        x = x_ref[...]
        part = stage.shape[4]
        for n, grad in enumerate((gate_grad, up_grad)):
            full = dot_tn(x, grad).astype(BF16)
            for k in range(D // part):
                stage[step % 2, k % 2, n, k // 2] = full[k * part : (k + 1) * part]
        trade(step).start()
        in_acc[...] += dot_nt(gate_grad, w_ref[0]) + dot_nt(up_grad, w_ref[1])
        out_acc[...] += dot(act_ref[...], d_ref[...])

    @pl.when(step > 0)
    def _():
        last = jnp.maximum(step - 1, 0)
        trade(last).wait_recv()
        full_ref[...] = (stage[last % 2, c].astype(F32) + inbox[last].astype(F32)).astype(BF16)

    @pl.when(step == steps)
    def _():
        trade(step - 1).wait_send()
        in_ref[...] = in_acc[...].astype(BF16)
        out_ref[...] = out_acc[...].astype(BF16)


def feed_back_pair(x, dy, raw, act, gateup_weight, down_weight, count):
    rows, width = act.shape
    tile = 256
    steps = width // tile
    part = D // count
    whole = lambda i: (0, 0)
    now = lambda i: jnp.minimum(i, steps - 1)
    full, in_partial, out_partial = pl.pallas_call(
        feed_back_pair_kernel,
        name="feed_back_pair",
        grid=(steps + 1,),
        out_shape=(
            jax.ShapeDtypeStruct((2, count // 2, part, width), BF16),
            jax.ShapeDtypeStruct((rows, D), BF16),
            jax.ShapeDtypeStruct((rows, D), BF16),
        ),
        in_specs=[
            pl.BlockSpec((rows, D), whole),
            pl.BlockSpec((rows, D), whole),
            pl.BlockSpec((2, rows, tile), lambda i: (0, 0, now(i))),
            pl.BlockSpec((rows, tile), lambda i: (0, now(i))),
            pl.BlockSpec((2, D, tile), lambda i: (0, 0, now(i))),
            pl.BlockSpec((tile, D), lambda i: (now(i), 0)),
        ],
        out_specs=(
            pl.BlockSpec((2, count // 2, part, tile), lambda i: (0, 0, 0, jnp.maximum(i - 1, 0))),
            pl.BlockSpec((rows, D), whole),
            pl.BlockSpec((rows, D), whole),
        ),
        scratch_shapes=[
            pltpu.VMEM((rows, D), F32),
            pltpu.VMEM((rows, D), F32),
            pltpu.VMEM((2, 2, 2, count // 2, part, tile), BF16),
            pltpu.VMEM((steps, 2, count // 2, part, tile), BF16),
        ]
        + dma_sems(steps),
        cost_estimate=cost(1, 1),
        compiler_params=remote_params(11),
    )(x, dy, raw, act, gateup_weight, down_weight)
    return full.reshape(2, D // 2, width), in_partial, out_partial


def project_back_pair_kernel(
    x_ref, q_ref, kv_ref, wq_ref, wkv_ref, out_ref, in_ref, full_ref, stage, inbox, send, recv
):
    step, steps = pl.program_id(0), pl.num_programs(0) - 1
    c, mate = mate_of()
    q_width, kv_width = wq_ref.shape[1], wkv_ref.shape[2]
    part = full_ref.shape[1]

    def trade(i):
        return wide_copy(stage.at[i % 2, 1 - c], inbox.at[i], send, recv, i, mate)

    @pl.when(step == 0)
    def _():
        greet_mate()

    @pl.when((step >= 2) & (step <= steps))
    def _():
        trade(step - 2).wait_send()

    @pl.when(step < steps)
    def _():
        x = x_ref[...]
        q_full = dot_tn(x, q_ref[...]).astype(BF16)
        kv_full = dot_tn(x, kv_ref[...]).astype(BF16)
        for k in range(2):
            at = slice(k * part, (k + 1) * part)
            stage[step % 2, k, :, :q_width] = q_full[at]
            stage[step % 2, k, :, q_width : q_width + 2 * kv_width] = kv_full[at]
            stage[step % 2, k, :, q_width + 2 * kv_width :] = out_ref[at, :]
        trade(step).start()
        key, value = kv_ref[:, :kv_width], kv_ref[:, kv_width:]
        in_ref[...] = (
            dot_nt(q_ref[...], wq_ref[...]) + dot_nt(key, wkv_ref[0]) + dot_nt(value, wkv_ref[1])
        ).astype(BF16)

    @pl.when(step > 0)
    def _():
        last = jnp.maximum(step - 1, 0)
        trade(last).wait_recv()
        full_ref[0] = (stage[last % 2, c].astype(F32) + inbox[last].astype(F32)).astype(BF16)

    @pl.when(step == steps)
    def _():
        trade(step - 1).wait_send()


def project_back_pair(x, q_back, kv_back, query_weight, keyvalue_weight, output_full, count):
    rows, out_width = x.shape[0], output_full.shape[1]
    q_width, kv_width = query_weight.shape[1], keyvalue_weight.shape[2]
    width = q_width + 2 * kv_width + out_width
    part = D // count
    tile = 2 * part
    steps = count // 2
    whole = lambda i: (0, 0)
    now = lambda i: jnp.minimum(i, steps - 1)
    in_partial, full = pl.pallas_call(
        project_back_pair_kernel,
        name="project_back_pair",
        grid=(steps + 1,),
        out_shape=(
            jax.ShapeDtypeStruct((rows, D), BF16),
            jax.ShapeDtypeStruct((steps, part, width), BF16),
        ),
        in_specs=[
            pl.BlockSpec((rows, tile), lambda i: (0, now(i))),
            pl.BlockSpec((rows, q_width), whole),
            pl.BlockSpec((rows, 2 * kv_width), whole),
            pl.BlockSpec((tile, q_width), lambda i: (now(i), 0)),
            pl.BlockSpec((2, tile, kv_width), lambda i: (0, now(i), 0)),
            pl.BlockSpec((tile, out_width), lambda i: (now(i), 0)),
        ],
        out_specs=(
            pl.BlockSpec((rows, tile), lambda i: (0, now(i))),
            pl.BlockSpec((1, part, width), lambda i: (jnp.maximum(i - 1, 0), 0, 0)),
        ),
        scratch_shapes=[
            pltpu.VMEM((2, 2, part, width), BF16),
            pltpu.VMEM((steps, part, width), BF16),
        ]
        + dma_sems(steps),
        cost_estimate=cost(1, 1),
        compiler_params=remote_params(12),
    )(x, q_back, kv_back, query_weight, keyvalue_weight, output_full)
    return in_partial, full.reshape(D // 2, width)


def rest_adamw_kernel(total_ref, *refs):
    q_width, kv_width = refs[0].shape[1], refs[4].shape[2]
    ins, outs = refs[:12], refs[12:]
    total = total_ref[...].astype(F32)
    rate = 2.0 * D ** (-0.5)
    for n, new in enumerate(
        adamw(total[:, :q_width], *[r[...] for r in ins[:4]], rate, WEIGHT_DECAY)
    ):
        outs[n][...] = new
    for k in range(2):
        low = q_width + k * kv_width
        for n, new in enumerate(
            adamw(total[:, low : low + kv_width], *[r[k] for r in ins[4:8]], rate, WEIGHT_DECAY)
        ):
            outs[5 + n][k] = new
    turned = jnp.transpose(total[:, q_width + 2 * kv_width :])
    for n, new in enumerate(
        adamw(turned, *[r[...] for r in ins[8:]], 2.0 * WO_FAN ** (-0.5), WEIGHT_DECAY)
    ):
        outs[10 + n][...] = new


def rest_adamw(total, query_state, keyvalue_state, output_state):
    tile = 128
    rows, width = total.shape
    q_spec = pl.BlockSpec((tile, query_state[0].shape[1]), lambda i: (i, 0))
    kv_spec = pl.BlockSpec((2, tile, keyvalue_state[0].shape[2]), lambda i: (0, i, 0))
    o_spec = pl.BlockSpec((output_state[0].shape[0], tile), lambda i: (0, i))
    like = lambda a: jax.ShapeDtypeStruct(a.shape, F32)
    out = pl.pallas_call(
        rest_adamw_kernel,
        name="rest_adamw",
        grid=(rows // tile,),
        out_shape=tuple(
            like(state[0]) for state in (query_state, keyvalue_state, output_state) for _ in range(5)
        ),
        in_specs=[pl.BlockSpec((tile, width), lambda i: (i, 0))]
        + [q_spec] * 4
        + [kv_spec] * 4
        + [o_spec] * 4,
        out_specs=tuple([q_spec] * 5 + [kv_spec] * 5 + [o_spec] * 5),
        compiler_params=params("arbitrary"),
        cost_estimate=cost(1, 1),
    )(total, *query_state, *keyvalue_state, *output_state)
    return out[:5], out[5:10], out[10:]


def wide_scatter(partial, axis):
    return lax.psum_scatter(partial, "wide", scatter_dimension=axis, tiled=True)


def line_scatter(partial, axis, count):
    groups = [[2 * z + c for z in range(count // 2)] for c in range(2)]
    return lax.psum_scatter(
        partial, "wide", scatter_dimension=axis, tiled=True, axis_index_groups=groups
    )


def body(
    tokens,
    cotangent,
    gain_copy,
    query_weight,
    keyvalue_weight,
    output_weight,
    gateup_weight,
    down_weight,
    query_master,
    query_moment,
    query_second,
    query_average,
    keyvalue_master,
    keyvalue_moment,
    keyvalue_second,
    keyvalue_average,
    output_master,
    output_moment,
    output_second,
    output_average,
    gateup_master,
    gateup_moment,
    gateup_second,
    gateup_average,
    down_master,
    down_moment,
    down_second,
    down_average,
    gain_master,
    gain_moment,
    gain_second,
    gain_average,
):
    narrow, wide = lax.axis_size("narrow"), lax.axis_size("wide")
    special = narrow == 4 and wide == 8
    stretch_rows = tokens.shape[0] * narrow
    wide_index = lax.axis_index("wide")
    w_scalar = wide_index.astype(jnp.int32).reshape(1)
    kv_heads = keyvalue_weight.shape[2] // HD
    q_heads = query_weight.shape[1] // HD
    group = q_heads // kv_heads
    q_width, kv_width = q_heads * HD, kv_heads * HD
    attn_gain = gain_copy[:D].reshape(1, D)
    mlp_gain = gain_copy[D : 2 * D].reshape(1, D)
    query_gain = gain_copy[2 * D : 2 * D + HD].reshape(1, HD)
    key_gain = gain_copy[2 * D + HD :].reshape(1, HD)

    positions = (wide_index * stretch_rows + jnp.arange(stretch_rows, dtype=jnp.int32)).astype(F32)
    cosine, sine = rope_tables(positions)
    if special:
        back_mlp, attn_input, query_low, query_raw, key_raw, kv_all, attn_out, attn_low, lse = front(
            tokens,
            cotangent,
            attn_gain,
            query_weight,
            keyvalue_weight,
            query_gain,
            key_gain,
            cosine,
            sine,
            wide,
        )
    else:
        hidden = tokens.astype(F32)
        normed = (hidden * row_scale(hidden) * attn_gain).astype(BF16)
        attn_input = lax.all_gather(normed, "narrow", axis=0, tiled=True)
        kv_low, key_raw = keys_values(attn_input, keyvalue_weight, key_gain, cosine, sine)
        query_low, query_raw = queries(attn_input, query_weight, query_gain, cosine, sine)
        kv_all = lax.all_gather(kv_low, "wide", axis=0)
        attn_out, attn_low, lse = attend(w_scalar, query_low, kv_all, q_heads, group)
        back_mlp = lax.all_gather(cotangent, "narrow", axis=0, tiled=True)
    hidden_mid, mlp_input = mid_forward(attn_low, output_weight, tokens, mlp_gain, special)
    if special:
        raw, act, down_full = feed_pair(mlp_input, back_mlp, gateup_weight, down_weight.shape[0], wide)
        down_total = line_scatter(down_full, 0, wide)[0]
        gateup_full, in_partial, out_partial = feed_back_pair(
            mlp_input, back_mlp, raw, act, gateup_weight, down_weight, wide
        )
        gateup_total = line_scatter(gateup_full, 1, wide)
    else:
        act, act_grads, down_full = feed(mlp_input, back_mlp, gateup_weight, down_weight)
        down_total = wide_scatter(down_full, 1)
        gateup_full, in_partial, out_partial = feed_back(
            mlp_input, act, act_grads, gateup_weight, down_weight
        )
        gateup_total = wide_scatter(gateup_full, 1)
    mid_grad, back_attn, mlp_gain_grad = mid_backward(
        in_partial, hidden_mid, cotangent, mlp_gain, special
    )
    attn_grad, output_full = out_back(back_attn, output_weight, attn_low)
    query_sum, kv_sums = attend_back(
        w_scalar, query_low, kv_all, attn_grad, attn_out, lse, q_heads, group
    )
    down_new = adamw(
        down_total.astype(F32),
        down_master,
        down_moment,
        down_second,
        down_average,
        2.0 * FF ** (-0.5),
        WEIGHT_DECAY,
    )
    kv_sums, down_new = lax.optimization_barrier((kv_sums, down_new))
    query_back, query_gain_grad = unspin(query_sum, query_raw, query_gain, cosine, sine)
    kv_sum = return_grads(kv_sums, wide, special)
    kv_back, key_gain_grad = unspin(kv_sum, key_raw, key_gain, cosine, sine)
    back_args = (attn_input, query_back, kv_back, query_weight, keyvalue_weight, output_full)
    if special:
        normed_partial, project_full = project_back_pair(*back_args, wide)
    else:
        normed_partial, project_full = project_back(*back_args)
    project_full, gateup_total, out_partial, normed_partial = lax.optimization_barrier(
        (project_full, gateup_total, out_partial, normed_partial)
    )
    rest_total = line_scatter(project_full, 0, wide) if special else wide_scatter(project_full, 0)
    block_output = out_scatter(out_partial, hidden_mid, special)
    input_grad, attn_gain_grad = in_scatter(normed_partial, tokens, mid_grad, attn_gain, special)
    gain_partial = jnp.concatenate(
        [attn_gain_grad, mlp_gain_grad, query_gain_grad, key_gain_grad], axis=1
    ).reshape(-1)
    gain_total = gain_sums(gain_partial, wide, narrow, special)

    query_new, keyvalue_new, output_new = rest_adamw(
        rest_total,
        (query_master, query_moment, query_second, query_average),
        (keyvalue_master, keyvalue_moment, keyvalue_second, keyvalue_average),
        (output_master, output_moment, output_second, output_average),
    )
    gateup_new = adamw(
        gateup_total.astype(F32),
        gateup_master,
        gateup_moment,
        gateup_second,
        gateup_average,
        2.0 * D ** (-0.5),
        WEIGHT_DECAY,
    )
    gain_new = adamw(
        gain_total, gain_master, gain_moment, gain_second, gain_average, RATE_GAIN, 0.0
    )
    return (
        block_output,
        input_grad,
        *query_new,
        *keyvalue_new,
        *output_new,
        *gateup_new,
        *down_new,
        *gain_new,
    )


def solution(mesh):
    rows = P(("wide", "narrow"), None)
    flat = P(("wide", "narrow"))
    stacked = P(None, "wide", "narrow")
    query, output = P("wide", "narrow"), P("narrow", "wide")
    states = (
        *[query] * 4,
        *[stacked] * 4,
        *[output] * 4,
        *[stacked] * 4,
        *[output] * 4,
        *[flat] * 4,
    )
    return jax.shard_map(
        body,
        mesh=mesh,
        in_specs=(
            rows,
            rows,
            P(),
            P(None, "narrow"),
            P(None, None, "narrow"),
            P("narrow", None),
            P(None, None, "narrow"),
            P("narrow", None),
            *states,
        ),
        out_specs=(
            rows,
            rows,
            *[query] * 5,
            *[stacked] * 5,
            *[output] * 5,
            *[stacked] * 5,
            *[output] * 5,
            *[flat] * 5,
        ),
        check_vma=False,
    )
```

```python
import functools

import jax
import jax.numpy as jnp
from jax import lax
from jax.experimental import pallas as pl
from jax.experimental.pallas import tpu as pltpu
from jax.sharding import PartitionSpec as P

D = 2048
HD = 128
FF = 6144
STEP = 10
WO_FAN = 32

EPSILON = 1e-06
THETA = 1000000.0
BETA_ONE = 0.9
BETA_TWO = 0.999
ADAM_EPS = 1e-08
WEIGHT_DECAY = 0.1
EMA_KEEP = 0.5
RATE_GAIN = 0.4
FACTOR = HD ** (-0.5)
LOG2E = 1.4426950408889634

F32 = jnp.float32
BF16 = jnp.bfloat16
MESH = pl.DeviceIdType.MESH
VM = pl.BlockSpec(memory_space=pltpu.VMEM)
SM = pl.BlockSpec(memory_space=pltpu.SMEM)
VMEM_LIMIT = 60 << 20

NT = (((1,), (1,)), ((), ()))
TN = (((0,), (0,)), ((), ()))


def dot(left, right):
    return jnp.dot(left, right, preferred_element_type=F32)


def dot_nt(left, right):
    return lax.dot_general(left, right, NT, preferred_element_type=F32)


def dot_tn(left, right):
    return lax.dot_general(left, right, TN, preferred_element_type=F32)


def rope_tables(positions):
    half_width = HD // 2
    inverse_freq = THETA ** (-(2.0 * jnp.arange(half_width, dtype=F32)) / HD)
    angles = positions[:, None] * inverse_freq[None, :]
    cosine, sine = jnp.cos(angles), jnp.sin(angles)
    return (
        jnp.concatenate([cosine, cosine], axis=-1),
        jnp.concatenate([-sine, sine], axis=-1),
    )


def adamw(gradient, master, moment, second, average, step_rate, decay_rate):
    moment_new = BETA_ONE * moment + (1.0 - BETA_ONE) * gradient
    second_new = BETA_TWO * second + (1.0 - BETA_TWO) * gradient * gradient
    moment_hat = moment_new / (1.0 - BETA_ONE**STEP)
    second_hat = second_new / (1.0 - BETA_TWO**STEP)
    master_new = master - step_rate * (
        moment_hat / (jnp.sqrt(second_hat) + ADAM_EPS) + decay_rate * master
    )
    average_new = EMA_KEEP * average + (1.0 - EMA_KEEP) * master_new
    return (gradient, master_new, moment_new, second_new, average_new)


def row_scale(values_in):
    return lax.rsqrt(jnp.mean(values_in * values_in, axis=-1, keepdims=True) + EPSILON)


def norm_back(gradient, unit_rows, inv_scale, gain_row):
    scaled = gradient * gain_row
    inner = scaled - unit_rows * jnp.mean(scaled * unit_rows, axis=-1, keepdims=True)
    return inv_scale * inner, jnp.sum(gradient * unit_rows, axis=0, keepdims=True)


def square():
    me = lax.axis_index("narrow")
    xn = me + 1 - 2 * (me % 2)
    yn = (me + 2) % 4
    dg = (xn + 2) % 4
    return me, xn, yn, dg


def greet(axis, peers):
    barrier = pltpu.get_barrier_semaphore()
    for peer in peers:
        pl.semaphore_signal(barrier, inc=1, device_id={axis: peer}, device_id_type=MESH)
    pl.semaphore_wait(barrier, len(peers))


class Copies:
    def __init__(self, send, recv):
        self.send, self.recv, self.sent = send, recv, []

    def go(self, src, dst, slot, peer):
        copy = pltpu.make_async_remote_copy(
            src_ref=src,
            dst_ref=dst,
            send_sem=self.send.at[slot],
            recv_sem=self.recv.at[slot],
            device_id={"narrow": peer},
            device_id_type=MESH,
        )
        copy.start()
        self.sent.append(copy)
        return copy

    def finish(self):
        for copy in self.sent:
            copy.wait_send()


def gather_square(copies, slot, x_ref, o_ref, first=None, later=None, relay=None):
    me, xn, yn, dg = square()
    rows = x_ref.shape[0]
    half = rows // 2

    def part(owner, low):
        return o_ref.at[pl.ds(pl.multiple_of(owner * rows + low, half), half)]

    upper, lower = x_ref.at[pl.ds(0, half)], x_ref.at[pl.ds(half, half)]
    xa = copies.go(upper, part(me, 0), slot, xn)
    yb = copies.go(lower, part(me, half), slot + 1, yn)
    xb = copies.go(lower, part(me, half), slot + 2, xn)
    ya = copies.go(upper, part(me, 0), slot + 3, yn)
    o_ref[pl.ds(pl.multiple_of(me * rows, rows), rows)] = x_ref[...]
    if first is not None:
        first()
    xa.wait_recv()
    yf = copies.go(part(xn, 0), part(xn, 0), slot + 4, yn)
    yb.wait_recv()
    xf = copies.go(part(yn, half), part(yn, half), slot + 5, xn)
    if relay is not None:
        relay()
    for pair, owner in (((xb,), xn), ((ya,), yn), ((yf, xf), dg)):
        for copy in pair:
            copy.wait_recv()
        if later is not None:
            later(owner)


def scatter_square(copies, slot, p_ref, buf, stage, emit, fill=None, early=None, middle=None):
    me, xn, yn, dg = square()
    rows = p_ref.shape[0] // 4
    half = rows // 2

    def part(owner, low):
        return p_ref.at[pl.ds(pl.multiple_of(owner * rows + low, half), half)]

    if fill is None:
        fill = lambda owner: None
    fill(dg)
    c0 = copies.go(part(dg, 0), buf.at[0], slot, xn)
    c1 = copies.go(part(dg, half), buf.at[1], slot + 1, yn)
    fill(xn)
    c2 = copies.go(part(xn, 0), buf.at[2], slot + 2, xn)
    fill(yn)
    c3 = copies.go(part(yn, half), buf.at[3], slot + 3, yn)
    fill(me)
    if early is not None:
        early()
    c0.wait_recv()
    stage[0] = (part(yn, 0)[...].astype(F32) + buf[0].astype(F32)).astype(BF16)
    c4 = copies.go(stage.at[0], buf.at[4], slot + 4, yn)
    c1.wait_recv()
    stage[1] = (part(xn, half)[...].astype(F32) + buf[1].astype(F32)).astype(BF16)
    c5 = copies.go(stage.at[1], buf.at[5], slot + 5, xn)
    if middle is not None:
        middle()
    c2.wait_recv()
    c4.wait_recv()
    emit(0, part(me, 0)[...].astype(F32) + buf[2].astype(F32) + buf[4].astype(F32))
    c3.wait_recv()
    c5.wait_recv()
    emit(half, part(me, half)[...].astype(F32) + buf[3].astype(F32) + buf[5].astype(F32))


def dma_sems(count):
    return [pltpu.SemaphoreType.DMA((count,)), pltpu.SemaphoreType.DMA((count,))]


def scatter_space(rows):
    return [pltpu.VMEM((6, rows // 2, D), BF16), pltpu.VMEM((2, rows // 2, D), BF16)]


def remote_params(collective_id):
    return pltpu.CompilerParams(
        collective_id=collective_id, has_side_effects=True, vmem_limit_bytes=VMEM_LIMIT
    )


def mid_kernel(
    a_ref, w_ref, t_ref, g_ref, dy_hbm, gu_hbm, d_hbm,
    h_ref, x_hbm, grad_hbm, act_hbm, down_hbm,
    p_ref, buf, stage, own, x, weight, dy, down, act_grad, grad, act, mine, inbox,
    send, recv, m_send, m_recv, load_sem, store_sem, down_sem,
):
    me, xn, yn, dg = square()
    c, mate = mate_of()
    rows = t_ref.shape[0]
    half = rows // 2
    tiles, tile, part = inbox.shape[0], inbox.shape[2], inbox.shape[3]
    loads = [
        pltpu.make_async_copy(src, dst, load_sem.at[n])
        for n, (src, dst) in enumerate(((dy_hbm, dy), (d_hbm, down), (gu_hbm, weight)))
    ]
    for load in loads:
        load.start()
    barrier = pltpu.get_barrier_semaphore()
    for peer in (xn, yn):
        pl.semaphore_signal(barrier, inc=1, device_id={"narrow": peer}, device_id_type=MESH)
    pl.semaphore_signal(barrier, inc=1, device_id={"wide": mate}, device_id_type=MESH)
    pl.semaphore_wait(barrier, 3)
    copies = Copies(send, recv)

    def rows_of(owner):
        return pl.ds(pl.multiple_of(owner * rows, rows), rows)

    def fill(owner):
        p_ref[rows_of(owner), :] = dot(a_ref[rows_of(owner), :], w_ref[...]).astype(BF16)

    def emit(low, total):
        hidden = t_ref[pl.ds(low, half)].astype(F32) + total
        h_ref[pl.ds(low, half)] = hidden
        own[pl.ds(low, half)] = (hidden * row_scale(hidden) * g_ref[...]).astype(BF16)

    def act_grads(low, high):
        @pl.loop(low, high)
        def _(t):
            cols = pl.ds(pl.multiple_of(t * tile, tile), tile)
            act_grad[:, cols] = dot_nt(dy[...], down[cols, :])

    def early():
        loads[0].wait()
        loads[1].wait()
        act_grads(0, tiles // 2)

    def middle():
        act_grads(tiles // 2, tiles)

    scatter_square(copies, 0, p_ref, buf, stage, emit, fill, early, middle)

    def expand(owner):
        at = rows_of(owner)

        @pl.loop(0, tiles)
        def _(t):
            cols = pl.ds(pl.multiple_of(t * tile, tile), tile)
            gate = dot(x[at, :], weight[0, :, cols])
            upper = dot(x[at, :], weight[1, :, cols])
            sig = jax.nn.sigmoid(gate)
            swish = gate * sig
            back = act_grad[at, cols]
            act[at, cols] = (swish * upper).astype(BF16)
            grad[0, at, cols] = (back * upper * sig * (1.0 + gate * (1.0 - sig))).astype(BF16)
            grad[1, at, cols] = (back * swish).astype(BF16)

    def first():
        loads[2].wait()
        expand(me)

    def later(owner):
        expand(owner)

    gather_square(copies, 6, own, x, first, later)
    stores = [
        pltpu.make_async_copy(src, dst, store_sem.at[n])
        for n, (src, dst) in enumerate(((x, x_hbm), (grad, grad_hbm), (act, act_hbm)))
    ]
    for store in stores:
        store.start()

    def trade(t):
        return wide_copy(mine.at[t, 1 - c], inbox.at[t], m_send, m_recv, t, mate)

    def keep(t):
        at = pl.ds(pl.multiple_of(t * tile, tile), tile)
        return pltpu.make_async_copy(mine.at[t, c], down_hbm.at[:, at], down_sem.at[t])

    @pl.loop(0, tiles)
    def _(t):
        cols = pl.ds(pl.multiple_of(t * tile, tile), tile)
        full = dot_tn(act[:, cols], dy[...]).astype(BF16)
        for k in range(D // part):
            mine[t, k % 2, k // 2] = full[:, k * part : (k + 1) * part]
        trade(t).start()

    @pl.loop(0, tiles)
    def _(t):
        trade(t).wait_recv()
        mine[t, c] = (mine[t, c].astype(F32) + inbox[t].astype(F32)).astype(BF16)
        keep(t).start()

    copies.finish()

    @pl.loop(0, tiles)
    def _(t):
        trade(t).wait_send()
        keep(t).wait()

    for store in stores:
        store.wait()


def mid_pair(attn_low, weight, tokens, gain_row, dy, gateup_weight, down_weight, count):
    rows = tokens.shape[0]
    width = gateup_weight.shape[2]
    tile, part, chips = 256, D // count, count // 2
    tiles = width // tile
    anywhere = pl.BlockSpec(memory_space=pl.ANY)
    return pl.pallas_call(
        mid_kernel,
        name="mid_pair",
        out_shape=(
            jax.ShapeDtypeStruct((rows, D), F32),
            jax.ShapeDtypeStruct((4 * rows, D), BF16),
            jax.ShapeDtypeStruct((2, 4 * rows, width), BF16),
            jax.ShapeDtypeStruct((4 * rows, width), BF16),
            jax.ShapeDtypeStruct((chips, width, part), BF16),
        ),
        in_specs=[VM] * 4 + [anywhere] * 3,
        out_specs=(VM,) + (anywhere,) * 4,
        scratch_shapes=[pltpu.VMEM((4 * rows, D), BF16)]
        + scatter_space(rows)
        + [
            pltpu.VMEM((rows, D), BF16),
            pltpu.VMEM((4 * rows, D), BF16),
            pltpu.VMEM((2, D, width), BF16),
            pltpu.VMEM((4 * rows, D), BF16),
            pltpu.VMEM((width, D), BF16),
            pltpu.VMEM((4 * rows, width), F32),
            pltpu.VMEM((2, 4 * rows, width), BF16),
            pltpu.VMEM((4 * rows, width), BF16),
            pltpu.VMEM((tiles, 2, chips, tile, part), BF16),
            pltpu.VMEM((tiles, chips, tile, part), BF16),
        ]
        + dma_sems(12)
        + dma_sems(tiles)
        + [
            pltpu.SemaphoreType.DMA((3,)),
            pltpu.SemaphoreType.DMA((3,)),
            pltpu.SemaphoreType.DMA((tiles,)),
        ],
        cost_estimate=cost(1, 1),
        compiler_params=remote_params(2),
    )(attn_low, weight, tokens, gain_row, dy, gateup_weight, down_weight)


def mid_forward(attn_low, weight, tokens, gain_row):
    partial = dot(attn_low, weight).astype(BF16)
    hidden = tokens.astype(F32) + lax.psum_scatter(
        partial, "narrow", scatter_dimension=0, tiled=True
    ).astype(F32)
    normed = (hidden * row_scale(hidden) * gain_row).astype(BF16)
    return hidden, lax.all_gather(normed, "narrow", axis=0, tiled=True)


def mid_backward_kernel(
    h_ref, c_ref, g_ref, x_hbm, grad_hbm, gu_hbm,
    m_ref, o_ref, gg_ref, full_hbm,
    p_ref, buf, stage, own, x, grad, weight, mine, inbox,
    send, recv, m_send, m_recv, load_sem, full_sem,
):
    me, xn, yn, dg = square()
    c, mate = mate_of()
    half = h_ref.shape[0] // 2
    tiles, part, tile = inbox.shape[0], inbox.shape[3], inbox.shape[4]
    loads = [
        pltpu.make_async_copy(src, dst, load_sem.at[n])
        for n, (src, dst) in enumerate(((grad_hbm, grad), (gu_hbm, weight), (x_hbm, x)))
    ]
    for load in loads:
        load.start()
    barrier = pltpu.get_barrier_semaphore()
    for peer in (xn, yn):
        pl.semaphore_signal(barrier, inc=1, device_id={"narrow": peer}, device_id_type=MESH)
    pl.semaphore_signal(barrier, inc=1, device_id={"wide": mate}, device_id_type=MESH)
    pl.semaphore_wait(barrier, 3)
    copies = Copies(send, recv)
    gg_ref[...] = jnp.zeros_like(gg_ref)

    def emit(low, total):
        hidden = h_ref[pl.ds(low, half)]
        scale = row_scale(hidden)
        back, gain_sum = norm_back(total, hidden * scale, scale, g_ref[...])
        gg_ref[...] += gain_sum
        mid = c_ref[pl.ds(low, half)].astype(F32) + back
        m_ref[pl.ds(low, half)] = mid
        own[pl.ds(low, half)] = mid.astype(BF16)

    def trade(t):
        return wide_copy(mine.at[t, 1 - c], inbox.at[t], m_send, m_recv, t, mate)

    def keep(t):
        cols = pl.ds(pl.multiple_of(t * tile, tile), tile)
        return pltpu.make_async_copy(mine.at[t, c], full_hbm.at[:, :, :, cols], full_sem.at[t])

    def products(low, high):
        @pl.loop(low, high)
        def _(t):
            cols = pl.ds(pl.multiple_of(t * tile, tile), tile)
            for n in range(2):
                full = dot_tn(x[...], grad[n, :, cols]).astype(BF16)
                for k in range(D // part):
                    mine[t, k % 2, n, k // 2] = full[k * part : (k + 1) * part]
            trade(t).start()

    rows = 2 * half
    loads[0].wait()
    loads[1].wait()

    def fill(owner):
        at = pl.ds(pl.multiple_of(owner * rows, rows), rows)

        @pl.loop(0, D // 512)
        def _(t):
            cols = pl.ds(pl.multiple_of(t * 512, 512), 512)
            p_ref[at, cols] = (
                dot_nt(grad[0, at, :], weight[0, cols, :])
                + dot_nt(grad[1, at, :], weight[1, cols, :])
            ).astype(BF16)

    def early():
        loads[2].wait()
        products(0, tiles // 2)

    def middle():
        products(tiles // 2, tiles)

    def relay():
        @pl.loop(0, tiles)
        def _(t):
            trade(t).wait_recv()
            mine[t, c] = (mine[t, c].astype(F32) + inbox[t].astype(F32)).astype(BF16)
            keep(t).start()

    scatter_square(copies, 0, p_ref, buf, stage, emit, fill, early, middle)
    gather_square(copies, 6, own, o_ref, relay=relay)
    copies.finish()

    @pl.loop(0, tiles)
    def _(t):
        trade(t).wait_send()
        keep(t).wait()


def mid_backward_pair(hidden_mid, cotangent, gain_row, x, grads, gateup_weight, count):
    rows = hidden_mid.shape[0]
    width = grads.shape[2]
    tile, part, chips = 256, D // count, count // 2
    tiles = width // tile
    anywhere = pl.BlockSpec(memory_space=pl.ANY)
    mid_grad, back_attn, gain_sum, full = pl.pallas_call(
        mid_backward_kernel,
        name="mid_backward_pair",
        out_shape=(
            jax.ShapeDtypeStruct((rows, D), F32),
            jax.ShapeDtypeStruct((4 * rows, D), BF16),
            jax.ShapeDtypeStruct((1, D), F32),
            jax.ShapeDtypeStruct((2, chips, part, width), BF16),
        ),
        in_specs=[VM] * 3 + [anywhere] * 3,
        out_specs=(VM,) * 3 + (anywhere,),
        scratch_shapes=[pltpu.VMEM((4 * rows, D), BF16)]
        + scatter_space(rows)
        + [
            pltpu.VMEM((rows, D), BF16),
            pltpu.VMEM(x.shape, BF16),
            pltpu.VMEM(grads.shape, BF16),
            pltpu.VMEM(gateup_weight.shape, BF16),
            pltpu.VMEM((tiles, 2, 2, chips, part, tile), BF16),
            pltpu.VMEM((tiles, 2, chips, part, tile), BF16),
        ]
        + dma_sems(12)
        + dma_sems(tiles)
        + [pltpu.SemaphoreType.DMA((3,)), pltpu.SemaphoreType.DMA((tiles,))],
        cost_estimate=cost(1, 1),
        compiler_params=remote_params(3),
    )(hidden_mid, cotangent, gain_row, x, grads, gateup_weight)
    return mid_grad, back_attn, gain_sum, full.reshape(2, D // 2, width)


def mid_backward(partial, hidden_mid, cotangent, gain_row):
    total = lax.psum_scatter(partial, "narrow", scatter_dimension=0, tiled=True).astype(F32)
    scale = row_scale(hidden_mid)
    back, gain_sum = norm_back(total, hidden_mid * scale, scale, gain_row)
    mid = cotangent.astype(F32) + back
    return mid, lax.all_gather(mid.astype(BF16), "narrow", axis=0, tiled=True), gain_sum


def in_scatter_kernel(p_ref, t_ref, m_ref, g_ref, o_ref, gg_ref, buf, stage, send, recv):
    _, xn, yn, _ = square()
    half = t_ref.shape[0] // 2
    greet("narrow", (xn, yn))
    copies = Copies(send, recv)
    gg_ref[...] = jnp.zeros_like(gg_ref)

    def emit(low, total):
        hidden = t_ref[pl.ds(low, half)].astype(F32)
        scale = row_scale(hidden)
        back, gain_sum = norm_back(total, hidden * scale, scale, g_ref[...])
        gg_ref[...] += gain_sum
        o_ref[pl.ds(low, half)] = m_ref[pl.ds(low, half)] + back

    scatter_square(copies, 0, p_ref, buf, stage, emit)
    copies.finish()


def in_scatter(partial, tokens, mid_grad, gain_row, special):
    rows = tokens.shape[0]
    if not special:
        total = lax.psum_scatter(partial, "narrow", scatter_dimension=0, tiled=True).astype(F32)
        hidden = tokens.astype(F32)
        scale = row_scale(hidden)
        back, gain_sum = norm_back(total, hidden * scale, scale, gain_row)
        return mid_grad + back, gain_sum
    return pl.pallas_call(
        in_scatter_kernel,
        name="in_scatter",
        out_shape=(
            jax.ShapeDtypeStruct((rows, D), F32),
            jax.ShapeDtypeStruct((1, D), F32),
        ),
        in_specs=[VM] * 4,
        out_specs=(VM,) * 2,
        scratch_shapes=scatter_space(rows) + dma_sems(6),
        cost_estimate=cost(1, 1),
        compiler_params=remote_params(4),
    )(partial, tokens, mid_grad, gain_row)


def line(count):
    w = lax.axis_index("wide")
    z, c = w // 2, w % 2
    return w, z, c, count // 2, w + 1 - 2 * c, jnp.minimum(w + 2, count - 1), jnp.maximum(w - 2, 0)


def wide_copy(src, dst, send, recv, slot, peer):
    return pltpu.make_async_remote_copy(
        src_ref=src,
        dst_ref=dst,
        send_sem=send.at[slot],
        recv_sem=recv.at[slot],
        device_id={"wide": peer},
        device_id_type=MESH,
    )


def return_grads_kernel(
    count, x_ref, h_ref, act_hbm, d_hbm, o_ref, b_ref,
    from_mate, from_above, stage, p_ref, buf, out_stage, act, weight,
    send, recv, mate_send, mate_recv, n_send, n_recv, load_sem,
):
    w, z, c, chips, mate, above, below = line(count)
    me, xn, yn, dg = square()
    rows = h_ref.shape[0]
    half = rows // 2
    loads = [
        pltpu.make_async_copy(src, dst, load_sem.at[n])
        for n, (src, dst) in enumerate(((act_hbm, act), (d_hbm, weight)))
    ]
    for load in loads:
        load.start()
    has_above, has_below = z < chips - 1, z > 0
    barrier = pltpu.get_barrier_semaphore()
    for peer in (xn, yn):
        pl.semaphore_signal(barrier, inc=1, device_id={"narrow": peer}, device_id_type=MESH)

    @pl.when(has_above)
    def _():
        pl.semaphore_signal(barrier, inc=1, device_id={"wide": above}, device_id_type=MESH)

    @pl.when(has_below)
    def _():
        pl.semaphore_signal(barrier, inc=1, device_id={"wide": below}, device_id_type=MESH)

    pl.semaphore_signal(barrier, inc=1, device_id={"wide": mate}, device_id_type=MESH)
    pl.semaphore_wait(barrier, 3 + has_above.astype(jnp.int32) + has_below.astype(jnp.int32))

    def to_mate(s):
        return wide_copy(
            x_ref.at[jnp.minimum(2 * s + 1 - c, count - 1)],
            from_mate.at[s],
            mate_send,
            mate_recv,
            s,
            mate,
        )

    def sends_mate(s):
        return (z > s) | ((z == s) & (c == 1))

    def down(s):
        return wide_copy(stage.at[s], from_above.at[s], send, recv, s, below)

    for s in range(chips):

        @pl.when(sends_mate(s))
        def _():
            to_mate(s).start()

    def chain():
        for s in range(chips - 1):
            block = 2 * s + c

            @pl.when(z > s)
            def _():
                to_mate(s).wait_recv()

                @pl.when(z == chips - 1)
                def _():
                    stage[s] = (x_ref[block].astype(F32) + from_mate[s].astype(F32)).astype(BF16)

                @pl.when(z < chips - 1)
                def _():
                    down(s).wait_recv()
                    stage[s] = (
                        x_ref[block].astype(F32)
                        + from_mate[s].astype(F32)
                        + from_above[s].astype(F32)
                    ).astype(BF16)

                down(s).start()

    def emit(low, total):
        b_ref[pl.ds(low, half)] = h_ref[pl.ds(low, half)] + total

    def fill(owner):
        at = pl.ds(pl.multiple_of(owner * rows, rows), rows)

        @pl.loop(0, D // 512)
        def _(t):
            cols = pl.ds(pl.multiple_of(t * 512, 512), 512)
            p_ref[at, cols] = dot(act[at, :], weight[:, cols]).astype(BF16)

    for load in loads:
        load.wait()
    copies = Copies(n_send, n_recv)
    scatter_square(copies, 0, p_ref, buf, out_stage, emit, fill, middle=chain)
    for s in range(chips):
        block = 2 * s + c

        @pl.when(z == s)
        def _():
            o_ref[...] = x_ref[block].astype(F32)

            @pl.when(c == 0)
            def _():
                to_mate(s).wait_recv()
                o_ref[...] += from_mate[s].astype(F32)

            if s < chips - 1:
                down(s).wait_recv()
                o_ref[...] += from_above[s].astype(F32)

    copies.finish()
    for s in range(chips):

        @pl.when(sends_mate(s))
        def _():
            to_mate(s).wait_send()

        @pl.when(z > s)
        def _():
            down(s).wait_send()


def return_grads_out(grads, act, down_weight, hidden_mid, count):
    _, rows, width = grads.shape
    chips = count // 2
    return pl.pallas_call(
        functools.partial(return_grads_kernel, count),
        name="return_grads",
        out_shape=(
            jax.ShapeDtypeStruct((rows, width), F32),
            jax.ShapeDtypeStruct(hidden_mid.shape, F32),
        ),
        in_specs=[VM] * 2 + [pl.BlockSpec(memory_space=pl.ANY)] * 2,
        out_specs=(VM, VM),
        scratch_shapes=[
            pltpu.VMEM((chips, rows, width), BF16),
            pltpu.VMEM((chips, rows, width), BF16),
            pltpu.VMEM((chips, rows, width), BF16),
            pltpu.VMEM((act.shape[0], D), BF16),
        ]
        + scatter_space(hidden_mid.shape[0])
        + [pltpu.VMEM(act.shape, BF16), pltpu.VMEM(down_weight.shape, BF16)]
        + dma_sems(chips)
        + dma_sems(chips)
        + dma_sems(6)
        + [pltpu.SemaphoreType.DMA((2,))],
        cost_estimate=cost(1, 1),
        compiler_params=remote_params(6),
    )(grads, hidden_mid, act, down_weight)


def return_grads(grads, count):
    _, rows, width = grads.shape
    w = lax.axis_index("wide")
    seen = (jnp.arange(count) <= w)[:, None, None]
    total = lax.psum_scatter(
        jnp.where(seen, grads, 0).reshape(count * rows, width),
        "wide",
        scatter_dimension=0,
        tiled=True,
    )
    return total.astype(F32)


def gain_kernel(wide, x_ref, o_ref, near, mid, far, send, recv, wide_send, wide_recv):
    me, xn, yn, dg = square()
    w = lax.axis_index("wide")
    barrier = pltpu.get_barrier_semaphore()
    for peer in (xn, yn, dg):
        pl.semaphore_signal(barrier, inc=1, device_id={"narrow": peer}, device_id_type=MESH)
    for step in range(1, wide):
        pl.semaphore_signal(
            barrier, inc=1, device_id={"wide": (w + step) % wide}, device_id_type=MESH
        )
    pl.semaphore_wait(barrier, 3 + wide - 1)
    copies = Copies(send, recv)
    sent = [
        copies.go(x_ref.at[peer], near.at[slot], slot, peer)
        for slot, peer in enumerate((xn, yn, dg))
    ]
    for copy in sent:
        copy.wait_recv()
    mid[...] = x_ref[me] + near[0] + near[1] + near[2]
    away = []
    for step in range(1, wide):
        peer = (w + step) % wide
        copy = wide_copy(
            mid.at[peer], far.at[step - 1], wide_send, wide_recv, step - 1, peer
        )
        copy.start()
        away.append(copy)
    total = mid[w]
    for step in range(1, wide):
        away[step - 1].wait_recv()
        total = total + far[step - 1]
    o_ref[...] = total
    copies.finish()
    for copy in away:
        copy.wait_send()


def gain_sums(partial, wide, narrow, special):
    if not special:
        return lax.psum_scatter(partial, ("wide", "narrow"), scatter_dimension=0, tiled=True)
    count = partial.shape[0] // (wide * narrow)
    padded = -(-count // 128) * 128
    shaped = partial.reshape(wide, narrow, count).transpose(1, 0, 2)
    shaped = jnp.pad(shaped, ((0, 0), (0, 0), (0, padded - count)))
    shaped = shaped.reshape(narrow, wide, padded // 128, 128)
    out = pl.pallas_call(
        functools.partial(gain_kernel, wide),
        name="gain_sums",
        out_shape=jax.ShapeDtypeStruct((padded // 128, 128), F32),
        in_specs=[VM],
        out_specs=VM,
        scratch_shapes=[
            pltpu.VMEM((3, wide, padded // 128, 128), F32),
            pltpu.VMEM((wide, padded // 128, 128), F32),
            pltpu.VMEM((wide - 1, padded // 128, 128), F32),
        ]
        + dma_sems(3)
        + dma_sems(wide - 1),
        cost_estimate=cost(1, 1),
        compiler_params=remote_params(7),
    )(shaped)
    return out.reshape(padded)[:count]


def cost(flops, moved, exps=0):
    return pl.CostEstimate(flops=1, bytes_accessed=1, transcendentals=0)


def params(*semantics):
    if not semantics:
        return pltpu.CompilerParams(vmem_limit_bytes=VMEM_LIMIT)
    return pltpu.CompilerParams(vmem_limit_bytes=VMEM_LIMIT, dimension_semantics=semantics)


def spin(raw, gain_row, cosine, sine):
    normed = raw * row_scale(raw) * gain_row
    return normed * cosine + pltpu.roll(normed, HD // 2, axis=1) * sine


def keys_kernel(x_ref, w_ref, g_ref, cos_ref, sin_ref, kv_ref, raw_ref):
    which = pl.program_id(0)
    width = w_ref.shape[2]
    out = dot(x_ref[...], w_ref[0])

    @pl.when(which == 0)
    def _():
        raw_ref[...] = out
        for h in range(width // HD):
            part = out[:, h * HD : (h + 1) * HD]
            kv_ref[:, h * HD : (h + 1) * HD] = spin(
                part, g_ref[...], cos_ref[...], sin_ref[...]
            ).astype(BF16)

    @pl.when(which == 1)
    def _():
        kv_ref[...] = out.astype(BF16)


def keys_values(x, weight, gain_row, cosine, sine):
    rows, width = x.shape[0], weight.shape[2]
    whole = lambda i: (0, 0)
    return pl.pallas_call(
        keys_kernel,
        name="keys_values",
        grid=(2,),
        out_shape=(
            jax.ShapeDtypeStruct((rows, 2 * width), BF16),
            jax.ShapeDtypeStruct((rows, width), F32),
        ),
        in_specs=[
            pl.BlockSpec((rows, D), whole),
            pl.BlockSpec((1, D, width), lambda i: (i, 0, 0)),
            pl.BlockSpec((1, HD), whole),
            pl.BlockSpec((rows, HD), whole),
            pl.BlockSpec((rows, HD), whole),
        ],
        out_specs=(
            pl.BlockSpec((rows, width), lambda i: (0, i)),
            pl.BlockSpec((rows, width), whole),
        ),
        compiler_params=params("arbitrary"),
        cost_estimate=cost(4 * rows * D * width, 2 * rows * D + 4 * D * width),
    )(x, weight, gain_row, cosine, sine)


def queries_kernel(x_ref, w_ref, g_ref, cos_ref, sin_ref, q_ref, raw_ref):
    out = dot(x_ref[...], w_ref[...])
    raw_ref[...] = out
    for h in range(w_ref.shape[1] // HD):
        part = out[:, h * HD : (h + 1) * HD]
        q_ref[:, h * HD : (h + 1) * HD] = spin(
            part, g_ref[...], cos_ref[...], sin_ref[...]
        ).astype(BF16)


def queries(x, weight, gain_row, cosine, sine):
    rows, width = x.shape[0], weight.shape[1]
    tile = 256
    whole = lambda i: (0, 0)
    return pl.pallas_call(
        queries_kernel,
        name="queries",
        grid=(width // tile,),
        out_shape=(
            jax.ShapeDtypeStruct((rows, width), BF16),
            jax.ShapeDtypeStruct((rows, width), F32),
        ),
        in_specs=[
            pl.BlockSpec((rows, D), whole),
            pl.BlockSpec((D, tile), lambda i: (0, i)),
            pl.BlockSpec((1, HD), whole),
            pl.BlockSpec((rows, HD), whole),
            pl.BlockSpec((rows, HD), whole),
        ],
        out_specs=(
            pl.BlockSpec((rows, tile), lambda i: (0, i)),
            pl.BlockSpec((rows, tile), lambda i: (0, i)),
        ),
        compiler_params=params("arbitrary"),
        cost_estimate=cost(2 * rows * D * width, 2 * rows * D + 2 * D * width),
    )(x, weight, gain_row, cosine, sine)


def attend_kernel(heads, group, w_ref, q_ref, kv_ref, o_ref, low_ref, lse_ref, acc):
    rows = q_ref.shape[0]
    kv_width = kv_ref.shape[2] // 2
    w = w_ref[0]
    acc[...] = jnp.zeros_like(acc)
    ones = jnp.ones((rows, HD), BF16)

    def block(j, masked):
        for h in range(heads):
            kv = h // group
            key = kv_ref[j, :, kv * HD : (kv + 1) * HD]
            value = kv_ref[j, :, kv_width + kv * HD : kv_width + (kv + 1) * HD]
            query = q_ref[:, h * HD : (h + 1) * HD]
            terms = jnp.exp2(dot_nt(query, key) * (FACTOR * LOG2E))
            if masked:
                at = lax.broadcasted_iota(jnp.int32, (rows, rows), 0)
                key_at = lax.broadcasted_iota(jnp.int32, (rows, rows), 1)
                terms = jnp.where(key_at <= at, terms, 0.0)
            acc[h] += dot(terms.astype(BF16), jnp.concatenate([value, ones], axis=1))

    @pl.loop(0, w)
    def _(j):
        block(j, False)

    block(w, True)
    for h in range(heads):
        total = acc[h, :, HD:]
        out = acc[h, :, :HD] / total
        o_ref[:, h * HD : (h + 1) * HD] = out
        low_ref[:, h * HD : (h + 1) * HD] = out.astype(BF16)
        lse_ref[h : h + 1, :] = jnp.transpose(jnp.log2(total))[0:1]


def attend(w_index, query, kv_all, heads, group):
    rows, width = query.shape
    count = kv_all.shape[0]
    return pl.pallas_call(
        functools.partial(attend_kernel, heads, group),
        name="attend",
        out_shape=(
            jax.ShapeDtypeStruct((rows, width), F32),
            jax.ShapeDtypeStruct((rows, width), BF16),
            jax.ShapeDtypeStruct((heads, rows), F32),
        ),
        in_specs=[SM, VM, VM],
        out_specs=(VM, VM, VM),
        scratch_shapes=[pltpu.VMEM((heads, rows, 2 * HD), F32)],
        compiler_params=params(),
        cost_estimate=cost(4 * rows * rows * count * width, 2 * kv_all.size, rows * rows * heads * count),
    )(w_index, query, kv_all)


def attend_back_kernel(
    heads, group, w_ref, q_ref, kv_ref, do_ref, o_ref, lse_ref, dq_ref, dkv_ref, delta
):
    rows = q_ref.shape[0]
    kv_width = kv_ref.shape[2] // 2
    w = w_ref[0]
    for h in range(heads):
        part = slice(h * HD, (h + 1) * HD)
        delta[h : h + 1, :] = jnp.sum(
            jnp.transpose(do_ref[:, part].astype(F32) * o_ref[:, part]), axis=0, keepdims=True
        )
    dq_ref[...] = jnp.zeros_like(dq_ref)

    def block(j, masked):
        for kv in range(heads // group):
            key = kv_ref[j, :, kv * HD : (kv + 1) * HD]
            value = kv_ref[j, :, kv_width + kv * HD : kv_width + (kv + 1) * HD]
            key_sum = jnp.zeros((rows, HD), F32)
            value_sum = jnp.zeros((rows, HD), F32)
            for h in range(kv * group, (kv + 1) * group):
                part = slice(h * HD, (h + 1) * HD)
                query, out_grad = q_ref[:, part], do_ref[:, part]
                probs = jnp.exp2(
                    dot_nt(key, query) * (FACTOR * LOG2E) - lse_ref[h : h + 1, :]
                )
                if masked:
                    key_at = lax.broadcasted_iota(jnp.int32, (rows, rows), 0)
                    at = lax.broadcasted_iota(jnp.int32, (rows, rows), 1)
                    probs = jnp.where(key_at <= at, probs, 0.0)
                value_sum += dot(probs.astype(BF16), out_grad)
                prob_grad = dot_nt(value, out_grad)
                score_grad = (probs * (prob_grad - delta[h : h + 1, :])).astype(BF16)
                key_sum += dot(score_grad, query)
                dq_ref[:, part] += dot_tn(score_grad, key)
            dkv_ref[j, :, kv * HD : (kv + 1) * HD] = (key_sum * FACTOR).astype(BF16)
            dkv_ref[j, :, kv_width + kv * HD : kv_width + (kv + 1) * HD] = value_sum.astype(BF16)

    @pl.loop(0, w)
    def _(j):
        block(j, False)

    block(w, True)
    dq_ref[...] = dq_ref[...] * FACTOR


def attend_back(w_index, query, kv_all, out_grad, out, lse, heads, group):
    rows, width = query.shape
    count = kv_all.shape[0]
    return pl.pallas_call(
        functools.partial(attend_back_kernel, heads, group),
        name="attend_back",
        out_shape=(
            jax.ShapeDtypeStruct((rows, width), F32),
            jax.ShapeDtypeStruct(kv_all.shape, BF16),
        ),
        in_specs=[SM] + [VM] * 5,
        out_specs=(VM, VM),
        scratch_shapes=[pltpu.VMEM((heads, rows), F32)],
        compiler_params=params(),
        cost_estimate=cost(10 * rows * rows * count * width, 4 * kv_all.size, rows * rows * heads * count),
    )(w_index, query, kv_all, out_grad, out, lse)


def unspin_kernel(width, e_ref, raw_ref, g_ref, cos_ref, sin_ref, o_ref, gg_ref):
    gain_sum = jnp.zeros((1, HD), F32)
    for h in range(raw_ref.shape[1] // HD):
        part = slice(h * HD, (h + 1) * HD)
        grad = e_ref[:, part]
        turned = grad * cos_ref[...] - pltpu.roll(grad, HD // 2, axis=1) * sin_ref[...]
        raw = raw_ref[:, part]
        scale = row_scale(raw)
        back, total = norm_back(turned, raw * scale, scale, g_ref[...])
        o_ref[:, part] = back.astype(BF16)
        gain_sum += total
    if width > raw_ref.shape[1]:
        o_ref[:, raw_ref.shape[1] :] = e_ref[:, raw_ref.shape[1] :].astype(BF16)
    gg_ref[...] = gain_sum


def unspin(grad, raw, gain_row, cosine, sine):
    rows, width = grad.shape
    return pl.pallas_call(
        functools.partial(unspin_kernel, width),
        name="unspin",
        out_shape=(
            jax.ShapeDtypeStruct((rows, width), BF16),
            jax.ShapeDtypeStruct((1, HD), F32),
        ),
        in_specs=[VM] * 5,
        out_specs=(VM, VM),
        compiler_params=params(),
        cost_estimate=cost(20 * grad.size, 10 * grad.size),
    )(grad, raw, gain_row, cosine, sine)


def front_kernel(
    count, heads, group,
    t_ref, c_ref, g_ref, wq_hbm, wkv_hbm, qg_ref, kg_ref, cos_ref, sin_ref,
    dy_hbm, x_hbm, q_hbm, qraw_hbm, kraw_hbm, kv_hbm, o_ref, low_ref, lse_ref,
    own, x, weight, q, qraw, kraw, kv, acc,
    send, recv, z_send, z_recv, m_send, m_recv, c_send, c_recv, load_sem, store_sem, kv_sem,
):
    me, xn, yn, dg = square()
    w, z, c, chips, mate, above, below = line(count)
    rows = t_ref.shape[0]
    half = rows // 2
    all_rows = 4 * rows
    q_width, kv_width = wq_hbm.shape[1], wkv_hbm.shape[2]
    owners = (me, xn, yn, dg)
    loads = [
        pltpu.make_async_copy(wq_hbm, weight.at[:, pl.ds(0, q_width)], load_sem.at[0]),
        pltpu.make_async_copy(wkv_hbm.at[0], weight.at[:, pl.ds(q_width, kv_width)], load_sem.at[1]),
        pltpu.make_async_copy(
            wkv_hbm.at[1], weight.at[:, pl.ds(q_width + kv_width, kv_width)], load_sem.at[2]
        ),
    ]
    for load in loads:
        load.start()

    has_above, has_below = z < chips - 1, z > 0
    barrier = pltpu.get_barrier_semaphore()
    for peer in (xn, yn, dg):
        pl.semaphore_signal(barrier, inc=1, device_id={"narrow": peer}, device_id_type=MESH)

    @pl.when(has_above)
    def _():
        pl.semaphore_signal(barrier, inc=1, device_id={"wide": above}, device_id_type=MESH)

    @pl.when(has_below)
    def _():
        pl.semaphore_signal(barrier, inc=1, device_id={"wide": below}, device_id_type=MESH)

    pl.semaphore_signal(barrier, inc=1, device_id={"wide": mate}, device_id_type=MESH)
    hidden = t_ref[...].astype(F32)
    own[...] = (hidden * row_scale(hidden) * g_ref[...]).astype(BF16)
    pl.semaphore_wait(barrier, 4 + has_above.astype(jnp.int32) + has_below.astype(jnp.int32))

    copies = Copies(send, recv)

    def part(owner, low):
        return x.at[pl.ds(pl.multiple_of(owner * rows + low, half), half)]

    upper, lower = own.at[pl.ds(0, half)], own.at[pl.ds(half, half)]
    xa = copies.go(upper, part(me, 0), 0, xn)
    yb = copies.go(lower, part(me, half), 1, yn)
    xb = copies.go(lower, part(me, half), 2, xn)
    ya = copies.go(upper, part(me, 0), 3, yn)

    def unit_rows(unit):
        return pl.ds(pl.multiple_of(owners[unit] * rows, rows), rows)

    def unit(block, k):
        return kv.at[block, unit_rows(k)]

    def to_above(s, k):
        block = jnp.maximum(w - 2 * s, 0)
        return wide_copy(unit(block, k), unit(block, k), z_send, z_recv, 4 * s + k, above)

    def from_below(s, k):
        block = jnp.maximum(w - 2 * s, 0)
        return wide_copy(unit(block, k), unit(block, k), z_send, z_recv, 4 * (s - 1) + k, above)

    def to_mate(s, k):
        block = jnp.maximum(w - 2 * s, 0)
        return wide_copy(unit(block, k), unit(block, k), m_send, m_recv, 4 * s + k, mate)

    def project(k):
        at = unit_rows(k)
        out = dot(x[at, :], weight[...])
        cosine, sine = cos_ref[at, :], sin_ref[at, :]
        qraw[at, :] = out[:, :q_width]
        kraw[at, :] = out[:, q_width : q_width + kv_width]
        for h in range(heads):
            lanes = slice(h * HD, (h + 1) * HD)
            q[at, lanes] = spin(out[:, lanes], qg_ref[...], cosine, sine).astype(BF16)
        for h in range(heads // group):
            lanes = slice(q_width + h * HD, q_width + (h + 1) * HD)
            kv[w, at, h * HD : (h + 1) * HD] = spin(
                out[:, lanes], kg_ref[...], cosine, sine
            ).astype(BF16)
        kv[w, at, kv_width:] = out[:, q_width + kv_width :].astype(BF16)

        @pl.when(has_above)
        def _():
            to_above(0, k).start()

        @pl.when(c == 0)
        def _():
            to_mate(0, k).start()

    def receive(s, k):
        @pl.when(z >= s)
        def _():
            from_below(s, k).wait_recv()
            if s < chips - 1:

                @pl.when(has_above)
                def _():
                    to_above(s, k).start()

            to_mate(s, k).start()

    x[unit_rows(0), :] = own[...]
    for load in loads:
        load.wait()
    project(0)
    xa.wait_recv()
    yf = copies.go(part(xn, 0), part(xn, 0), 4, yn)
    yb.wait_recv()
    xf = copies.go(part(yn, half), part(yn, half), 5, xn)
    receive(1, 0)
    xb.wait_recv()
    project(1)
    ya.wait_recv()
    project(2)
    receive(2, 0)
    receive(1, 1)
    receive(1, 2)
    receive(3, 0)
    yf.wait_recv()
    xf.wait_recv()
    project(3)
    away = Copies(c_send, c_recv)
    dy_part = dy_hbm.at[unit_rows(0)]
    for slot, peer in enumerate((dg, xn, yn)):
        away.go(c_ref, dy_part, slot, peer)
    stores = [
        pltpu.make_async_copy(src, dst, store_sem.at[n])
        for n, (src, dst) in enumerate(
            ((x, x_hbm), (q, q_hbm), (qraw, qraw_hbm), (kraw, kraw_hbm), (c_ref, dy_part))
        )
    ]
    for store in stores:
        store.start()
    acc[...] = jnp.zeros_like(acc)
    ones = jnp.ones((all_rows, HD), BF16)

    def keep(j):
        return pltpu.make_async_copy(kv.at[j], kv_hbm.at[j], kv_sem.at[j])

    def block(j, masked):
        for h in range(heads):
            head = h // group
            key = kv[j, :, head * HD : (head + 1) * HD]
            value = kv[j, :, kv_width + head * HD : kv_width + (head + 1) * HD]
            terms = jnp.exp2(dot_nt(q[:, h * HD : (h + 1) * HD], key) * (FACTOR * LOG2E))
            if masked:
                at = lax.broadcasted_iota(jnp.int32, (all_rows, all_rows), 0)
                key_at = lax.broadcasted_iota(jnp.int32, (all_rows, all_rows), 1)
                terms = jnp.where(key_at <= at, terms, 0.0)
            acc[h] += dot(terms.astype(BF16), jnp.concatenate([value, ones], axis=1))
        keep(j).start()

    block(w, True)

    @pl.loop(1 - c, 2 * z + 1)
    def _(i):
        for s, units in ((1, ((2, 1), (2, 2), (1, 3))), (2, ((3, 1), (3, 2), (2, 3))), (3, ((3, 3),))):

            @pl.when(i == 2 * s - 1)
            def _():
                for pair in units:
                    receive(*pair)

        for s in range(chips):

            @pl.when(i == 2 * s)
            def _():
                for k in range(4):
                    to_mate(s, k).wait_recv()

        odd = i % 2
        step = (i + 1) // 2
        block(2 * (z - step) + c + (1 - odd) * (1 - 2 * c), False)

    for h in range(heads):
        total = acc[h, :, HD:]
        out = acc[h, :, :HD] / total
        o_ref[:, h * HD : (h + 1) * HD] = out
        low_ref[:, h * HD : (h + 1) * HD] = out.astype(BF16)
        lse_ref[h : h + 1, :] = jnp.transpose(jnp.log2(total))[0:1]

    copies.finish()
    for copy in away.sent:
        copy.wait()
    for s in range(chips):
        for k in range(4):

            @pl.when((z >= s) & has_above)
            def _():
                to_above(s, k).wait_send()

            @pl.when((z >= s) & ((c == 0) | (s > 0)))
            def _():
                to_mate(s, k).wait_send()

    for store in stores:
        store.wait()

    @pl.loop(0, w + 1)
    def _(j):
        keep(j).wait()


def front(tokens, cotangent, gain_row, query_weight, keyvalue_weight, query_gain, key_gain, cosine, sine, count):
    rows = tokens.shape[0]
    all_rows = 4 * rows
    q_width, kv_width = query_weight.shape[1], keyvalue_weight.shape[2]
    heads, group = q_width // HD, q_width // kv_width
    chips = count // 2
    anywhere = pl.BlockSpec(memory_space=pl.ANY)
    return pl.pallas_call(
        functools.partial(front_kernel, count, heads, group),
        name="front",
        out_shape=(
            jax.ShapeDtypeStruct((all_rows, D), BF16),
            jax.ShapeDtypeStruct((all_rows, D), BF16),
            jax.ShapeDtypeStruct((all_rows, q_width), BF16),
            jax.ShapeDtypeStruct((all_rows, q_width), F32),
            jax.ShapeDtypeStruct((all_rows, kv_width), F32),
            jax.ShapeDtypeStruct((count, all_rows, 2 * kv_width), BF16),
            jax.ShapeDtypeStruct((all_rows, q_width), F32),
            jax.ShapeDtypeStruct((all_rows, q_width), BF16),
            jax.ShapeDtypeStruct((heads, all_rows), F32),
        ),
        in_specs=[VM, VM, VM, anywhere, anywhere, VM, VM, VM, VM],
        out_specs=(anywhere,) * 6 + (VM,) * 3,
        scratch_shapes=[
            pltpu.VMEM((rows, D), BF16),
            pltpu.VMEM((all_rows, D), BF16),
            pltpu.VMEM((D, q_width + 2 * kv_width), BF16),
            pltpu.VMEM((all_rows, q_width), BF16),
            pltpu.VMEM((all_rows, q_width), F32),
            pltpu.VMEM((all_rows, kv_width), F32),
            pltpu.VMEM((count, all_rows, 2 * kv_width), BF16),
            pltpu.VMEM((heads, all_rows, 2 * HD), F32),
        ]
        + dma_sems(6)
        + dma_sems(4 * chips)
        + dma_sems(4 * chips)
        + dma_sems(3)
        + [
            pltpu.SemaphoreType.DMA((3,)),
            pltpu.SemaphoreType.DMA((5,)),
            pltpu.SemaphoreType.DMA((count,)),
        ],
        cost_estimate=cost(1, 1),
        compiler_params=remote_params(8),
    )(tokens, cotangent, gain_row, query_weight, keyvalue_weight, query_gain, key_gain, cosine, sine)


def feed_kernel(x_ref, dy_ref, w_ref, d_ref, act_ref, grad_ref, down_ref):
    x, dy = x_ref[...], dy_ref[...]
    gate = dot(x, w_ref[0])
    upper = dot(x, w_ref[1])
    act_grad = dot_nt(dy, d_ref[...])
    sig = jax.nn.sigmoid(gate)
    swish = gate * sig
    act = (swish * upper).astype(BF16)
    act_ref[...] = act
    grad_ref[0] = (act_grad * upper * sig * (1.0 + gate * (1.0 - sig))).astype(BF16)
    grad_ref[1] = (act_grad * swish).astype(BF16)
    down_ref[...] = dot_tn(act, dy).astype(BF16)


def feed(x, dy, gateup_weight, down_weight):
    rows, width = x.shape[0], down_weight.shape[0]
    tile = 256
    whole = lambda i: (0, 0)
    return pl.pallas_call(
        feed_kernel,
        name="feed",
        grid=(width // tile,),
        out_shape=(
            jax.ShapeDtypeStruct((rows, width), BF16),
            jax.ShapeDtypeStruct((2, rows, width), BF16),
            jax.ShapeDtypeStruct((width, D), BF16),
        ),
        in_specs=[
            pl.BlockSpec((rows, D), whole),
            pl.BlockSpec((rows, D), whole),
            pl.BlockSpec((2, D, tile), lambda i: (0, 0, i)),
            pl.BlockSpec((tile, D), lambda i: (i, 0)),
        ],
        out_specs=(
            pl.BlockSpec((rows, tile), lambda i: (0, i)),
            pl.BlockSpec((2, rows, tile), lambda i: (0, 0, i)),
            pl.BlockSpec((tile, D), lambda i: (i, 0)),
        ),
        compiler_params=params("arbitrary"),
        cost_estimate=cost(8 * rows * D * width, 4 * rows * D + 8 * D * width),
    )(x, dy, gateup_weight, down_weight)


def feed_back_kernel(x_ref, act_ref, grad_ref, w_ref, d_ref, full_ref, in_ref, out_ref, in_acc, out_acc):
    step = pl.program_id(0)

    @pl.when(step == 0)
    def _():
        in_acc[...] = jnp.zeros_like(in_acc)
        out_acc[...] = jnp.zeros_like(out_acc)

    in_acc[...] += dot_nt(grad_ref[0], w_ref[0]) + dot_nt(grad_ref[1], w_ref[1])
    out_acc[...] += dot(act_ref[...], d_ref[...])
    x = x_ref[...]
    full_ref[0] = dot_tn(x, grad_ref[0]).astype(BF16)
    full_ref[1] = dot_tn(x, grad_ref[1]).astype(BF16)

    @pl.when(step == pl.num_programs(0) - 1)
    def _():
        in_ref[...] = in_acc[...].astype(BF16)
        out_ref[...] = out_acc[...].astype(BF16)


def feed_back(x, act, grads, gateup_weight, down_weight):
    rows, width = x.shape[0], down_weight.shape[0]
    tile = 256
    whole = lambda i: (0, 0)
    return pl.pallas_call(
        feed_back_kernel,
        name="feed_back",
        grid=(width // tile,),
        out_shape=(
            jax.ShapeDtypeStruct((2, D, width), BF16),
            jax.ShapeDtypeStruct((rows, D), BF16),
            jax.ShapeDtypeStruct((rows, D), BF16),
        ),
        in_specs=[
            pl.BlockSpec((rows, D), whole),
            pl.BlockSpec((rows, tile), lambda i: (0, i)),
            pl.BlockSpec((2, rows, tile), lambda i: (0, 0, i)),
            pl.BlockSpec((2, D, tile), lambda i: (0, 0, i)),
            pl.BlockSpec((tile, D), lambda i: (i, 0)),
        ],
        out_specs=(
            pl.BlockSpec((2, D, tile), lambda i: (0, 0, i)),
            pl.BlockSpec((rows, D), whole),
            pl.BlockSpec((rows, D), whole),
        ),
        scratch_shapes=[pltpu.VMEM((rows, D), F32), pltpu.VMEM((rows, D), F32)],
        compiler_params=params("arbitrary"),
        cost_estimate=cost(10 * rows * D * width, 8 * rows * D + 10 * D * width),
    )(x, act, grads, gateup_weight, down_weight)


def out_back_kernel(dy_ref, w_ref, low_ref, grad_ref, full_ref):
    dy = dy_ref[...]
    grad_ref[...] = dot_nt(dy, w_ref[...]).astype(BF16)
    full_ref[...] = dot_tn(dy, low_ref[...]).astype(BF16)


def out_back(dy, weight, attn_low):
    rows, width = attn_low.shape
    tile = 256
    whole = lambda i: (0, 0)
    return pl.pallas_call(
        out_back_kernel,
        name="out_back",
        grid=(width // tile,),
        out_shape=(
            jax.ShapeDtypeStruct((rows, width), BF16),
            jax.ShapeDtypeStruct((D, width), BF16),
        ),
        in_specs=[
            pl.BlockSpec((rows, D), whole),
            pl.BlockSpec((tile, D), lambda i: (i, 0)),
            pl.BlockSpec((rows, tile), lambda i: (0, i)),
        ],
        out_specs=(
            pl.BlockSpec((rows, tile), lambda i: (0, i)),
            pl.BlockSpec((D, tile), lambda i: (0, i)),
        ),
        compiler_params=params("arbitrary"),
        cost_estimate=cost(4 * rows * D * width, 2 * rows * D + 4 * D * width),
    )(dy, weight, attn_low)


def project_back_kernel(x_ref, q_ref, kv_ref, wq_ref, wkv_ref, out_ref, in_ref, full_ref):
    q_width, kv_width = wq_ref.shape[1], wkv_ref.shape[2]
    x = x_ref[...]
    key, value = kv_ref[:, :kv_width], kv_ref[:, kv_width:]
    in_ref[...] = (
        dot_nt(q_ref[...], wq_ref[...]) + dot_nt(key, wkv_ref[0]) + dot_nt(value, wkv_ref[1])
    ).astype(BF16)
    full_ref[:, :q_width] = dot_tn(x, q_ref[...]).astype(BF16)
    full_ref[:, q_width : q_width + 2 * kv_width] = dot_tn(x, kv_ref[...]).astype(BF16)
    full_ref[:, q_width + 2 * kv_width :] = out_ref[...]


def project_back(x, q_back, kv_back, query_weight, keyvalue_weight, output_full):
    rows, out_width = x.shape[0], output_full.shape[1]
    q_width, kv_width = query_weight.shape[1], keyvalue_weight.shape[2]
    tile = 512
    whole = lambda i: (0, 0)
    return pl.pallas_call(
        project_back_kernel,
        name="project_back",
        grid=(D // tile,),
        out_shape=(
            jax.ShapeDtypeStruct((rows, D), BF16),
            jax.ShapeDtypeStruct((D, q_width + 2 * kv_width + out_width), BF16),
        ),
        in_specs=[
            pl.BlockSpec((rows, tile), lambda i: (0, i)),
            pl.BlockSpec((rows, q_width), whole),
            pl.BlockSpec((rows, 2 * kv_width), whole),
            pl.BlockSpec((tile, q_width), lambda i: (i, 0)),
            pl.BlockSpec((2, tile, kv_width), lambda i: (0, i, 0)),
            pl.BlockSpec((tile, out_width), lambda i: (i, 0)),
        ],
        out_specs=(
            pl.BlockSpec((rows, tile), lambda i: (0, i)),
            pl.BlockSpec((tile, q_width + 2 * kv_width + out_width), lambda i: (i, 0)),
        ),
        compiler_params=params("arbitrary"),
        cost_estimate=cost(4 * rows * D * (q_width + 2 * kv_width), 6 * D * (q_width + 2 * kv_width)),
    )(x, q_back, kv_back, query_weight, keyvalue_weight, output_full)


def mate_of():
    w = lax.axis_index("wide")
    c = w % 2
    return c, w + 1 - 2 * c


def greet_mate():
    _, mate = mate_of()
    barrier = pltpu.get_barrier_semaphore()
    pl.semaphore_signal(barrier, inc=1, device_id={"wide": mate}, device_id_type=MESH)
    pl.semaphore_wait(barrier, 1)


def project_back_pair_kernel(
    x_ref, q_ref, kv_ref, wq_ref, wkv_ref, out_ref, in_ref, full_ref, stage, inbox, send, recv
):
    step, steps = pl.program_id(0), pl.num_programs(0) - 1
    c, mate = mate_of()
    q_width, kv_width = wq_ref.shape[1], wkv_ref.shape[2]
    part = full_ref.shape[1]

    def trade(i):
        return wide_copy(stage.at[i % 2, 1 - c], inbox.at[i], send, recv, i, mate)

    @pl.when(step == 0)
    def _():
        greet_mate()

    @pl.when((step >= 2) & (step <= steps))
    def _():
        trade(step - 2).wait_send()

    @pl.when(step < steps)
    def _():
        x = x_ref[...]
        q_full = dot_tn(x, q_ref[...]).astype(BF16)
        kv_full = dot_tn(x, kv_ref[...]).astype(BF16)
        for k in range(2):
            at = slice(k * part, (k + 1) * part)
            stage[step % 2, k, :, :q_width] = q_full[at]
            stage[step % 2, k, :, q_width : q_width + 2 * kv_width] = kv_full[at]
            stage[step % 2, k, :, q_width + 2 * kv_width :] = out_ref[at, :]
        trade(step).start()
        key, value = kv_ref[:, :kv_width], kv_ref[:, kv_width:]
        in_ref[...] = (
            dot_nt(q_ref[...], wq_ref[...]) + dot_nt(key, wkv_ref[0]) + dot_nt(value, wkv_ref[1])
        ).astype(BF16)

    @pl.when(step > 0)
    def _():
        last = jnp.maximum(step - 1, 0)
        trade(last).wait_recv()
        full_ref[0] = (stage[last % 2, c].astype(F32) + inbox[last].astype(F32)).astype(BF16)

    @pl.when(step == steps)
    def _():
        trade(step - 1).wait_send()


def project_back_pair(x, q_back, kv_back, query_weight, keyvalue_weight, output_full, count):
    rows, out_width = x.shape[0], output_full.shape[1]
    q_width, kv_width = query_weight.shape[1], keyvalue_weight.shape[2]
    width = q_width + 2 * kv_width + out_width
    part = D // count
    tile = 2 * part
    steps = count // 2
    whole = lambda i: (0, 0)
    now = lambda i: jnp.minimum(i, steps - 1)
    in_partial, full = pl.pallas_call(
        project_back_pair_kernel,
        name="project_back_pair",
        grid=(steps + 1,),
        out_shape=(
            jax.ShapeDtypeStruct((rows, D), BF16),
            jax.ShapeDtypeStruct((steps, part, width), BF16),
        ),
        in_specs=[
            pl.BlockSpec((rows, tile), lambda i: (0, now(i))),
            pl.BlockSpec((rows, q_width), whole),
            pl.BlockSpec((rows, 2 * kv_width), whole),
            pl.BlockSpec((tile, q_width), lambda i: (now(i), 0)),
            pl.BlockSpec((2, tile, kv_width), lambda i: (0, now(i), 0)),
            pl.BlockSpec((tile, out_width), lambda i: (now(i), 0)),
        ],
        out_specs=(
            pl.BlockSpec((rows, tile), lambda i: (0, now(i))),
            pl.BlockSpec((1, part, width), lambda i: (jnp.maximum(i - 1, 0), 0, 0)),
        ),
        scratch_shapes=[
            pltpu.VMEM((2, 2, part, width), BF16),
            pltpu.VMEM((steps, part, width), BF16),
        ]
        + dma_sems(steps),
        cost_estimate=cost(1, 1),
        compiler_params=remote_params(12),
    )(x, q_back, kv_back, query_weight, keyvalue_weight, output_full)
    return in_partial, full.reshape(D // 2, width)


def rest_adamw_kernel(total_ref, *refs):
    q_width, kv_width = refs[0].shape[1], refs[4].shape[2]
    ins, outs = refs[:12], refs[12:]
    total = total_ref[...].astype(F32)
    rate = 2.0 * D ** (-0.5)
    for n, new in enumerate(
        adamw(total[:, :q_width], *[r[...] for r in ins[:4]], rate, WEIGHT_DECAY)
    ):
        outs[n][...] = new
    for k in range(2):
        low = q_width + k * kv_width
        for n, new in enumerate(
            adamw(total[:, low : low + kv_width], *[r[k] for r in ins[4:8]], rate, WEIGHT_DECAY)
        ):
            outs[5 + n][k] = new
    turned = jnp.transpose(total[:, q_width + 2 * kv_width :])
    for n, new in enumerate(
        adamw(turned, *[r[...] for r in ins[8:]], 2.0 * WO_FAN ** (-0.5), WEIGHT_DECAY)
    ):
        outs[10 + n][...] = new


def rest_adamw(total, query_state, keyvalue_state, output_state):
    tile = 128
    rows, width = total.shape
    q_spec = pl.BlockSpec((tile, query_state[0].shape[1]), lambda i: (i, 0))
    kv_spec = pl.BlockSpec((2, tile, keyvalue_state[0].shape[2]), lambda i: (0, i, 0))
    o_spec = pl.BlockSpec((output_state[0].shape[0], tile), lambda i: (0, i))
    like = lambda a: jax.ShapeDtypeStruct(a.shape, F32)
    out = pl.pallas_call(
        rest_adamw_kernel,
        name="rest_adamw",
        grid=(rows // tile,),
        out_shape=tuple(
            like(state[0]) for state in (query_state, keyvalue_state, output_state) for _ in range(5)
        ),
        in_specs=[pl.BlockSpec((tile, width), lambda i: (i, 0))]
        + [q_spec] * 4
        + [kv_spec] * 4
        + [o_spec] * 4,
        out_specs=tuple([q_spec] * 5 + [kv_spec] * 5 + [o_spec] * 5),
        compiler_params=params("arbitrary"),
        cost_estimate=cost(1, 1),
    )(total, *query_state, *keyvalue_state, *output_state)
    return out[:5], out[5:10], out[10:]


def wide_scatter(partial, axis):
    return lax.psum_scatter(partial, "wide", scatter_dimension=axis, tiled=True)


def line_scatter(partial, axis, count):
    groups = [[2 * z + c for z in range(count // 2)] for c in range(2)]
    return lax.psum_scatter(
        partial, "wide", scatter_dimension=axis, tiled=True, axis_index_groups=groups
    )


def body(
    tokens,
    cotangent,
    gain_copy,
    query_weight,
    keyvalue_weight,
    output_weight,
    gateup_weight,
    down_weight,
    query_master,
    query_moment,
    query_second,
    query_average,
    keyvalue_master,
    keyvalue_moment,
    keyvalue_second,
    keyvalue_average,
    output_master,
    output_moment,
    output_second,
    output_average,
    gateup_master,
    gateup_moment,
    gateup_second,
    gateup_average,
    down_master,
    down_moment,
    down_second,
    down_average,
    gain_master,
    gain_moment,
    gain_second,
    gain_average,
):
    narrow, wide = lax.axis_size("narrow"), lax.axis_size("wide")
    special = narrow == 4 and wide == 8
    stretch_rows = tokens.shape[0] * narrow
    wide_index = lax.axis_index("wide")
    w_scalar = wide_index.astype(jnp.int32).reshape(1)
    kv_heads = keyvalue_weight.shape[2] // HD
    q_heads = query_weight.shape[1] // HD
    group = q_heads // kv_heads
    q_width, kv_width = q_heads * HD, kv_heads * HD
    attn_gain = gain_copy[:D].reshape(1, D)
    mlp_gain = gain_copy[D : 2 * D].reshape(1, D)
    query_gain = gain_copy[2 * D : 2 * D + HD].reshape(1, HD)
    key_gain = gain_copy[2 * D + HD :].reshape(1, HD)

    positions = (wide_index * stretch_rows + jnp.arange(stretch_rows, dtype=jnp.int32)).astype(F32)
    cosine, sine = rope_tables(positions)
    if special:
        back_mlp, attn_input, query_low, query_raw, key_raw, kv_all, attn_out, attn_low, lse = front(
            tokens,
            cotangent,
            attn_gain,
            query_weight,
            keyvalue_weight,
            query_gain,
            key_gain,
            cosine,
            sine,
            wide,
        )
    else:
        hidden = tokens.astype(F32)
        normed = (hidden * row_scale(hidden) * attn_gain).astype(BF16)
        attn_input = lax.all_gather(normed, "narrow", axis=0, tiled=True)
        kv_low, key_raw = keys_values(attn_input, keyvalue_weight, key_gain, cosine, sine)
        query_low, query_raw = queries(attn_input, query_weight, query_gain, cosine, sine)
        kv_all = lax.all_gather(kv_low, "wide", axis=0)
        attn_out, attn_low, lse = attend(w_scalar, query_low, kv_all, q_heads, group)
        back_mlp = lax.all_gather(cotangent, "narrow", axis=0, tiled=True)
    if special:
        hidden_mid, mlp_input, act_grads, act, down_full = mid_pair(
            attn_low, output_weight, tokens, mlp_gain, back_mlp, gateup_weight, down_weight, wide
        )
        down_total = line_scatter(down_full, 0, wide)[0]
        mid_grad, back_attn, mlp_gain_grad, gateup_full = mid_backward_pair(
            hidden_mid, cotangent, mlp_gain, mlp_input, act_grads, gateup_weight, wide
        )
        gateup_total = line_scatter(gateup_full, 1, wide)
    else:
        hidden_mid, mlp_input = mid_forward(attn_low, output_weight, tokens, mlp_gain)
        act, act_grads, down_full = feed(mlp_input, back_mlp, gateup_weight, down_weight)
        down_total = wide_scatter(down_full, 1)
        gateup_full, in_partial, out_partial = feed_back(
            mlp_input, act, act_grads, gateup_weight, down_weight
        )
        gateup_total = wide_scatter(gateup_full, 1)
        mid_grad, back_attn, mlp_gain_grad = mid_backward(
            in_partial, hidden_mid, cotangent, mlp_gain
        )
    attn_grad, output_full = out_back(back_attn, output_weight, attn_low)
    query_sum, kv_sums = attend_back(
        w_scalar, query_low, kv_all, attn_grad, attn_out, lse, q_heads, group
    )
    query_back, query_gain_grad = unspin(query_sum, query_raw, query_gain, cosine, sine)
    if special:
        kv_sum, block_output = return_grads_out(kv_sums, act, down_weight, hidden_mid, wide)
    else:
        kv_sum = return_grads(kv_sums, wide)
        block_output = hidden_mid + lax.psum_scatter(
            out_partial, "narrow", scatter_dimension=0, tiled=True
        ).astype(F32)
    kv_back, key_gain_grad = unspin(kv_sum, key_raw, key_gain, cosine, sine)
    back_args = (attn_input, query_back, kv_back, query_weight, keyvalue_weight, output_full)
    if special:
        normed_partial, project_full = project_back_pair(*back_args, wide)
    else:
        normed_partial, project_full = project_back(*back_args)
    project_full, gateup_total, down_total, normed_partial = lax.optimization_barrier(
        (project_full, gateup_total, down_total, normed_partial)
    )
    rest_total = line_scatter(project_full, 0, wide) if special else wide_scatter(project_full, 0)
    input_grad, attn_gain_grad = in_scatter(normed_partial, tokens, mid_grad, attn_gain, special)
    gain_partial = jnp.concatenate(
        [attn_gain_grad, mlp_gain_grad, query_gain_grad, key_gain_grad], axis=1
    ).reshape(-1)
    gain_total = gain_sums(gain_partial, wide, narrow, special)

    query_new, keyvalue_new, output_new = rest_adamw(
        rest_total,
        (query_master, query_moment, query_second, query_average),
        (keyvalue_master, keyvalue_moment, keyvalue_second, keyvalue_average),
        (output_master, output_moment, output_second, output_average),
    )
    gateup_new = adamw(
        gateup_total.astype(F32),
        gateup_master,
        gateup_moment,
        gateup_second,
        gateup_average,
        2.0 * D ** (-0.5),
        WEIGHT_DECAY,
    )
    down_new = adamw(
        down_total.astype(F32),
        down_master,
        down_moment,
        down_second,
        down_average,
        2.0 * FF ** (-0.5),
        WEIGHT_DECAY,
    )
    gain_new = adamw(
        gain_total, gain_master, gain_moment, gain_second, gain_average, RATE_GAIN, 0.0
    )
    return (
        block_output,
        input_grad,
        *query_new,
        *keyvalue_new,
        *output_new,
        *gateup_new,
        *down_new,
        *gain_new,
    )


def solution(mesh):
    rows = P(("wide", "narrow"), None)
    flat = P(("wide", "narrow"))
    stacked = P(None, "wide", "narrow")
    query, output = P("wide", "narrow"), P("narrow", "wide")
    states = (
        *[query] * 4,
        *[stacked] * 4,
        *[output] * 4,
        *[stacked] * 4,
        *[output] * 4,
        *[flat] * 4,
    )
    return jax.shard_map(
        body,
        mesh=mesh,
        in_specs=(
            rows,
            rows,
            P(),
            P(None, "narrow"),
            P(None, None, "narrow"),
            P("narrow", None),
            P(None, None, "narrow"),
            P("narrow", None),
            *states,
        ),
        out_specs=(
            rows,
            rows,
            *[query] * 5,
            *[stacked] * 5,
            *[output] * 5,
            *[stacked] * 5,
            *[output] * 5,
            *[flat] * 5,
        ),
        check_vma=False,
    )
```

```python
import functools

import jax
import jax.numpy as jnp
import numpy as np
from jax import lax
from jax.experimental import pallas as pl
from jax.experimental.pallas import tpu as pltpu
from jax.sharding import PartitionSpec as P

D = 2048
HD = 128
FF = 6144
STEP = 10
WO_FAN = 32

EPSILON = 1e-06
THETA = 1000000.0
BETA_ONE = 0.9
BETA_TWO = 0.999
ADAM_EPS = 1e-08
WEIGHT_DECAY = 0.1
EMA_KEEP = 0.5
RATE_GAIN = 0.4
FACTOR = HD ** (-0.5)
LOG2E = 1.4426950408889634

F32 = jnp.float32
BF16 = jnp.bfloat16
MESH = pl.DeviceIdType.MESH
VM = pl.BlockSpec(memory_space=pltpu.VMEM)
SM = pl.BlockSpec(memory_space=pltpu.SMEM)
VMEM_LIMIT = 60 << 20

NT = (((1,), (1,)), ((), ()))
TN = (((0,), (0,)), ((), ()))


def dot(left, right):
    return jnp.dot(left, right, preferred_element_type=F32)


def dot_nt(left, right):
    return lax.dot_general(left, right, NT, preferred_element_type=F32)


def dot_tn(left, right):
    return lax.dot_general(left, right, TN, preferred_element_type=F32)


def rope_tables(positions):
    half_width = HD // 2
    inverse_freq = jnp.asarray(
        THETA ** (-2.0 * np.arange(half_width, dtype=np.float64) / HD), dtype=F32
    )
    angles = positions[:, None] * inverse_freq[None, :]
    cosine, sine = jnp.cos(angles), jnp.sin(angles)
    return (
        jnp.concatenate([cosine, cosine], axis=-1),
        jnp.concatenate([-sine, sine], axis=-1),
    )


def adamw(gradient, master, moment, second, average, step_rate, decay_rate):
    moment_new = BETA_ONE * moment + (1.0 - BETA_ONE) * gradient
    second_new = BETA_TWO * second + (1.0 - BETA_TWO) * gradient * gradient
    moment_hat = moment_new / (1.0 - BETA_ONE**STEP)
    second_hat = second_new / (1.0 - BETA_TWO**STEP)
    master_new = master - step_rate * (
        moment_hat / (jnp.sqrt(second_hat) + ADAM_EPS) + decay_rate * master
    )
    average_new = EMA_KEEP * average + (1.0 - EMA_KEEP) * master_new
    return (gradient, master_new, moment_new, second_new, average_new)


def row_scale(values_in):
    return lax.rsqrt(jnp.mean(values_in * values_in, axis=-1, keepdims=True) + EPSILON)


def gain_row(g_ref, base):
    return jnp.concatenate([g_ref[base + j : base + j + 1, :] for j in range(D // HD)], axis=1)


def norm_back(gradient, unit_rows, inv_scale, gain):
    scaled = gradient * gain
    inner = scaled - unit_rows * jnp.mean(scaled * unit_rows, axis=-1, keepdims=True)
    return inv_scale * inner, jnp.sum(gradient * unit_rows, axis=0, keepdims=True)


def square():
    me = lax.axis_index("narrow")
    xn = me + 1 - 2 * (me % 2)
    yn = (me + 2) % 4
    dg = (xn + 2) % 4
    return me, xn, yn, dg


def greet(axis, peers):
    barrier = pltpu.get_barrier_semaphore()
    for peer in peers:
        pl.semaphore_signal(barrier, inc=1, device_id={axis: peer}, device_id_type=MESH)
    pl.semaphore_wait(barrier, len(peers))


class Copies:
    def __init__(self, send, recv):
        self.send, self.recv, self.sent = send, recv, []

    def make(self, src, dst, slot, peer):
        copy = pltpu.make_async_remote_copy(
            src_ref=src,
            dst_ref=dst,
            send_sem=self.send.at[slot],
            recv_sem=self.recv.at[slot],
            device_id={"narrow": peer},
            device_id_type=MESH,
        )
        self.sent.append(copy)
        return copy

    def go(self, src, dst, slot, peer):
        copy = self.make(src, dst, slot, peer)
        copy.start()
        return copy

    def finish(self):
        for copy in self.sent:
            copy.wait_send()


def scatter_square(copies, slot, p_ref, buf, stage, emit, fill=None, early=None, middle=None):
    me, xn, yn, dg = square()
    rows = p_ref.shape[0] // 4
    half = rows // 2

    def part(owner, low):
        return p_ref.at[pl.ds(pl.multiple_of(owner * rows + low, half), half)]

    c0 = copies.make(part(dg, 0), buf.at[0], slot, xn)
    c1 = copies.make(part(dg, half), buf.at[1], slot + 1, yn)
    c2 = copies.make(part(xn, 0), buf.at[2], slot + 2, xn)
    c3 = copies.make(part(yn, half), buf.at[3], slot + 3, yn)
    if fill is None:
        for copy in (c0, c1, c2, c3):
            copy.start()
    else:

        @pl.loop(0, 4)
        def _(k):
            fill(jnp.where(k == 0, dg, jnp.where(k == 1, xn, jnp.where(k == 2, yn, me))))
            for n, ready in ((0, (c0, c1)), (1, (c2,)), (2, (c3,))):

                @pl.when(k == n)
                def _():
                    for copy in ready:
                        copy.start()

    if early is not None:
        early()
    c0.wait_recv()
    stage[0] = (part(yn, 0)[...].astype(F32) + buf[0].astype(F32)).astype(BF16)
    c4 = copies.go(stage.at[0], buf.at[4], slot + 4, yn)
    c1.wait_recv()
    stage[1] = (part(xn, half)[...].astype(F32) + buf[1].astype(F32)).astype(BF16)
    c5 = copies.go(stage.at[1], buf.at[5], slot + 5, xn)
    if middle is not None:
        middle()
    c2.wait_recv()
    c4.wait_recv()
    emit(0, part(me, 0)[...].astype(F32) + buf[2].astype(F32) + buf[4].astype(F32))
    c3.wait_recv()
    c5.wait_recv()
    emit(half, part(me, half)[...].astype(F32) + buf[3].astype(F32) + buf[5].astype(F32))


def exchange_square(copies, p_ref, buf, stage, own, o_ref, emit, fill, early, middle, use=None, relay=None):
    me, xn, yn, dg = square()
    rows = p_ref.shape[0] // 4
    group, piece = rows // 2, rows // 4

    def at(ref, owner, g, h):
        return ref.at[pl.ds(pl.multiple_of(owner * rows + g * group + h * piece, piece), piece)]

    def mine(g, h):
        return own.at[pl.ds(g * group + h * piece, piece)]

    sums, firsts, relays = [], [], []
    for g in range(2):
        s, t = 6 * g, 12 + 6 * g
        sums.append(
            (
                copies.make(at(p_ref, dg, g, 0), buf.at[g, 0], s, xn),
                copies.make(at(p_ref, dg, g, 1), buf.at[g, 1], s + 1, yn),
                copies.make(at(p_ref, xn, g, 0), buf.at[g, 2], s + 2, xn),
                copies.make(at(p_ref, yn, g, 1), buf.at[g, 3], s + 3, yn),
                copies.make(stage.at[g, 0], buf.at[g, 4], s + 4, yn),
                copies.make(stage.at[g, 1], buf.at[g, 5], s + 5, xn),
            )
        )
        firsts.append(
            (
                copies.make(mine(g, 0), at(o_ref, me, g, 0), t, xn),
                copies.make(mine(g, 1), at(o_ref, me, g, 1), t + 1, yn),
                copies.make(mine(g, 1), at(o_ref, me, g, 1), t + 2, xn),
                copies.make(mine(g, 0), at(o_ref, me, g, 0), t + 3, yn),
            )
        )
        relays.append(
            (
                copies.make(at(o_ref, xn, g, 0), at(o_ref, xn, g, 0), t + 4, yn),
                copies.make(at(o_ref, yn, g, 1), at(o_ref, yn, g, 1), t + 5, xn),
            )
        )

    def merge(g):
        for h, other in ((0, yn), (1, xn)):
            sums[g][h].wait_recv()
            stage[g, h] = (at(p_ref, other, g, h)[...].astype(F32) + buf[g, h].astype(F32)).astype(
                BF16
            )
            sums[g][4 + h].start()

    def close(g):
        for h in range(2):
            sums[g][2 + h].wait_recv()
            sums[g][4 + h].wait_recv()
            emit(
                g * group + h * piece,
                piece,
                at(p_ref, me, g, h)[...].astype(F32)
                + buf[g, 2 + h].astype(F32)
                + buf[g, 4 + h].astype(F32),
            )
        for copy in firsts[g]:
            copy.start()

    @pl.loop(0, 4)
    def _(k):
        fill(jnp.where(k == 0, dg, jnp.where(k == 1, xn, jnp.where(k == 2, yn, me))))
        for n, ready in ((0, sums[0][:2]), (1, sums[0][2:3]), (2, sums[0][3:4])):

            @pl.when(k == n)
            def _():
                for copy in ready:
                    copy.start()

    merge(0)
    for copy in sums[1][:4]:
        copy.start()
    early()
    merge(1)
    close(0)
    middle()
    close(1)
    o_ref[pl.ds(pl.multiple_of(me * rows, rows), rows)] = own[...]

    def pass_on():
        for g in range(2):
            for h in range(2):
                firsts[g][h].wait_recv()
                relays[g][h].start()
        if relay is not None:
            relay()
        for g in range(2):
            firsts[g][2].wait_recv()

    def from_y():
        for g in range(2):
            firsts[g][3].wait_recv()

    def from_far():
        for g in range(2):
            for copy in relays[g]:
                copy.wait_recv()

    if use is None:
        pass_on()
        from_y()
        from_far()
        return

    @pl.loop(0, 4)
    def _(k):
        pl.when(k == 1)(pass_on)
        pl.when(k == 2)(from_y)
        pl.when(k == 3)(from_far)
        use(jnp.where(k == 0, me, jnp.where(k == 1, xn, jnp.where(k == 2, yn, dg))))


def exchange_space(rows):
    return [pltpu.VMEM((2, 6, rows // 4, D), BF16), pltpu.VMEM((2, 2, rows // 4, D), BF16)]


def dma_sems(count):
    return [pltpu.SemaphoreType.DMA((count,)), pltpu.SemaphoreType.DMA((count,))]


def scatter_space(rows):
    return [pltpu.VMEM((6, rows // 2, D), BF16), pltpu.VMEM((2, rows // 2, D), BF16)]


def remote_params(collective_id):
    return pltpu.CompilerParams(
        collective_id=collective_id, has_side_effects=True, vmem_limit_bytes=VMEM_LIMIT
    )


def mid_kernel(
    a_ref, w_ref, t_ref, g_ref, dy_hbm, gu_hbm, d_hbm,
    h_ref, x_hbm, grad_hbm, act_hbm, down_hbm,
    p_ref, buf, stage, own, x, weight, dy, down, act_grad, grad, act, mine, inbox,
    send, recv, m_send, m_recv, load_sem, store_sem, down_sem,
):
    me, xn, yn, dg = square()
    c, mate = mate_of()
    rows = t_ref.shape[0]
    half = rows // 2
    tiles, tile, part = inbox.shape[0], inbox.shape[2], inbox.shape[3]
    loads = [
        pltpu.make_async_copy(src, dst, load_sem.at[n])
        for n, (src, dst) in enumerate(((dy_hbm, dy), (d_hbm, down), (gu_hbm, weight)))
    ]
    for load in loads:
        load.start()
    barrier = pltpu.get_barrier_semaphore()
    for peer in (xn, yn):
        pl.semaphore_signal(barrier, inc=1, device_id={"narrow": peer}, device_id_type=MESH)
    pl.semaphore_signal(barrier, inc=1, device_id={"wide": mate}, device_id_type=MESH)
    pl.semaphore_wait(barrier, 3)
    copies = Copies(send, recv)

    def rows_of(owner):
        return pl.ds(pl.multiple_of(owner * rows, rows), rows)

    def fill(owner):
        p_ref[rows_of(owner), :] = dot(a_ref[rows_of(owner), :], w_ref[...]).astype(BF16)

    gain = gain_row(g_ref, D // HD)

    def emit(low, size, total):
        hidden = t_ref[pl.ds(low, size)].astype(F32) + total
        h_ref[pl.ds(low, size)] = hidden
        own[pl.ds(low, size)] = (hidden * row_scale(hidden) * gain).astype(BF16)

    def act_grads(low, high):
        @pl.loop(low, high)
        def _(t):
            cols = pl.ds(pl.multiple_of(t * tile, tile), tile)
            act_grad[:, cols] = dot_nt(dy[...], down[cols, :])

    def early():
        loads[0].wait()
        loads[1].wait()
        act_grads(0, tiles // 2)

    def middle():
        act_grads(tiles // 2, tiles)
        loads[2].wait()

    def expand(owner):
        at = rows_of(owner)

        @pl.loop(0, tiles)
        def _(t):
            cols = pl.ds(pl.multiple_of(t * tile, tile), tile)
            gate = dot(x[at, :], weight[0, :, cols])
            upper = dot(x[at, :], weight[1, :, cols])
            sig = jax.nn.sigmoid(gate)
            swish = gate * sig
            back = act_grad[at, cols]
            act[at, cols] = (swish * upper).astype(BF16)
            grad[0, at, cols] = (back * upper * sig * (1.0 + gate * (1.0 - sig))).astype(BF16)
            grad[1, at, cols] = (back * swish).astype(BF16)

    exchange_square(copies, p_ref, buf, stage, own, x, emit, fill, early, middle, expand)
    stores = [
        pltpu.make_async_copy(src, dst, store_sem.at[n])
        for n, (src, dst) in enumerate(((x, x_hbm), (grad, grad_hbm), (act, act_hbm)))
    ]
    for store in stores:
        store.start()

    def trade(t):
        return wide_copy(mine.at[t, 1 - c], inbox.at[t], m_send, m_recv, t, mate)

    def keep(t):
        at = pl.ds(pl.multiple_of(t * tile, tile), tile)
        return pltpu.make_async_copy(mine.at[t, c], down_hbm.at[:, at], down_sem.at[t])

    @pl.loop(0, tiles)
    def _(t):
        cols = pl.ds(pl.multiple_of(t * tile, tile), tile)
        full = dot_tn(act[:, cols], dy[...]).astype(BF16)
        for k in range(D // part):
            mine[t, k % 2, k // 2] = full[:, k * part : (k + 1) * part]
        trade(t).start()

    @pl.loop(0, tiles)
    def _(t):
        trade(t).wait_recv()
        mine[t, c] = (mine[t, c].astype(F32) + inbox[t].astype(F32)).astype(BF16)
        keep(t).start()

    copies.finish()

    @pl.loop(0, tiles)
    def _(t):
        trade(t).wait_send()
        keep(t).wait()

    for store in stores:
        store.wait()


def mid_pair(attn_low, weight, tokens, gains, dy, gateup_weight, down_weight, count):
    rows = tokens.shape[0]
    width = gateup_weight.shape[2]
    tile, part, chips = 256, D // count, count // 2
    tiles = width // tile
    anywhere = pl.BlockSpec(memory_space=pl.ANY)
    return pl.pallas_call(
        mid_kernel,
        name="mid_pair",
        out_shape=(
            jax.ShapeDtypeStruct((rows, D), F32),
            jax.ShapeDtypeStruct((4 * rows, D), BF16),
            jax.ShapeDtypeStruct((2, 4 * rows, width), BF16),
            jax.ShapeDtypeStruct((4 * rows, width), BF16),
            jax.ShapeDtypeStruct((chips, width, part), BF16),
        ),
        in_specs=[VM] * 4 + [anywhere] * 3,
        out_specs=(VM,) + (anywhere,) * 4,
        scratch_shapes=[pltpu.VMEM((4 * rows, D), BF16)]
        + exchange_space(rows)
        + [
            pltpu.VMEM((rows, D), BF16),
            pltpu.VMEM((4 * rows, D), BF16),
            pltpu.VMEM((2, D, width), BF16),
            pltpu.VMEM((4 * rows, D), BF16),
            pltpu.VMEM((width, D), BF16),
            pltpu.VMEM((4 * rows, width), F32),
            pltpu.VMEM((2, 4 * rows, width), BF16),
            pltpu.VMEM((4 * rows, width), BF16),
            pltpu.VMEM((tiles, 2, chips, tile, part), BF16),
            pltpu.VMEM((tiles, chips, tile, part), BF16),
        ]
        + dma_sems(24)
        + dma_sems(tiles)
        + [
            pltpu.SemaphoreType.DMA((3,)),
            pltpu.SemaphoreType.DMA((3,)),
            pltpu.SemaphoreType.DMA((tiles,)),
        ],
        cost_estimate=cost(1, 1),
        compiler_params=remote_params(2),
    )(attn_low, weight, tokens, gains, dy, gateup_weight, down_weight)


def mid_forward(attn_low, weight, tokens, gain):
    partial = dot(attn_low, weight).astype(BF16)
    hidden = tokens.astype(F32) + lax.psum_scatter(
        partial, "narrow", scatter_dimension=0, tiled=True
    ).astype(F32)
    normed = (hidden * row_scale(hidden) * gain).astype(BF16)
    return hidden, lax.all_gather(normed, "narrow", axis=0, tiled=True)


def mid_backward_kernel(
    h_ref, c_ref, g_ref, x_hbm, grad_hbm, gu_hbm,
    m_ref, o_ref, gg_ref, full_hbm,
    p_ref, buf, stage, own, x, grad, weight, mine, inbox,
    send, recv, m_send, m_recv, load_sem, full_sem,
):
    me, xn, yn, dg = square()
    c, mate = mate_of()
    half = h_ref.shape[0] // 2
    tiles, part, tile = inbox.shape[0], inbox.shape[3], inbox.shape[4]
    loads = [
        pltpu.make_async_copy(src, dst, load_sem.at[n])
        for n, (src, dst) in enumerate(((grad_hbm, grad), (gu_hbm, weight), (x_hbm, x)))
    ]
    for load in loads:
        load.start()
    barrier = pltpu.get_barrier_semaphore()
    for peer in (xn, yn):
        pl.semaphore_signal(barrier, inc=1, device_id={"narrow": peer}, device_id_type=MESH)
    pl.semaphore_signal(barrier, inc=1, device_id={"wide": mate}, device_id_type=MESH)
    pl.semaphore_wait(barrier, 3)
    copies = Copies(send, recv)
    gg_ref[...] = jnp.zeros_like(gg_ref)
    gain = gain_row(g_ref, D // HD)

    def emit(low, size, total):
        hidden = h_ref[pl.ds(low, size)]
        scale = row_scale(hidden)
        back, gain_sum = norm_back(total, hidden * scale, scale, gain)
        gg_ref[...] += gain_sum
        mid = c_ref[pl.ds(low, size)].astype(F32) + back
        m_ref[pl.ds(low, size)] = mid
        own[pl.ds(low, size)] = mid.astype(BF16)

    def trade(t):
        return wide_copy(mine.at[t, 1 - c], inbox.at[t], m_send, m_recv, t, mate)

    def keep(t):
        cols = pl.ds(pl.multiple_of(t * tile, tile), tile)
        return pltpu.make_async_copy(mine.at[t, c], full_hbm.at[:, :, :, cols], full_sem.at[t])

    def products(low, high):
        @pl.loop(low, high)
        def _(t):
            cols = pl.ds(pl.multiple_of(t * tile, tile), tile)
            for n in range(2):
                full = dot_tn(x[...], grad[n, :, cols]).astype(BF16)
                for k in range(D // part):
                    mine[t, k % 2, n, k // 2] = full[k * part : (k + 1) * part]
            trade(t).start()

    rows = 2 * half
    loads[0].wait()
    loads[1].wait()

    def fill(owner):
        at = pl.ds(pl.multiple_of(owner * rows, rows), rows)

        @pl.loop(0, D // 512)
        def _(t):
            cols = pl.ds(pl.multiple_of(t * 512, 512), 512)
            p_ref[at, cols] = (
                dot_nt(grad[0, at, :], weight[0, cols, :])
                + dot_nt(grad[1, at, :], weight[1, cols, :])
            ).astype(BF16)

    def early():
        loads[2].wait()
        products(0, tiles // 2)

    def middle():
        products(tiles // 2, tiles)

    def relay():
        @pl.loop(0, tiles)
        def _(t):
            trade(t).wait_recv()
            mine[t, c] = (mine[t, c].astype(F32) + inbox[t].astype(F32)).astype(BF16)
            keep(t).start()

    exchange_square(copies, p_ref, buf, stage, own, o_ref, emit, fill, early, middle, relay=relay)
    copies.finish()

    @pl.loop(0, tiles)
    def _(t):
        trade(t).wait_send()
        keep(t).wait()


def mid_backward_pair(hidden_mid, cotangent, gains, x, grads, gateup_weight, count):
    rows = hidden_mid.shape[0]
    width = grads.shape[2]
    tile, part, chips = 256, D // count, count // 2
    tiles = width // tile
    anywhere = pl.BlockSpec(memory_space=pl.ANY)
    mid_grad, back_attn, gain_sum, full = pl.pallas_call(
        mid_backward_kernel,
        name="mid_backward_pair",
        out_shape=(
            jax.ShapeDtypeStruct((rows, D), F32),
            jax.ShapeDtypeStruct((4 * rows, D), BF16),
            jax.ShapeDtypeStruct((1, D), F32),
            jax.ShapeDtypeStruct((2, chips, part, width), BF16),
        ),
        in_specs=[VM] * 3 + [anywhere] * 3,
        out_specs=(VM,) * 3 + (anywhere,),
        scratch_shapes=[pltpu.VMEM((4 * rows, D), BF16)]
        + exchange_space(rows)
        + [
            pltpu.VMEM((rows, D), BF16),
            pltpu.VMEM(x.shape, BF16),
            pltpu.VMEM(grads.shape, BF16),
            pltpu.VMEM(gateup_weight.shape, BF16),
            pltpu.VMEM((tiles, 2, 2, chips, part, tile), BF16),
            pltpu.VMEM((tiles, 2, chips, part, tile), BF16),
        ]
        + dma_sems(24)
        + dma_sems(tiles)
        + [pltpu.SemaphoreType.DMA((3,)), pltpu.SemaphoreType.DMA((tiles,))],
        cost_estimate=cost(1, 1),
        compiler_params=remote_params(3),
    )(hidden_mid, cotangent, gains, x, grads, gateup_weight)
    return mid_grad, back_attn, gain_sum, full.reshape(2, D // 2, width)


def mid_backward(partial, hidden_mid, cotangent, gain):
    total = lax.psum_scatter(partial, "narrow", scatter_dimension=0, tiled=True).astype(F32)
    scale = row_scale(hidden_mid)
    back, gain_sum = norm_back(total, hidden_mid * scale, scale, gain)
    mid = cotangent.astype(F32) + back
    return mid, lax.all_gather(mid.astype(BF16), "narrow", axis=0, tiled=True), gain_sum


def in_scatter_kernel(p_ref, t_ref, g_ref, o_ref, gg_ref, buf, stage, send, recv):
    _, xn, yn, _ = square()
    half = t_ref.shape[0] // 2
    greet("narrow", (xn, yn))
    copies = Copies(send, recv)
    gg_ref[...] = jnp.zeros_like(gg_ref)
    gain = gain_row(g_ref, 0)

    def emit(low, total):
        hidden = t_ref[pl.ds(low, half)].astype(F32)
        scale = row_scale(hidden)
        back, gain_sum = norm_back(total, hidden * scale, scale, gain)
        gg_ref[...] += gain_sum
        o_ref[pl.ds(low, half)] = back

    scatter_square(copies, 0, p_ref, buf, stage, emit)
    copies.finish()


def in_scatter(partial, tokens, gains, special):
    rows = tokens.shape[0]
    if not special:
        total = lax.psum_scatter(partial, "narrow", scatter_dimension=0, tiled=True).astype(F32)
        hidden = tokens.astype(F32)
        scale = row_scale(hidden)
        back, gain_sum = norm_back(total, hidden * scale, scale, gains[: D // HD].reshape(1, D))
        return back, gain_sum
    return pl.pallas_call(
        in_scatter_kernel,
        name="in_scatter",
        out_shape=(
            jax.ShapeDtypeStruct((rows, D), F32),
            jax.ShapeDtypeStruct((1, D), F32),
        ),
        in_specs=[VM] * 3,
        out_specs=(VM,) * 2,
        scratch_shapes=scatter_space(rows) + dma_sems(6),
        cost_estimate=cost(1, 1),
        compiler_params=remote_params(4),
    )(partial, tokens, gains)


def line(count):
    w = lax.axis_index("wide")
    z, c = w // 2, w % 2
    return w, z, c, count // 2, w + 1 - 2 * c, jnp.minimum(w + 2, count - 1), jnp.maximum(w - 2, 0)


def wide_copy(src, dst, send, recv, slot, peer):
    return pltpu.make_async_remote_copy(
        src_ref=src,
        dst_ref=dst,
        send_sem=send.at[slot],
        recv_sem=recv.at[slot],
        device_id={"wide": peer},
        device_id_type=MESH,
    )


def return_grads_kernel(
    count, x_ref, act_hbm, d_hbm, o_ref, b_ref,
    from_mate, from_above, stage, p_ref, buf, out_stage, act, weight,
    send, recv, mate_send, mate_recv, n_send, n_recv, load_sem,
):
    w, z, c, chips, mate, above, below = line(count)
    me, xn, yn, dg = square()
    rows = b_ref.shape[0]
    half = rows // 2
    loads = [
        pltpu.make_async_copy(src, dst, load_sem.at[n])
        for n, (src, dst) in enumerate(((act_hbm, act), (d_hbm, weight)))
    ]
    for load in loads:
        load.start()
    has_above, has_below = z < chips - 1, z > 0
    barrier = pltpu.get_barrier_semaphore()
    for peer in (xn, yn):
        pl.semaphore_signal(barrier, inc=1, device_id={"narrow": peer}, device_id_type=MESH)

    @pl.when(has_above)
    def _():
        pl.semaphore_signal(barrier, inc=1, device_id={"wide": above}, device_id_type=MESH)

    @pl.when(has_below)
    def _():
        pl.semaphore_signal(barrier, inc=1, device_id={"wide": below}, device_id_type=MESH)

    pl.semaphore_signal(barrier, inc=1, device_id={"wide": mate}, device_id_type=MESH)
    pl.semaphore_wait(barrier, 3 + has_above.astype(jnp.int32) + has_below.astype(jnp.int32))

    def to_mate(s):
        return wide_copy(
            x_ref.at[jnp.minimum(2 * s + 1 - c, count - 1)],
            from_mate.at[s],
            mate_send,
            mate_recv,
            s,
            mate,
        )

    def sends_mate(s):
        return (z > s) | ((z == s) & (c == 1))

    def down(s):
        return wide_copy(stage.at[s], from_above.at[s], send, recv, s, below)

    for s in range(chips):

        @pl.when(sends_mate(s))
        def _():
            to_mate(s).start()

    def chain():
        for s in range(chips - 1):
            block = 2 * s + c

            @pl.when(z > s)
            def _():
                to_mate(s).wait_recv()

                @pl.when(z == chips - 1)
                def _():
                    stage[s] = (x_ref[block].astype(F32) + from_mate[s].astype(F32)).astype(BF16)

                @pl.when(z < chips - 1)
                def _():
                    down(s).wait_recv()
                    stage[s] = (
                        x_ref[block].astype(F32)
                        + from_mate[s].astype(F32)
                        + from_above[s].astype(F32)
                    ).astype(BF16)

                down(s).start()

    def emit(low, total):
        b_ref[pl.ds(low, half)] = total

    def fill(owner):
        at = pl.ds(pl.multiple_of(owner * rows, rows), rows)

        @pl.loop(0, D // 512)
        def _(t):
            cols = pl.ds(pl.multiple_of(t * 512, 512), 512)
            p_ref[at, cols] = dot(act[at, :], weight[:, cols]).astype(BF16)

    for load in loads:
        load.wait()
    copies = Copies(n_send, n_recv)
    scatter_square(copies, 0, p_ref, buf, out_stage, emit, fill, middle=chain)
    for s in range(chips):
        block = 2 * s + c

        @pl.when(z == s)
        def _():
            o_ref[...] = x_ref[block].astype(F32)

            @pl.when(c == 0)
            def _():
                to_mate(s).wait_recv()
                o_ref[...] += from_mate[s].astype(F32)

            if s < chips - 1:
                down(s).wait_recv()
                o_ref[...] += from_above[s].astype(F32)

    copies.finish()
    for s in range(chips):

        @pl.when(sends_mate(s))
        def _():
            to_mate(s).wait_send()

        @pl.when(z > s)
        def _():
            down(s).wait_send()


def return_grads_out(grads, act, down_weight, own_rows, count):
    _, rows, width = grads.shape
    chips = count // 2
    return pl.pallas_call(
        functools.partial(return_grads_kernel, count),
        name="return_grads",
        out_shape=(
            jax.ShapeDtypeStruct((rows, width), F32),
            jax.ShapeDtypeStruct((own_rows, D), F32),
        ),
        in_specs=[VM] + [pl.BlockSpec(memory_space=pl.ANY)] * 2,
        out_specs=(VM, VM),
        scratch_shapes=[
            pltpu.VMEM((chips, rows, width), BF16),
            pltpu.VMEM((chips, rows, width), BF16),
            pltpu.VMEM((chips, rows, width), BF16),
            pltpu.VMEM((act.shape[0], D), BF16),
        ]
        + scatter_space(own_rows)
        + [pltpu.VMEM(act.shape, BF16), pltpu.VMEM(down_weight.shape, BF16)]
        + dma_sems(chips)
        + dma_sems(chips)
        + dma_sems(6)
        + [pltpu.SemaphoreType.DMA((2,))],
        cost_estimate=cost(1, 1),
        compiler_params=remote_params(6),
    )(grads, act, down_weight)


def return_grads(grads, count):
    _, rows, width = grads.shape
    w = lax.axis_index("wide")
    seen = (jnp.arange(count) <= w)[:, None, None]
    total = lax.psum_scatter(
        jnp.where(seen, grads, 0).reshape(count * rows, width),
        "wide",
        scatter_dimension=0,
        tiled=True,
    )
    return total.astype(F32)


def gain_kernel(wide, x_ref, o_ref, near, mid, far, send, recv, wide_send, wide_recv):
    me, xn, yn, dg = square()
    w = lax.axis_index("wide")
    barrier = pltpu.get_barrier_semaphore()
    for peer in (xn, yn, dg):
        pl.semaphore_signal(barrier, inc=1, device_id={"narrow": peer}, device_id_type=MESH)
    for step in range(1, wide):
        pl.semaphore_signal(
            barrier, inc=1, device_id={"wide": (w + step) % wide}, device_id_type=MESH
        )
    pl.semaphore_wait(barrier, 3 + wide - 1)
    copies = Copies(send, recv)
    sent = [
        copies.go(x_ref.at[peer], near.at[slot], slot, peer)
        for slot, peer in enumerate((xn, yn, dg))
    ]
    for copy in sent:
        copy.wait_recv()
    mid[...] = x_ref[me] + near[0] + near[1] + near[2]
    away = []
    for step in range(1, wide):
        peer = (w + step) % wide
        copy = wide_copy(
            mid.at[peer], far.at[step - 1], wide_send, wide_recv, step - 1, peer
        )
        copy.start()
        away.append(copy)
    total = mid[w]
    for step in range(1, wide):
        away[step - 1].wait_recv()
        total = total + far[step - 1]
    o_ref[...] = total
    copies.finish()
    for copy in away:
        copy.wait_send()


def gain_sums(partial, wide, narrow, special):
    if not special:
        return lax.psum_scatter(partial, ("wide", "narrow"), scatter_dimension=0, tiled=True)
    count = partial.shape[0] // (wide * narrow)
    padded = -(-count // 128) * 128
    shaped = partial.reshape(wide, narrow, count).transpose(1, 0, 2)
    shaped = jnp.pad(shaped, ((0, 0), (0, 0), (0, padded - count)))
    shaped = shaped.reshape(narrow, wide, padded // 128, 128)
    out = pl.pallas_call(
        functools.partial(gain_kernel, wide),
        name="gain_sums",
        out_shape=jax.ShapeDtypeStruct((padded // 128, 128), F32),
        in_specs=[VM],
        out_specs=VM,
        scratch_shapes=[
            pltpu.VMEM((3, wide, padded // 128, 128), F32),
            pltpu.VMEM((wide, padded // 128, 128), F32),
            pltpu.VMEM((wide - 1, padded // 128, 128), F32),
        ]
        + dma_sems(3)
        + dma_sems(wide - 1),
        cost_estimate=cost(1, 1),
        compiler_params=remote_params(7),
    )(shaped)
    return out.reshape(padded)[:count]


def cost(flops, moved, exps=0):
    return pl.CostEstimate(flops=1, bytes_accessed=1, transcendentals=0)


def params(*semantics):
    if not semantics:
        return pltpu.CompilerParams(vmem_limit_bytes=VMEM_LIMIT)
    return pltpu.CompilerParams(vmem_limit_bytes=VMEM_LIMIT, dimension_semantics=semantics)


def spin(raw, gain_row, cosine, sine):
    normed = raw * row_scale(raw) * gain_row
    return normed * cosine + pltpu.roll(normed, HD // 2, axis=1) * sine


def keys_kernel(x_ref, w_ref, g_ref, cos_ref, sin_ref, kv_ref, raw_ref):
    which = pl.program_id(0)
    width = w_ref.shape[2]
    out = dot(x_ref[...], w_ref[0])

    @pl.when(which == 0)
    def _():
        raw_ref[...] = out
        for h in range(width // HD):
            part = out[:, h * HD : (h + 1) * HD]
            kv_ref[:, h * HD : (h + 1) * HD] = spin(
                part, g_ref[...], cos_ref[...], sin_ref[...]
            ).astype(BF16)

    @pl.when(which == 1)
    def _():
        kv_ref[...] = out.astype(BF16)


def keys_values(x, weight, gain_row, cosine, sine):
    rows, width = x.shape[0], weight.shape[2]
    whole = lambda i: (0, 0)
    return pl.pallas_call(
        keys_kernel,
        name="keys_values",
        grid=(2,),
        out_shape=(
            jax.ShapeDtypeStruct((rows, 2 * width), BF16),
            jax.ShapeDtypeStruct((rows, width), F32),
        ),
        in_specs=[
            pl.BlockSpec((rows, D), whole),
            pl.BlockSpec((1, D, width), lambda i: (i, 0, 0)),
            pl.BlockSpec((1, HD), whole),
            pl.BlockSpec((rows, HD), whole),
            pl.BlockSpec((rows, HD), whole),
        ],
        out_specs=(
            pl.BlockSpec((rows, width), lambda i: (0, i)),
            pl.BlockSpec((rows, width), whole),
        ),
        compiler_params=params("arbitrary"),
        cost_estimate=cost(4 * rows * D * width, 2 * rows * D + 4 * D * width),
    )(x, weight, gain_row, cosine, sine)


def queries_kernel(x_ref, w_ref, g_ref, cos_ref, sin_ref, q_ref, raw_ref):
    out = dot(x_ref[...], w_ref[...])
    raw_ref[...] = out
    for h in range(w_ref.shape[1] // HD):
        part = out[:, h * HD : (h + 1) * HD]
        q_ref[:, h * HD : (h + 1) * HD] = spin(
            part, g_ref[...], cos_ref[...], sin_ref[...]
        ).astype(BF16)


def queries(x, weight, gain_row, cosine, sine):
    rows, width = x.shape[0], weight.shape[1]
    tile = 256
    whole = lambda i: (0, 0)
    return pl.pallas_call(
        queries_kernel,
        name="queries",
        grid=(width // tile,),
        out_shape=(
            jax.ShapeDtypeStruct((rows, width), BF16),
            jax.ShapeDtypeStruct((rows, width), F32),
        ),
        in_specs=[
            pl.BlockSpec((rows, D), whole),
            pl.BlockSpec((D, tile), lambda i: (0, i)),
            pl.BlockSpec((1, HD), whole),
            pl.BlockSpec((rows, HD), whole),
            pl.BlockSpec((rows, HD), whole),
        ],
        out_specs=(
            pl.BlockSpec((rows, tile), lambda i: (0, i)),
            pl.BlockSpec((rows, tile), lambda i: (0, i)),
        ),
        compiler_params=params("arbitrary"),
        cost_estimate=cost(2 * rows * D * width, 2 * rows * D + 2 * D * width),
    )(x, weight, gain_row, cosine, sine)


def attend_kernel(heads, group, w_ref, q_ref, kv_ref, o_ref, low_ref, lse_ref, acc):
    rows = q_ref.shape[0]
    kv_width = kv_ref.shape[2] // 2
    w = w_ref[0]
    acc[...] = jnp.zeros_like(acc)
    ones = jnp.ones((rows, HD), BF16)

    def block(j, masked):
        for h in range(heads):
            kv = h // group
            key = kv_ref[j, :, kv * HD : (kv + 1) * HD]
            value = kv_ref[j, :, kv_width + kv * HD : kv_width + (kv + 1) * HD]
            query = q_ref[:, h * HD : (h + 1) * HD]
            terms = jnp.exp2(dot_nt(query, key) * (FACTOR * LOG2E))
            if masked:
                at = lax.broadcasted_iota(jnp.int32, (rows, rows), 0)
                key_at = lax.broadcasted_iota(jnp.int32, (rows, rows), 1)
                terms = jnp.where(key_at <= at, terms, 0.0)
            acc[h] += dot(terms.astype(BF16), jnp.concatenate([value, ones], axis=1))

    @pl.loop(0, w)
    def _(j):
        block(j, False)

    block(w, True)
    for h in range(heads):
        total = acc[h, :, HD:]
        out = acc[h, :, :HD] / total
        o_ref[:, h * HD : (h + 1) * HD] = out
        low_ref[:, h * HD : (h + 1) * HD] = out.astype(BF16)
        lse_ref[h : h + 1, :] = jnp.transpose(jnp.log2(total))[0:1]


def attend(w_index, query, kv_all, heads, group):
    rows, width = query.shape
    count = kv_all.shape[0]
    return pl.pallas_call(
        functools.partial(attend_kernel, heads, group),
        name="attend",
        out_shape=(
            jax.ShapeDtypeStruct((rows, width), F32),
            jax.ShapeDtypeStruct((rows, width), BF16),
            jax.ShapeDtypeStruct((heads, rows), F32),
        ),
        in_specs=[SM, VM, VM],
        out_specs=(VM, VM, VM),
        scratch_shapes=[pltpu.VMEM((heads, rows, 2 * HD), F32)],
        compiler_params=params(),
        cost_estimate=cost(4 * rows * rows * count * width, 2 * kv_all.size, rows * rows * heads * count),
    )(w_index, query, kv_all)


def attend_back_kernel(
    heads, group, w_ref, q_ref, kv_ref, do_ref, o_ref, lse_ref, dq_ref, dkv_ref, delta
):
    rows = q_ref.shape[0]
    kv_width = kv_ref.shape[2] // 2
    w = w_ref[0]
    for h in range(heads):
        part = slice(h * HD, (h + 1) * HD)
        delta[h : h + 1, :] = jnp.sum(
            jnp.transpose(do_ref[:, part].astype(F32) * o_ref[:, part]), axis=0, keepdims=True
        )
    dq_ref[...] = jnp.zeros_like(dq_ref)

    @pl.loop(0, w + 1)
    def _(j):
        seen = jnp.where(j == w, 0, rows)

        @pl.loop(0, heads // group)
        def _(kv):
            key_at_lane = pl.ds(pl.multiple_of(kv * HD, HD), HD)
            value_at_lane = pl.ds(pl.multiple_of(kv_width + kv * HD, HD), HD)
            key, value = kv_ref[j, :, key_at_lane], kv_ref[j, :, value_at_lane]
            key_sum = jnp.zeros((rows, HD), F32)
            value_sum = jnp.zeros((rows, HD), F32)
            for n in range(group):
                h = kv * group + n
                part = pl.ds(pl.multiple_of(h * HD, HD), HD)
                query, out_grad = q_ref[:, part], do_ref[:, part]
                probs = jnp.exp2(
                    dot_nt(key, query) * (FACTOR * LOG2E) - lse_ref[pl.ds(h, 1), :]
                )
                key_at = lax.broadcasted_iota(jnp.int32, (rows, rows), 0)
                at = lax.broadcasted_iota(jnp.int32, (rows, rows), 1)
                probs = jnp.where(key_at - at <= seen, probs, 0.0)
                value_sum += dot(probs.astype(BF16), out_grad)
                prob_grad = dot_nt(value, out_grad)
                score_grad = (probs * (prob_grad - delta[pl.ds(h, 1), :])).astype(BF16)
                key_sum += dot(score_grad, query)
                dq_ref[:, part] += dot_tn(score_grad, key)
            dkv_ref[j, :, key_at_lane] = (key_sum * FACTOR).astype(BF16)
            dkv_ref[j, :, value_at_lane] = value_sum.astype(BF16)

    dq_ref[...] = dq_ref[...] * FACTOR


def attend_back(w_index, query, kv_all, out_grad, out, lse, heads, group):
    rows, width = query.shape
    count = kv_all.shape[0]
    return pl.pallas_call(
        functools.partial(attend_back_kernel, heads, group),
        name="attend_back",
        out_shape=(
            jax.ShapeDtypeStruct((rows, width), F32),
            jax.ShapeDtypeStruct(kv_all.shape, BF16),
        ),
        in_specs=[SM] + [VM] * 5,
        out_specs=(VM, VM),
        scratch_shapes=[pltpu.VMEM((heads, rows), F32)],
        compiler_params=params(),
        cost_estimate=cost(10 * rows * rows * count * width, 4 * kv_all.size, rows * rows * heads * count),
    )(w_index, query, kv_all, out_grad, out, lse)


def unspin_kernel(width, row, e_ref, raw_ref, g_ref, cos_ref, sin_ref, o_ref, gg_ref):
    gain_sum = jnp.zeros((1, HD), F32)
    for h in range(raw_ref.shape[1] // HD):
        part = slice(h * HD, (h + 1) * HD)
        grad = e_ref[:, part]
        turned = grad * cos_ref[...] - pltpu.roll(grad, HD // 2, axis=1) * sin_ref[...]
        raw = raw_ref[:, part]
        scale = row_scale(raw)
        back, total = norm_back(turned, raw * scale, scale, g_ref[row : row + 1, :])
        o_ref[:, part] = back.astype(BF16)
        gain_sum += total
    if width > raw_ref.shape[1]:
        o_ref[:, raw_ref.shape[1] :] = e_ref[:, raw_ref.shape[1] :].astype(BF16)
    gg_ref[...] = gain_sum


def unspin(grad, raw, gains, row, cosine, sine):
    rows, width = grad.shape
    return pl.pallas_call(
        functools.partial(unspin_kernel, width, row),
        name="unspin",
        out_shape=(
            jax.ShapeDtypeStruct((rows, width), BF16),
            jax.ShapeDtypeStruct((1, HD), F32),
        ),
        in_specs=[VM] * 5,
        out_specs=(VM, VM),
        compiler_params=params(),
        cost_estimate=cost(20 * grad.size, 10 * grad.size),
    )(grad, raw, gains, cosine, sine)


def front_kernel(
    count, heads, group,
    t_ref, c_ref, g_ref, wq_hbm, wkv_hbm, cos_ref, sin_ref,
    dy_hbm, x_hbm, q_hbm, qraw_hbm, kraw_hbm, kv_hbm, o_ref, low_ref, lse_ref,
    own, x, weight, q, qraw, kraw, kv, acc,
    send, recv, z_send, z_recv, m_send, m_recv, c_send, c_recv, load_sem, store_sem, kv_sem,
):
    me, xn, yn, dg = square()
    w, z, c, chips, mate, above, below = line(count)
    rows = t_ref.shape[0]
    half = rows // 2
    all_rows = 4 * rows
    q_width, kv_width = wq_hbm.shape[1], wkv_hbm.shape[2]
    loads = [
        pltpu.make_async_copy(wq_hbm, weight.at[:, pl.ds(0, q_width)], load_sem.at[0]),
        pltpu.make_async_copy(wkv_hbm.at[0], weight.at[:, pl.ds(q_width, kv_width)], load_sem.at[1]),
        pltpu.make_async_copy(
            wkv_hbm.at[1], weight.at[:, pl.ds(q_width + kv_width, kv_width)], load_sem.at[2]
        ),
    ]
    for load in loads[::-1]:
        load.start()

    has_above, has_below = z < chips - 1, z > 0
    barrier = pltpu.get_barrier_semaphore()
    for peer in (xn, yn):
        pl.semaphore_signal(barrier, inc=1, device_id={"narrow": peer}, device_id_type=MESH)

    @pl.when(has_above)
    def _():
        pl.semaphore_signal(barrier, inc=1, device_id={"wide": above}, device_id_type=MESH)

    @pl.when(has_below)
    def _():
        pl.semaphore_signal(barrier, inc=1, device_id={"wide": below}, device_id_type=MESH)

    pl.semaphore_signal(barrier, inc=1, device_id={"wide": mate}, device_id_type=MESH)
    hidden = t_ref[...].astype(F32)
    own[...] = (hidden * row_scale(hidden) * gain_row(g_ref, 0)).astype(BF16)
    pl.semaphore_wait(barrier, 3 + has_above.astype(jnp.int32) + has_below.astype(jnp.int32))

    def half_of(ref, owner, low):
        return ref.at[pl.ds(pl.multiple_of(owner * rows + low, half), half)]

    def spread(copies, src, dst):
        upper, lower = src.at[pl.ds(0, half)], src.at[pl.ds(half, half)]
        return (
            copies.go(upper, half_of(dst, me, 0), 0, xn),
            copies.go(lower, half_of(dst, me, half), 1, yn),
            copies.go(lower, half_of(dst, me, half), 2, xn),
            copies.go(upper, half_of(dst, me, 0), 3, yn),
        )

    def lazy(copies, slot, owner, low, dst, peer):
        return pltpu.make_async_remote_copy(
            src_ref=half_of(dst, owner, low),
            dst_ref=half_of(dst, owner, low),
            send_sem=copies.send.at[slot],
            recv_sem=copies.recv.at[slot],
            device_id={"narrow": peer},
            device_id_type=MESH,
        )

    copies, away = Copies(send, recv), Copies(c_send, c_recv)
    xa, yb, xb, ya = spread(copies, own, x)
    yf, xf = lazy(copies, 4, xn, 0, x, yn), lazy(copies, 5, yn, half, x, xn)
    c_yf, c_xf = lazy(away, 4, xn, 0, dy_hbm, yn), lazy(away, 5, yn, half, dy_hbm, xn)
    dy_part = dy_hbm.at[pl.ds(pl.multiple_of(me * rows, rows), rows)]
    c_own = pltpu.make_async_copy(c_ref, dy_part, store_sem.at[4])

    def piece(k, j):
        owner = jnp.where(k == 0, me, jnp.where(k == 3, dg, xn if j == 0 else yn))
        low = jnp.where((k == 2) == (j == 0), half, 0)
        return pl.ds(pl.multiple_of(owner * rows + low, half), half)

    def unit(block, k, j):
        return kv.at[block, piece(k, j)]

    def to_above(s, k, j):
        block = jnp.maximum(w - 2 * s, 0)
        return wide_copy(
            unit(block, k, j), unit(block, k, j), z_send, z_recv, 8 * s + 2 * k + j, above
        )

    def from_below(s, k, j):
        block = jnp.maximum(w - 2 * s, 0)
        return wide_copy(
            unit(block, k, j), unit(block, k, j), z_send, z_recv, 8 * (s - 1) + 2 * k + j, above
        )

    def to_mate(s, k, j):
        block = jnp.maximum(w - 2 * s, 0)
        return wide_copy(
            unit(block, k, j), unit(block, k, j), m_send, m_recv, 8 * s + 2 * k + j, mate
        )

    def project(k):
        rows_in = jnp.concatenate([x[piece(k, 0), :], x[piece(k, 1), :]], axis=0)
        out = dot(rows_in, weight[:, q_width:])
        cosine = jnp.concatenate([cos_ref[piece(k, 0), :], cos_ref[piece(k, 1), :]], axis=0)
        sine = jnp.concatenate([sin_ref[piece(k, 0), :], sin_ref[piece(k, 1), :]], axis=0)
        base = 2 * (D // HD)
        parts = [slice(0, half), slice(half, rows)]
        for h in range(heads // group):
            lanes = slice(h * HD, (h + 1) * HD)
            key = spin(out[:, lanes], g_ref[base + 1 : base + 2, :], cosine, sine).astype(BF16)
            for j in range(2):
                kv[w, piece(k, j), h * HD : (h + 1) * HD] = key[parts[j]]
        for j in range(2):
            kv[w, piece(k, j), kv_width:] = out[parts[j], kv_width:].astype(BF16)

            @pl.when(has_above)
            def _():
                to_above(0, k, j).start()

            @pl.when(c == 0)
            def _():
                to_mate(0, k, j).start()

        for j in range(2):
            kraw[piece(k, j), :] = out[parts[j], :kv_width]
        pl.when(k == 0)(loads[0].wait)
        out = dot(rows_in, weight[:, :q_width])
        for h in range(heads):
            lanes = slice(h * HD, (h + 1) * HD)
            query = spin(out[:, lanes], g_ref[base : base + 1, :], cosine, sine).astype(BF16)
            for j in range(2):
                q[piece(k, j), lanes] = query[parts[j]]
        for j in range(2):
            qraw[piece(k, j), :] = out[parts[j], :]

    def receive(s, k):
        @pl.when(z >= s)
        def _():
            for j in range(2):
                from_below(s, k, j).wait_recv()
                if s < chips - 1:

                    @pl.when(has_above)
                    def _():
                        to_above(s, k, j).start()

                to_mate(s, k, j).start()

    x[pl.ds(pl.multiple_of(me * rows, rows), rows), :] = own[...]
    loads[1].wait()
    loads[2].wait()

    @pl.loop(0, 4)
    def _(k):
        @pl.when(k == 1)
        def _():
            xa.wait_recv()
            yf.start()
            yb.wait_recv()
            xf.start()

        @pl.when(k == 2)
        def _():
            receive(1, 0)
            xb.wait_recv()
            ya.wait_recv()

        @pl.when(k == 3)
        def _():
            receive(2, 0)
            receive(1, 1)
            receive(3, 0)
            yf.wait_recv()
            xf.wait_recv()

        project(k)

    c_first = spread(away, c_ref, dy_hbm)
    stores = [
        pltpu.make_async_copy(src, dst, store_sem.at[n])
        for n, (src, dst) in enumerate(((x, x_hbm), (q, q_hbm), (qraw, qraw_hbm), (kraw, kraw_hbm)))
    ] + [c_own]
    for store in stores:
        store.start()
    receive(2, 1)
    receive(1, 2)
    acc[...] = jnp.zeros_like(acc)
    ones = jnp.ones((all_rows, HD), BF16)

    def keep(j):
        return pltpu.make_async_copy(kv.at[j], kv_hbm.at[j], kv_sem.at[j])

    def c_relay():
        c_first[0].wait_recv()
        c_yf.start()
        c_first[1].wait_recv()
        c_xf.start()

    @pl.loop(0, 2 * z + 1 + c)
    def _(n):
        i = n - c
        for s, units in ((1, ((3, 1), (2, 2), (1, 3))), (2, ((3, 2), (2, 3))), (3, ((3, 3),))):

            @pl.when(i == 2 * s - 1)
            def _():
                for pair in units:
                    receive(*pair)

                if s == 2:
                    c_relay()

        for s in range(chips):

            @pl.when((i == 2 * s) & (n > 0))
            def _():
                for k in range(4):
                    for j in range(2):
                        to_mate(s, k, j).wait_recv()

        odd = i % 2
        step = (i + 1) // 2
        j = jnp.where(n == 0, w, 2 * (z - step) + c + (1 - odd) * (1 - 2 * c))
        seen = jnp.where(n == 0, 0, all_rows)
        for h in range(heads):
            head = h // group
            key = kv[j, :, head * HD : (head + 1) * HD]
            value = kv[j, :, kv_width + head * HD : kv_width + (head + 1) * HD]
            terms = jnp.exp2(dot_nt(q[:, h * HD : (h + 1) * HD], key) * (FACTOR * LOG2E))
            at = lax.broadcasted_iota(jnp.int32, (all_rows, all_rows), 0)
            key_at = lax.broadcasted_iota(jnp.int32, (all_rows, all_rows), 1)
            terms = jnp.where(key_at - at <= seen, terms, 0.0)
            acc[h] += dot(terms.astype(BF16), jnp.concatenate([value, ones], axis=1))
        keep(j).start()

    @pl.when(z < 2)
    def _():
        c_relay()

    for h in range(heads):
        total = acc[h, :, HD:]
        out = acc[h, :, :HD] / total
        o_ref[:, h * HD : (h + 1) * HD] = out
        low_ref[:, h * HD : (h + 1) * HD] = out.astype(BF16)
        lse_ref[h : h + 1, :] = jnp.transpose(jnp.log2(total))[0:1]

    copies.finish()
    yf.wait_send()
    xf.wait_send()
    for copy in c_first[2:] + (c_yf, c_xf):
        copy.wait_recv()
    away.finish()
    c_yf.wait_send()
    c_xf.wait_send()
    for s in range(chips):

        @pl.when((z >= s) & has_above)
        def _():
            for k in range(4):
                for j in range(2):
                    to_above(s, k, j).wait_send()

        @pl.when((z >= s) & ((c == 0) | (s > 0)))
        def _():
            for k in range(4):
                for j in range(2):
                    to_mate(s, k, j).wait_send()

    for store in stores:
        store.wait()

    @pl.loop(0, w + 1)
    def _(j):
        keep(j).wait()


def front(tokens, cotangent, gains, query_weight, keyvalue_weight, cosine, sine, count):
    rows = tokens.shape[0]
    all_rows = 4 * rows
    q_width, kv_width = query_weight.shape[1], keyvalue_weight.shape[2]
    heads, group = q_width // HD, q_width // kv_width
    chips = count // 2
    anywhere = pl.BlockSpec(memory_space=pl.ANY)
    return pl.pallas_call(
        functools.partial(front_kernel, count, heads, group),
        name="front",
        out_shape=(
            jax.ShapeDtypeStruct((all_rows, D), BF16),
            jax.ShapeDtypeStruct((all_rows, D), BF16),
            jax.ShapeDtypeStruct((all_rows, q_width), BF16),
            jax.ShapeDtypeStruct((all_rows, q_width), F32),
            jax.ShapeDtypeStruct((all_rows, kv_width), F32),
            jax.ShapeDtypeStruct((count, all_rows, 2 * kv_width), BF16),
            jax.ShapeDtypeStruct((all_rows, q_width), F32),
            jax.ShapeDtypeStruct((all_rows, q_width), BF16),
            jax.ShapeDtypeStruct((heads, all_rows), F32),
        ),
        in_specs=[VM, VM, VM, anywhere, anywhere, VM, VM],
        out_specs=(anywhere,) * 6 + (VM,) * 3,
        scratch_shapes=[
            pltpu.VMEM((rows, D), BF16),
            pltpu.VMEM((all_rows, D), BF16),
            pltpu.VMEM((D, q_width + 2 * kv_width), BF16),
            pltpu.VMEM((all_rows, q_width), BF16),
            pltpu.VMEM((all_rows, q_width), F32),
            pltpu.VMEM((all_rows, kv_width), F32),
            pltpu.VMEM((count, all_rows, 2 * kv_width), BF16),
            pltpu.VMEM((heads, all_rows, 2 * HD), F32),
        ]
        + dma_sems(6)
        + dma_sems(8 * chips)
        + dma_sems(8 * chips)
        + dma_sems(6)
        + [
            pltpu.SemaphoreType.DMA((3,)),
            pltpu.SemaphoreType.DMA((5,)),
            pltpu.SemaphoreType.DMA((count,)),
        ],
        cost_estimate=cost(1, 1),
        compiler_params=remote_params(8),
    )(tokens, cotangent, gains, query_weight, keyvalue_weight, cosine, sine)


def feed_kernel(x_ref, dy_ref, w_ref, d_ref, act_ref, grad_ref, down_ref):
    x, dy = x_ref[...], dy_ref[...]
    gate = dot(x, w_ref[0])
    upper = dot(x, w_ref[1])
    act_grad = dot_nt(dy, d_ref[...])
    sig = jax.nn.sigmoid(gate)
    swish = gate * sig
    act = (swish * upper).astype(BF16)
    act_ref[...] = act
    grad_ref[0] = (act_grad * upper * sig * (1.0 + gate * (1.0 - sig))).astype(BF16)
    grad_ref[1] = (act_grad * swish).astype(BF16)
    down_ref[...] = dot_tn(act, dy).astype(BF16)


def feed(x, dy, gateup_weight, down_weight):
    rows, width = x.shape[0], down_weight.shape[0]
    tile = 256
    whole = lambda i: (0, 0)
    return pl.pallas_call(
        feed_kernel,
        name="feed",
        grid=(width // tile,),
        out_shape=(
            jax.ShapeDtypeStruct((rows, width), BF16),
            jax.ShapeDtypeStruct((2, rows, width), BF16),
            jax.ShapeDtypeStruct((width, D), BF16),
        ),
        in_specs=[
            pl.BlockSpec((rows, D), whole),
            pl.BlockSpec((rows, D), whole),
            pl.BlockSpec((2, D, tile), lambda i: (0, 0, i)),
            pl.BlockSpec((tile, D), lambda i: (i, 0)),
        ],
        out_specs=(
            pl.BlockSpec((rows, tile), lambda i: (0, i)),
            pl.BlockSpec((2, rows, tile), lambda i: (0, 0, i)),
            pl.BlockSpec((tile, D), lambda i: (i, 0)),
        ),
        compiler_params=params("arbitrary"),
        cost_estimate=cost(8 * rows * D * width, 4 * rows * D + 8 * D * width),
    )(x, dy, gateup_weight, down_weight)


def feed_back_kernel(x_ref, act_ref, grad_ref, w_ref, d_ref, full_ref, in_ref, out_ref, in_acc, out_acc):
    step = pl.program_id(0)

    @pl.when(step == 0)
    def _():
        in_acc[...] = jnp.zeros_like(in_acc)
        out_acc[...] = jnp.zeros_like(out_acc)

    in_acc[...] += dot_nt(grad_ref[0], w_ref[0]) + dot_nt(grad_ref[1], w_ref[1])
    out_acc[...] += dot(act_ref[...], d_ref[...])
    x = x_ref[...]
    full_ref[0] = dot_tn(x, grad_ref[0]).astype(BF16)
    full_ref[1] = dot_tn(x, grad_ref[1]).astype(BF16)

    @pl.when(step == pl.num_programs(0) - 1)
    def _():
        in_ref[...] = in_acc[...].astype(BF16)
        out_ref[...] = out_acc[...].astype(BF16)


def feed_back(x, act, grads, gateup_weight, down_weight):
    rows, width = x.shape[0], down_weight.shape[0]
    tile = 256
    whole = lambda i: (0, 0)
    return pl.pallas_call(
        feed_back_kernel,
        name="feed_back",
        grid=(width // tile,),
        out_shape=(
            jax.ShapeDtypeStruct((2, D, width), BF16),
            jax.ShapeDtypeStruct((rows, D), BF16),
            jax.ShapeDtypeStruct((rows, D), BF16),
        ),
        in_specs=[
            pl.BlockSpec((rows, D), whole),
            pl.BlockSpec((rows, tile), lambda i: (0, i)),
            pl.BlockSpec((2, rows, tile), lambda i: (0, 0, i)),
            pl.BlockSpec((2, D, tile), lambda i: (0, 0, i)),
            pl.BlockSpec((tile, D), lambda i: (i, 0)),
        ],
        out_specs=(
            pl.BlockSpec((2, D, tile), lambda i: (0, 0, i)),
            pl.BlockSpec((rows, D), whole),
            pl.BlockSpec((rows, D), whole),
        ),
        scratch_shapes=[pltpu.VMEM((rows, D), F32), pltpu.VMEM((rows, D), F32)],
        compiler_params=params("arbitrary"),
        cost_estimate=cost(10 * rows * D * width, 8 * rows * D + 10 * D * width),
    )(x, act, grads, gateup_weight, down_weight)


def out_back_kernel(dy_ref, w_ref, low_ref, grad_ref, full_ref):
    dy = dy_ref[...]
    grad_ref[...] = dot_nt(dy, w_ref[...]).astype(BF16)
    full_ref[...] = dot_tn(dy, low_ref[...]).astype(BF16)


def out_back(dy, weight, attn_low):
    rows, width = attn_low.shape
    tile = 256
    whole = lambda i: (0, 0)
    return pl.pallas_call(
        out_back_kernel,
        name="out_back",
        grid=(width // tile,),
        out_shape=(
            jax.ShapeDtypeStruct((rows, width), BF16),
            jax.ShapeDtypeStruct((D, width), BF16),
        ),
        in_specs=[
            pl.BlockSpec((rows, D), whole),
            pl.BlockSpec((tile, D), lambda i: (i, 0)),
            pl.BlockSpec((rows, tile), lambda i: (0, i)),
        ],
        out_specs=(
            pl.BlockSpec((rows, tile), lambda i: (0, i)),
            pl.BlockSpec((D, tile), lambda i: (0, i)),
        ),
        compiler_params=params("arbitrary"),
        cost_estimate=cost(4 * rows * D * width, 2 * rows * D + 4 * D * width),
    )(dy, weight, attn_low)


def project_back_kernel(x_ref, q_ref, kv_ref, wq_ref, wkv_ref, out_ref, in_ref, full_ref):
    q_width, kv_width = wq_ref.shape[1], wkv_ref.shape[2]
    x = x_ref[...]
    key, value = kv_ref[:, :kv_width], kv_ref[:, kv_width:]
    in_ref[...] = (
        dot_nt(q_ref[...], wq_ref[...]) + dot_nt(key, wkv_ref[0]) + dot_nt(value, wkv_ref[1])
    ).astype(BF16)
    full_ref[:, :q_width] = dot_tn(x, q_ref[...]).astype(BF16)
    full_ref[:, q_width : q_width + 2 * kv_width] = dot_tn(x, kv_ref[...]).astype(BF16)
    full_ref[:, q_width + 2 * kv_width :] = out_ref[...]


def project_back(x, q_back, kv_back, query_weight, keyvalue_weight, output_full):
    rows, out_width = x.shape[0], output_full.shape[1]
    q_width, kv_width = query_weight.shape[1], keyvalue_weight.shape[2]
    tile = 512
    whole = lambda i: (0, 0)
    return pl.pallas_call(
        project_back_kernel,
        name="project_back",
        grid=(D // tile,),
        out_shape=(
            jax.ShapeDtypeStruct((rows, D), BF16),
            jax.ShapeDtypeStruct((D, q_width + 2 * kv_width + out_width), BF16),
        ),
        in_specs=[
            pl.BlockSpec((rows, tile), lambda i: (0, i)),
            pl.BlockSpec((rows, q_width), whole),
            pl.BlockSpec((rows, 2 * kv_width), whole),
            pl.BlockSpec((tile, q_width), lambda i: (i, 0)),
            pl.BlockSpec((2, tile, kv_width), lambda i: (0, i, 0)),
            pl.BlockSpec((tile, out_width), lambda i: (i, 0)),
        ],
        out_specs=(
            pl.BlockSpec((rows, tile), lambda i: (0, i)),
            pl.BlockSpec((tile, q_width + 2 * kv_width + out_width), lambda i: (i, 0)),
        ),
        compiler_params=params("arbitrary"),
        cost_estimate=cost(4 * rows * D * (q_width + 2 * kv_width), 6 * D * (q_width + 2 * kv_width)),
    )(x, q_back, kv_back, query_weight, keyvalue_weight, output_full)


def mate_of():
    w = lax.axis_index("wide")
    c = w % 2
    return c, w + 1 - 2 * c


def greet_mate():
    _, mate = mate_of()
    barrier = pltpu.get_barrier_semaphore()
    pl.semaphore_signal(barrier, inc=1, device_id={"wide": mate}, device_id_type=MESH)
    pl.semaphore_wait(barrier, 1)


def project_back_pair_kernel(
    x_ref, q_ref, kv_ref, wq_ref, wkv_ref, out_ref, in_ref, full_ref, stage, inbox, send, recv
):
    step, steps = pl.program_id(0), pl.num_programs(0) - 1
    c, mate = mate_of()
    q_width, kv_width = wq_ref.shape[1], wkv_ref.shape[2]
    part = full_ref.shape[1]

    def trade(i):
        return wide_copy(stage.at[i % 2, 1 - c], inbox.at[i], send, recv, i, mate)

    @pl.when(step == 0)
    def _():
        greet_mate()

    @pl.when((step >= 2) & (step <= steps))
    def _():
        trade(step - 2).wait_send()

    @pl.when(step < steps)
    def _():
        x = x_ref[...]
        q_full = dot_tn(x, q_ref[...]).astype(BF16)
        kv_full = dot_tn(x, kv_ref[...]).astype(BF16)
        for k in range(2):
            at = slice(k * part, (k + 1) * part)
            stage[step % 2, k, :, :q_width] = q_full[at]
            stage[step % 2, k, :, q_width : q_width + 2 * kv_width] = kv_full[at]
            stage[step % 2, k, :, q_width + 2 * kv_width :] = out_ref[at, :]
        trade(step).start()
        key, value = kv_ref[:, :kv_width], kv_ref[:, kv_width:]
        in_ref[...] = (
            dot_nt(q_ref[...], wq_ref[...]) + dot_nt(key, wkv_ref[0]) + dot_nt(value, wkv_ref[1])
        ).astype(BF16)

    @pl.when(step > 0)
    def _():
        last = jnp.maximum(step - 1, 0)
        trade(last).wait_recv()
        full_ref[0] = (stage[last % 2, c].astype(F32) + inbox[last].astype(F32)).astype(BF16)

    @pl.when(step == steps)
    def _():
        trade(step - 1).wait_send()


def project_back_pair(x, q_back, kv_back, query_weight, keyvalue_weight, output_full, count):
    rows, out_width = x.shape[0], output_full.shape[1]
    q_width, kv_width = query_weight.shape[1], keyvalue_weight.shape[2]
    width = q_width + 2 * kv_width + out_width
    part = D // count
    tile = 2 * part
    steps = count // 2
    whole = lambda i: (0, 0)
    now = lambda i: jnp.minimum(i, steps - 1)
    in_partial, full = pl.pallas_call(
        project_back_pair_kernel,
        name="project_back_pair",
        grid=(steps + 1,),
        out_shape=(
            jax.ShapeDtypeStruct((rows, D), BF16),
            jax.ShapeDtypeStruct((steps, part, width), BF16),
        ),
        in_specs=[
            pl.BlockSpec((rows, tile), lambda i: (0, now(i))),
            pl.BlockSpec((rows, q_width), whole),
            pl.BlockSpec((rows, 2 * kv_width), whole),
            pl.BlockSpec((tile, q_width), lambda i: (now(i), 0)),
            pl.BlockSpec((2, tile, kv_width), lambda i: (0, now(i), 0)),
            pl.BlockSpec((tile, out_width), lambda i: (now(i), 0)),
        ],
        out_specs=(
            pl.BlockSpec((rows, tile), lambda i: (0, now(i))),
            pl.BlockSpec((1, part, width), lambda i: (jnp.maximum(i - 1, 0), 0, 0)),
        ),
        scratch_shapes=[
            pltpu.VMEM((2, 2, part, width), BF16),
            pltpu.VMEM((steps, part, width), BF16),
        ]
        + dma_sems(steps),
        cost_estimate=cost(1, 1),
        compiler_params=remote_params(12),
    )(x, q_back, kv_back, query_weight, keyvalue_weight, output_full)
    return in_partial, full.reshape(D // 2, width)


def rest_adamw_kernel(total_ref, *refs):
    q_width, kv_width = refs[0].shape[1], refs[4].shape[2]
    ins, outs = refs[:12], refs[12:]
    total = total_ref[...].astype(F32)
    rate = 2.0 * D ** (-0.5)
    for n, new in enumerate(
        adamw(total[:, :q_width], *[r[...] for r in ins[:4]], rate, WEIGHT_DECAY)
    ):
        outs[n][...] = new
    for k in range(2):
        low = q_width + k * kv_width
        for n, new in enumerate(
            adamw(total[:, low : low + kv_width], *[r[k] for r in ins[4:8]], rate, WEIGHT_DECAY)
        ):
            outs[5 + n][k] = new
    turned = jnp.transpose(total[:, q_width + 2 * kv_width :])
    for n, new in enumerate(
        adamw(turned, *[r[...] for r in ins[8:]], 2.0 * WO_FAN ** (-0.5), WEIGHT_DECAY)
    ):
        outs[10 + n][...] = new


def rest_adamw(total, query_state, keyvalue_state, output_state):
    tile = 128
    rows, width = total.shape
    q_spec = pl.BlockSpec((tile, query_state[0].shape[1]), lambda i: (i, 0))
    kv_spec = pl.BlockSpec((2, tile, keyvalue_state[0].shape[2]), lambda i: (0, i, 0))
    o_spec = pl.BlockSpec((output_state[0].shape[0], tile), lambda i: (0, i))
    like = lambda a: jax.ShapeDtypeStruct(a.shape, F32)
    out = pl.pallas_call(
        rest_adamw_kernel,
        name="rest_adamw",
        grid=(rows // tile,),
        out_shape=tuple(
            like(state[0]) for state in (query_state, keyvalue_state, output_state) for _ in range(5)
        ),
        in_specs=[pl.BlockSpec((tile, width), lambda i: (i, 0))]
        + [q_spec] * 4
        + [kv_spec] * 4
        + [o_spec] * 4,
        out_specs=tuple([q_spec] * 5 + [kv_spec] * 5 + [o_spec] * 5),
        compiler_params=params("arbitrary"),
        cost_estimate=cost(1, 1),
    )(total, *query_state, *keyvalue_state, *output_state)
    return out[:5], out[5:10], out[10:]


def wide_scatter(partial, axis):
    return lax.psum_scatter(partial, "wide", scatter_dimension=axis, tiled=True)


def line_scatter(partial, axis, count):
    groups = [[2 * z + c for z in range(count // 2)] for c in range(2)]
    return lax.psum_scatter(
        partial, "wide", scatter_dimension=axis, tiled=True, axis_index_groups=groups
    )


def body(
    tokens,
    cotangent,
    gain_copy,
    query_weight,
    keyvalue_weight,
    output_weight,
    gateup_weight,
    down_weight,
    query_master,
    query_moment,
    query_second,
    query_average,
    keyvalue_master,
    keyvalue_moment,
    keyvalue_second,
    keyvalue_average,
    output_master,
    output_moment,
    output_second,
    output_average,
    gateup_master,
    gateup_moment,
    gateup_second,
    gateup_average,
    down_master,
    down_moment,
    down_second,
    down_average,
    gain_master,
    gain_moment,
    gain_second,
    gain_average,
):
    narrow, wide = lax.axis_size("narrow"), lax.axis_size("wide")
    special = narrow == 4 and wide == 8
    stretch_rows = tokens.shape[0] * narrow
    wide_index = lax.axis_index("wide")
    w_scalar = wide_index.astype(jnp.int32).reshape(1)
    kv_heads = keyvalue_weight.shape[2] // HD
    q_heads = query_weight.shape[1] // HD
    group = q_heads // kv_heads
    q_width, kv_width = q_heads * HD, kv_heads * HD
    gains = gain_copy.reshape(-1, HD)

    positions = (wide_index * stretch_rows + jnp.arange(stretch_rows, dtype=jnp.int32)).astype(F32)
    cosine, sine = rope_tables(positions)
    if special:
        back_mlp, attn_input, query_low, query_raw, key_raw, kv_all, attn_out, attn_low, lse = front(
            tokens,
            cotangent,
            gains,
            query_weight,
            keyvalue_weight,
            cosine,
            sine,
            wide,
        )
    else:
        attn_gain = gain_copy[:D].reshape(1, D)
        mlp_gain = gain_copy[D : 2 * D].reshape(1, D)
        query_gain = gain_copy[2 * D : 2 * D + HD].reshape(1, HD)
        key_gain = gain_copy[2 * D + HD :].reshape(1, HD)
        hidden = tokens.astype(F32)
        normed = (hidden * row_scale(hidden) * attn_gain).astype(BF16)
        attn_input = lax.all_gather(normed, "narrow", axis=0, tiled=True)
        kv_low, key_raw = keys_values(attn_input, keyvalue_weight, key_gain, cosine, sine)
        query_low, query_raw = queries(attn_input, query_weight, query_gain, cosine, sine)
        kv_all = lax.all_gather(kv_low, "wide", axis=0)
        attn_out, attn_low, lse = attend(w_scalar, query_low, kv_all, q_heads, group)
        back_mlp = lax.all_gather(cotangent, "narrow", axis=0, tiled=True)
    if special:
        hidden_mid, mlp_input, act_grads, act, down_full = mid_pair(
            attn_low, output_weight, tokens, gains, back_mlp, gateup_weight, down_weight, wide
        )
        down_total = line_scatter(down_full, 0, wide)[0]
        mid_grad, back_attn, mlp_gain_grad, gateup_full = mid_backward_pair(
            hidden_mid, cotangent, gains, mlp_input, act_grads, gateup_weight, wide
        )
        gateup_total = line_scatter(gateup_full, 1, wide)
    else:
        hidden_mid, mlp_input = mid_forward(attn_low, output_weight, tokens, mlp_gain)
        act, act_grads, down_full = feed(mlp_input, back_mlp, gateup_weight, down_weight)
        down_total = wide_scatter(down_full, 1)
        gateup_full, in_partial, out_partial = feed_back(
            mlp_input, act, act_grads, gateup_weight, down_weight
        )
        gateup_total = wide_scatter(gateup_full, 1)
        mid_grad, back_attn, mlp_gain_grad = mid_backward(
            in_partial, hidden_mid, cotangent, mlp_gain
        )
    attn_grad, output_full = out_back(back_attn, output_weight, attn_low)
    query_sum, kv_sums = attend_back(
        w_scalar, query_low, kv_all, attn_grad, attn_out, lse, q_heads, group
    )
    query_back, query_gain_grad = unspin(query_sum, query_raw, gains, 2 * (D // HD), cosine, sine)
    if special:
        kv_sum, out_sum = return_grads_out(kv_sums, act, down_weight, tokens.shape[0], wide)
        block_output = hidden_mid + out_sum
    else:
        kv_sum = return_grads(kv_sums, wide)
        block_output = hidden_mid + lax.psum_scatter(
            out_partial, "narrow", scatter_dimension=0, tiled=True
        ).astype(F32)
    kv_back, key_gain_grad = unspin(kv_sum, key_raw, gains, 2 * (D // HD) + 1, cosine, sine)
    back_args = (attn_input, query_back, kv_back, query_weight, keyvalue_weight, output_full)
    if special:
        normed_partial, project_full = project_back_pair(*back_args, wide)
    else:
        normed_partial, project_full = project_back(*back_args)
    project_full, gateup_total, down_total, normed_partial = lax.optimization_barrier(
        (project_full, gateup_total, down_total, normed_partial)
    )
    rest_total = line_scatter(project_full, 0, wide) if special else wide_scatter(project_full, 0)
    in_norm_grad, attn_gain_grad = in_scatter(normed_partial, tokens, gains, special)
    input_grad = mid_grad + in_norm_grad
    gain_partial = jnp.concatenate(
        [attn_gain_grad, mlp_gain_grad, query_gain_grad, key_gain_grad], axis=1
    ).reshape(-1)
    gain_total = gain_sums(gain_partial, wide, narrow, special)

    rest_total, input_grad, block_output = lax.optimization_barrier(
        (rest_total, input_grad, block_output)
    )
    query_new, keyvalue_new, output_new = rest_adamw(
        rest_total,
        (query_master, query_moment, query_second, query_average),
        (keyvalue_master, keyvalue_moment, keyvalue_second, keyvalue_average),
        (output_master, output_moment, output_second, output_average),
    )
    gateup_new = adamw(
        gateup_total.astype(F32),
        gateup_master,
        gateup_moment,
        gateup_second,
        gateup_average,
        2.0 * D ** (-0.5),
        WEIGHT_DECAY,
    )
    down_new = adamw(
        down_total.astype(F32),
        down_master,
        down_moment,
        down_second,
        down_average,
        2.0 * FF ** (-0.5),
        WEIGHT_DECAY,
    )
    gain_new = adamw(
        gain_total, gain_master, gain_moment, gain_second, gain_average, RATE_GAIN, 0.0
    )
    return (
        block_output,
        input_grad,
        *query_new,
        *keyvalue_new,
        *output_new,
        *gateup_new,
        *down_new,
        *gain_new,
    )


def solution(mesh):
    rows = P(("wide", "narrow"), None)
    flat = P(("wide", "narrow"))
    stacked = P(None, "wide", "narrow")
    query, output = P("wide", "narrow"), P("narrow", "wide")
    states = (
        *[query] * 4,
        *[stacked] * 4,
        *[output] * 4,
        *[stacked] * 4,
        *[output] * 4,
        *[flat] * 4,
    )
    return jax.shard_map(
        body,
        mesh=mesh,
        in_specs=(
            rows,
            rows,
            P(),
            P(None, "narrow"),
            P(None, None, "narrow"),
            P("narrow", None),
            P(None, None, "narrow"),
            P("narrow", None),
            *states,
        ),
        out_specs=(
            rows,
            rows,
            *[query] * 5,
            *[stacked] * 5,
            *[output] * 5,
            *[stacked] * 5,
            *[output] * 5,
            *[flat] * 5,
        ),
        check_vma=False,
    )
```

```python
import functools

import jax
import jax.numpy as jnp
import numpy as np
from jax import lax
from jax.experimental import pallas as pl
from jax.experimental.pallas import tpu as pltpu
from jax.sharding import PartitionSpec as P

D = 2048
HD = 128
FF = 6144
STEP = 10
WO_FAN = 32

EPSILON = 1e-06
THETA = 1000000.0
BETA_ONE = 0.9
BETA_TWO = 0.999
ADAM_EPS = 1e-08
WEIGHT_DECAY = 0.1
EMA_KEEP = 0.5
RATE_GAIN = 0.4
FACTOR = HD ** (-0.5)
LOG2E = 1.4426950408889634

F32 = jnp.float32
BF16 = jnp.bfloat16
MESH = pl.DeviceIdType.MESH
VM = pl.BlockSpec(memory_space=pltpu.VMEM)
SM = pl.BlockSpec(memory_space=pltpu.SMEM)
VMEM_LIMIT = 60 << 20

NT = (((1,), (1,)), ((), ()))
TN = (((0,), (0,)), ((), ()))


def dot(left, right):
    return jnp.dot(left, right, preferred_element_type=F32)


def dot_nt(left, right):
    return lax.dot_general(left, right, NT, preferred_element_type=F32)


def dot_tn(left, right):
    return lax.dot_general(left, right, TN, preferred_element_type=F32)


def rope_freq():
    inverse_freq = THETA ** (-2.0 * np.arange(HD // 2, dtype=np.float64) / HD)
    return jnp.asarray(np.tile(inverse_freq, (8, 2)), dtype=F32)


def rope_table(positions):
    angles = positions[:, None] * rope_freq()[:1]
    first = jnp.arange(HD)[None, :] < HD // 2
    return jnp.where(first, jnp.cos(angles), jnp.sin(angles))


def cos_sin(table, turn):
    first = lax.broadcasted_iota(jnp.int32, table.shape, 1) < HD // 2
    other = turn(table)
    return jnp.where(first, table, other), jnp.where(first, -other, table)


def swap_lanes(table):
    return pltpu.roll(table, HD // 2, axis=1)


def adamw(gradient, master, moment, second, average, step_rate, decay_rate):
    moment_new = BETA_ONE * moment + (1.0 - BETA_ONE) * gradient
    second_new = BETA_TWO * second + (1.0 - BETA_TWO) * gradient * gradient
    moment_hat = moment_new / (1.0 - BETA_ONE**STEP)
    second_hat = second_new / (1.0 - BETA_TWO**STEP)
    master_new = master - step_rate * (
        moment_hat / (jnp.sqrt(second_hat) + ADAM_EPS) + decay_rate * master
    )
    average_new = EMA_KEEP * average + (1.0 - EMA_KEEP) * master_new
    return (gradient, master_new, moment_new, second_new, average_new)


def row_scale(values_in):
    return lax.rsqrt(jnp.mean(values_in * values_in, axis=-1, keepdims=True) + EPSILON)


def gain_row(g_ref, base):
    return jnp.concatenate([g_ref[base + j : base + j + 1, :] for j in range(D // HD)], axis=1)


def norm_back(gradient, unit_rows, inv_scale, gain):
    scaled = gradient * gain
    inner = scaled - unit_rows * jnp.mean(scaled * unit_rows, axis=-1, keepdims=True)
    return inv_scale * inner, jnp.sum(gradient * unit_rows, axis=0, keepdims=True)


def square():
    me = lax.axis_index("narrow")
    xn = me + 1 - 2 * (me % 2)
    yn = (me + 2) % 4
    dg = (xn + 2) % 4
    return me, xn, yn, dg


def greet(axis, peers):
    barrier = pltpu.get_barrier_semaphore()
    for peer in peers:
        pl.semaphore_signal(barrier, inc=1, device_id={axis: peer}, device_id_type=MESH)
    pl.semaphore_wait(barrier, len(peers))


class Copies:
    def __init__(self, send, recv):
        self.send, self.recv, self.sent = send, recv, []

    def make(self, src, dst, slot, peer):
        copy = pltpu.make_async_remote_copy(
            src_ref=src,
            dst_ref=dst,
            send_sem=self.send.at[slot],
            recv_sem=self.recv.at[slot],
            device_id={"narrow": peer},
            device_id_type=MESH,
        )
        self.sent.append(copy)
        return copy

    def go(self, src, dst, slot, peer):
        copy = self.make(src, dst, slot, peer)
        copy.start()
        return copy

    def finish(self):
        for copy in self.sent:
            copy.wait_send()


def scatter_square(copies, slot, p_ref, buf, stage, emit, fill=None, early=None, middle=None):
    me, xn, yn, dg = square()
    rows = p_ref.shape[0] // 4
    half = rows // 2

    def part(owner, low):
        return p_ref.at[pl.ds(pl.multiple_of(owner * rows + low, half), half)]

    c0 = copies.make(part(dg, 0), buf.at[0], slot, xn)
    c1 = copies.make(part(dg, half), buf.at[1], slot + 1, yn)
    c2 = copies.make(part(xn, 0), buf.at[2], slot + 2, xn)
    c3 = copies.make(part(yn, half), buf.at[3], slot + 3, yn)
    if fill is None:
        for copy in (c0, c1, c2, c3):
            copy.start()
    else:

        @pl.loop(0, 4)
        def _(k):
            fill(jnp.where(k == 0, dg, jnp.where(k == 1, xn, jnp.where(k == 2, yn, me))), k)
            for n, ready in ((0, (c0, c1)), (1, (c2,)), (2, (c3,))):

                @pl.when(k == n)
                def _():
                    for copy in ready:
                        copy.start()

    if early is not None:
        early()
    c0.wait_recv()
    stage[0] = (part(yn, 0)[...].astype(F32) + buf[0].astype(F32)).astype(BF16)
    c4 = copies.go(stage.at[0], buf.at[4], slot + 4, yn)
    c1.wait_recv()
    stage[1] = (part(xn, half)[...].astype(F32) + buf[1].astype(F32)).astype(BF16)
    c5 = copies.go(stage.at[1], buf.at[5], slot + 5, xn)
    if middle is not None:
        middle()
    c2.wait_recv()
    c4.wait_recv()
    emit(0, part(me, 0)[...].astype(F32) + buf[2].astype(F32) + buf[4].astype(F32))
    c3.wait_recv()
    c5.wait_recv()
    emit(half, part(me, half)[...].astype(F32) + buf[3].astype(F32) + buf[5].astype(F32))


def exchange_square(copies, p_ref, buf, stage, own, o_ref, emit, fill, early, middle, use=None, relay=None):
    me, xn, yn, dg = square()
    rows = p_ref.shape[0] // 4
    group, piece = rows // 2, rows // 4

    def at(ref, owner, g, h):
        return ref.at[pl.ds(pl.multiple_of(owner * rows + g * group + h * piece, piece), piece)]

    def mine(g, h):
        return own.at[pl.ds(g * group + h * piece, piece)]

    sums, firsts, relays = [], [], []
    for g in range(2):
        s, t = 6 * g, 12 + 6 * g
        sums.append(
            (
                copies.make(at(p_ref, dg, g, 0), buf.at[g, 0], s, xn),
                copies.make(at(p_ref, dg, g, 1), buf.at[g, 1], s + 1, yn),
                copies.make(at(p_ref, xn, g, 0), buf.at[g, 2], s + 2, xn),
                copies.make(at(p_ref, yn, g, 1), buf.at[g, 3], s + 3, yn),
                copies.make(stage.at[g, 0], buf.at[g, 4], s + 4, yn),
                copies.make(stage.at[g, 1], buf.at[g, 5], s + 5, xn),
            )
        )
        firsts.append(
            (
                copies.make(mine(g, 0), at(o_ref, me, g, 0), t, xn),
                copies.make(mine(g, 1), at(o_ref, me, g, 1), t + 1, yn),
                copies.make(mine(g, 1), at(o_ref, me, g, 1), t + 2, xn),
                copies.make(mine(g, 0), at(o_ref, me, g, 0), t + 3, yn),
            )
        )
        relays.append(
            (
                copies.make(at(o_ref, xn, g, 0), at(o_ref, xn, g, 0), t + 4, yn),
                copies.make(at(o_ref, yn, g, 1), at(o_ref, yn, g, 1), t + 5, xn),
            )
        )

    def merge(g):
        for h, other in ((0, yn), (1, xn)):
            sums[g][h].wait_recv()
            stage[g, h] = (at(p_ref, other, g, h)[...].astype(F32) + buf[g, h].astype(F32)).astype(
                BF16
            )
            sums[g][4 + h].start()

    def close(g):
        for h in range(2):
            sums[g][2 + h].wait_recv()
            sums[g][4 + h].wait_recv()
            emit(
                g * group + h * piece,
                piece,
                at(p_ref, me, g, h)[...].astype(F32)
                + buf[g, 2 + h].astype(F32)
                + buf[g, 4 + h].astype(F32),
            )
        for copy in firsts[g]:
            copy.start()

    @pl.loop(0, 4)
    def _(k):
        fill(jnp.where(k == 0, dg, jnp.where(k == 1, xn, jnp.where(k == 2, yn, me))), k)
        for n, ready in ((0, sums[0][:2]), (1, sums[0][2:3]), (2, sums[0][3:4])):

            @pl.when(k == n)
            def _():
                for copy in ready:
                    copy.start()

    merge(0)
    for copy in sums[1][:4]:
        copy.start()
    early()
    merge(1)
    close(0)
    middle()
    close(1)
    o_ref[pl.ds(pl.multiple_of(me * rows, rows), rows)] = own[...]

    def pass_on():
        for g in range(2):
            for h in range(2):
                firsts[g][h].wait_recv()
                relays[g][h].start()
        if relay is not None:
            relay()
        for g in range(2):
            firsts[g][2].wait_recv()

    def from_y():
        for g in range(2):
            firsts[g][3].wait_recv()

    def from_far():
        for g in range(2):
            for copy in relays[g]:
                copy.wait_recv()

    if use is None:
        pass_on()
        from_y()
        from_far()
        return

    @pl.loop(0, 4)
    def _(k):
        pl.when(k == 1)(pass_on)
        pl.when(k == 2)(from_y)
        pl.when(k == 3)(from_far)
        use(jnp.where(k == 0, me, jnp.where(k == 1, xn, jnp.where(k == 2, yn, dg))))


def exchange_space(rows):
    return [pltpu.VMEM((2, 6, rows // 4, D), BF16), pltpu.VMEM((2, 2, rows // 4, D), BF16)]


def dma_sems(count):
    return [pltpu.SemaphoreType.DMA((count,)), pltpu.SemaphoreType.DMA((count,))]


def scatter_space(rows):
    return [pltpu.VMEM((6, rows // 2, D), BF16), pltpu.VMEM((2, rows // 2, D), BF16)]


def remote_params(collective_id):
    return pltpu.CompilerParams(
        collective_id=collective_id, has_side_effects=True, vmem_limit_bytes=VMEM_LIMIT
    )


def mid_kernel(
    t_ref, g_ref, a_hbm, w_hbm, dy_hbm, gu_hbm, d_hbm,
    h_ref, x_hbm, grad_hbm, act_hbm, down_hbm,
    a_ref, w_ref, p_ref, buf, stage, own, x, weight, dy, down, act_grad, grad, act, mine, theirs, inbox,
    send, recv, m_send, m_recv, load_sem, store_sem, down_sem,
):
    me, xn, yn, dg = square()
    c, mate = mate_of()
    rows = t_ref.shape[0]
    half = rows // 2
    tiles, tile, part = inbox.shape[0], inbox.shape[2], inbox.shape[3]
    loads = [
        pltpu.make_async_copy(src, dst, load_sem.at[n])
        for n, (src, dst) in enumerate(((a_hbm, a_ref), (w_hbm, w_ref), (gu_hbm, weight)))
    ]
    for n, (src, dst) in enumerate(((dy_hbm, dy), (d_hbm, down))):
        for k in range(D // part):
            loads.append(
                pltpu.make_async_copy(
                    src.at[:, pl.ds(k * part, part)],
                    dst.at[k % 2, :, pl.ds(k // 2 * part, part)],
                    load_sem.at[3 + n * (D // part) + k],
                )
            )
    for load in loads[:2] + loads[3:] + loads[2:3]:
        load.start()
    barrier = pltpu.get_barrier_semaphore()
    for peer in (xn, yn):
        pl.semaphore_signal(barrier, inc=1, device_id={"narrow": peer}, device_id_type=MESH)
    pl.semaphore_signal(barrier, inc=1, device_id={"wide": mate}, device_id_type=MESH)
    pl.semaphore_wait(barrier, 3)
    copies = Copies(send, recv)

    def rows_of(owner):
        return pl.ds(pl.multiple_of(owner * rows, rows), rows)

    loads[0].wait()
    loads[1].wait()

    def fill(owner, k):
        p_ref[rows_of(owner), :] = dot(a_ref[rows_of(owner), :], w_ref[...]).astype(BF16)

    gain = gain_row(g_ref, D // HD)

    def emit(low, size, total):
        hidden = t_ref[pl.ds(low, size)].astype(F32) + total
        h_ref[pl.ds(low, size)] = hidden
        own[pl.ds(low, size)] = (hidden * row_scale(hidden) * gain).astype(BF16)

    def act_grads(low, high):
        @pl.loop(low, high)
        def _(t):
            cols = pl.ds(pl.multiple_of(t * tile, tile), tile)
            act_grad[:, cols] = dot_nt(dy[0], down[0, cols, :]) + dot_nt(dy[1], down[1, cols, :])

    def early():
        for load in loads[3:]:
            load.wait()
        act_grads(0, tiles // 2)

    def middle():
        act_grads(tiles // 2, tiles)
        loads[2].wait()

    def expand(owner, t):
        at = rows_of(owner)
        cols = pl.ds(pl.multiple_of(t * tile, tile), tile)
        gate = dot(x[at, :], weight[0, :, cols])
        upper = dot(x[at, :], weight[1, :, cols])
        sig = jax.nn.sigmoid(gate)
        swish = gate * sig
        back = act_grad[at, cols]
        act[at, cols] = (swish * upper).astype(BF16)
        grad[0, at, cols] = (back * upper * sig * (1.0 + gate * (1.0 - sig))).astype(BF16)
        grad[1, at, cols] = (back * swish).astype(BF16)

    def use(owner):
        @pl.loop(0, tiles)
        def _(t):
            expand(owner, t)

    def trade(t):
        return wide_copy(theirs.at[t], inbox.at[t], m_send, m_recv, t, mate)

    def keep(t):
        at = pl.ds(pl.multiple_of(t * tile, tile), tile)
        return pltpu.make_async_copy(mine.at[t], down_hbm.at[:, at], down_sem.at[t])

    exchange_square(copies, p_ref, buf, stage, own, x, emit, fill, early, middle, use)
    stores = [
        pltpu.make_async_copy(src, dst, store_sem.at[n])
        for n, (src, dst) in enumerate(((x, x_hbm), (grad, grad_hbm), (act, act_hbm)))
    ]
    for store in stores:
        store.start()

    @pl.loop(0, tiles)
    def _(t):
        cols = pl.ds(pl.multiple_of(t * tile, tile), tile)
        half_full = dot_tn(act[:, cols], dy[1 - c]).astype(BF16)
        for k in range(D // part // 2):
            theirs[t, k] = half_full[:, k * part : (k + 1) * part]
        trade(t).start()

    @pl.loop(0, tiles)
    def _(t):
        trade(t).wait_recv()
        cols = pl.ds(pl.multiple_of(t * tile, tile), tile)
        half_full = dot_tn(act[:, cols], dy[c])
        for k in range(D // part // 2):
            mine[t, k] = (half_full[:, k * part : (k + 1) * part] + inbox[t, k].astype(F32)).astype(
                BF16
            )
        keep(t).start()

    copies.finish()

    @pl.loop(0, tiles)
    def _(t):
        trade(t).wait_send()
        keep(t).wait()

    for store in stores:
        store.wait()


def mid_pair(attn_low, weight, tokens, gains, dy, gateup_weight, down_weight, count):
    rows = tokens.shape[0]
    width = gateup_weight.shape[2]
    tile, part, chips = 256, D // count, count // 2
    tiles = width // tile
    anywhere = pl.BlockSpec(memory_space=pl.ANY)
    return pl.pallas_call(
        mid_kernel,
        name="mid_pair",
        out_shape=(
            jax.ShapeDtypeStruct((rows, D), F32),
            jax.ShapeDtypeStruct((4 * rows, D), BF16),
            jax.ShapeDtypeStruct((2, 4 * rows, width), BF16),
            jax.ShapeDtypeStruct((4 * rows, width), BF16),
            jax.ShapeDtypeStruct((chips, width, part), BF16),
        ),
        in_specs=[VM] * 2 + [anywhere] * 5,
        out_specs=(VM,) + (anywhere,) * 4,
        scratch_shapes=[
            pltpu.VMEM(attn_low.shape, BF16),
            pltpu.VMEM(weight.shape, BF16),
            pltpu.VMEM((4 * rows, D), BF16),
        ]
        + exchange_space(rows)
        + [
            pltpu.VMEM((rows, D), BF16),
            pltpu.VMEM((4 * rows, D), BF16),
            pltpu.VMEM((2, D, width), BF16),
            pltpu.VMEM((2, 4 * rows, D // 2), BF16),
            pltpu.VMEM((2, width, D // 2), BF16),
            pltpu.VMEM((4 * rows, width), F32),
            pltpu.VMEM((2, 4 * rows, width), BF16),
            pltpu.VMEM((4 * rows, width), BF16),
            pltpu.VMEM((tiles, chips, tile, part), BF16),
            pltpu.VMEM((tiles, chips, tile, part), BF16),
            pltpu.VMEM((tiles, chips, tile, part), BF16),
        ]
        + dma_sems(24)
        + dma_sems(tiles)
        + [
            pltpu.SemaphoreType.DMA((3 + 2 * count,)),
            pltpu.SemaphoreType.DMA((3,)),
            pltpu.SemaphoreType.DMA((tiles,)),
        ],
        cost_estimate=cost(1, 1),
        compiler_params=remote_params(2),
    )(tokens, gains, attn_low, weight, dy, gateup_weight, down_weight)


def mid_forward(attn_low, weight, tokens, gain):
    partial = dot(attn_low, weight).astype(BF16)
    hidden = tokens.astype(F32) + lax.psum_scatter(
        partial, "narrow", scatter_dimension=0, tiled=True
    ).astype(F32)
    normed = (hidden * row_scale(hidden) * gain).astype(BF16)
    return hidden, lax.all_gather(normed, "narrow", axis=0, tiled=True)


def mid_backward_kernel(
    h_ref, c_ref, g_ref, x_hbm, grad_hbm, gu_hbm,
    m_ref, o_ref, gg_ref, full_hbm,
    p_ref, buf, stage, own, x, grad, weight, mine, inbox,
    send, recv, m_send, m_recv, load_sem, full_sem,
):
    me, xn, yn, dg = square()
    c, mate = mate_of()
    half = h_ref.shape[0] // 2
    tiles, part, tile = inbox.shape[0], inbox.shape[3], inbox.shape[4]
    def load_weight(t):
        rows_at = pl.ds(pl.multiple_of(t * 512, 512), 512)
        return pltpu.make_async_copy(
            gu_hbm.at[:, rows_at], weight.at[:, rows_at], load_sem.at[2 + t]
        )

    loads = [
        pltpu.make_async_copy(src, dst, load_sem.at[n])
        for n, (src, dst) in enumerate(((grad_hbm, grad), (x_hbm, x)))
    ]
    loads[0].start()
    for t in range(D // 512):
        load_weight(t).start()
    loads[1].start()
    barrier = pltpu.get_barrier_semaphore()
    for peer in (xn, yn):
        pl.semaphore_signal(barrier, inc=1, device_id={"narrow": peer}, device_id_type=MESH)
    pl.semaphore_signal(barrier, inc=1, device_id={"wide": mate}, device_id_type=MESH)
    pl.semaphore_wait(barrier, 3)
    copies = Copies(send, recv)
    gg_ref[...] = jnp.zeros_like(gg_ref)
    gain = gain_row(g_ref, D // HD)

    def emit(low, size, total):
        hidden = h_ref[pl.ds(low, size)]
        scale = row_scale(hidden)
        back, gain_sum = norm_back(total, hidden * scale, scale, gain)
        gg_ref[...] += gain_sum
        mid = c_ref[pl.ds(low, size)].astype(F32) + back
        m_ref[pl.ds(low, size)] = mid
        own[pl.ds(low, size)] = mid.astype(BF16)

    def trade(t):
        return wide_copy(mine.at[t, 1 - c], inbox.at[t], m_send, m_recv, t, mate)

    def keep(t):
        cols = pl.ds(pl.multiple_of(t * tile, tile), tile)
        return pltpu.make_async_copy(mine.at[t, c], full_hbm.at[:, :, :, cols], full_sem.at[t])

    def products(low, high):
        @pl.loop(low, high)
        def _(t):
            cols = pl.ds(pl.multiple_of(t * tile, tile), tile)
            for n in range(2):
                full = dot_tn(x[...], grad[n, :, cols]).astype(BF16)
                for k in range(D // part):
                    mine[t, k % 2, n, k // 2] = full[k * part : (k + 1) * part]
            trade(t).start()

    rows = 2 * half
    loads[0].wait()

    def fill(owner, k):
        at = pl.ds(pl.multiple_of(owner * rows, rows), rows)

        @pl.loop(0, D // 512)
        def _(t):
            pl.when(k == 0)(load_weight(t).wait)
            cols = pl.ds(pl.multiple_of(t * 512, 512), 512)
            p_ref[at, cols] = (
                dot_nt(grad[0, at, :], weight[0, cols, :])
                + dot_nt(grad[1, at, :], weight[1, cols, :])
            ).astype(BF16)

    def early():
        loads[1].wait()
        products(0, tiles // 2)

    def middle():
        products(tiles // 2, tiles)

    def relay():
        @pl.loop(0, tiles)
        def _(t):
            trade(t).wait_recv()
            mine[t, c] = (mine[t, c].astype(F32) + inbox[t].astype(F32)).astype(BF16)
            keep(t).start()

    exchange_square(copies, p_ref, buf, stage, own, o_ref, emit, fill, early, middle, relay=relay)
    copies.finish()

    @pl.loop(0, tiles)
    def _(t):
        trade(t).wait_send()
        keep(t).wait()


def mid_backward_pair(hidden_mid, cotangent, gains, x, grads, gateup_weight, count):
    rows = hidden_mid.shape[0]
    width = grads.shape[2]
    tile, part, chips = 256, D // count, count // 2
    tiles = width // tile
    anywhere = pl.BlockSpec(memory_space=pl.ANY)
    mid_grad, back_attn, gain_sum, full = pl.pallas_call(
        mid_backward_kernel,
        name="mid_backward_pair",
        out_shape=(
            jax.ShapeDtypeStruct((rows, D), F32),
            jax.ShapeDtypeStruct((4 * rows, D), BF16),
            jax.ShapeDtypeStruct((1, D), F32),
            jax.ShapeDtypeStruct((2, chips, part, width), BF16),
        ),
        in_specs=[VM] * 3 + [anywhere] * 3,
        out_specs=(VM,) * 3 + (anywhere,),
        scratch_shapes=[pltpu.VMEM((4 * rows, D), BF16)]
        + exchange_space(rows)
        + [
            pltpu.VMEM((rows, D), BF16),
            pltpu.VMEM(x.shape, BF16),
            pltpu.VMEM(grads.shape, BF16),
            pltpu.VMEM(gateup_weight.shape, BF16),
            pltpu.VMEM((tiles, 2, 2, chips, part, tile), BF16),
            pltpu.VMEM((tiles, 2, chips, part, tile), BF16),
        ]
        + dma_sems(24)
        + dma_sems(tiles)
        + [pltpu.SemaphoreType.DMA((2 + D // 512,)), pltpu.SemaphoreType.DMA((tiles,))],
        cost_estimate=cost(1, 1),
        compiler_params=remote_params(3),
    )(hidden_mid, cotangent, gains, x, grads, gateup_weight)
    return mid_grad, back_attn, gain_sum, full.reshape(2, D // 2, width)


def mid_backward(partial, hidden_mid, cotangent, gain):
    total = lax.psum_scatter(partial, "narrow", scatter_dimension=0, tiled=True).astype(F32)
    scale = row_scale(hidden_mid)
    back, gain_sum = norm_back(total, hidden_mid * scale, scale, gain)
    mid = cotangent.astype(F32) + back
    return mid, lax.all_gather(mid.astype(BF16), "narrow", axis=0, tiled=True), gain_sum


def in_scatter_kernel(p_ref, t_ref, g_ref, o_ref, gg_ref, buf, stage, send, recv):
    _, xn, yn, _ = square()
    half = t_ref.shape[0] // 2
    greet("narrow", (xn, yn))
    copies = Copies(send, recv)
    gg_ref[...] = jnp.zeros_like(gg_ref)
    gain = gain_row(g_ref, 0)

    def emit(low, total):
        hidden = t_ref[pl.ds(low, half)].astype(F32)
        scale = row_scale(hidden)
        back, gain_sum = norm_back(total, hidden * scale, scale, gain)
        gg_ref[...] += gain_sum
        o_ref[pl.ds(low, half)] = back

    scatter_square(copies, 0, p_ref, buf, stage, emit)
    copies.finish()


def in_scatter(partial, tokens, gains, special):
    rows = tokens.shape[0]
    if not special:
        total = lax.psum_scatter(partial, "narrow", scatter_dimension=0, tiled=True).astype(F32)
        hidden = tokens.astype(F32)
        scale = row_scale(hidden)
        back, gain_sum = norm_back(total, hidden * scale, scale, gains[: D // HD].reshape(1, D))
        return back, gain_sum
    return pl.pallas_call(
        in_scatter_kernel,
        name="in_scatter",
        out_shape=(
            jax.ShapeDtypeStruct((rows, D), F32),
            jax.ShapeDtypeStruct((1, D), F32),
        ),
        in_specs=[VM] * 3,
        out_specs=(VM,) * 2,
        scratch_shapes=scatter_space(rows) + dma_sems(6),
        cost_estimate=cost(1, 1),
        compiler_params=remote_params(4),
    )(partial, tokens, gains)


def line(count):
    w = lax.axis_index("wide")
    z, c = w // 2, w % 2
    return w, z, c, count // 2, w + 1 - 2 * c, jnp.minimum(w + 2, count - 1), jnp.maximum(w - 2, 0)


def wide_copy(src, dst, send, recv, slot, peer):
    return pltpu.make_async_remote_copy(
        src_ref=src,
        dst_ref=dst,
        send_sem=send.at[slot],
        recv_sem=recv.at[slot],
        device_id={"wide": peer},
        device_id_type=MESH,
    )


def return_grads_kernel(
    count, x_ref, act_hbm, d_hbm, o_ref, b_ref,
    from_mate, from_above, stage, p_ref, buf, out_stage, act, weight,
    send, recv, mate_send, mate_recv, n_send, n_recv, load_sem,
):
    w, z, c, chips, mate, above, below = line(count)
    me, xn, yn, dg = square()
    rows = b_ref.shape[0]
    half = rows // 2
    loads = [
        pltpu.make_async_copy(src, dst, load_sem.at[n])
        for n, (src, dst) in enumerate(((act_hbm, act), (d_hbm, weight)))
    ]
    for load in loads:
        load.start()
    has_above, has_below = z < chips - 1, z > 0
    barrier = pltpu.get_barrier_semaphore()
    for peer in (xn, yn):
        pl.semaphore_signal(barrier, inc=1, device_id={"narrow": peer}, device_id_type=MESH)

    @pl.when(has_above)
    def _():
        pl.semaphore_signal(barrier, inc=1, device_id={"wide": above}, device_id_type=MESH)

    @pl.when(has_below)
    def _():
        pl.semaphore_signal(barrier, inc=1, device_id={"wide": below}, device_id_type=MESH)

    pl.semaphore_signal(barrier, inc=1, device_id={"wide": mate}, device_id_type=MESH)
    pl.semaphore_wait(barrier, 3 + has_above.astype(jnp.int32) + has_below.astype(jnp.int32))

    def to_mate(s):
        return wide_copy(
            x_ref.at[jnp.minimum(2 * s + 1 - c, count - 1)],
            from_mate.at[s],
            mate_send,
            mate_recv,
            s,
            mate,
        )

    def sends_mate(s):
        return (z > s) | ((z == s) & (c == 1))

    def down(s):
        return wide_copy(stage.at[s], from_above.at[s], send, recv, s, below)

    for s in range(chips):

        @pl.when(sends_mate(s))
        def _():
            to_mate(s).start()

    def chain():
        for s in range(chips - 1):
            block = 2 * s + c

            @pl.when(z > s)
            def _():
                to_mate(s).wait_recv()

                @pl.when(z == chips - 1)
                def _():
                    stage[s] = (x_ref[block].astype(F32) + from_mate[s].astype(F32)).astype(BF16)

                @pl.when(z < chips - 1)
                def _():
                    down(s).wait_recv()
                    stage[s] = (
                        x_ref[block].astype(F32)
                        + from_mate[s].astype(F32)
                        + from_above[s].astype(F32)
                    ).astype(BF16)

                down(s).start()

    def emit(low, total):
        b_ref[pl.ds(low, half)] = total

    def fill(owner, k):
        at = pl.ds(pl.multiple_of(owner * rows, rows), rows)

        @pl.loop(0, D // 512)
        def _(t):
            cols = pl.ds(pl.multiple_of(t * 512, 512), 512)
            p_ref[at, cols] = dot(act[at, :], weight[:, cols]).astype(BF16)

    for load in loads:
        load.wait()
    copies = Copies(n_send, n_recv)
    scatter_square(copies, 0, p_ref, buf, out_stage, emit, fill, middle=chain)
    for s in range(chips):
        block = 2 * s + c

        @pl.when(z == s)
        def _():
            o_ref[...] = x_ref[block].astype(F32)

            @pl.when(c == 0)
            def _():
                to_mate(s).wait_recv()
                o_ref[...] += from_mate[s].astype(F32)

            if s < chips - 1:
                down(s).wait_recv()
                o_ref[...] += from_above[s].astype(F32)

    copies.finish()
    for s in range(chips):

        @pl.when(sends_mate(s))
        def _():
            to_mate(s).wait_send()

        @pl.when(z > s)
        def _():
            down(s).wait_send()


def return_grads_out(grads, act, down_weight, own_rows, count):
    _, rows, width = grads.shape
    chips = count // 2
    return pl.pallas_call(
        functools.partial(return_grads_kernel, count),
        name="return_grads",
        out_shape=(
            jax.ShapeDtypeStruct((rows, width), F32),
            jax.ShapeDtypeStruct((own_rows, D), F32),
        ),
        in_specs=[VM] + [pl.BlockSpec(memory_space=pl.ANY)] * 2,
        out_specs=(VM, VM),
        scratch_shapes=[
            pltpu.VMEM((chips, rows, width), BF16),
            pltpu.VMEM((chips, rows, width), BF16),
            pltpu.VMEM((chips, rows, width), BF16),
            pltpu.VMEM((act.shape[0], D), BF16),
        ]
        + scatter_space(own_rows)
        + [pltpu.VMEM(act.shape, BF16), pltpu.VMEM(down_weight.shape, BF16)]
        + dma_sems(chips)
        + dma_sems(chips)
        + dma_sems(6)
        + [pltpu.SemaphoreType.DMA((2,))],
        cost_estimate=cost(1, 1),
        compiler_params=remote_params(6),
    )(grads, act, down_weight)


def return_grads(grads, count):
    _, rows, width = grads.shape
    w = lax.axis_index("wide")
    seen = (jnp.arange(count) <= w)[:, None, None]
    total = lax.psum_scatter(
        jnp.where(seen, grads, 0).reshape(count * rows, width),
        "wide",
        scatter_dimension=0,
        tiled=True,
    )
    return total.astype(F32)


def gain_kernel(wide, x_ref, o_ref, near, mid, far, send, recv, wide_send, wide_recv):
    me, xn, yn, dg = square()
    w = lax.axis_index("wide")
    barrier = pltpu.get_barrier_semaphore()
    for peer in (xn, yn, dg):
        pl.semaphore_signal(barrier, inc=1, device_id={"narrow": peer}, device_id_type=MESH)
    for step in range(1, wide):
        pl.semaphore_signal(
            barrier, inc=1, device_id={"wide": (w + step) % wide}, device_id_type=MESH
        )
    pl.semaphore_wait(barrier, 3 + wide - 1)
    copies = Copies(send, recv)
    sent = [
        copies.go(x_ref.at[peer], near.at[slot], slot, peer)
        for slot, peer in enumerate((xn, yn, dg))
    ]
    for copy in sent:
        copy.wait_recv()
    mid[...] = x_ref[me] + near[0] + near[1] + near[2]
    away = []
    for step in range(1, wide):
        peer = (w + step) % wide
        copy = wide_copy(
            mid.at[peer], far.at[step - 1], wide_send, wide_recv, step - 1, peer
        )
        copy.start()
        away.append(copy)
    total = mid[w]
    for step in range(1, wide):
        away[step - 1].wait_recv()
        total = total + far[step - 1]
    o_ref[...] = total
    copies.finish()
    for copy in away:
        copy.wait_send()


def gain_sums(partial, wide, narrow, special):
    if not special:
        return lax.psum_scatter(partial, ("wide", "narrow"), scatter_dimension=0, tiled=True)
    count = partial.shape[0] // (wide * narrow)
    padded = -(-count // 128) * 128
    shaped = partial.reshape(wide, narrow, count).transpose(1, 0, 2)
    shaped = jnp.pad(shaped, ((0, 0), (0, 0), (0, padded - count)))
    shaped = shaped.reshape(narrow, wide, padded // 128, 128)
    out = pl.pallas_call(
        functools.partial(gain_kernel, wide),
        name="gain_sums",
        out_shape=jax.ShapeDtypeStruct((padded // 128, 128), F32),
        in_specs=[VM],
        out_specs=VM,
        scratch_shapes=[
            pltpu.VMEM((3, wide, padded // 128, 128), F32),
            pltpu.VMEM((wide, padded // 128, 128), F32),
            pltpu.VMEM((wide - 1, padded // 128, 128), F32),
        ]
        + dma_sems(3)
        + dma_sems(wide - 1),
        cost_estimate=cost(1, 1),
        compiler_params=remote_params(7),
    )(shaped)
    return out.reshape(padded)[:count]


def cost(flops, moved, exps=0):
    return pl.CostEstimate(flops=1, bytes_accessed=1, transcendentals=0)


def params(*semantics):
    if not semantics:
        return pltpu.CompilerParams(vmem_limit_bytes=VMEM_LIMIT)
    return pltpu.CompilerParams(vmem_limit_bytes=VMEM_LIMIT, dimension_semantics=semantics)


def spin(raw, gain_row, cosine, sine):
    normed = raw * row_scale(raw) * gain_row
    return normed * cosine + pltpu.roll(normed, HD // 2, axis=1) * sine


def keys_kernel(x_ref, w_ref, g_ref, cos_ref, sin_ref, kv_ref, raw_ref):
    which = pl.program_id(0)
    width = w_ref.shape[2]
    out = dot(x_ref[...], w_ref[0])

    @pl.when(which == 0)
    def _():
        raw_ref[...] = out
        for h in range(width // HD):
            part = out[:, h * HD : (h + 1) * HD]
            kv_ref[:, h * HD : (h + 1) * HD] = spin(
                part, g_ref[...], cos_ref[...], sin_ref[...]
            ).astype(BF16)

    @pl.when(which == 1)
    def _():
        kv_ref[...] = out.astype(BF16)


def keys_values(x, weight, gain_row, cosine, sine):
    rows, width = x.shape[0], weight.shape[2]
    whole = lambda i: (0, 0)
    return pl.pallas_call(
        keys_kernel,
        name="keys_values",
        grid=(2,),
        out_shape=(
            jax.ShapeDtypeStruct((rows, 2 * width), BF16),
            jax.ShapeDtypeStruct((rows, width), F32),
        ),
        in_specs=[
            pl.BlockSpec((rows, D), whole),
            pl.BlockSpec((1, D, width), lambda i: (i, 0, 0)),
            pl.BlockSpec((1, HD), whole),
            pl.BlockSpec((rows, HD), whole),
            pl.BlockSpec((rows, HD), whole),
        ],
        out_specs=(
            pl.BlockSpec((rows, width), lambda i: (0, i)),
            pl.BlockSpec((rows, width), whole),
        ),
        compiler_params=params("arbitrary"),
        cost_estimate=cost(4 * rows * D * width, 2 * rows * D + 4 * D * width),
    )(x, weight, gain_row, cosine, sine)


def queries_kernel(x_ref, w_ref, g_ref, cos_ref, sin_ref, q_ref, raw_ref):
    out = dot(x_ref[...], w_ref[...])
    raw_ref[...] = out
    for h in range(w_ref.shape[1] // HD):
        part = out[:, h * HD : (h + 1) * HD]
        q_ref[:, h * HD : (h + 1) * HD] = spin(
            part, g_ref[...], cos_ref[...], sin_ref[...]
        ).astype(BF16)


def queries(x, weight, gain_row, cosine, sine):
    rows, width = x.shape[0], weight.shape[1]
    tile = 256
    whole = lambda i: (0, 0)
    return pl.pallas_call(
        queries_kernel,
        name="queries",
        grid=(width // tile,),
        out_shape=(
            jax.ShapeDtypeStruct((rows, width), BF16),
            jax.ShapeDtypeStruct((rows, width), F32),
        ),
        in_specs=[
            pl.BlockSpec((rows, D), whole),
            pl.BlockSpec((D, tile), lambda i: (0, i)),
            pl.BlockSpec((1, HD), whole),
            pl.BlockSpec((rows, HD), whole),
            pl.BlockSpec((rows, HD), whole),
        ],
        out_specs=(
            pl.BlockSpec((rows, tile), lambda i: (0, i)),
            pl.BlockSpec((rows, tile), lambda i: (0, i)),
        ),
        compiler_params=params("arbitrary"),
        cost_estimate=cost(2 * rows * D * width, 2 * rows * D + 2 * D * width),
    )(x, weight, gain_row, cosine, sine)


def attend_kernel(heads, group, w_ref, q_ref, kv_ref, o_ref, low_ref, lse_ref, acc):
    rows = q_ref.shape[0]
    kv_width = kv_ref.shape[2] // 2
    w = w_ref[0]
    acc[...] = jnp.zeros_like(acc)
    ones = jnp.ones((rows, HD), BF16)

    def block(j, masked):
        for h in range(heads):
            kv = h // group
            key = kv_ref[j, :, kv * HD : (kv + 1) * HD]
            value = kv_ref[j, :, kv_width + kv * HD : kv_width + (kv + 1) * HD]
            query = q_ref[:, h * HD : (h + 1) * HD]
            terms = jnp.exp2(dot_nt(query, key) * (FACTOR * LOG2E))
            if masked:
                at = lax.broadcasted_iota(jnp.int32, (rows, rows), 0)
                key_at = lax.broadcasted_iota(jnp.int32, (rows, rows), 1)
                terms = jnp.where(key_at <= at, terms, 0.0)
            acc[h] += dot(terms.astype(BF16), jnp.concatenate([value, ones], axis=1))

    @pl.loop(0, w)
    def _(j):
        block(j, False)

    block(w, True)
    for h in range(heads):
        total = acc[h, :, HD:]
        out = acc[h, :, :HD] / total
        o_ref[:, h * HD : (h + 1) * HD] = out
        low_ref[:, h * HD : (h + 1) * HD] = out.astype(BF16)
        lse_ref[h : h + 1, :] = jnp.transpose(jnp.log2(total))[0:1]


def attend(w_index, query, kv_all, heads, group):
    rows, width = query.shape
    count = kv_all.shape[0]
    return pl.pallas_call(
        functools.partial(attend_kernel, heads, group),
        name="attend",
        out_shape=(
            jax.ShapeDtypeStruct((rows, width), F32),
            jax.ShapeDtypeStruct((rows, width), BF16),
            jax.ShapeDtypeStruct((heads, rows), F32),
        ),
        in_specs=[SM, VM, VM],
        out_specs=(VM, VM, VM),
        scratch_shapes=[pltpu.VMEM((heads, rows, 2 * HD), F32)],
        compiler_params=params(),
        cost_estimate=cost(4 * rows * rows * count * width, 2 * kv_all.size, rows * rows * heads * count),
    )(w_index, query, kv_all)


def attend_back_kernel(
    heads, group, w_ref, q_ref, kv_ref, do_ref, o_ref, lse_ref, dq_ref, dkv_ref, delta
):
    rows = q_ref.shape[0]
    kv_width = kv_ref.shape[2] // 2
    w = w_ref[0]
    for h in range(heads):
        part = slice(h * HD, (h + 1) * HD)
        delta[h : h + 1, :] = jnp.sum(
            jnp.transpose(do_ref[:, part].astype(F32) * o_ref[:, part]), axis=0, keepdims=True
        )
    dq_ref[...] = jnp.zeros_like(dq_ref)

    @pl.loop(0, w + 1)
    def _(j):
        seen = jnp.where(j == w, 0, rows)

        @pl.loop(0, heads // group)
        def _(kv):
            key_at_lane = pl.ds(pl.multiple_of(kv * HD, HD), HD)
            value_at_lane = pl.ds(pl.multiple_of(kv_width + kv * HD, HD), HD)
            key, value = kv_ref[j, :, key_at_lane], kv_ref[j, :, value_at_lane]
            key_sum = jnp.zeros((rows, HD), F32)
            value_sum = jnp.zeros((rows, HD), F32)
            for n in range(group):
                h = kv * group + n
                part = pl.ds(pl.multiple_of(h * HD, HD), HD)
                query, out_grad = q_ref[:, part], do_ref[:, part]
                probs = jnp.exp2(
                    dot_nt(key, query) * (FACTOR * LOG2E) - lse_ref[pl.ds(h, 1), :]
                )
                key_at = lax.broadcasted_iota(jnp.int32, (rows, rows), 0)
                at = lax.broadcasted_iota(jnp.int32, (rows, rows), 1)
                probs = jnp.where(key_at - at <= seen, probs, 0.0)
                value_sum += dot(probs.astype(BF16), out_grad)
                prob_grad = dot_nt(value, out_grad)
                score_grad = (probs * (prob_grad - delta[pl.ds(h, 1), :])).astype(BF16)
                key_sum += dot(score_grad, query)
                dq_ref[:, part] += dot_tn(score_grad, key)
            dkv_ref[j, :, key_at_lane] = (key_sum * FACTOR).astype(BF16)
            dkv_ref[j, :, value_at_lane] = value_sum.astype(BF16)

    dq_ref[...] = dq_ref[...] * FACTOR


def attend_back(w_index, query, kv_all, out_grad, out, lse, heads, group):
    rows, width = query.shape
    count = kv_all.shape[0]
    return pl.pallas_call(
        functools.partial(attend_back_kernel, heads, group),
        name="attend_back",
        out_shape=(
            jax.ShapeDtypeStruct((rows, width), F32),
            jax.ShapeDtypeStruct(kv_all.shape, BF16),
        ),
        in_specs=[SM] + [VM] * 5,
        out_specs=(VM, VM),
        scratch_shapes=[pltpu.VMEM((heads, rows), F32)],
        compiler_params=params(),
        cost_estimate=cost(10 * rows * rows * count * width, 4 * kv_all.size, rows * rows * heads * count),
    )(w_index, query, kv_all, out_grad, out, lse)


def unspin_kernel(width, row, e_ref, raw_ref, g_ref, tab_ref, o_ref, gg_ref):
    gg_ref[...] = jnp.zeros_like(gg_ref)

    @pl.loop(0, raw_ref.shape[1] // HD)
    def _(h):
        part = pl.ds(pl.multiple_of(h * HD, HD), HD)
        cosine, sine = cos_sin(tab_ref[...], swap_lanes)
        grad = e_ref[:, part]
        turned = grad * cosine - pltpu.roll(grad, HD // 2, axis=1) * sine
        raw = raw_ref[:, part]
        scale = row_scale(raw)
        back, total = norm_back(turned, raw * scale, scale, g_ref[row : row + 1, :])
        o_ref[:, part] = back.astype(BF16)
        gg_ref[...] += total

    if width > raw_ref.shape[1]:
        o_ref[:, raw_ref.shape[1] :] = e_ref[:, raw_ref.shape[1] :].astype(BF16)


def unspin(grad, raw, gains, row, table):
    rows, width = grad.shape
    return pl.pallas_call(
        functools.partial(unspin_kernel, width, row),
        name="unspin",
        out_shape=(
            jax.ShapeDtypeStruct((rows, width), BF16),
            jax.ShapeDtypeStruct((1, HD), F32),
        ),
        in_specs=[VM] * 4,
        out_specs=(VM, VM),
        compiler_params=params(),
        cost_estimate=cost(1, 1),
    )(grad, raw, gains, table)


def front_kernel(
    count, heads, group,
    t_ref, c_ref, g_ref, f_ref, wq_hbm, wkv_hbm,
    dy_hbm, x_hbm, q_hbm, qraw_hbm, kraw_hbm, kv_hbm, o_ref, low_ref, lse_ref, tab_ref,
    own, x, weight, q, qraw, kraw, kv, acc,
    send, recv, z_send, z_recv, m_send, m_recv, c_send, c_recv, load_sem, store_sem, kv_sem,
):
    me, xn, yn, dg = square()
    w, z, c, chips, mate, above, below = line(count)
    rows = t_ref.shape[0]
    half = rows // 2
    all_rows = 4 * rows
    q_width, kv_width = wq_hbm.shape[1], wkv_hbm.shape[2]
    loads = [
        pltpu.make_async_copy(wq_hbm, weight.at[:, pl.ds(0, q_width)], load_sem.at[0]),
        pltpu.make_async_copy(wkv_hbm.at[0], weight.at[:, pl.ds(q_width, kv_width)], load_sem.at[1]),
        pltpu.make_async_copy(
            wkv_hbm.at[1], weight.at[:, pl.ds(q_width + kv_width, kv_width)], load_sem.at[2]
        ),
    ]
    for load in loads[::-1]:
        load.start()

    has_above, has_below = z < chips - 1, z > 0
    barrier = pltpu.get_barrier_semaphore()
    for peer in (xn, yn):
        pl.semaphore_signal(barrier, inc=1, device_id={"narrow": peer}, device_id_type=MESH)

    @pl.when(has_above)
    def _():
        pl.semaphore_signal(barrier, inc=1, device_id={"wide": above}, device_id_type=MESH)

    @pl.when(has_below)
    def _():
        pl.semaphore_signal(barrier, inc=1, device_id={"wide": below}, device_id_type=MESH)

    pl.semaphore_signal(barrier, inc=1, device_id={"wide": mate}, device_id_type=MESH)
    hidden = t_ref[...].astype(F32)
    own[...] = (hidden * row_scale(hidden) * gain_row(g_ref, 0)).astype(BF16)
    fill_table(tab_ref, f_ref, w * all_rows)
    pl.semaphore_wait(barrier, 3 + has_above.astype(jnp.int32) + has_below.astype(jnp.int32))

    def half_of(ref, owner, low):
        return ref.at[pl.ds(pl.multiple_of(owner * rows + low, half), half)]

    def spread(copies, src, dst):
        upper, lower = src.at[pl.ds(0, half)], src.at[pl.ds(half, half)]
        return (
            copies.go(upper, half_of(dst, me, 0), 0, xn),
            copies.go(lower, half_of(dst, me, half), 1, yn),
            copies.go(lower, half_of(dst, me, half), 2, xn),
            copies.go(upper, half_of(dst, me, 0), 3, yn),
        )

    def lazy(copies, slot, owner, low, dst, peer):
        return pltpu.make_async_remote_copy(
            src_ref=half_of(dst, owner, low),
            dst_ref=half_of(dst, owner, low),
            send_sem=copies.send.at[slot],
            recv_sem=copies.recv.at[slot],
            device_id={"narrow": peer},
            device_id_type=MESH,
        )

    copies, away = Copies(send, recv), Copies(c_send, c_recv)
    xa, yb, xb, ya = spread(copies, own, x)
    yf, xf = lazy(copies, 4, xn, 0, x, yn), lazy(copies, 5, yn, half, x, xn)
    c_yf, c_xf = lazy(away, 4, xn, 0, dy_hbm, yn), lazy(away, 5, yn, half, dy_hbm, xn)
    dy_part = dy_hbm.at[pl.ds(pl.multiple_of(me * rows, rows), rows)]
    c_own = pltpu.make_async_copy(c_ref, dy_part, store_sem.at[4])

    def piece(k, j):
        owner = jnp.where(k == 0, me, jnp.where(k == 3, dg, xn if j == 0 else yn))
        low = jnp.where((k == 2) == (j == 0), half, 0)
        return pl.ds(pl.multiple_of(owner * rows + low, half), half)

    def unit(block, k, j):
        return kv.at[block, piece(k, j)]

    def to_above(s, k, j):
        block = jnp.maximum(w - 2 * s, 0)
        return wide_copy(
            unit(block, k, j), unit(block, k, j), z_send, z_recv, 8 * s + 2 * k + j, above
        )

    def from_below(s, k, j):
        block = jnp.maximum(w - 2 * s, 0)
        return wide_copy(
            unit(block, k, j), unit(block, k, j), z_send, z_recv, 8 * (s - 1) + 2 * k + j, above
        )

    def to_mate(s, k, j):
        block = jnp.maximum(w - 2 * s, 0)
        return wide_copy(
            unit(block, k, j), unit(block, k, j), m_send, m_recv, 8 * s + 2 * k + j, mate
        )

    def project(k):
        rows_in = jnp.concatenate([x[piece(k, 0), :], x[piece(k, 1), :]], axis=0)
        out = dot(rows_in, weight[:, q_width:])
        cosine, sine = cos_sin(
            jnp.concatenate([tab_ref[piece(k, 0), :], tab_ref[piece(k, 1), :]], axis=0), swap_lanes
        )
        base = 2 * (D // HD)
        parts = [slice(0, half), slice(half, rows)]
        for h in range(heads // group):
            lanes = slice(h * HD, (h + 1) * HD)
            key = spin(out[:, lanes], g_ref[base + 1 : base + 2, :], cosine, sine).astype(BF16)
            for j in range(2):
                kv[w, piece(k, j), h * HD : (h + 1) * HD] = key[parts[j]]
        for j in range(2):
            kv[w, piece(k, j), kv_width:] = out[parts[j], kv_width:].astype(BF16)

            @pl.when(has_above)
            def _():
                to_above(0, k, j).start()

            @pl.when(c == 0)
            def _():
                to_mate(0, k, j).start()

        for j in range(2):
            kraw[piece(k, j), :] = out[parts[j], :kv_width]
        pl.when(k == 0)(loads[0].wait)
        out = dot(rows_in, weight[:, :q_width])
        for h in range(heads):
            lanes = slice(h * HD, (h + 1) * HD)
            query = spin(out[:, lanes], g_ref[base : base + 1, :], cosine, sine).astype(BF16)
            for j in range(2):
                q[piece(k, j), lanes] = query[parts[j]]
        for j in range(2):
            qraw[piece(k, j), :] = out[parts[j], :]

    def receive(s, k):
        @pl.when(z >= s)
        def _():
            for j in range(2):
                from_below(s, k, j).wait_recv()
                if s < chips - 1:

                    @pl.when(has_above)
                    def _():
                        to_above(s, k, j).start()

                to_mate(s, k, j).start()

    x[pl.ds(pl.multiple_of(me * rows, rows), rows), :] = own[...]
    loads[1].wait()
    loads[2].wait()

    @pl.loop(0, 4)
    def _(k):
        @pl.when(k == 1)
        def _():
            xa.wait_recv()
            yf.start()
            yb.wait_recv()
            xf.start()

        @pl.when(k == 2)
        def _():
            receive(1, 0)
            xb.wait_recv()
            ya.wait_recv()

        @pl.when(k == 3)
        def _():
            receive(2, 0)
            receive(1, 1)
            receive(3, 0)
            yf.wait_recv()
            xf.wait_recv()

        project(k)

    c_first = spread(away, c_ref, dy_hbm)
    stores = [
        pltpu.make_async_copy(src, dst, store_sem.at[n])
        for n, (src, dst) in enumerate(((x, x_hbm), (q, q_hbm), (qraw, qraw_hbm), (kraw, kraw_hbm)))
    ] + [c_own]
    for store in stores:
        store.start()
    receive(2, 1)
    receive(1, 2)
    acc[...] = jnp.zeros_like(acc)
    ones = jnp.ones((all_rows, HD), BF16)

    def keep(j):
        return pltpu.make_async_copy(kv.at[j], kv_hbm.at[j], kv_sem.at[j])

    def c_relay():
        c_first[0].wait_recv()
        c_yf.start()
        c_first[1].wait_recv()
        c_xf.start()

    @pl.loop(0, 2 * z + 1 + c)
    def _(n):
        i = n - c
        for s, units in ((1, ((3, 1), (2, 2), (1, 3))), (2, ((3, 2), (2, 3))), (3, ((3, 3),))):

            @pl.when(i == 2 * s - 1)
            def _():
                for pair in units:
                    receive(*pair)

                if s == 2:
                    c_relay()

        for s in range(chips):

            @pl.when((i == 2 * s) & (n > 0))
            def _():
                for k in range(4):
                    for j in range(2):
                        to_mate(s, k, j).wait_recv()

        odd = i % 2
        step = (i + 1) // 2
        j = jnp.where(n == 0, w, 2 * (z - step) + c + (1 - odd) * (1 - 2 * c))
        seen = jnp.where(n == 0, 0, all_rows)
        for h in range(heads):
            head = h // group
            key = kv[j, :, head * HD : (head + 1) * HD]
            value = kv[j, :, kv_width + head * HD : kv_width + (head + 1) * HD]
            terms = jnp.exp2(dot_nt(q[:, h * HD : (h + 1) * HD], key) * (FACTOR * LOG2E))
            at = lax.broadcasted_iota(jnp.int32, (all_rows, all_rows), 0)
            key_at = lax.broadcasted_iota(jnp.int32, (all_rows, all_rows), 1)
            terms = jnp.where(key_at - at <= seen, terms, 0.0)
            acc[h] += dot(terms.astype(BF16), jnp.concatenate([value, ones], axis=1))
        keep(j).start()

    @pl.when(z < 2)
    def _():
        c_relay()

    for h in range(heads):
        total = acc[h, :, HD:]
        out = acc[h, :, :HD] / total
        o_ref[:, h * HD : (h + 1) * HD] = out
        low_ref[:, h * HD : (h + 1) * HD] = out.astype(BF16)
        lse_ref[h : h + 1, :] = jnp.transpose(jnp.log2(total))[0:1]

    copies.finish()
    yf.wait_send()
    xf.wait_send()
    for copy in c_first[2:] + (c_yf, c_xf):
        copy.wait_recv()
    away.finish()
    c_yf.wait_send()
    c_xf.wait_send()
    for s in range(chips):

        @pl.when((z >= s) & has_above)
        def _():
            for k in range(4):
                for j in range(2):
                    to_above(s, k, j).wait_send()

        @pl.when((z >= s) & ((c == 0) | (s > 0)))
        def _():
            for k in range(4):
                for j in range(2):
                    to_mate(s, k, j).wait_send()

    for store in stores:
        store.wait()

    @pl.loop(0, w + 1)
    def _(j):
        keep(j).wait()


def fill_table(tab_ref, f_ref, start):
    rows, fine = tab_ref.shape[0], 32
    freq = f_ref[0:1, :]
    high = start + fine * lax.broadcasted_iota(jnp.int32, (rows // fine, HD), 0)
    low = lax.broadcasted_iota(jnp.int32, (fine, HD), 0).astype(F32) * freq
    high = high.astype(F32) * freq
    cos_high, sin_high, cos_low, sin_low = jnp.cos(high), jnp.sin(high), jnp.cos(low), jnp.sin(low)
    first = lax.broadcasted_iota(jnp.int32, (fine, HD), 1) < HD // 2
    for n in range(rows // fine):
        c, s = cos_high[n : n + 1], sin_high[n : n + 1]
        tab_ref[n * fine : (n + 1) * fine, :] = jnp.where(
            first, c * cos_low - s * sin_low, s * cos_low + c * sin_low
        )


def front(tokens, cotangent, gains, query_weight, keyvalue_weight, count):
    rows = tokens.shape[0]
    all_rows = 4 * rows
    q_width, kv_width = query_weight.shape[1], keyvalue_weight.shape[2]
    heads, group = q_width // HD, q_width // kv_width
    chips = count // 2
    anywhere = pl.BlockSpec(memory_space=pl.ANY)
    return pl.pallas_call(
        functools.partial(front_kernel, count, heads, group),
        name="front",
        out_shape=(
            jax.ShapeDtypeStruct((all_rows, D), BF16),
            jax.ShapeDtypeStruct((all_rows, D), BF16),
            jax.ShapeDtypeStruct((all_rows, q_width), BF16),
            jax.ShapeDtypeStruct((all_rows, q_width), F32),
            jax.ShapeDtypeStruct((all_rows, kv_width), F32),
            jax.ShapeDtypeStruct((count, all_rows, 2 * kv_width), BF16),
            jax.ShapeDtypeStruct((all_rows, q_width), F32),
            jax.ShapeDtypeStruct((all_rows, q_width), BF16),
            jax.ShapeDtypeStruct((heads, all_rows), F32),
            jax.ShapeDtypeStruct((all_rows, HD), F32),
        ),
        in_specs=[VM] * 4 + [anywhere] * 2,
        out_specs=(anywhere,) * 6 + (VM,) * 4,
        scratch_shapes=[
            pltpu.VMEM((rows, D), BF16),
            pltpu.VMEM((all_rows, D), BF16),
            pltpu.VMEM((D, q_width + 2 * kv_width), BF16),
            pltpu.VMEM((all_rows, q_width), BF16),
            pltpu.VMEM((all_rows, q_width), F32),
            pltpu.VMEM((all_rows, kv_width), F32),
            pltpu.VMEM((count, all_rows, 2 * kv_width), BF16),
            pltpu.VMEM((heads, all_rows, 2 * HD), F32),
        ]
        + dma_sems(6)
        + dma_sems(8 * chips)
        + dma_sems(8 * chips)
        + dma_sems(6)
        + [
            pltpu.SemaphoreType.DMA((3,)),
            pltpu.SemaphoreType.DMA((5,)),
            pltpu.SemaphoreType.DMA((count,)),
        ],
        cost_estimate=cost(1, 1),
        compiler_params=remote_params(8),
    )(tokens, cotangent, gains, rope_freq(), query_weight, keyvalue_weight)


def feed_kernel(x_ref, dy_ref, w_ref, d_ref, act_ref, grad_ref, down_ref):
    x, dy = x_ref[...], dy_ref[...]
    gate = dot(x, w_ref[0])
    upper = dot(x, w_ref[1])
    act_grad = dot_nt(dy, d_ref[...])
    sig = jax.nn.sigmoid(gate)
    swish = gate * sig
    act = (swish * upper).astype(BF16)
    act_ref[...] = act
    grad_ref[0] = (act_grad * upper * sig * (1.0 + gate * (1.0 - sig))).astype(BF16)
    grad_ref[1] = (act_grad * swish).astype(BF16)
    down_ref[...] = dot_tn(act, dy).astype(BF16)


def feed(x, dy, gateup_weight, down_weight):
    rows, width = x.shape[0], down_weight.shape[0]
    tile = 256
    whole = lambda i: (0, 0)
    return pl.pallas_call(
        feed_kernel,
        name="feed",
        grid=(width // tile,),
        out_shape=(
            jax.ShapeDtypeStruct((rows, width), BF16),
            jax.ShapeDtypeStruct((2, rows, width), BF16),
            jax.ShapeDtypeStruct((width, D), BF16),
        ),
        in_specs=[
            pl.BlockSpec((rows, D), whole),
            pl.BlockSpec((rows, D), whole),
            pl.BlockSpec((2, D, tile), lambda i: (0, 0, i)),
            pl.BlockSpec((tile, D), lambda i: (i, 0)),
        ],
        out_specs=(
            pl.BlockSpec((rows, tile), lambda i: (0, i)),
            pl.BlockSpec((2, rows, tile), lambda i: (0, 0, i)),
            pl.BlockSpec((tile, D), lambda i: (i, 0)),
        ),
        compiler_params=params("arbitrary"),
        cost_estimate=cost(8 * rows * D * width, 4 * rows * D + 8 * D * width),
    )(x, dy, gateup_weight, down_weight)


def feed_back_kernel(x_ref, act_ref, grad_ref, w_ref, d_ref, full_ref, in_ref, out_ref, in_acc, out_acc):
    step = pl.program_id(0)

    @pl.when(step == 0)
    def _():
        in_acc[...] = jnp.zeros_like(in_acc)
        out_acc[...] = jnp.zeros_like(out_acc)

    in_acc[...] += dot_nt(grad_ref[0], w_ref[0]) + dot_nt(grad_ref[1], w_ref[1])
    out_acc[...] += dot(act_ref[...], d_ref[...])
    x = x_ref[...]
    full_ref[0] = dot_tn(x, grad_ref[0]).astype(BF16)
    full_ref[1] = dot_tn(x, grad_ref[1]).astype(BF16)

    @pl.when(step == pl.num_programs(0) - 1)
    def _():
        in_ref[...] = in_acc[...].astype(BF16)
        out_ref[...] = out_acc[...].astype(BF16)


def feed_back(x, act, grads, gateup_weight, down_weight):
    rows, width = x.shape[0], down_weight.shape[0]
    tile = 256
    whole = lambda i: (0, 0)
    return pl.pallas_call(
        feed_back_kernel,
        name="feed_back",
        grid=(width // tile,),
        out_shape=(
            jax.ShapeDtypeStruct((2, D, width), BF16),
            jax.ShapeDtypeStruct((rows, D), BF16),
            jax.ShapeDtypeStruct((rows, D), BF16),
        ),
        in_specs=[
            pl.BlockSpec((rows, D), whole),
            pl.BlockSpec((rows, tile), lambda i: (0, i)),
            pl.BlockSpec((2, rows, tile), lambda i: (0, 0, i)),
            pl.BlockSpec((2, D, tile), lambda i: (0, 0, i)),
            pl.BlockSpec((tile, D), lambda i: (i, 0)),
        ],
        out_specs=(
            pl.BlockSpec((2, D, tile), lambda i: (0, 0, i)),
            pl.BlockSpec((rows, D), whole),
            pl.BlockSpec((rows, D), whole),
        ),
        scratch_shapes=[pltpu.VMEM((rows, D), F32), pltpu.VMEM((rows, D), F32)],
        compiler_params=params("arbitrary"),
        cost_estimate=cost(10 * rows * D * width, 8 * rows * D + 10 * D * width),
    )(x, act, grads, gateup_weight, down_weight)


def out_back_kernel(dy_ref, w_ref, low_ref, grad_ref, full_ref):
    dy = dy_ref[...]
    grad_ref[...] = dot_nt(dy, w_ref[...]).astype(BF16)
    full_ref[...] = dot_tn(dy, low_ref[...]).astype(BF16)


def out_back(dy, weight, attn_low):
    rows, width = attn_low.shape
    tile = 256
    whole = lambda i: (0, 0)
    return pl.pallas_call(
        out_back_kernel,
        name="out_back",
        grid=(width // tile,),
        out_shape=(
            jax.ShapeDtypeStruct((rows, width), BF16),
            jax.ShapeDtypeStruct((D, width), BF16),
        ),
        in_specs=[
            pl.BlockSpec((rows, D), whole),
            pl.BlockSpec((tile, D), lambda i: (i, 0)),
            pl.BlockSpec((rows, tile), lambda i: (0, i)),
        ],
        out_specs=(
            pl.BlockSpec((rows, tile), lambda i: (0, i)),
            pl.BlockSpec((D, tile), lambda i: (0, i)),
        ),
        compiler_params=params("arbitrary"),
        cost_estimate=cost(4 * rows * D * width, 2 * rows * D + 4 * D * width),
    )(dy, weight, attn_low)


def project_back_kernel(x_ref, q_ref, kv_ref, wq_ref, wkv_ref, out_ref, in_ref, full_ref):
    q_width, kv_width = wq_ref.shape[1], wkv_ref.shape[2]
    x = x_ref[...]
    key, value = kv_ref[:, :kv_width], kv_ref[:, kv_width:]
    in_ref[...] = (
        dot_nt(q_ref[...], wq_ref[...]) + dot_nt(key, wkv_ref[0]) + dot_nt(value, wkv_ref[1])
    ).astype(BF16)
    full_ref[:, :q_width] = dot_tn(x, q_ref[...]).astype(BF16)
    full_ref[:, q_width : q_width + 2 * kv_width] = dot_tn(x, kv_ref[...]).astype(BF16)
    full_ref[:, q_width + 2 * kv_width :] = out_ref[...]


def project_back(x, q_back, kv_back, query_weight, keyvalue_weight, output_full):
    rows, out_width = x.shape[0], output_full.shape[1]
    q_width, kv_width = query_weight.shape[1], keyvalue_weight.shape[2]
    tile = 512
    whole = lambda i: (0, 0)
    return pl.pallas_call(
        project_back_kernel,
        name="project_back",
        grid=(D // tile,),
        out_shape=(
            jax.ShapeDtypeStruct((rows, D), BF16),
            jax.ShapeDtypeStruct((D, q_width + 2 * kv_width + out_width), BF16),
        ),
        in_specs=[
            pl.BlockSpec((rows, tile), lambda i: (0, i)),
            pl.BlockSpec((rows, q_width), whole),
            pl.BlockSpec((rows, 2 * kv_width), whole),
            pl.BlockSpec((tile, q_width), lambda i: (i, 0)),
            pl.BlockSpec((2, tile, kv_width), lambda i: (0, i, 0)),
            pl.BlockSpec((tile, out_width), lambda i: (i, 0)),
        ],
        out_specs=(
            pl.BlockSpec((rows, tile), lambda i: (0, i)),
            pl.BlockSpec((tile, q_width + 2 * kv_width + out_width), lambda i: (i, 0)),
        ),
        compiler_params=params("arbitrary"),
        cost_estimate=cost(4 * rows * D * (q_width + 2 * kv_width), 6 * D * (q_width + 2 * kv_width)),
    )(x, q_back, kv_back, query_weight, keyvalue_weight, output_full)


def mate_of():
    w = lax.axis_index("wide")
    c = w % 2
    return c, w + 1 - 2 * c


def greet_mate():
    _, mate = mate_of()
    barrier = pltpu.get_barrier_semaphore()
    pl.semaphore_signal(barrier, inc=1, device_id={"wide": mate}, device_id_type=MESH)
    pl.semaphore_wait(barrier, 1)


def project_back_pair_kernel(
    x_ref, q_ref, kv_ref, wq_ref, wkv_ref, out_ref, in_ref, full_ref, stage, inbox, send, recv
):
    step, steps = pl.program_id(0), pl.num_programs(0) - 1
    c, mate = mate_of()
    q_width, kv_width = wq_ref.shape[1], wkv_ref.shape[2]
    part = full_ref.shape[1]

    def trade(i):
        return wide_copy(stage.at[i % 2, 1 - c], inbox.at[i], send, recv, i, mate)

    @pl.when(step == 0)
    def _():
        greet_mate()

    @pl.when((step >= 2) & (step <= steps))
    def _():
        trade(step - 2).wait_send()

    @pl.when(step < steps)
    def _():
        x = x_ref[...]
        q_full = dot_tn(x, q_ref[...]).astype(BF16)
        kv_full = dot_tn(x, kv_ref[...]).astype(BF16)
        for k in range(2):
            at = slice(k * part, (k + 1) * part)
            stage[step % 2, k, :, :q_width] = q_full[at]
            stage[step % 2, k, :, q_width : q_width + 2 * kv_width] = kv_full[at]
            stage[step % 2, k, :, q_width + 2 * kv_width :] = out_ref[at, :]
        trade(step).start()
        key, value = kv_ref[:, :kv_width], kv_ref[:, kv_width:]
        in_ref[...] = (
            dot_nt(q_ref[...], wq_ref[...]) + dot_nt(key, wkv_ref[0]) + dot_nt(value, wkv_ref[1])
        ).astype(BF16)

    @pl.when(step > 0)
    def _():
        last = jnp.maximum(step - 1, 0)
        trade(last).wait_recv()
        full_ref[0] = (stage[last % 2, c].astype(F32) + inbox[last].astype(F32)).astype(BF16)

    @pl.when(step == steps)
    def _():
        trade(step - 1).wait_send()


def project_back_pair(x, q_back, kv_back, query_weight, keyvalue_weight, output_full, count):
    rows, out_width = x.shape[0], output_full.shape[1]
    q_width, kv_width = query_weight.shape[1], keyvalue_weight.shape[2]
    width = q_width + 2 * kv_width + out_width
    part = D // count
    tile = 2 * part
    steps = count // 2
    whole = lambda i: (0, 0)
    now = lambda i: jnp.minimum(i, steps - 1)
    in_partial, full = pl.pallas_call(
        project_back_pair_kernel,
        name="project_back_pair",
        grid=(steps + 1,),
        out_shape=(
            jax.ShapeDtypeStruct((rows, D), BF16),
            jax.ShapeDtypeStruct((steps, part, width), BF16),
        ),
        in_specs=[
            pl.BlockSpec((rows, tile), lambda i: (0, now(i))),
            pl.BlockSpec((rows, q_width), whole),
            pl.BlockSpec((rows, 2 * kv_width), whole),
            pl.BlockSpec((tile, q_width), lambda i: (now(i), 0)),
            pl.BlockSpec((2, tile, kv_width), lambda i: (0, now(i), 0)),
            pl.BlockSpec((tile, out_width), lambda i: (now(i), 0)),
        ],
        out_specs=(
            pl.BlockSpec((rows, tile), lambda i: (0, now(i))),
            pl.BlockSpec((1, part, width), lambda i: (jnp.maximum(i - 1, 0), 0, 0)),
        ),
        scratch_shapes=[
            pltpu.VMEM((2, 2, part, width), BF16),
            pltpu.VMEM((steps, part, width), BF16),
        ]
        + dma_sems(steps),
        cost_estimate=cost(1, 1),
        compiler_params=remote_params(12),
    )(x, q_back, kv_back, query_weight, keyvalue_weight, output_full)
    return in_partial, full.reshape(D // 2, width)


def rest_adamw_kernel(total_ref, *refs):
    q_width, kv_width = refs[0].shape[1], refs[4].shape[2]
    ins, outs = refs[:12], refs[12:]
    total = total_ref[...].astype(F32)
    rate = 2.0 * D ** (-0.5)
    for n, new in enumerate(
        adamw(total[:, :q_width], *[r[...] for r in ins[:4]], rate, WEIGHT_DECAY)
    ):
        outs[n][...] = new
    for k in range(2):
        low = q_width + k * kv_width
        for n, new in enumerate(
            adamw(total[:, low : low + kv_width], *[r[k] for r in ins[4:8]], rate, WEIGHT_DECAY)
        ):
            outs[5 + n][k] = new
    turned = jnp.transpose(total[:, q_width + 2 * kv_width :])
    for n, new in enumerate(
        adamw(turned, *[r[...] for r in ins[8:]], 2.0 * WO_FAN ** (-0.5), WEIGHT_DECAY)
    ):
        outs[10 + n][...] = new


def rest_adamw(total, query_state, keyvalue_state, output_state):
    tile = 128
    rows, width = total.shape
    q_spec = pl.BlockSpec((tile, query_state[0].shape[1]), lambda i: (i, 0))
    kv_spec = pl.BlockSpec((2, tile, keyvalue_state[0].shape[2]), lambda i: (0, i, 0))
    o_spec = pl.BlockSpec((output_state[0].shape[0], tile), lambda i: (0, i))
    like = lambda a: jax.ShapeDtypeStruct(a.shape, F32)
    out = pl.pallas_call(
        rest_adamw_kernel,
        name="rest_adamw",
        grid=(rows // tile,),
        out_shape=tuple(
            like(state[0]) for state in (query_state, keyvalue_state, output_state) for _ in range(5)
        ),
        in_specs=[pl.BlockSpec((tile, width), lambda i: (i, 0))]
        + [q_spec] * 4
        + [kv_spec] * 4
        + [o_spec] * 4,
        out_specs=tuple([q_spec] * 5 + [kv_spec] * 5 + [o_spec] * 5),
        compiler_params=params("arbitrary"),
        cost_estimate=cost(1, 1),
    )(total, *query_state, *keyvalue_state, *output_state)
    return out[:5], out[5:10], out[10:]


def wide_scatter(partial, axis):
    return lax.psum_scatter(partial, "wide", scatter_dimension=axis, tiled=True)


def line_scatter(partial, axis, count):
    groups = [[2 * z + c for z in range(count // 2)] for c in range(2)]
    return lax.psum_scatter(
        partial, "wide", scatter_dimension=axis, tiled=True, axis_index_groups=groups
    )


def body(
    tokens,
    cotangent,
    gain_copy,
    query_weight,
    keyvalue_weight,
    output_weight,
    gateup_weight,
    down_weight,
    query_master,
    query_moment,
    query_second,
    query_average,
    keyvalue_master,
    keyvalue_moment,
    keyvalue_second,
    keyvalue_average,
    output_master,
    output_moment,
    output_second,
    output_average,
    gateup_master,
    gateup_moment,
    gateup_second,
    gateup_average,
    down_master,
    down_moment,
    down_second,
    down_average,
    gain_master,
    gain_moment,
    gain_second,
    gain_average,
):
    narrow, wide = lax.axis_size("narrow"), lax.axis_size("wide")
    special = narrow == 4 and wide == 8
    stretch_rows = tokens.shape[0] * narrow
    wide_index = lax.axis_index("wide")
    w_scalar = wide_index.astype(jnp.int32).reshape(1)
    kv_heads = keyvalue_weight.shape[2] // HD
    q_heads = query_weight.shape[1] // HD
    group = q_heads // kv_heads
    q_width, kv_width = q_heads * HD, kv_heads * HD
    gains = gain_copy.reshape(-1, HD)

    if special:
        (
            back_mlp,
            attn_input,
            query_low,
            query_raw,
            key_raw,
            kv_all,
            attn_out,
            attn_low,
            lse,
            table,
        ) = front(tokens, cotangent, gains, query_weight, keyvalue_weight, wide)
    else:
        positions = wide_index * stretch_rows + jnp.arange(stretch_rows, dtype=jnp.int32)
        table = rope_table(positions.astype(F32))
        cosine, sine = cos_sin(
            table, lambda a: jnp.concatenate([a[:, HD // 2 :], a[:, : HD // 2]], axis=1)
        )
        attn_gain = gain_copy[:D].reshape(1, D)
        mlp_gain = gain_copy[D : 2 * D].reshape(1, D)
        query_gain = gain_copy[2 * D : 2 * D + HD].reshape(1, HD)
        key_gain = gain_copy[2 * D + HD :].reshape(1, HD)
        hidden = tokens.astype(F32)
        normed = (hidden * row_scale(hidden) * attn_gain).astype(BF16)
        attn_input = lax.all_gather(normed, "narrow", axis=0, tiled=True)
        kv_low, key_raw = keys_values(attn_input, keyvalue_weight, key_gain, cosine, sine)
        query_low, query_raw = queries(attn_input, query_weight, query_gain, cosine, sine)
        kv_all = lax.all_gather(kv_low, "wide", axis=0)
        attn_out, attn_low, lse = attend(w_scalar, query_low, kv_all, q_heads, group)
        back_mlp = lax.all_gather(cotangent, "narrow", axis=0, tiled=True)
    if special:
        hidden_mid, mlp_input, act_grads, act, down_full = mid_pair(
            attn_low, output_weight, tokens, gains, back_mlp, gateup_weight, down_weight, wide
        )
        down_total = line_scatter(down_full, 0, wide)[0]
        mid_grad, back_attn, mlp_gain_grad, gateup_full = mid_backward_pair(
            hidden_mid, cotangent, gains, mlp_input, act_grads, gateup_weight, wide
        )
        gateup_total = line_scatter(gateup_full, 1, wide)
    else:
        hidden_mid, mlp_input = mid_forward(attn_low, output_weight, tokens, mlp_gain)
        act, act_grads, down_full = feed(mlp_input, back_mlp, gateup_weight, down_weight)
        down_total = wide_scatter(down_full, 1)
        gateup_full, in_partial, out_partial = feed_back(
            mlp_input, act, act_grads, gateup_weight, down_weight
        )
        gateup_total = wide_scatter(gateup_full, 1)
        mid_grad, back_attn, mlp_gain_grad = mid_backward(
            in_partial, hidden_mid, cotangent, mlp_gain
        )
    attn_grad, output_full = out_back(back_attn, output_weight, attn_low)
    query_sum, kv_sums = attend_back(
        w_scalar, query_low, kv_all, attn_grad, attn_out, lse, q_heads, group
    )
    query_back, query_gain_grad = unspin(query_sum, query_raw, gains, 2 * (D // HD), table)
    if special:
        kv_sum, out_sum = return_grads_out(kv_sums, act, down_weight, tokens.shape[0], wide)
        block_output = hidden_mid + out_sum
    else:
        kv_sum = return_grads(kv_sums, wide)
        block_output = hidden_mid + lax.psum_scatter(
            out_partial, "narrow", scatter_dimension=0, tiled=True
        ).astype(F32)
    kv_back, key_gain_grad = unspin(kv_sum, key_raw, gains, 2 * (D // HD) + 1, table)
    back_args = (attn_input, query_back, kv_back, query_weight, keyvalue_weight, output_full)
    if special:
        normed_partial, project_full = project_back_pair(*back_args, wide)
    else:
        normed_partial, project_full = project_back(*back_args)
    project_full, gateup_total, down_total, normed_partial = lax.optimization_barrier(
        (project_full, gateup_total, down_total, normed_partial)
    )
    rest_total = line_scatter(project_full, 0, wide) if special else wide_scatter(project_full, 0)
    in_norm_grad, attn_gain_grad = in_scatter(normed_partial, tokens, gains, special)
    input_grad = mid_grad + in_norm_grad
    gain_partial = jnp.concatenate(
        [attn_gain_grad, mlp_gain_grad, query_gain_grad, key_gain_grad], axis=1
    ).reshape(-1)
    gain_total = gain_sums(gain_partial, wide, narrow, special)

    rest_total, input_grad, block_output = lax.optimization_barrier(
        (rest_total, input_grad, block_output)
    )
    query_new, keyvalue_new, output_new = rest_adamw(
        rest_total,
        (query_master, query_moment, query_second, query_average),
        (keyvalue_master, keyvalue_moment, keyvalue_second, keyvalue_average),
        (output_master, output_moment, output_second, output_average),
    )
    gateup_new = adamw(
        gateup_total.astype(F32),
        gateup_master,
        gateup_moment,
        gateup_second,
        gateup_average,
        2.0 * D ** (-0.5),
        WEIGHT_DECAY,
    )
    down_new = adamw(
        down_total.astype(F32),
        down_master,
        down_moment,
        down_second,
        down_average,
        2.0 * FF ** (-0.5),
        WEIGHT_DECAY,
    )
    gain_new = adamw(
        gain_total, gain_master, gain_moment, gain_second, gain_average, RATE_GAIN, 0.0
    )
    return (
        block_output,
        input_grad,
        *query_new,
        *keyvalue_new,
        *output_new,
        *gateup_new,
        *down_new,
        *gain_new,
    )


def solution(mesh):
    rows = P(("wide", "narrow"), None)
    flat = P(("wide", "narrow"))
    stacked = P(None, "wide", "narrow")
    query, output = P("wide", "narrow"), P("narrow", "wide")
    states = (
        *[query] * 4,
        *[stacked] * 4,
        *[output] * 4,
        *[stacked] * 4,
        *[output] * 4,
        *[flat] * 4,
    )
    return jax.shard_map(
        body,
        mesh=mesh,
        in_specs=(
            rows,
            rows,
            P(),
            P(None, "narrow"),
            P(None, None, "narrow"),
            P("narrow", None),
            P(None, None, "narrow"),
            P("narrow", None),
            *states,
        ),
        out_specs=(
            rows,
            rows,
            *[query] * 5,
            *[stacked] * 5,
            *[output] * 5,
            *[stacked] * 5,
            *[output] * 5,
            *[flat] * 5,
        ),
        check_vma=False,
    )
```

```python
import functools

import jax
import jax.numpy as jnp
import numpy as np
from jax import lax
from jax.experimental import pallas as pl
from jax.experimental.pallas import tpu as pltpu
from jax.sharding import PartitionSpec as P

D = 2048
HD = 128
FF = 6144
STEP = 10
WO_FAN = 32

EPSILON = 1e-06
THETA = 1000000.0
BETA_ONE = 0.9
BETA_TWO = 0.999
ADAM_EPS = 1e-08
WEIGHT_DECAY = 0.1
EMA_KEEP = 0.5
RATE_GAIN = 0.4
FACTOR = HD ** (-0.5)
LOG2E = 1.4426950408889634

F32 = jnp.float32
BF16 = jnp.bfloat16
MESH = pl.DeviceIdType.MESH
VM = pl.BlockSpec(memory_space=pltpu.VMEM)
SM = pl.BlockSpec(memory_space=pltpu.SMEM)
VMEM_LIMIT = 60 << 20

NT = (((1,), (1,)), ((), ()))
TN = (((0,), (0,)), ((), ()))


def dot(left, right):
    return jnp.dot(left, right, preferred_element_type=F32)


def dot_nt(left, right):
    return lax.dot_general(left, right, NT, preferred_element_type=F32)


def dot_tn(left, right):
    return lax.dot_general(left, right, TN, preferred_element_type=F32)


def rope_freq():
    inverse_freq = THETA ** (-2.0 * np.arange(HD // 2, dtype=np.float64) / HD)
    return jnp.asarray(np.tile(inverse_freq, (8, 2)), dtype=F32)


def rope_table(positions):
    angles = positions[:, None] * rope_freq()[:1]
    first = jnp.arange(HD)[None, :] < HD // 2
    return jnp.where(first, jnp.cos(angles), jnp.sin(angles))


def cos_sin(table, turn):
    first = lax.broadcasted_iota(jnp.int32, table.shape, 1) < HD // 2
    other = turn(table)
    return jnp.where(first, table, other), jnp.where(first, -other, table)


def swap_lanes(table):
    return pltpu.roll(table, HD // 2, axis=1)


def adamw(gradient, master, moment, second, average, step_rate, decay_rate):
    moment_new = BETA_ONE * moment + (1.0 - BETA_ONE) * gradient
    second_new = BETA_TWO * second + (1.0 - BETA_TWO) * gradient * gradient
    moment_hat = moment_new / (1.0 - BETA_ONE**STEP)
    second_hat = second_new / (1.0 - BETA_TWO**STEP)
    master_new = master - step_rate * (
        moment_hat / (jnp.sqrt(second_hat) + ADAM_EPS) + decay_rate * master
    )
    average_new = EMA_KEEP * average + (1.0 - EMA_KEEP) * master_new
    return (gradient, master_new, moment_new, second_new, average_new)


def row_scale(values_in):
    return lax.rsqrt(jnp.mean(values_in * values_in, axis=-1, keepdims=True) + EPSILON)


def gain_row(g_ref, base):
    return jnp.concatenate([g_ref[base + j : base + j + 1, :] for j in range(D // HD)], axis=1)


def norm_back(gradient, unit_rows, inv_scale, gain):
    scaled = gradient * gain
    inner = scaled - unit_rows * jnp.mean(scaled * unit_rows, axis=-1, keepdims=True)
    return inv_scale * inner, jnp.sum(gradient * unit_rows, axis=0, keepdims=True)


def square():
    me = lax.axis_index("narrow")
    xn = me + 1 - 2 * (me % 2)
    yn = (me + 2) % 4
    dg = (xn + 2) % 4
    return me, xn, yn, dg


def greet(axis, peers):
    barrier = pltpu.get_barrier_semaphore()
    for peer in peers:
        pl.semaphore_signal(barrier, inc=1, device_id={axis: peer}, device_id_type=MESH)
    pl.semaphore_wait(barrier, len(peers))


class Copies:
    def __init__(self, send, recv):
        self.send, self.recv, self.sent = send, recv, []

    def make(self, src, dst, slot, peer):
        copy = pltpu.make_async_remote_copy(
            src_ref=src,
            dst_ref=dst,
            send_sem=self.send.at[slot],
            recv_sem=self.recv.at[slot],
            device_id={"narrow": peer},
            device_id_type=MESH,
        )
        self.sent.append(copy)
        return copy

    def go(self, src, dst, slot, peer):
        copy = self.make(src, dst, slot, peer)
        copy.start()
        return copy

    def finish(self):
        for copy in self.sent:
            copy.wait_send()


def scatter_square(copies, slot, p_ref, buf, stage, emit, fill=None, early=None, middle=None):
    me, xn, yn, dg = square()
    rows = p_ref.shape[0] // 4
    half = rows // 2

    def part(owner, low):
        return p_ref.at[pl.ds(pl.multiple_of(owner * rows + low, half), half)]

    c0 = copies.make(part(dg, 0), buf.at[0], slot, xn)
    c1 = copies.make(part(dg, half), buf.at[1], slot + 1, yn)
    c2 = copies.make(part(xn, 0), buf.at[2], slot + 2, xn)
    c3 = copies.make(part(yn, half), buf.at[3], slot + 3, yn)
    if fill is None:
        for copy in (c0, c1, c2, c3):
            copy.start()
    else:

        @pl.loop(0, 4)
        def _(k):
            fill(jnp.where(k == 0, dg, jnp.where(k == 1, xn, jnp.where(k == 2, yn, me))), k)
            for n, ready in ((0, (c0, c1)), (1, (c2,)), (2, (c3,))):

                @pl.when(k == n)
                def _():
                    for copy in ready:
                        copy.start()

    if early is not None:
        early()
    c0.wait_recv()
    stage[0] = (part(yn, 0)[...].astype(F32) + buf[0].astype(F32)).astype(BF16)
    c4 = copies.go(stage.at[0], buf.at[4], slot + 4, yn)
    c1.wait_recv()
    stage[1] = (part(xn, half)[...].astype(F32) + buf[1].astype(F32)).astype(BF16)
    c5 = copies.go(stage.at[1], buf.at[5], slot + 5, xn)
    if middle is not None:
        middle()
    c2.wait_recv()
    c4.wait_recv()
    emit(0, part(me, 0)[...].astype(F32) + buf[2].astype(F32) + buf[4].astype(F32))
    c3.wait_recv()
    c5.wait_recv()
    emit(half, part(me, half)[...].astype(F32) + buf[3].astype(F32) + buf[5].astype(F32))


def exchange_square(copies, p_ref, buf, stage, own, o_ref, emit, fill, early, middle, use=None, relay=None):
    me, xn, yn, dg = square()
    rows = p_ref.shape[0] // 4
    group, piece = rows // 2, rows // 4

    def at(ref, owner, g, h):
        return ref.at[pl.ds(pl.multiple_of(owner * rows + g * group + h * piece, piece), piece)]

    def mine(g, h):
        return own.at[pl.ds(g * group + h * piece, piece)]

    sums, firsts, relays = [], [], []
    for g in range(2):
        s, t = 6 * g, 12 + 6 * g
        sums.append(
            (
                copies.make(at(p_ref, dg, g, 0), buf.at[g, 0], s, xn),
                copies.make(at(p_ref, dg, g, 1), buf.at[g, 1], s + 1, yn),
                copies.make(at(p_ref, xn, g, 0), buf.at[g, 2], s + 2, xn),
                copies.make(at(p_ref, yn, g, 1), buf.at[g, 3], s + 3, yn),
                copies.make(stage.at[g, 0], buf.at[g, 4], s + 4, yn),
                copies.make(stage.at[g, 1], buf.at[g, 5], s + 5, xn),
            )
        )
        firsts.append(
            (
                copies.make(mine(g, 0), at(o_ref, me, g, 0), t, xn),
                copies.make(mine(g, 1), at(o_ref, me, g, 1), t + 1, yn),
                copies.make(mine(g, 1), at(o_ref, me, g, 1), t + 2, xn),
                copies.make(mine(g, 0), at(o_ref, me, g, 0), t + 3, yn),
            )
        )
        relays.append(
            (
                copies.make(at(o_ref, xn, g, 0), at(o_ref, xn, g, 0), t + 4, yn),
                copies.make(at(o_ref, yn, g, 1), at(o_ref, yn, g, 1), t + 5, xn),
            )
        )

    def merge(g):
        for h, other in ((0, yn), (1, xn)):
            sums[g][h].wait_recv()
            stage[g, h] = (at(p_ref, other, g, h)[...].astype(F32) + buf[g, h].astype(F32)).astype(
                BF16
            )
            sums[g][4 + h].start()

    def close(g):
        for h in range(2):
            sums[g][2 + h].wait_recv()
            sums[g][4 + h].wait_recv()
            emit(
                g * group + h * piece,
                piece,
                at(p_ref, me, g, h)[...].astype(F32)
                + buf[g, 2 + h].astype(F32)
                + buf[g, 4 + h].astype(F32),
            )
        for copy in firsts[g]:
            copy.start()

    @pl.loop(0, 4)
    def _(k):
        fill(jnp.where(k == 0, dg, jnp.where(k == 1, xn, jnp.where(k == 2, yn, me))), k)
        for n, ready in ((0, sums[0][:2]), (1, sums[0][2:3]), (2, sums[0][3:4])):

            @pl.when(k == n)
            def _():
                for copy in ready:
                    copy.start()

    merge(0)
    for copy in sums[1][:4]:
        copy.start()
    early()
    merge(1)
    close(0)
    middle()
    close(1)
    o_ref[pl.ds(pl.multiple_of(me * rows, rows), rows)] = own[...]

    def pass_on():
        for g in range(2):
            for h in range(2):
                firsts[g][h].wait_recv()
                relays[g][h].start()
        if relay is not None:
            relay()
        for g in range(2):
            firsts[g][2].wait_recv()

    def from_y():
        for g in range(2):
            firsts[g][3].wait_recv()

    def from_far():
        for g in range(2):
            for copy in relays[g]:
                copy.wait_recv()

    if use is None:
        pass_on()
        from_y()
        from_far()
        return

    @pl.loop(0, 4)
    def _(k):
        pl.when(k == 1)(pass_on)
        pl.when(k == 2)(from_y)
        pl.when(k == 3)(from_far)
        use(jnp.where(k == 0, me, jnp.where(k == 1, xn, jnp.where(k == 2, yn, dg))))


def exchange_space(rows):
    return [pltpu.VMEM((2, 6, rows // 4, D), BF16), pltpu.VMEM((2, 2, rows // 4, D), BF16)]


def dma_sems(count):
    return [pltpu.SemaphoreType.DMA((count,)), pltpu.SemaphoreType.DMA((count,))]


def scatter_space(rows):
    return [pltpu.VMEM((6, rows // 2, D), BF16), pltpu.VMEM((2, rows // 2, D), BF16)]


def remote_params(collective_id):
    return pltpu.CompilerParams(
        collective_id=collective_id, has_side_effects=True, vmem_limit_bytes=VMEM_LIMIT
    )


def mid_kernel(
    t_ref, g_ref, a_hbm, w_hbm, dy_hbm, gu_hbm, d_hbm,
    h_ref, x_hbm, grad_hbm, act_hbm, down_hbm,
    a_ref, w_ref, p_ref, buf, stage, own, x, weight, dy, down, act_grad, grad, act, mine, theirs, inbox,
    send, recv, m_send, m_recv, load_sem, store_sem, down_sem,
):
    me, xn, yn, dg = square()
    c, mate = mate_of()
    rows = t_ref.shape[0]
    half = rows // 2
    tiles, tile, part = inbox.shape[0], inbox.shape[2], inbox.shape[3]
    loads = [
        pltpu.make_async_copy(src, dst, load_sem.at[n])
        for n, (src, dst) in enumerate(((a_hbm, a_ref), (w_hbm, w_ref), (gu_hbm, weight)))
    ]
    for n, (src, dst) in enumerate(((dy_hbm, dy), (d_hbm, down))):
        for k in range(D // part):
            loads.append(
                pltpu.make_async_copy(
                    src.at[:, pl.ds(k * part, part)],
                    dst.at[k % 2, :, pl.ds(k // 2 * part, part)],
                    load_sem.at[3 + n * (D // part) + k],
                )
            )
    for load in loads[:2] + loads[3:] + loads[2:3]:
        load.start()
    barrier = pltpu.get_barrier_semaphore()
    for peer in (xn, yn):
        pl.semaphore_signal(barrier, inc=1, device_id={"narrow": peer}, device_id_type=MESH)
    pl.semaphore_signal(barrier, inc=1, device_id={"wide": mate}, device_id_type=MESH)
    pl.semaphore_wait(barrier, 3)
    copies = Copies(send, recv)

    def rows_of(owner):
        return pl.ds(pl.multiple_of(owner * rows, rows), rows)

    loads[0].wait()
    loads[1].wait()

    def fill(owner, k):
        p_ref[rows_of(owner), :] = dot(a_ref[rows_of(owner), :], w_ref[...]).astype(BF16)

    gain = gain_row(g_ref, D // HD)

    def emit(low, size, total):
        hidden = t_ref[pl.ds(low, size)].astype(F32) + total
        h_ref[pl.ds(low, size)] = hidden
        own[pl.ds(low, size)] = (hidden * row_scale(hidden) * gain).astype(BF16)

    def act_grads(low, high):
        @pl.loop(low, high)
        def _(t):
            cols = pl.ds(pl.multiple_of(t * tile, tile), tile)
            act_grad[:, cols] = dot_nt(dy[0], down[0, cols, :]) + dot_nt(dy[1], down[1, cols, :])

    def early():
        for load in loads[3:]:
            load.wait()
        act_grads(0, tiles // 2)

    def middle():
        act_grads(tiles // 2, tiles)
        loads[2].wait()

    def expand(owner, t):
        at = rows_of(owner)
        cols = pl.ds(pl.multiple_of(t * tile, tile), tile)
        gate = dot(x[at, :], weight[0, :, cols])
        upper = dot(x[at, :], weight[1, :, cols])
        sig = jax.nn.sigmoid(gate)
        swish = gate * sig
        back = act_grad[at, cols]
        act[at, cols] = (swish * upper).astype(BF16)
        grad[0, at, cols] = (back * upper * sig * (1.0 + gate * (1.0 - sig))).astype(BF16)
        grad[1, at, cols] = (back * swish).astype(BF16)

    def use(owner):
        @pl.loop(0, tiles)
        def _(t):
            expand(owner, t)

    def trade(t):
        return wide_copy(theirs.at[t], inbox.at[t], m_send, m_recv, t, mate)

    def keep(t):
        at = pl.ds(pl.multiple_of(t * tile, tile), tile)
        return pltpu.make_async_copy(mine.at[t], down_hbm.at[:, at], down_sem.at[t])

    exchange_square(copies, p_ref, buf, stage, own, x, emit, fill, early, middle, use)
    stores = [
        pltpu.make_async_copy(src, dst, store_sem.at[n])
        for n, (src, dst) in enumerate(((x, x_hbm), (grad, grad_hbm), (act, act_hbm)))
    ]
    for store in stores:
        store.start()

    @pl.loop(0, tiles)
    def _(t):
        cols = pl.ds(pl.multiple_of(t * tile, tile), tile)
        half_full = dot_tn(act[:, cols], dy[1 - c]).astype(BF16)
        for k in range(D // part // 2):
            theirs[t, k] = half_full[:, k * part : (k + 1) * part]
        trade(t).start()

    @pl.loop(0, tiles)
    def _(t):
        trade(t).wait_recv()
        cols = pl.ds(pl.multiple_of(t * tile, tile), tile)
        half_full = dot_tn(act[:, cols], dy[c])
        for k in range(D // part // 2):
            mine[t, k] = (half_full[:, k * part : (k + 1) * part] + inbox[t, k].astype(F32)).astype(
                BF16
            )
        keep(t).start()

    copies.finish()

    @pl.loop(0, tiles)
    def _(t):
        trade(t).wait_send()
        keep(t).wait()

    for store in stores:
        store.wait()


def mid_pair(attn_low, weight, tokens, gains, dy, gateup_weight, down_weight, count):
    rows = tokens.shape[0]
    width = gateup_weight.shape[2]
    tile, part, chips = 256, D // count, count // 2
    tiles = width // tile
    anywhere = pl.BlockSpec(memory_space=pl.ANY)
    return pl.pallas_call(
        mid_kernel,
        name="mid_pair",
        out_shape=(
            jax.ShapeDtypeStruct((rows, D), F32),
            jax.ShapeDtypeStruct((4 * rows, D), BF16),
            jax.ShapeDtypeStruct((2, 4 * rows, width), BF16),
            jax.ShapeDtypeStruct((4 * rows, width), BF16),
            jax.ShapeDtypeStruct((chips, width, part), BF16),
        ),
        in_specs=[VM] * 2 + [anywhere] * 5,
        out_specs=(VM,) + (anywhere,) * 4,
        scratch_shapes=[
            pltpu.VMEM(attn_low.shape, BF16),
            pltpu.VMEM(weight.shape, BF16),
            pltpu.VMEM((4 * rows, D), BF16),
        ]
        + exchange_space(rows)
        + [
            pltpu.VMEM((rows, D), BF16),
            pltpu.VMEM((4 * rows, D), BF16),
            pltpu.VMEM((2, D, width), BF16),
            pltpu.VMEM((2, 4 * rows, D // 2), BF16),
            pltpu.VMEM((2, width, D // 2), BF16),
            pltpu.VMEM((4 * rows, width), F32),
            pltpu.VMEM((2, 4 * rows, width), BF16),
            pltpu.VMEM((4 * rows, width), BF16),
            pltpu.VMEM((tiles, chips, tile, part), BF16),
            pltpu.VMEM((tiles, chips, tile, part), BF16),
            pltpu.VMEM((tiles, chips, tile, part), BF16),
        ]
        + dma_sems(24)
        + dma_sems(tiles)
        + [
            pltpu.SemaphoreType.DMA((3 + 2 * count,)),
            pltpu.SemaphoreType.DMA((3,)),
            pltpu.SemaphoreType.DMA((tiles,)),
        ],
        cost_estimate=cost(1, 1),
        compiler_params=remote_params(2),
    )(tokens, gains, attn_low, weight, dy, gateup_weight, down_weight)


def mid_forward(attn_low, weight, tokens, gain):
    partial = dot(attn_low, weight).astype(BF16)
    hidden = tokens.astype(F32) + lax.psum_scatter(
        partial, "narrow", scatter_dimension=0, tiled=True
    ).astype(F32)
    normed = (hidden * row_scale(hidden) * gain).astype(BF16)
    return hidden, lax.all_gather(normed, "narrow", axis=0, tiled=True)


def mid_backward_kernel(
    h_ref, c_ref, g_ref, x_hbm, grad_hbm, gu_hbm,
    m_ref, o_ref, gg_ref, full_hbm,
    p_ref, buf, stage, own, x, grad, weight, mine, inbox,
    send, recv, m_send, m_recv, load_sem, full_sem,
):
    me, xn, yn, dg = square()
    c, mate = mate_of()
    half = h_ref.shape[0] // 2
    tiles, part, tile = inbox.shape[0], inbox.shape[3], inbox.shape[4]
    def load_weight(t):
        rows_at = pl.ds(pl.multiple_of(t * 512, 512), 512)
        return pltpu.make_async_copy(
            gu_hbm.at[:, rows_at], weight.at[:, rows_at], load_sem.at[2 + t]
        )

    loads = [
        pltpu.make_async_copy(src, dst, load_sem.at[n])
        for n, (src, dst) in enumerate(((grad_hbm, grad), (x_hbm, x)))
    ]
    loads[0].start()
    for t in range(D // 512):
        load_weight(t).start()
    loads[1].start()
    barrier = pltpu.get_barrier_semaphore()
    for peer in (xn, yn):
        pl.semaphore_signal(barrier, inc=1, device_id={"narrow": peer}, device_id_type=MESH)
    pl.semaphore_signal(barrier, inc=1, device_id={"wide": mate}, device_id_type=MESH)
    pl.semaphore_wait(barrier, 3)
    copies = Copies(send, recv)
    gg_ref[...] = jnp.zeros_like(gg_ref)
    gain = gain_row(g_ref, D // HD)

    def emit(low, size, total):
        hidden = h_ref[pl.ds(low, size)]
        scale = row_scale(hidden)
        back, gain_sum = norm_back(total, hidden * scale, scale, gain)
        gg_ref[...] += gain_sum
        mid = c_ref[pl.ds(low, size)].astype(F32) + back
        m_ref[pl.ds(low, size)] = mid
        own[pl.ds(low, size)] = mid.astype(BF16)

    def trade(t):
        return wide_copy(mine.at[t, 1 - c], inbox.at[t], m_send, m_recv, t, mate)

    def keep(t):
        cols = pl.ds(pl.multiple_of(t * tile, tile), tile)
        return pltpu.make_async_copy(mine.at[t, c], full_hbm.at[:, :, :, cols], full_sem.at[t])

    def products(low, high):
        @pl.loop(low, high)
        def _(t):
            cols = pl.ds(pl.multiple_of(t * tile, tile), tile)
            for n in range(2):
                full = dot_tn(x[...], grad[n, :, cols]).astype(BF16)
                for k in range(D // part):
                    mine[t, k % 2, n, k // 2] = full[k * part : (k + 1) * part]
            trade(t).start()

    rows = 2 * half
    loads[0].wait()

    def fill(owner, k):
        at = pl.ds(pl.multiple_of(owner * rows, rows), rows)

        @pl.loop(0, D // 512)
        def _(t):
            pl.when(k == 0)(load_weight(t).wait)
            cols = pl.ds(pl.multiple_of(t * 512, 512), 512)
            p_ref[at, cols] = (
                dot_nt(grad[0, at, :], weight[0, cols, :])
                + dot_nt(grad[1, at, :], weight[1, cols, :])
            ).astype(BF16)

    def early():
        loads[1].wait()
        products(0, tiles // 2)

    def middle():
        products(tiles // 2, tiles)

    def relay():
        @pl.loop(0, tiles)
        def _(t):
            trade(t).wait_recv()
            mine[t, c] = (mine[t, c].astype(F32) + inbox[t].astype(F32)).astype(BF16)
            keep(t).start()

    exchange_square(copies, p_ref, buf, stage, own, o_ref, emit, fill, early, middle, relay=relay)
    copies.finish()

    @pl.loop(0, tiles)
    def _(t):
        trade(t).wait_send()
        keep(t).wait()


def mid_backward_pair(hidden_mid, cotangent, gains, x, grads, gateup_weight, count):
    rows = hidden_mid.shape[0]
    width = grads.shape[2]
    tile, part, chips = 256, D // count, count // 2
    tiles = width // tile
    anywhere = pl.BlockSpec(memory_space=pl.ANY)
    mid_grad, back_attn, gain_sum, full = pl.pallas_call(
        mid_backward_kernel,
        name="mid_backward_pair",
        out_shape=(
            jax.ShapeDtypeStruct((rows, D), F32),
            jax.ShapeDtypeStruct((4 * rows, D), BF16),
            jax.ShapeDtypeStruct((1, D), F32),
            jax.ShapeDtypeStruct((2, chips, part, width), BF16),
        ),
        in_specs=[VM] * 3 + [anywhere] * 3,
        out_specs=(VM,) * 3 + (anywhere,),
        scratch_shapes=[pltpu.VMEM((4 * rows, D), BF16)]
        + exchange_space(rows)
        + [
            pltpu.VMEM((rows, D), BF16),
            pltpu.VMEM(x.shape, BF16),
            pltpu.VMEM(grads.shape, BF16),
            pltpu.VMEM(gateup_weight.shape, BF16),
            pltpu.VMEM((tiles, 2, 2, chips, part, tile), BF16),
            pltpu.VMEM((tiles, 2, chips, part, tile), BF16),
        ]
        + dma_sems(24)
        + dma_sems(tiles)
        + [pltpu.SemaphoreType.DMA((2 + D // 512,)), pltpu.SemaphoreType.DMA((tiles,))],
        cost_estimate=cost(1, 1),
        compiler_params=remote_params(3),
    )(hidden_mid, cotangent, gains, x, grads, gateup_weight)
    return mid_grad, back_attn, gain_sum, full.reshape(2, D // 2, width)


def mid_backward(partial, hidden_mid, cotangent, gain):
    total = lax.psum_scatter(partial, "narrow", scatter_dimension=0, tiled=True).astype(F32)
    scale = row_scale(hidden_mid)
    back, gain_sum = norm_back(total, hidden_mid * scale, scale, gain)
    mid = cotangent.astype(F32) + back
    return mid, lax.all_gather(mid.astype(BF16), "narrow", axis=0, tiled=True), gain_sum


def in_scatter_kernel(p_ref, t_ref, g_ref, o_ref, gg_ref, buf, stage, send, recv):
    _, xn, yn, _ = square()
    half = t_ref.shape[0] // 2
    greet("narrow", (xn, yn))
    copies = Copies(send, recv)
    gg_ref[...] = jnp.zeros_like(gg_ref)
    gain = gain_row(g_ref, 0)

    def emit(low, total):
        hidden = t_ref[pl.ds(low, half)].astype(F32)
        scale = row_scale(hidden)
        back, gain_sum = norm_back(total, hidden * scale, scale, gain)
        gg_ref[...] += gain_sum
        o_ref[pl.ds(low, half)] = back

    scatter_square(copies, 0, p_ref, buf, stage, emit)
    copies.finish()


def in_scatter(partial, tokens, gains, special):
    rows = tokens.shape[0]
    if not special:
        total = lax.psum_scatter(partial, "narrow", scatter_dimension=0, tiled=True).astype(F32)
        hidden = tokens.astype(F32)
        scale = row_scale(hidden)
        back, gain_sum = norm_back(total, hidden * scale, scale, gains[: D // HD].reshape(1, D))
        return back, gain_sum
    return pl.pallas_call(
        in_scatter_kernel,
        name="in_scatter",
        out_shape=(
            jax.ShapeDtypeStruct((rows, D), F32),
            jax.ShapeDtypeStruct((1, D), F32),
        ),
        in_specs=[VM] * 3,
        out_specs=(VM,) * 2,
        scratch_shapes=scatter_space(rows) + dma_sems(6),
        cost_estimate=cost(1, 1),
        compiler_params=remote_params(4),
    )(partial, tokens, gains)


def line(count):
    w = lax.axis_index("wide")
    z, c = w // 2, w % 2
    return w, z, c, count // 2, w + 1 - 2 * c, jnp.minimum(w + 2, count - 1), jnp.maximum(w - 2, 0)


def wide_copy(src, dst, send, recv, slot, peer):
    return pltpu.make_async_remote_copy(
        src_ref=src,
        dst_ref=dst,
        send_sem=send.at[slot],
        recv_sem=recv.at[slot],
        device_id={"wide": peer},
        device_id_type=MESH,
    )


def return_grads_kernel(
    count, x_ref, act_hbm, d_hbm, o_ref, b_ref,
    from_mate, from_above, stage, p_ref, buf, out_stage, act, weight,
    send, recv, mate_send, mate_recv, n_send, n_recv, load_sem,
):
    w, z, c, chips, mate, above, below = line(count)
    me, xn, yn, dg = square()
    rows = b_ref.shape[0]
    half = rows // 2
    loads = [
        pltpu.make_async_copy(src, dst, load_sem.at[n])
        for n, (src, dst) in enumerate(((act_hbm, act), (d_hbm, weight)))
    ]
    for load in loads:
        load.start()
    has_above, has_below = z < chips - 1, z > 0
    barrier = pltpu.get_barrier_semaphore()
    for peer in (xn, yn):
        pl.semaphore_signal(barrier, inc=1, device_id={"narrow": peer}, device_id_type=MESH)

    @pl.when(has_above)
    def _():
        pl.semaphore_signal(barrier, inc=1, device_id={"wide": above}, device_id_type=MESH)

    @pl.when(has_below)
    def _():
        pl.semaphore_signal(barrier, inc=1, device_id={"wide": below}, device_id_type=MESH)

    pl.semaphore_signal(barrier, inc=1, device_id={"wide": mate}, device_id_type=MESH)
    pl.semaphore_wait(barrier, 3 + has_above.astype(jnp.int32) + has_below.astype(jnp.int32))

    def to_mate(s):
        return wide_copy(
            x_ref.at[jnp.minimum(2 * s + 1 - c, count - 1)],
            from_mate.at[s],
            mate_send,
            mate_recv,
            s,
            mate,
        )

    def sends_mate(s):
        return (z > s) | ((z == s) & (c == 1))

    def down(s):
        return wide_copy(stage.at[s], from_above.at[s], send, recv, s, below)

    for s in range(chips):

        @pl.when(sends_mate(s))
        def _():
            to_mate(s).start()

    def chain():
        for s in range(chips - 1):
            block = 2 * s + c

            @pl.when(z > s)
            def _():
                to_mate(s).wait_recv()

                @pl.when(z == chips - 1)
                def _():
                    stage[s] = (x_ref[block].astype(F32) + from_mate[s].astype(F32)).astype(BF16)

                @pl.when(z < chips - 1)
                def _():
                    down(s).wait_recv()
                    stage[s] = (
                        x_ref[block].astype(F32)
                        + from_mate[s].astype(F32)
                        + from_above[s].astype(F32)
                    ).astype(BF16)

                down(s).start()

    def emit(low, total):
        b_ref[pl.ds(low, half)] = total

    def fill(owner, k):
        at = pl.ds(pl.multiple_of(owner * rows, rows), rows)

        @pl.loop(0, D // 512)
        def _(t):
            cols = pl.ds(pl.multiple_of(t * 512, 512), 512)
            p_ref[at, cols] = dot(act[at, :], weight[:, cols]).astype(BF16)

    for load in loads:
        load.wait()
    copies = Copies(n_send, n_recv)
    scatter_square(copies, 0, p_ref, buf, out_stage, emit, fill, middle=chain)
    for s in range(chips):
        block = 2 * s + c

        @pl.when(z == s)
        def _():
            o_ref[...] = x_ref[block].astype(F32)

            @pl.when(c == 0)
            def _():
                to_mate(s).wait_recv()
                o_ref[...] += from_mate[s].astype(F32)

            if s < chips - 1:
                down(s).wait_recv()
                o_ref[...] += from_above[s].astype(F32)

    copies.finish()
    for s in range(chips):

        @pl.when(sends_mate(s))
        def _():
            to_mate(s).wait_send()

        @pl.when(z > s)
        def _():
            down(s).wait_send()


def return_grads_out(grads, act, down_weight, own_rows, count):
    _, rows, width = grads.shape
    chips = count // 2
    return pl.pallas_call(
        functools.partial(return_grads_kernel, count),
        name="return_grads",
        out_shape=(
            jax.ShapeDtypeStruct((rows, width), F32),
            jax.ShapeDtypeStruct((own_rows, D), F32),
        ),
        in_specs=[VM] + [pl.BlockSpec(memory_space=pl.ANY)] * 2,
        out_specs=(VM, VM),
        scratch_shapes=[
            pltpu.VMEM((chips, rows, width), BF16),
            pltpu.VMEM((chips, rows, width), BF16),
            pltpu.VMEM((chips, rows, width), BF16),
            pltpu.VMEM((act.shape[0], D), BF16),
        ]
        + scatter_space(own_rows)
        + [pltpu.VMEM(act.shape, BF16), pltpu.VMEM(down_weight.shape, BF16)]
        + dma_sems(chips)
        + dma_sems(chips)
        + dma_sems(6)
        + [pltpu.SemaphoreType.DMA((2,))],
        cost_estimate=cost(1, 1),
        compiler_params=remote_params(6),
    )(grads, act, down_weight)


def return_grads(grads, count):
    _, rows, width = grads.shape
    w = lax.axis_index("wide")
    seen = (jnp.arange(count) <= w)[:, None, None]
    total = lax.psum_scatter(
        jnp.where(seen, grads, 0).reshape(count * rows, width),
        "wide",
        scatter_dimension=0,
        tiled=True,
    )
    return total.astype(F32)


def gain_kernel(wide, x_ref, o_ref, near, mid, far, send, recv, wide_send, wide_recv):
    me, xn, yn, dg = square()
    w = lax.axis_index("wide")
    barrier = pltpu.get_barrier_semaphore()
    for peer in (xn, yn, dg):
        pl.semaphore_signal(barrier, inc=1, device_id={"narrow": peer}, device_id_type=MESH)
    for step in range(1, wide):
        pl.semaphore_signal(
            barrier, inc=1, device_id={"wide": (w + step) % wide}, device_id_type=MESH
        )
    pl.semaphore_wait(barrier, 3 + wide - 1)
    copies = Copies(send, recv)
    sent = [
        copies.go(x_ref.at[peer], near.at[slot], slot, peer)
        for slot, peer in enumerate((xn, yn, dg))
    ]
    for copy in sent:
        copy.wait_recv()
    mid[...] = x_ref[me] + near[0] + near[1] + near[2]
    away = []
    for step in range(1, wide):
        peer = (w + step) % wide
        copy = wide_copy(
            mid.at[peer], far.at[step - 1], wide_send, wide_recv, step - 1, peer
        )
        copy.start()
        away.append(copy)
    total = mid[w]
    for step in range(1, wide):
        away[step - 1].wait_recv()
        total = total + far[step - 1]
    o_ref[...] = total
    copies.finish()
    for copy in away:
        copy.wait_send()


def gain_sums(partial, wide, narrow, special):
    if not special:
        return lax.psum_scatter(partial, ("wide", "narrow"), scatter_dimension=0, tiled=True)
    count = partial.shape[0] // (wide * narrow)
    padded = -(-count // 128) * 128
    shaped = partial.reshape(wide, narrow, count).transpose(1, 0, 2)
    shaped = jnp.pad(shaped, ((0, 0), (0, 0), (0, padded - count)))
    shaped = shaped.reshape(narrow, wide, padded // 128, 128)
    out = pl.pallas_call(
        functools.partial(gain_kernel, wide),
        name="gain_sums",
        out_shape=jax.ShapeDtypeStruct((padded // 128, 128), F32),
        in_specs=[VM],
        out_specs=VM,
        scratch_shapes=[
            pltpu.VMEM((3, wide, padded // 128, 128), F32),
            pltpu.VMEM((wide, padded // 128, 128), F32),
            pltpu.VMEM((wide - 1, padded // 128, 128), F32),
        ]
        + dma_sems(3)
        + dma_sems(wide - 1),
        cost_estimate=cost(1, 1),
        compiler_params=remote_params(7),
    )(shaped)
    return out.reshape(padded)[:count]


def cost(flops, moved, exps=0):
    return pl.CostEstimate(flops=1, bytes_accessed=1, transcendentals=0)


def params(*semantics):
    if not semantics:
        return pltpu.CompilerParams(vmem_limit_bytes=VMEM_LIMIT)
    return pltpu.CompilerParams(vmem_limit_bytes=VMEM_LIMIT, dimension_semantics=semantics)


def spin(raw, gain_row, cosine, sine):
    normed = raw * row_scale(raw) * gain_row
    return normed * cosine + pltpu.roll(normed, HD // 2, axis=1) * sine


def keys_kernel(x_ref, w_ref, g_ref, cos_ref, sin_ref, kv_ref, raw_ref):
    which = pl.program_id(0)
    width = w_ref.shape[2]
    out = dot(x_ref[...], w_ref[0])

    @pl.when(which == 0)
    def _():
        raw_ref[...] = out
        for h in range(width // HD):
            part = out[:, h * HD : (h + 1) * HD]
            kv_ref[:, h * HD : (h + 1) * HD] = spin(
                part, g_ref[...], cos_ref[...], sin_ref[...]
            ).astype(BF16)

    @pl.when(which == 1)
    def _():
        kv_ref[...] = out.astype(BF16)


def keys_values(x, weight, gain_row, cosine, sine):
    rows, width = x.shape[0], weight.shape[2]
    whole = lambda i: (0, 0)
    return pl.pallas_call(
        keys_kernel,
        name="keys_values",
        grid=(2,),
        out_shape=(
            jax.ShapeDtypeStruct((rows, 2 * width), BF16),
            jax.ShapeDtypeStruct((rows, width), F32),
        ),
        in_specs=[
            pl.BlockSpec((rows, D), whole),
            pl.BlockSpec((1, D, width), lambda i: (i, 0, 0)),
            pl.BlockSpec((1, HD), whole),
            pl.BlockSpec((rows, HD), whole),
            pl.BlockSpec((rows, HD), whole),
        ],
        out_specs=(
            pl.BlockSpec((rows, width), lambda i: (0, i)),
            pl.BlockSpec((rows, width), whole),
        ),
        compiler_params=params("arbitrary"),
        cost_estimate=cost(4 * rows * D * width, 2 * rows * D + 4 * D * width),
    )(x, weight, gain_row, cosine, sine)


def queries_kernel(x_ref, w_ref, g_ref, cos_ref, sin_ref, q_ref, raw_ref):
    out = dot(x_ref[...], w_ref[...])
    raw_ref[...] = out
    for h in range(w_ref.shape[1] // HD):
        part = out[:, h * HD : (h + 1) * HD]
        q_ref[:, h * HD : (h + 1) * HD] = spin(
            part, g_ref[...], cos_ref[...], sin_ref[...]
        ).astype(BF16)


def queries(x, weight, gain_row, cosine, sine):
    rows, width = x.shape[0], weight.shape[1]
    tile = 256
    whole = lambda i: (0, 0)
    return pl.pallas_call(
        queries_kernel,
        name="queries",
        grid=(width // tile,),
        out_shape=(
            jax.ShapeDtypeStruct((rows, width), BF16),
            jax.ShapeDtypeStruct((rows, width), F32),
        ),
        in_specs=[
            pl.BlockSpec((rows, D), whole),
            pl.BlockSpec((D, tile), lambda i: (0, i)),
            pl.BlockSpec((1, HD), whole),
            pl.BlockSpec((rows, HD), whole),
            pl.BlockSpec((rows, HD), whole),
        ],
        out_specs=(
            pl.BlockSpec((rows, tile), lambda i: (0, i)),
            pl.BlockSpec((rows, tile), lambda i: (0, i)),
        ),
        compiler_params=params("arbitrary"),
        cost_estimate=cost(2 * rows * D * width, 2 * rows * D + 2 * D * width),
    )(x, weight, gain_row, cosine, sine)


def attend_kernel(heads, group, w_ref, q_ref, kv_ref, o_ref, low_ref, lse_ref, acc):
    rows = q_ref.shape[0]
    kv_width = kv_ref.shape[2] // 2
    w = w_ref[0]
    acc[...] = jnp.zeros_like(acc)
    ones = jnp.ones((rows, HD), BF16)

    def block(j, masked):
        for h in range(heads):
            kv = h // group
            key = kv_ref[j, :, kv * HD : (kv + 1) * HD]
            value = kv_ref[j, :, kv_width + kv * HD : kv_width + (kv + 1) * HD]
            query = q_ref[:, h * HD : (h + 1) * HD]
            terms = jnp.exp2(dot_nt(query, key) * (FACTOR * LOG2E))
            if masked:
                at = lax.broadcasted_iota(jnp.int32, (rows, rows), 0)
                key_at = lax.broadcasted_iota(jnp.int32, (rows, rows), 1)
                terms = jnp.where(key_at <= at, terms, 0.0)
            acc[h] += dot(terms.astype(BF16), jnp.concatenate([value, ones], axis=1))

    @pl.loop(0, w)
    def _(j):
        block(j, False)

    block(w, True)
    for h in range(heads):
        total = acc[h, :, HD:]
        out = acc[h, :, :HD] / total
        o_ref[:, h * HD : (h + 1) * HD] = out
        low_ref[:, h * HD : (h + 1) * HD] = out.astype(BF16)
        lse_ref[h : h + 1, :] = jnp.transpose(jnp.log2(total))[0:1]


def attend(w_index, query, kv_all, heads, group):
    rows, width = query.shape
    count = kv_all.shape[0]
    return pl.pallas_call(
        functools.partial(attend_kernel, heads, group),
        name="attend",
        out_shape=(
            jax.ShapeDtypeStruct((rows, width), F32),
            jax.ShapeDtypeStruct((rows, width), BF16),
            jax.ShapeDtypeStruct((heads, rows), F32),
        ),
        in_specs=[SM, VM, VM],
        out_specs=(VM, VM, VM),
        scratch_shapes=[pltpu.VMEM((heads, rows, 2 * HD), F32)],
        compiler_params=params(),
        cost_estimate=cost(4 * rows * rows * count * width, 2 * kv_all.size, rows * rows * heads * count),
    )(w_index, query, kv_all)


def attend_back_kernel(
    heads, group, w_ref, q_ref, kv_ref, do_ref, o_ref, lse_ref, dq_ref, dkv_ref, delta
):
    rows = q_ref.shape[0]
    kv_width = kv_ref.shape[2] // 2
    w = w_ref[0]
    for h in range(heads):
        part = slice(h * HD, (h + 1) * HD)
        delta[h : h + 1, :] = jnp.sum(
            jnp.transpose(do_ref[:, part].astype(F32) * o_ref[:, part]), axis=0, keepdims=True
        )
    dq_ref[...] = jnp.zeros_like(dq_ref)

    @pl.loop(0, w + 1)
    def _(j):
        seen = jnp.where(j == w, 0, rows)

        @pl.loop(0, heads // group)
        def _(kv):
            key_at_lane = pl.ds(pl.multiple_of(kv * HD, HD), HD)
            value_at_lane = pl.ds(pl.multiple_of(kv_width + kv * HD, HD), HD)
            key, value = kv_ref[j, :, key_at_lane], kv_ref[j, :, value_at_lane]
            key_sum = jnp.zeros((rows, HD), F32)
            value_sum = jnp.zeros((rows, HD), F32)
            for n in range(group):
                h = kv * group + n
                part = pl.ds(pl.multiple_of(h * HD, HD), HD)
                query, out_grad = q_ref[:, part], do_ref[:, part]
                probs = jnp.exp2(
                    dot_nt(key, query) * (FACTOR * LOG2E) - lse_ref[pl.ds(h, 1), :]
                )
                key_at = lax.broadcasted_iota(jnp.int32, (rows, rows), 0)
                at = lax.broadcasted_iota(jnp.int32, (rows, rows), 1)
                probs = jnp.where(key_at - at <= seen, probs, 0.0)
                value_sum += dot(probs.astype(BF16), out_grad)
                prob_grad = dot_nt(value, out_grad)
                score_grad = (probs * (prob_grad - delta[pl.ds(h, 1), :])).astype(BF16)
                key_sum += dot(score_grad, query)
                dq_ref[:, part] += dot_tn(score_grad, key)
            dkv_ref[j, :, key_at_lane] = (key_sum * FACTOR).astype(BF16)
            dkv_ref[j, :, value_at_lane] = value_sum.astype(BF16)

    dq_ref[...] = dq_ref[...] * FACTOR


def attend_back(w_index, query, kv_all, out_grad, out, lse, heads, group):
    rows, width = query.shape
    count = kv_all.shape[0]
    return pl.pallas_call(
        functools.partial(attend_back_kernel, heads, group),
        name="attend_back",
        out_shape=(
            jax.ShapeDtypeStruct((rows, width), F32),
            jax.ShapeDtypeStruct(kv_all.shape, BF16),
        ),
        in_specs=[SM] + [VM] * 5,
        out_specs=(VM, VM),
        scratch_shapes=[pltpu.VMEM((heads, rows), F32)],
        compiler_params=params(),
        cost_estimate=cost(10 * rows * rows * count * width, 4 * kv_all.size, rows * rows * heads * count),
    )(w_index, query, kv_all, out_grad, out, lse)


def unspin_kernel(width, row, e_ref, raw_ref, g_ref, tab_ref, o_ref, gg_ref):
    gg_ref[...] = jnp.zeros_like(gg_ref)

    @pl.loop(0, raw_ref.shape[1] // HD)
    def _(h):
        part = pl.ds(pl.multiple_of(h * HD, HD), HD)
        cosine, sine = cos_sin(tab_ref[...], swap_lanes)
        grad = e_ref[:, part]
        turned = grad * cosine - pltpu.roll(grad, HD // 2, axis=1) * sine
        raw = raw_ref[:, part]
        scale = row_scale(raw)
        back, total = norm_back(turned, raw * scale, scale, g_ref[row : row + 1, :])
        o_ref[:, part] = back.astype(BF16)
        gg_ref[...] += total

    if width > raw_ref.shape[1]:
        o_ref[:, raw_ref.shape[1] :] = e_ref[:, raw_ref.shape[1] :].astype(BF16)


def unspin(grad, raw, gains, row, table):
    rows, width = grad.shape
    return pl.pallas_call(
        functools.partial(unspin_kernel, width, row),
        name="unspin",
        out_shape=(
            jax.ShapeDtypeStruct((rows, width), BF16),
            jax.ShapeDtypeStruct((1, HD), F32),
        ),
        in_specs=[VM] * 4,
        out_specs=(VM, VM),
        compiler_params=params(),
        cost_estimate=cost(1, 1),
    )(grad, raw, gains, table)


def front_kernel(
    count, heads, group,
    t_ref, c_ref, g_ref, f_ref, wq_hbm, wkv_hbm,
    dy_hbm, x_hbm, q_hbm, qraw_hbm, kraw_hbm, kv_hbm, o_hbm, low_hbm, tab_hbm, lse_ref,
    own, x, weight, q, qraw, kraw, kv, acc, o_ref, low_ref, tab_ref,
    send, recv, z_send, z_recv, m_send, m_recv, c_send, c_recv, load_sem, store_sem, kv_sem, out_sem,
):
    me, xn, yn, dg = square()
    w, z, c, chips, mate, above, below = line(count)
    rows = t_ref.shape[0]
    half = rows // 2
    all_rows = 4 * rows
    q_width, kv_width = wq_hbm.shape[1], wkv_hbm.shape[2]
    loads = [
        pltpu.make_async_copy(wq_hbm, weight.at[:, pl.ds(0, q_width)], load_sem.at[0]),
        pltpu.make_async_copy(wkv_hbm.at[0], weight.at[:, pl.ds(q_width, kv_width)], load_sem.at[1]),
        pltpu.make_async_copy(
            wkv_hbm.at[1], weight.at[:, pl.ds(q_width + kv_width, kv_width)], load_sem.at[2]
        ),
    ]
    for load in loads[::-1]:
        load.start()

    has_above, has_below = z < chips - 1, z > 0
    barrier = pltpu.get_barrier_semaphore()
    for peer in (xn, yn):
        pl.semaphore_signal(barrier, inc=1, device_id={"narrow": peer}, device_id_type=MESH)

    @pl.when(has_above)
    def _():
        pl.semaphore_signal(barrier, inc=1, device_id={"wide": above}, device_id_type=MESH)

    @pl.when(has_below)
    def _():
        pl.semaphore_signal(barrier, inc=1, device_id={"wide": below}, device_id_type=MESH)

    pl.semaphore_signal(barrier, inc=1, device_id={"wide": mate}, device_id_type=MESH)
    hidden = t_ref[...].astype(F32)
    own[...] = (hidden * row_scale(hidden) * gain_row(g_ref, 0)).astype(BF16)
    pl.semaphore_wait(barrier, 3 + has_above.astype(jnp.int32) + has_below.astype(jnp.int32))

    def half_of(ref, owner, low):
        return ref.at[pl.ds(pl.multiple_of(owner * rows + low, half), half)]

    def spread(copies, src, dst):
        upper, lower = src.at[pl.ds(0, half)], src.at[pl.ds(half, half)]
        return (
            copies.go(upper, half_of(dst, me, 0), 0, xn),
            copies.go(lower, half_of(dst, me, half), 1, yn),
            copies.go(lower, half_of(dst, me, half), 2, xn),
            copies.go(upper, half_of(dst, me, 0), 3, yn),
        )

    def lazy(copies, slot, owner, low, dst, peer):
        return pltpu.make_async_remote_copy(
            src_ref=half_of(dst, owner, low),
            dst_ref=half_of(dst, owner, low),
            send_sem=copies.send.at[slot],
            recv_sem=copies.recv.at[slot],
            device_id={"narrow": peer},
            device_id_type=MESH,
        )

    copies, away = Copies(send, recv), Copies(c_send, c_recv)
    xa, yb, xb, ya = spread(copies, own, x)
    yf, xf = lazy(copies, 4, xn, 0, x, yn), lazy(copies, 5, yn, half, x, xn)
    c_yf, c_xf = lazy(away, 4, xn, 0, dy_hbm, yn), lazy(away, 5, yn, half, dy_hbm, xn)
    dy_part = dy_hbm.at[pl.ds(pl.multiple_of(me * rows, rows), rows)]
    c_own = pltpu.make_async_copy(c_ref, dy_part, store_sem.at[4])

    def piece(k, j):
        owner = jnp.where(k == 0, me, jnp.where(k == 3, dg, xn if j == 0 else yn))
        low = jnp.where((k == 2) == (j == 0), half, 0)
        return pl.ds(pl.multiple_of(owner * rows + low, half), half)

    def unit(block, k, j):
        return kv.at[block, piece(k, j)]

    def to_above(s, k, j):
        block = jnp.maximum(w - 2 * s, 0)
        return wide_copy(
            unit(block, k, j), unit(block, k, j), z_send, z_recv, 8 * s + 2 * k + j, above
        )

    def from_below(s, k, j):
        block = jnp.maximum(w - 2 * s, 0)
        return wide_copy(
            unit(block, k, j), unit(block, k, j), z_send, z_recv, 8 * (s - 1) + 2 * k + j, above
        )

    def to_mate(s, k, j):
        block = jnp.maximum(w - 2 * s, 0)
        return wide_copy(
            unit(block, k, j), unit(block, k, j), m_send, m_recv, 8 * s + 2 * k + j, mate
        )

    def project(k):
        rows_in = jnp.concatenate([x[piece(k, 0), :], x[piece(k, 1), :]], axis=0)
        out = dot(rows_in, weight[:, q_width:])
        cosine, sine = cos_sin(
            jnp.concatenate([tab_ref[piece(k, 0), :], tab_ref[piece(k, 1), :]], axis=0), swap_lanes
        )
        base = 2 * (D // HD)
        parts = [slice(0, half), slice(half, rows)]
        for h in range(heads // group):
            lanes = slice(h * HD, (h + 1) * HD)
            key = spin(out[:, lanes], g_ref[base + 1 : base + 2, :], cosine, sine).astype(BF16)
            for j in range(2):
                kv[w, piece(k, j), h * HD : (h + 1) * HD] = key[parts[j]]
        for j in range(2):
            kv[w, piece(k, j), kv_width:] = out[parts[j], kv_width:].astype(BF16)

            @pl.when(has_above)
            def _():
                to_above(0, k, j).start()

            @pl.when(c == 0)
            def _():
                to_mate(0, k, j).start()

        for j in range(2):
            kraw[piece(k, j), :] = out[parts[j], :kv_width]
        pl.when(k == 0)(loads[0].wait)
        out = dot(rows_in, weight[:, :q_width])
        for h in range(heads):
            lanes = slice(h * HD, (h + 1) * HD)
            query = spin(out[:, lanes], g_ref[base : base + 1, :], cosine, sine).astype(BF16)
            for j in range(2):
                q[piece(k, j), lanes] = query[parts[j]]
        for j in range(2):
            qraw[piece(k, j), :] = out[parts[j], :]

    def receive(s, k):
        @pl.when(z >= s)
        def _():
            for j in range(2):
                from_below(s, k, j).wait_recv()
                if s < chips - 1:

                    @pl.when(has_above)
                    def _():
                        to_above(s, k, j).start()

                to_mate(s, k, j).start()

    fill_table(tab_ref, f_ref, w * all_rows)
    keep_table = pltpu.make_async_copy(tab_ref, tab_hbm, out_sem.at[2 * heads])
    keep_table.start()
    x[pl.ds(pl.multiple_of(me * rows, rows), rows), :] = own[...]
    loads[1].wait()
    loads[2].wait()

    @pl.loop(0, 4)
    def _(k):
        @pl.when(k == 1)
        def _():
            xa.wait_recv()
            yf.start()
            yb.wait_recv()
            xf.start()

        @pl.when(k == 2)
        def _():
            receive(1, 0)
            xb.wait_recv()
            ya.wait_recv()

        @pl.when(k == 3)
        def _():
            receive(2, 0)
            receive(1, 1)
            receive(3, 0)
            yf.wait_recv()
            xf.wait_recv()

        project(k)

    c_first = spread(away, c_ref, dy_hbm)
    stores = [
        pltpu.make_async_copy(src, dst, store_sem.at[n])
        for n, (src, dst) in enumerate(((x, x_hbm), (q, q_hbm), (qraw, qraw_hbm), (kraw, kraw_hbm)))
    ] + [c_own]
    for store in stores:
        store.start()
    receive(2, 1)
    receive(1, 2)
    acc[...] = jnp.zeros_like(acc)
    ones = jnp.ones((all_rows, HD), BF16)

    def keep(j):
        return pltpu.make_async_copy(kv.at[j], kv_hbm.at[j], kv_sem.at[j])

    def c_relay():
        c_first[0].wait_recv()
        c_yf.start()
        c_first[1].wait_recv()
        c_xf.start()

    @pl.loop(0, 2 * z + 1 + c)
    def _(n):
        i = n - c
        for s, units in ((1, ((3, 1), (2, 2), (1, 3))), (2, ((3, 2), (2, 3))), (3, ((3, 3),))):

            @pl.when(i == 2 * s - 1)
            def _():
                for pair in units:
                    receive(*pair)

                if s == 2:
                    c_relay()

        for s in range(chips):

            @pl.when((i == 2 * s) & (n > 0))
            def _():
                for k in range(4):
                    for j in range(2):
                        to_mate(s, k, j).wait_recv()

        odd = i % 2
        step = (i + 1) // 2
        j = jnp.where(n == 0, w, 2 * (z - step) + c + (1 - odd) * (1 - 2 * c))
        seen = jnp.where(n == 0, 0, all_rows)
        for h in range(heads):
            head = h // group
            key = kv[j, :, head * HD : (head + 1) * HD]
            value = kv[j, :, kv_width + head * HD : kv_width + (head + 1) * HD]
            terms = jnp.exp2(dot_nt(q[:, h * HD : (h + 1) * HD], key) * (FACTOR * LOG2E))
            at = lax.broadcasted_iota(jnp.int32, (all_rows, all_rows), 0)
            key_at = lax.broadcasted_iota(jnp.int32, (all_rows, all_rows), 1)
            terms = jnp.where(key_at - at <= seen, terms, 0.0)
            acc[h] += dot(terms.astype(BF16), jnp.concatenate([value, ones], axis=1))
        keep(j).start()

    @pl.when(z < 2)
    def _():
        c_relay()

    outs = [keep_table]
    for h in range(heads):
        total = acc[h, :, HD:]
        out = acc[h, :, :HD] / total
        lanes = slice(h * HD, (h + 1) * HD)
        low_ref[:, lanes] = out.astype(BF16)
        o_ref[:, lanes] = out
        for n, (src, dst) in enumerate(((low_ref, low_hbm), (o_ref, o_hbm))):
            copy = pltpu.make_async_copy(src.at[:, lanes], dst.at[:, lanes], out_sem.at[2 * h + n])
            copy.start()
            outs.append(copy)
        lse_ref[h : h + 1, :] = jnp.transpose(jnp.log2(total))[0:1]

    copies.finish()
    yf.wait_send()
    xf.wait_send()
    for copy in c_first[2:] + (c_yf, c_xf):
        copy.wait_recv()
    away.finish()
    c_yf.wait_send()
    c_xf.wait_send()
    for s in range(chips):

        @pl.when((z >= s) & has_above)
        def _():
            for k in range(4):
                for j in range(2):
                    to_above(s, k, j).wait_send()

        @pl.when((z >= s) & ((c == 0) | (s > 0)))
        def _():
            for k in range(4):
                for j in range(2):
                    to_mate(s, k, j).wait_send()

    for store in stores + outs:
        store.wait()

    @pl.loop(0, w + 1)
    def _(j):
        keep(j).wait()


def fill_table(tab_ref, f_ref, start):
    rows, fine = tab_ref.shape[0], 32
    freq = f_ref[0:1, :]
    high = start + fine * lax.broadcasted_iota(jnp.int32, (rows // fine, HD), 0)
    low = lax.broadcasted_iota(jnp.int32, (fine, HD), 0).astype(F32) * freq
    high = high.astype(F32) * freq
    cos_high, sin_high, cos_low, sin_low = jnp.cos(high), jnp.sin(high), jnp.cos(low), jnp.sin(low)
    first = lax.broadcasted_iota(jnp.int32, (fine, HD), 1) < HD // 2
    for n in range(rows // fine):
        c, s = cos_high[n : n + 1], sin_high[n : n + 1]
        tab_ref[n * fine : (n + 1) * fine, :] = jnp.where(
            first, c * cos_low - s * sin_low, s * cos_low + c * sin_low
        )


def front(tokens, cotangent, gains, query_weight, keyvalue_weight, count):
    rows = tokens.shape[0]
    all_rows = 4 * rows
    q_width, kv_width = query_weight.shape[1], keyvalue_weight.shape[2]
    heads, group = q_width // HD, q_width // kv_width
    chips = count // 2
    anywhere = pl.BlockSpec(memory_space=pl.ANY)
    return pl.pallas_call(
        functools.partial(front_kernel, count, heads, group),
        name="front",
        out_shape=(
            jax.ShapeDtypeStruct((all_rows, D), BF16),
            jax.ShapeDtypeStruct((all_rows, D), BF16),
            jax.ShapeDtypeStruct((all_rows, q_width), BF16),
            jax.ShapeDtypeStruct((all_rows, q_width), F32),
            jax.ShapeDtypeStruct((all_rows, kv_width), F32),
            jax.ShapeDtypeStruct((count, all_rows, 2 * kv_width), BF16),
            jax.ShapeDtypeStruct((all_rows, q_width), F32),
            jax.ShapeDtypeStruct((all_rows, q_width), BF16),
            jax.ShapeDtypeStruct((all_rows, HD), F32),
            jax.ShapeDtypeStruct((heads, all_rows), F32),
        ),
        in_specs=[VM] * 4 + [anywhere] * 2,
        out_specs=(anywhere,) * 9 + (VM,),
        scratch_shapes=[
            pltpu.VMEM((rows, D), BF16),
            pltpu.VMEM((all_rows, D), BF16),
            pltpu.VMEM((D, q_width + 2 * kv_width), BF16),
            pltpu.VMEM((all_rows, q_width), BF16),
            pltpu.VMEM((all_rows, q_width), F32),
            pltpu.VMEM((all_rows, kv_width), F32),
            pltpu.VMEM((count, all_rows, 2 * kv_width), BF16),
            pltpu.VMEM((heads, all_rows, 2 * HD), F32),
            pltpu.VMEM((all_rows, q_width), F32),
            pltpu.VMEM((all_rows, q_width), BF16),
            pltpu.VMEM((all_rows, HD), F32),
        ]
        + dma_sems(6)
        + dma_sems(8 * chips)
        + dma_sems(8 * chips)
        + dma_sems(6)
        + [
            pltpu.SemaphoreType.DMA((3,)),
            pltpu.SemaphoreType.DMA((5,)),
            pltpu.SemaphoreType.DMA((count,)),
            pltpu.SemaphoreType.DMA((2 * heads + 1,)),
        ],
        cost_estimate=cost(1, 1),
        compiler_params=remote_params(8),
    )(tokens, cotangent, gains, rope_freq(), query_weight, keyvalue_weight)


def feed_kernel(x_ref, dy_ref, w_ref, d_ref, act_ref, grad_ref, down_ref):
    x, dy = x_ref[...], dy_ref[...]
    gate = dot(x, w_ref[0])
    upper = dot(x, w_ref[1])
    act_grad = dot_nt(dy, d_ref[...])
    sig = jax.nn.sigmoid(gate)
    swish = gate * sig
    act = (swish * upper).astype(BF16)
    act_ref[...] = act
    grad_ref[0] = (act_grad * upper * sig * (1.0 + gate * (1.0 - sig))).astype(BF16)
    grad_ref[1] = (act_grad * swish).astype(BF16)
    down_ref[...] = dot_tn(act, dy).astype(BF16)


def feed(x, dy, gateup_weight, down_weight):
    rows, width = x.shape[0], down_weight.shape[0]
    tile = 256
    whole = lambda i: (0, 0)
    return pl.pallas_call(
        feed_kernel,
        name="feed",
        grid=(width // tile,),
        out_shape=(
            jax.ShapeDtypeStruct((rows, width), BF16),
            jax.ShapeDtypeStruct((2, rows, width), BF16),
            jax.ShapeDtypeStruct((width, D), BF16),
        ),
        in_specs=[
            pl.BlockSpec((rows, D), whole),
            pl.BlockSpec((rows, D), whole),
            pl.BlockSpec((2, D, tile), lambda i: (0, 0, i)),
            pl.BlockSpec((tile, D), lambda i: (i, 0)),
        ],
        out_specs=(
            pl.BlockSpec((rows, tile), lambda i: (0, i)),
            pl.BlockSpec((2, rows, tile), lambda i: (0, 0, i)),
            pl.BlockSpec((tile, D), lambda i: (i, 0)),
        ),
        compiler_params=params("arbitrary"),
        cost_estimate=cost(8 * rows * D * width, 4 * rows * D + 8 * D * width),
    )(x, dy, gateup_weight, down_weight)


def feed_back_kernel(x_ref, act_ref, grad_ref, w_ref, d_ref, full_ref, in_ref, out_ref, in_acc, out_acc):
    step = pl.program_id(0)

    @pl.when(step == 0)
    def _():
        in_acc[...] = jnp.zeros_like(in_acc)
        out_acc[...] = jnp.zeros_like(out_acc)

    in_acc[...] += dot_nt(grad_ref[0], w_ref[0]) + dot_nt(grad_ref[1], w_ref[1])
    out_acc[...] += dot(act_ref[...], d_ref[...])
    x = x_ref[...]
    full_ref[0] = dot_tn(x, grad_ref[0]).astype(BF16)
    full_ref[1] = dot_tn(x, grad_ref[1]).astype(BF16)

    @pl.when(step == pl.num_programs(0) - 1)
    def _():
        in_ref[...] = in_acc[...].astype(BF16)
        out_ref[...] = out_acc[...].astype(BF16)


def feed_back(x, act, grads, gateup_weight, down_weight):
    rows, width = x.shape[0], down_weight.shape[0]
    tile = 256
    whole = lambda i: (0, 0)
    return pl.pallas_call(
        feed_back_kernel,
        name="feed_back",
        grid=(width // tile,),
        out_shape=(
            jax.ShapeDtypeStruct((2, D, width), BF16),
            jax.ShapeDtypeStruct((rows, D), BF16),
            jax.ShapeDtypeStruct((rows, D), BF16),
        ),
        in_specs=[
            pl.BlockSpec((rows, D), whole),
            pl.BlockSpec((rows, tile), lambda i: (0, i)),
            pl.BlockSpec((2, rows, tile), lambda i: (0, 0, i)),
            pl.BlockSpec((2, D, tile), lambda i: (0, 0, i)),
            pl.BlockSpec((tile, D), lambda i: (i, 0)),
        ],
        out_specs=(
            pl.BlockSpec((2, D, tile), lambda i: (0, 0, i)),
            pl.BlockSpec((rows, D), whole),
            pl.BlockSpec((rows, D), whole),
        ),
        scratch_shapes=[pltpu.VMEM((rows, D), F32), pltpu.VMEM((rows, D), F32)],
        compiler_params=params("arbitrary"),
        cost_estimate=cost(10 * rows * D * width, 8 * rows * D + 10 * D * width),
    )(x, act, grads, gateup_weight, down_weight)


def out_back_kernel(dy_ref, w_ref, low_ref, grad_ref, full_ref):
    dy = dy_ref[...]
    grad_ref[...] = dot_nt(dy, w_ref[...]).astype(BF16)
    full_ref[...] = dot_tn(dy, low_ref[...]).astype(BF16)


def out_back(dy, weight, attn_low):
    rows, width = attn_low.shape
    tile = 256
    whole = lambda i: (0, 0)
    return pl.pallas_call(
        out_back_kernel,
        name="out_back",
        grid=(width // tile,),
        out_shape=(
            jax.ShapeDtypeStruct((rows, width), BF16),
            jax.ShapeDtypeStruct((D, width), BF16),
        ),
        in_specs=[
            pl.BlockSpec((rows, D), whole),
            pl.BlockSpec((tile, D), lambda i: (i, 0)),
            pl.BlockSpec((rows, tile), lambda i: (0, i)),
        ],
        out_specs=(
            pl.BlockSpec((rows, tile), lambda i: (0, i)),
            pl.BlockSpec((D, tile), lambda i: (0, i)),
        ),
        compiler_params=params("arbitrary"),
        cost_estimate=cost(4 * rows * D * width, 2 * rows * D + 4 * D * width),
    )(dy, weight, attn_low)


def project_back_kernel(x_ref, q_ref, kv_ref, wq_ref, wkv_ref, out_ref, in_ref, full_ref):
    q_width, kv_width = wq_ref.shape[1], wkv_ref.shape[2]
    x = x_ref[...]
    key, value = kv_ref[:, :kv_width], kv_ref[:, kv_width:]
    in_ref[...] = (
        dot_nt(q_ref[...], wq_ref[...]) + dot_nt(key, wkv_ref[0]) + dot_nt(value, wkv_ref[1])
    ).astype(BF16)
    full_ref[:, :q_width] = dot_tn(x, q_ref[...]).astype(BF16)
    full_ref[:, q_width : q_width + 2 * kv_width] = dot_tn(x, kv_ref[...]).astype(BF16)
    full_ref[:, q_width + 2 * kv_width :] = out_ref[...]


def project_back(x, q_back, kv_back, query_weight, keyvalue_weight, output_full):
    rows, out_width = x.shape[0], output_full.shape[1]
    q_width, kv_width = query_weight.shape[1], keyvalue_weight.shape[2]
    tile = 512
    whole = lambda i: (0, 0)
    return pl.pallas_call(
        project_back_kernel,
        name="project_back",
        grid=(D // tile,),
        out_shape=(
            jax.ShapeDtypeStruct((rows, D), BF16),
            jax.ShapeDtypeStruct((D, q_width + 2 * kv_width + out_width), BF16),
        ),
        in_specs=[
            pl.BlockSpec((rows, tile), lambda i: (0, i)),
            pl.BlockSpec((rows, q_width), whole),
            pl.BlockSpec((rows, 2 * kv_width), whole),
            pl.BlockSpec((tile, q_width), lambda i: (i, 0)),
            pl.BlockSpec((2, tile, kv_width), lambda i: (0, i, 0)),
            pl.BlockSpec((tile, out_width), lambda i: (i, 0)),
        ],
        out_specs=(
            pl.BlockSpec((rows, tile), lambda i: (0, i)),
            pl.BlockSpec((tile, q_width + 2 * kv_width + out_width), lambda i: (i, 0)),
        ),
        compiler_params=params("arbitrary"),
        cost_estimate=cost(4 * rows * D * (q_width + 2 * kv_width), 6 * D * (q_width + 2 * kv_width)),
    )(x, q_back, kv_back, query_weight, keyvalue_weight, output_full)


def mate_of():
    w = lax.axis_index("wide")
    c = w % 2
    return c, w + 1 - 2 * c


def greet_mate():
    _, mate = mate_of()
    barrier = pltpu.get_barrier_semaphore()
    pl.semaphore_signal(barrier, inc=1, device_id={"wide": mate}, device_id_type=MESH)
    pl.semaphore_wait(barrier, 1)


def project_back_pair_kernel(
    x_ref, q_ref, kv_ref, wq_ref, wkv_ref, out_ref, in_ref, full_ref, stage, inbox, send, recv
):
    step, steps = pl.program_id(0), pl.num_programs(0) - 1
    c, mate = mate_of()
    q_width, kv_width = wq_ref.shape[1], wkv_ref.shape[2]
    part = full_ref.shape[1]

    def trade(i):
        return wide_copy(stage.at[i % 2, 1 - c], inbox.at[i], send, recv, i, mate)

    @pl.when(step == 0)
    def _():
        greet_mate()

    @pl.when((step >= 2) & (step <= steps))
    def _():
        trade(step - 2).wait_send()

    @pl.when(step < steps)
    def _():
        x = x_ref[...]
        q_full = dot_tn(x, q_ref[...]).astype(BF16)
        kv_full = dot_tn(x, kv_ref[...]).astype(BF16)
        for k in range(2):
            at = slice(k * part, (k + 1) * part)
            stage[step % 2, k, :, :q_width] = q_full[at]
            stage[step % 2, k, :, q_width : q_width + 2 * kv_width] = kv_full[at]
            stage[step % 2, k, :, q_width + 2 * kv_width :] = out_ref[at, :]
        trade(step).start()
        key, value = kv_ref[:, :kv_width], kv_ref[:, kv_width:]
        in_ref[...] = (
            dot_nt(q_ref[...], wq_ref[...]) + dot_nt(key, wkv_ref[0]) + dot_nt(value, wkv_ref[1])
        ).astype(BF16)

    @pl.when(step > 0)
    def _():
        last = jnp.maximum(step - 1, 0)
        trade(last).wait_recv()
        full_ref[0] = (stage[last % 2, c].astype(F32) + inbox[last].astype(F32)).astype(BF16)

    @pl.when(step == steps)
    def _():
        trade(step - 1).wait_send()


def project_back_pair(x, q_back, kv_back, query_weight, keyvalue_weight, output_full, count):
    rows, out_width = x.shape[0], output_full.shape[1]
    q_width, kv_width = query_weight.shape[1], keyvalue_weight.shape[2]
    width = q_width + 2 * kv_width + out_width
    part = D // count
    tile = 2 * part
    steps = count // 2
    whole = lambda i: (0, 0)
    now = lambda i: jnp.minimum(i, steps - 1)
    in_partial, full = pl.pallas_call(
        project_back_pair_kernel,
        name="project_back_pair",
        grid=(steps + 1,),
        out_shape=(
            jax.ShapeDtypeStruct((rows, D), BF16),
            jax.ShapeDtypeStruct((steps, part, width), BF16),
        ),
        in_specs=[
            pl.BlockSpec((rows, tile), lambda i: (0, now(i))),
            pl.BlockSpec((rows, q_width), whole),
            pl.BlockSpec((rows, 2 * kv_width), whole),
            pl.BlockSpec((tile, q_width), lambda i: (now(i), 0)),
            pl.BlockSpec((2, tile, kv_width), lambda i: (0, now(i), 0)),
            pl.BlockSpec((tile, out_width), lambda i: (now(i), 0)),
        ],
        out_specs=(
            pl.BlockSpec((rows, tile), lambda i: (0, now(i))),
            pl.BlockSpec((1, part, width), lambda i: (jnp.maximum(i - 1, 0), 0, 0)),
        ),
        scratch_shapes=[
            pltpu.VMEM((2, 2, part, width), BF16),
            pltpu.VMEM((steps, part, width), BF16),
        ]
        + dma_sems(steps),
        cost_estimate=cost(1, 1),
        compiler_params=remote_params(12),
    )(x, q_back, kv_back, query_weight, keyvalue_weight, output_full)
    return in_partial, full.reshape(D // 2, width)


def rest_adamw_kernel(total_hbm, *refs):
    ins, refs = refs[:12], refs[12:]
    results, refs = refs[:15], refs[15:]
    total_ref, refs = refs[0], refs[1:]
    states, refs = refs[:12], refs[12:]
    outs, (in_sem, out_sem) = refs[:15], refs[15:]
    loads = [pltpu.make_async_copy(total_hbm, total_ref, in_sem.at[0])] + [
        pltpu.make_async_copy(ins[n], ref, in_sem.at[1 + n]) for n, ref in enumerate(states)
    ]
    for load in loads:
        load.start()
    q_width, kv_width = outs[0].shape[1], outs[5].shape[2]
    rate = 2.0 * D ** (-0.5)
    stores = [
        pltpu.make_async_copy(src, dst, out_sem.at[n])
        for n, (src, dst) in enumerate(zip(outs, results))
    ]
    for load in loads[:5]:
        load.wait()
    for n, new in enumerate(
        adamw(total_ref[:, :q_width].astype(F32), *[r[...] for r in states[:4]], rate, WEIGHT_DECAY)
    ):
        outs[n][...] = new
        stores[n].start()
    for load in loads[5:9]:
        load.wait()
    for k in range(2):
        low = q_width + k * kv_width
        total = total_ref[:, low : low + kv_width].astype(F32)
        for n, new in enumerate(adamw(total, *[r[k] for r in states[4:8]], rate, WEIGHT_DECAY)):
            outs[5 + n][k] = new
    for n in range(5, 10):
        stores[n].start()
    for load in loads[9:]:
        load.wait()
    turned = jnp.transpose(total_ref[:, q_width + 2 * kv_width :].astype(F32))
    for n, new in enumerate(
        adamw(turned, *[r[...] for r in states[8:]], 2.0 * WO_FAN ** (-0.5), WEIGHT_DECAY)
    ):
        outs[10 + n][...] = new
        stores[10 + n].start()
    for store in stores:
        store.wait()


def rest_adamw(total, states):
    hbm = pl.BlockSpec(memory_space=pltpu.HBM)
    shapes = [states[4 * n].shape for n in range(3) for _ in range(5)]
    out = pl.pallas_call(
        rest_adamw_kernel,
        name="rest_adamw",
        out_shape=tuple(jax.ShapeDtypeStruct(shape, F32) for shape in shapes),
        in_specs=[hbm] * 13,
        out_specs=(hbm,) * 15,
        scratch_shapes=[pltpu.VMEM(total.shape, total.dtype)]
        + [pltpu.VMEM(state.shape, F32) for state in states]
        + [pltpu.VMEM(shape, F32) for shape in shapes]
        + [pltpu.SemaphoreType.DMA((13,)), pltpu.SemaphoreType.DMA((15,))],
        compiler_params=params(),
        cost_estimate=cost(1, 1),
    )(total, *states)
    return out[:5], out[5:10], out[10:]


def wide_scatter(partial, axis):
    return lax.psum_scatter(partial, "wide", scatter_dimension=axis, tiled=True)


def line_scatter(partial, axis, count):
    groups = [[2 * z + c for z in range(count // 2)] for c in range(2)]
    return lax.psum_scatter(
        partial, "wide", scatter_dimension=axis, tiled=True, axis_index_groups=groups
    )


def body(
    tokens,
    cotangent,
    gain_copy,
    query_weight,
    keyvalue_weight,
    output_weight,
    gateup_weight,
    down_weight,
    query_master,
    query_moment,
    query_second,
    query_average,
    keyvalue_master,
    keyvalue_moment,
    keyvalue_second,
    keyvalue_average,
    output_master,
    output_moment,
    output_second,
    output_average,
    gateup_master,
    gateup_moment,
    gateup_second,
    gateup_average,
    down_master,
    down_moment,
    down_second,
    down_average,
    gain_master,
    gain_moment,
    gain_second,
    gain_average,
):
    narrow, wide = lax.axis_size("narrow"), lax.axis_size("wide")
    special = narrow == 4 and wide == 8
    stretch_rows = tokens.shape[0] * narrow
    wide_index = lax.axis_index("wide")
    w_scalar = wide_index.astype(jnp.int32).reshape(1)
    kv_heads = keyvalue_weight.shape[2] // HD
    q_heads = query_weight.shape[1] // HD
    group = q_heads // kv_heads
    q_width, kv_width = q_heads * HD, kv_heads * HD
    gains = gain_copy.reshape(-1, HD)

    if special:
        (
            back_mlp,
            attn_input,
            query_low,
            query_raw,
            key_raw,
            kv_all,
            attn_out,
            attn_low,
            table,
            lse,
        ) = front(tokens, cotangent, gains, query_weight, keyvalue_weight, wide)
    else:
        positions = wide_index * stretch_rows + jnp.arange(stretch_rows, dtype=jnp.int32)
        table = rope_table(positions.astype(F32))
        cosine, sine = cos_sin(
            table, lambda a: jnp.concatenate([a[:, HD // 2 :], a[:, : HD // 2]], axis=1)
        )
        attn_gain = gain_copy[:D].reshape(1, D)
        mlp_gain = gain_copy[D : 2 * D].reshape(1, D)
        query_gain = gain_copy[2 * D : 2 * D + HD].reshape(1, HD)
        key_gain = gain_copy[2 * D + HD :].reshape(1, HD)
        hidden = tokens.astype(F32)
        normed = (hidden * row_scale(hidden) * attn_gain).astype(BF16)
        attn_input = lax.all_gather(normed, "narrow", axis=0, tiled=True)
        kv_low, key_raw = keys_values(attn_input, keyvalue_weight, key_gain, cosine, sine)
        query_low, query_raw = queries(attn_input, query_weight, query_gain, cosine, sine)
        kv_all = lax.all_gather(kv_low, "wide", axis=0)
        attn_out, attn_low, lse = attend(w_scalar, query_low, kv_all, q_heads, group)
        back_mlp = lax.all_gather(cotangent, "narrow", axis=0, tiled=True)
    if special:
        hidden_mid, mlp_input, act_grads, act, down_full = mid_pair(
            attn_low, output_weight, tokens, gains, back_mlp, gateup_weight, down_weight, wide
        )
        down_total = line_scatter(down_full, 0, wide)[0]
        mid_grad, back_attn, mlp_gain_grad, gateup_full = mid_backward_pair(
            hidden_mid, cotangent, gains, mlp_input, act_grads, gateup_weight, wide
        )
        gateup_total = line_scatter(gateup_full, 1, wide)
    else:
        hidden_mid, mlp_input = mid_forward(attn_low, output_weight, tokens, mlp_gain)
        act, act_grads, down_full = feed(mlp_input, back_mlp, gateup_weight, down_weight)
        down_total = wide_scatter(down_full, 1)
        gateup_full, in_partial, out_partial = feed_back(
            mlp_input, act, act_grads, gateup_weight, down_weight
        )
        gateup_total = wide_scatter(gateup_full, 1)
        mid_grad, back_attn, mlp_gain_grad = mid_backward(
            in_partial, hidden_mid, cotangent, mlp_gain
        )
    attn_grad, output_full = out_back(back_attn, output_weight, attn_low)
    query_sum, kv_sums = attend_back(
        w_scalar, query_low, kv_all, attn_grad, attn_out, lse, q_heads, group
    )
    query_back, query_gain_grad = unspin(query_sum, query_raw, gains, 2 * (D // HD), table)
    if special:
        kv_sum, out_sum = return_grads_out(kv_sums, act, down_weight, tokens.shape[0], wide)
        block_output = hidden_mid + out_sum
    else:
        kv_sum = return_grads(kv_sums, wide)
        block_output = hidden_mid + lax.psum_scatter(
            out_partial, "narrow", scatter_dimension=0, tiled=True
        ).astype(F32)
    kv_back, key_gain_grad = unspin(kv_sum, key_raw, gains, 2 * (D // HD) + 1, table)
    back_args = (attn_input, query_back, kv_back, query_weight, keyvalue_weight, output_full)
    if special:
        normed_partial, project_full = project_back_pair(*back_args, wide)
    else:
        normed_partial, project_full = project_back(*back_args)
    project_full, gateup_total, down_total, normed_partial = lax.optimization_barrier(
        (project_full, gateup_total, down_total, normed_partial)
    )
    rest_total = line_scatter(project_full, 0, wide) if special else wide_scatter(project_full, 0)
    in_norm_grad, attn_gain_grad = in_scatter(normed_partial, tokens, gains, special)
    input_grad = mid_grad + in_norm_grad
    gain_partial = jnp.concatenate(
        [attn_gain_grad, mlp_gain_grad, query_gain_grad, key_gain_grad], axis=1
    ).reshape(-1)
    gain_total = gain_sums(gain_partial, wide, narrow, special)

    gateup_new = adamw(
        gateup_total.astype(F32),
        gateup_master,
        gateup_moment,
        gateup_second,
        gateup_average,
        2.0 * D ** (-0.5),
        WEIGHT_DECAY,
    )
    down_new = adamw(
        down_total.astype(F32),
        down_master,
        down_moment,
        down_second,
        down_average,
        2.0 * FF ** (-0.5),
        WEIGHT_DECAY,
    )
    gain_new = adamw(
        gain_total, gain_master, gain_moment, gain_second, gain_average, RATE_GAIN, 0.0
    )
    states = (
        query_master,
        query_moment,
        query_second,
        query_average,
        keyvalue_master,
        keyvalue_moment,
        keyvalue_second,
        keyvalue_average,
        output_master,
        output_moment,
        output_second,
        output_average,
    )
    states, gateup_new, down_new, gain_new, input_grad, block_output = lax.optimization_barrier(
        (states, gateup_new, down_new, gain_new, input_grad, block_output)
    )
    query_new, keyvalue_new, output_new = rest_adamw(rest_total, states)
    return (
        block_output,
        input_grad,
        *query_new,
        *keyvalue_new,
        *output_new,
        *gateup_new,
        *down_new,
        *gain_new,
    )


def solution(mesh):
    rows = P(("wide", "narrow"), None)
    flat = P(("wide", "narrow"))
    stacked = P(None, "wide", "narrow")
    query, output = P("wide", "narrow"), P("narrow", "wide")
    states = (
        *[query] * 4,
        *[stacked] * 4,
        *[output] * 4,
        *[stacked] * 4,
        *[output] * 4,
        *[flat] * 4,
    )
    return jax.shard_map(
        body,
        mesh=mesh,
        in_specs=(
            rows,
            rows,
            P(),
            P(None, "narrow"),
            P(None, None, "narrow"),
            P("narrow", None),
            P(None, None, "narrow"),
            P("narrow", None),
            *states,
        ),
        out_specs=(
            rows,
            rows,
            *[query] * 5,
            *[stacked] * 5,
            *[output] * 5,
            *[stacked] * 5,
            *[output] * 5,
            *[flat] * 5,
        ),
        check_vma=False,
    )
```
